128 devices in a mesh: comp: 4 (over y), lat: 4 (over z), lon: 8 (over x, core).
Axes of the slice: x: 4, y: 4, z: 4, core: 2. Of those that a mesh axis runs over, the one named last changes fastest.
Arguments:
- state: float32 [2048, 1024, 128], P(('comp', 'lat'), 'lon'), may hold values from -6 to 6
- land_mask: int32 [2048, 1024], P(('comp', 'lat'), 'lon'), may hold values 0 or 1
- intersection_list: int32 [2048, 8, 2, 3], P(('comp', 'lat'), 'lon'), may hold values from 0 to 127, as said below
- mix_atm: float32 [128, 128], replicated, may hold values from -0.5 to 0.5
- mix_ocn: float32 [128, 128], replicated, may hold values from -0.5 to 0.5
- flux_map: float32 [128, 8], replicated, may hold values from -0.5 to 0.5
- ocean_map: float32 [8, 128], replicated, may hold values from -2 to 2
- regrid_weights: bfloat16 [32, 128, 128], replicated, may hold values from -0.25 to 0.25
Outputs:
- state_out: float32 [2048, 1024, 128], P(('comp', 'lat'), 'lon')
- surface_out: float32 [2048, 1024], P(('comp', 'lat'), 'lon')
The draws below stay inside these ranges and needn't reach their ends.
Inputs may be any that keep to these rules, and one draw needn't show every extreme that they name: `intersection_list`: entry 0 is an ocean tile lat * 8 + lon, entry 1 a row of that tile below 128, entry 2 a weight block below 32. With t the tile lat * 8 + lon of the list's own rows and r = min(4, 8), the entries of one tile name exactly the 2 r tiles (t + a * 8 + b - (r - 1) // 2) mod (4 * 8) for a in 0, 1 and b in 0 to r - 1, each by exactly 32 entries.
All inputs are finite; a program needn't handle non-finite values. No bound on the sum of `land_mask` on one device may be relied on, other than what follows from the above.
Results may differ from the reference program's by a relative error of at most 0.0012.
Values may be sent and summed in bfloat16 or wider, within the bound.
A program may use at most 192 MiB of HBM per device.

```python
import jax
import jax.numpy as jnp
from jax import lax

RT = 128
CT = 128
LEV = 128
NF = 8
NW = 32
NOV = 2
NR = 2048
NC = 1024
N_COMP = 4
N_LAT = 4
N_LON = 8


def draw_intersection_list(key, part):
    device_total = N_COMP * N_LAT * N_LON
    tile_total = N_LAT * N_LON
    entry_total = NOV * RT
    reach = min(4, N_LON)
    capacity = entry_total // (2 * reach)
    order_key, target_key, weight_key = jax.random.split(jax.random.fold_in(key, 11), 3)
    orders = jax.vmap(lambda one_key: jax.random.permutation(one_key, entry_total))(jax.random.split(order_key, device_total))
    neighbour = orders.astype(jnp.int32) // capacity
    device_ids = jnp.arange(device_total, dtype=jnp.int32)
    tile_ids = device_ids % tile_total
    offsets = neighbour // reach * N_LON + neighbour % reach - (reach - 1) // 2
    owners = (tile_ids[:, None] + offsets + tile_total) % tile_total
    targets = jax.random.randint(target_key, (device_total, entry_total), 0, RT)
    weights = jax.random.randint(weight_key, (device_total, entry_total), 0, NW)
    table = jnp.stack([owners, targets, weights], axis=-1).astype(jnp.int32)
    table = table.reshape(N_COMP, N_LAT, N_LON, RT, NOV, 3).transpose(0, 1, 3, 2, 4, 5)
    return table.reshape(N_COMP * N_LAT * RT, N_LON, NOV, 3)


def set_ends(result, stream_key, low, largest):
    extent = result.shape
    spot = [jax.random.randint(jax.random.fold_in(stream_key, axis), (), 0, extent[axis]) for axis in range(len(extent))]
    result = result.at[tuple(spot)].set(low)
    longest = extent.index(max(extent))
    spot[longest] = (spot[longest] + 1) % extent[longest]
    return result.at[tuple(spot)].set(largest)


def steps_of(key, extent, shards, low, largest):
    def one(axis_at, parts):
        draws = jax.random.uniform(jax.random.fold_in(jax.random.fold_in(key, 6), axis_at), (parts,), jnp.float32, low / len(shards), largest / len(shards))
        return jnp.repeat(jnp.exp(draws), extent[axis_at] // parts).reshape((-1,) + (1,) * (len(extent) - axis_at - 1))

    gain = one(*shards[0])
    for cut in shards[1:]:
        gain = gain * one(*cut)
    return gain


def normal_values(stream_key, dims, scale, most, cuts=(), kind=jnp.bfloat16):
    values = scale * jax.random.normal(stream_key, dims, jnp.float32)
    if cuts:
        values = values * steps_of(stream_key, dims, cuts, -0.22, 0.18)
    return jnp.clip(values, -most, most).astype(kind)


def setup_inputs(seed: int = 0) -> dict:
    keys = jax.random.split(jax.random.key(seed), 9)
    return {
        "state": normal_values(keys[0], (NR, NC, LEV), 1.0, 6.0, ((0, 16), (1, 8)), jnp.float32),
        "land_mask": set_ends((jax.random.randint(keys[1], (NR, NC), 0, 10) < 7).astype(jnp.int32), jax.random.fold_in(keys[1], 1), 0, 1),
        "intersection_list": draw_intersection_list(jax.random.fold_in(keys[8], 71), 0),
        "mix_atm": normal_values(keys[3], (LEV, LEV), LEV ** -0.5, 0.5, (), jnp.float32),
        "mix_ocn": normal_values(keys[4], (LEV, LEV), LEV ** -0.5, 0.5, (), jnp.float32),
        "flux_map": normal_values(keys[5], (LEV, NF), LEV ** -0.5, 0.5, (), jnp.float32),
        "ocean_map": normal_values(keys[6], (NF, LEV), NF ** -0.5, 2.0, (), jnp.float32),
        "regrid_weights": normal_values(keys[7], (NW, CT, CT), (4 * CT) ** -0.5, 0.25),
    }


SMOOTHING = 0.2
PHYSICS = 0.5
HIGHEST = lax.Precision.HIGHEST


def laplace(values):
    padded = jnp.pad(values, ((1, 1), (0, 0), (0, 0)))
    left_side = jnp.roll(values, 1, axis=1)
    right_side = jnp.roll(values, -1, axis=1)
    return padded[:-2] + padded[2:] + left_side + right_side - 4.0 * values


def column_physics(values, mixing):
    return jnp.tanh(jnp.einsum('rck,kj->rcj', values, mixing, precision=HIGHEST))


def reference(state, land_mask, intersection_list, mix_atm, mix_ocn, flux_map, ocean_map, regrid_weights):
    atm_rows = (N_COMP - 1) * N_LAT * RT
    tile_total = N_LAT * N_LON
    atmosphere = state[:atm_rows]
    ocean = state[atm_rows:]
    sea_atm = land_mask[:atm_rows] == 1
    sea_ocn = land_mask[atm_rows:] == 1
    flux_total = jnp.zeros((NF, atm_rows, N_LON * CT), jnp.float32)
    for substep in range(2):
        smooth = atmosphere + SMOOTHING * laplace(atmosphere)
        atmosphere = smooth + PHYSICS * column_physics(smooth, mix_atm)
        flux_total = flux_total + jnp.einsum('rck,kf->frc', atmosphere, flux_map, precision=HIGHEST)
    flux_sent = jnp.where(sea_atm[None], 0.5 * flux_total, 0.0).astype(jnp.bfloat16)
    blocks = flux_sent.astype(jnp.float32).reshape(NF, atm_rows, N_LON, CT).transpose(1, 2, 0, 3)
    lists = intersection_list[:atm_rows]
    owners = lists[..., 0].astype(jnp.int32)
    targets = lists[..., 1].astype(jnp.int32)
    weight_ids = lists[..., 2].astype(jnp.int32)
    segment = (weight_ids * tile_total + owners) * RT + targets
    entries = jnp.broadcast_to(blocks[:, :, None], (atm_rows, N_LON, NOV, NF, CT)).reshape(-1, NF * CT)
    binned = jax.ops.segment_sum(entries, segment.reshape(-1), num_segments=NW * tile_total * RT)
    binned = binned.reshape(NW, tile_total * RT, NF, CT)
    weights_wide = regrid_weights.astype(jnp.float32)

    def add_block(total, pair):
        part, weight = pair
        return total + jnp.einsum('qfa,ab->qfb', part, weight, precision=HIGHEST), None

    regridded, _ = lax.scan(add_block, jnp.zeros((tile_total * RT, NF, CT), jnp.float32), (binned, weights_wide))
    forcing = regridded.reshape(N_LAT, N_LON, RT, NF, CT).transpose(3, 0, 2, 1, 4).reshape(NF, N_LAT * RT, N_LON * CT)
    smooth = ocean + SMOOTHING * laplace(ocean)
    moved = smooth + jnp.einsum('frc,fk->rck', forcing, ocean_map, precision=HIGHEST) + PHYSICS * column_physics(smooth, mix_ocn)
    ocean_new = jnp.where(sea_ocn[..., None], moved, ocean)
    surface_ocean = ocean_new[..., 0]
    surface_blocks = surface_ocean.reshape(N_LAT, RT, N_LON, CT).transpose(0, 2, 1, 3).reshape(tile_total * RT, CT)
    picked = jnp.take(surface_blocks, (owners * RT + targets).reshape(-1), axis=0).reshape(-1, NOV, CT)
    flat_ids = weight_ids.reshape(-1, NOV)

    def pull(total, pair):
        index, weight = pair
        term = jnp.einsum('enb,ab->ena', picked, weight, precision=HIGHEST)
        return total + jnp.where((flat_ids == index)[..., None], term, 0.0), None

    pulled, _ = lax.scan(pull, jnp.zeros(picked.shape, jnp.float32), (jnp.arange(NW, dtype=jnp.int32), weights_wide))
    returned = pulled.sum(axis=1).reshape(atm_rows, N_LON * CT)
    surface_atm = jnp.where(sea_atm, returned, atmosphere[..., 0])
    state_out = jnp.concatenate([atmosphere, ocean_new], axis=0)
    surface_out = jnp.concatenate([surface_atm, surface_ocean], axis=0)
    return state_out, surface_out
```

```python
import jax
import jax.numpy as jnp
from jax import lax
from jax.sharding import PartitionSpec as P

SMOOTHING = 0.2
PHYSICS = 0.5
HIGHEST = lax.Precision.HIGHEST


def from_behind(value, axis, steps):
    count = lax.axis_size(axis)
    pairs = [(source, (source + steps) % count) for source in range(count)]
    return lax.ppermute(value, axis, pairs)


def shortened(shard):
    return jax.tree.map(lambda a: a.astype(jnp.bfloat16) if a.dtype == jnp.float32 else a, shard)


def column_physics(values, mixing):
    return jnp.tanh(jnp.einsum("rck,kj->rcj", values, mixing, precision=HIGHEST))


def earlier_same(owners, usable):
    positions = jnp.arange(owners.shape[0], dtype=jnp.int32)
    before = (
        (owners[None, :] == owners[:, None])
        & (positions[None, :] < positions[:, None])
        & usable[None, :]
    )
    return jnp.sum(before.astype(jnp.int32), axis=1)


def pack_rows(blocks, owners, labels, usable, slots_each, owner_total):
    ranks = earlier_same(owners, usable)
    target_slot = owners * slots_each + ranks
    slot_ids = jnp.arange(owner_total * slots_each, dtype=jnp.int32)
    placing = (slot_ids[:, None] == target_slot[None, :]) & usable[None, :]
    packed = jnp.dot(
        placing.astype(jnp.bfloat16), blocks, preferred_element_type=jnp.float32
    ).astype(jnp.bfloat16)
    placed_labels = jnp.sum(jnp.where(placing, labels[None, :] + 1, 0), axis=1) - 1
    return (
        packed.reshape(owner_total, slots_each, blocks.shape[1]),
        placed_labels.reshape(owner_total, slots_each),
    )


def edge_rows(values, lower_valid, upper_valid):
    bands = lax.axis_size("comp") * lax.axis_size("lat")
    up = [(i, i + 1) for i in range(bands - 1)]
    down = [(j, i) for i, j in up]
    before = lax.ppermute(values[-1:], ("comp", "lat"), up)
    after = lax.ppermute(values[:1], ("comp", "lat"), down)
    return (jnp.where(lower_valid, before, 0.0), jnp.where(upper_valid, after, 0.0))


def edge_columns(values):
    size = lax.axis_size("lon")
    up = [(i, (i + 1) % size) for i in range(size)]
    down = [(j, i) for i, j in up]
    before = lax.ppermute(values[:, -1:], "lon", up)
    after = lax.ppermute(values[:, :1], "lon", down)
    return before, after


def laplace_local(values, lower_valid, upper_valid):
    top, bottom = edge_rows(values, lower_valid, upper_valid)
    left, right = edge_columns(values)
    up = jnp.concatenate([top, values[:-1]], axis=0)
    down = jnp.concatenate([values[1:], bottom], axis=0)
    west = jnp.concatenate([left, values[:, :-1]], axis=1)
    east = jnp.concatenate([values[:, 1:], right], axis=1)
    return up + down + west + east - 4.0 * values


def physics_step(values, spread, mixing):
    smooth = values + SMOOTHING * spread
    mixed = jnp.einsum("rck,kj->rcj", smooth, mixing, precision=lax.Precision.HIGH)
    return smooth + PHYSICS * jnp.tanh(mixed)


def local(
    state, land_mask, intersection_list, mix_atm, mix_ocn, flux_map, ocean_map, regrid_weights
):
    tile_rows, block_len, levels = state.shape
    flux_count = flux_map.shape[1]
    weight_count = regrid_weights.shape[0]
    intersections = intersection_list.shape[2]
    comp_count = lax.axis_size("comp")
    lat_count = lax.axis_size("lat")
    lon_count = lax.axis_size("lon")
    tile_count = lat_count * lon_count
    reach = min(4, lon_count)
    neighbour_count = 2 * reach
    capacity = intersections * tile_rows // neighbour_count
    quarter = capacity // comp_count
    width = flux_count * block_len
    comp_index = lax.axis_index("comp")
    tile_index = lax.axis_index("lat") * lon_count + lax.axis_index("lon")
    band = comp_index * lat_count + lax.axis_index("lat")
    ocean_band = (comp_count - 1) * lat_count
    ocean_side = comp_index == comp_count - 1
    lower_valid = (band > 0) & ((band - 1 >= ocean_band) == (band >= ocean_band))
    upper_valid = (band < comp_count * lat_count - 1) & (
        (band + 1 >= ocean_band) == (band >= ocean_band)
    )
    sea_cells = land_mask == 1

    spread = laplace_local(state, lower_valid, upper_valid)
    first = lax.cond(
        ocean_side,
        lambda v, s: physics_step(v, s, mix_ocn),
        lambda v, s: physics_step(v, s, mix_atm),
        state,
        spread,
    )
    spread_next = laplace_local(first, lower_valid, upper_valid)

    def atmosphere_second(values, spread_now):
        moved = physics_step(values, spread_now, mix_atm)
        total = jnp.einsum("rck,kf->frc", values + moved, flux_map, precision=HIGHEST)
        return moved, jnp.where(sea_cells[None], 0.5 * total, 0.0).astype(jnp.bfloat16)

    def ocean_second(values, spread_now):
        return values, jnp.zeros((flux_count, tile_rows, block_len), jnp.bfloat16)

    second, flux_sent = lax.cond(ocean_side, ocean_second, atmosphere_second, first, spread_next)
    entry_list = intersection_list.reshape(tile_rows * intersections, 3)
    owners = entry_list[:, 0]
    targets = entry_list[:, 1]
    weight_ids = entry_list[:, 2]
    labels = weight_ids * tile_rows + targets
    entry_blocks = jnp.repeat(flux_sent.transpose(1, 0, 2), intersections, axis=0).reshape(
        tile_rows * intersections, width
    )
    sending = jnp.broadcast_to(jnp.logical_not(ocean_side), owners.shape)
    offsets = [
        (n // reach * lon_count + n % reach - (reach - 1) // 2) % tile_count
        for n in range(neighbour_count)
    ]
    offset_table = jnp.array(offsets, jnp.int32)
    distance = (owners - tile_index + tile_count) % tile_count
    neighbour_ids = jnp.sum(
        jnp.where(
            distance[:, None] == offset_table[None, :],
            jnp.arange(neighbour_count, dtype=jnp.int32)[None, :],
            0,
        ),
        axis=1,
    )
    packed, packed_labels = pack_rows(
        entry_blocks, neighbour_ids, labels, sending, capacity, neighbour_count
    )
    moved_blocks = []
    moved_labels = []
    for neighbour in range(neighbour_count):
        if offsets[neighbour] == 0:
            one_blocks, one_labels = (packed[neighbour], packed_labels[neighbour])
        else:
            one_blocks, one_labels = from_behind(
                (packed[neighbour], packed_labels[neighbour]), ("lat", "lon"), offsets[neighbour]
            )
        moved_blocks.append(one_blocks)
        moved_labels.append(one_labels)
    stacked_blocks = jnp.stack(moved_blocks).reshape(neighbour_count, comp_count, quarter, width)
    stacked_labels = jnp.stack(moved_labels).reshape(neighbour_count, comp_count, quarter)
    arrived, arrived_labels = (
        lax.all_to_all(stacked_blocks, "comp", split_axis=1, concat_axis=1, tiled=True),
        lax.all_to_all(
            shortened(stacked_labels), "comp", split_axis=1, concat_axis=1, tiled=True
        ).astype(stacked_labels.dtype),
    )
    weights_wide = regrid_weights.astype(jnp.float32)
    label_ids = jnp.arange(weight_count * tile_rows, dtype=jnp.int32)
    flat_labels = arrived_labels.reshape(-1)
    selector = (flat_labels[:, None] == label_ids[None, :]).astype(jnp.bfloat16)
    binned = lax.dot_general(
        selector,
        arrived.reshape(flat_labels.shape[0], width),
        (((0,), (0,)), ((), ())),
        preferred_element_type=jnp.float32,
    )
    binned = binned.reshape(weight_count, tile_rows, flux_count, block_len)
    partial_forcing = jnp.einsum("wdfa,wab->fdb", binned, weights_wide, precision=HIGHEST)
    forcing = lax.psum(partial_forcing, "comp")

    def ocean_final(values):
        moved = values + jnp.einsum("frc,fk->rck", forcing, ocean_map, precision=HIGHEST)
        return jnp.where(sea_cells[:, :, None], moved, state)

    final_state = lax.cond(ocean_side, ocean_final, lambda values: values, second)
    surface = final_state[:, :, 0]
    ocean_only = lax.psum(jnp.where(ocean_side, surface, 0.0), "comp")
    ocean_surface = lax.all_gather(ocean_only, ("lat", "lon"), axis=0, tiled=True)
    picked = jnp.take(ocean_surface, owners * tile_rows + targets, axis=0)
    images = jnp.einsum("eb,wab->ewa", picked, weights_wide, precision=HIGHEST)
    which_block = weight_ids[:, None] == jnp.arange(weight_count, dtype=jnp.int32)[None, :]
    chosen = jnp.sum(jnp.where(which_block[:, :, None], images, 0.0), axis=1)
    returned = chosen.reshape(tile_rows, intersections, block_len).sum(axis=1)
    surface_out = jnp.where(ocean_side, surface, jnp.where(sea_cells, returned, surface))
    return (final_state, surface_out)


def solution(mesh):
    placed = (
        P(("comp", "lat"), "lon", None),
        P(("comp", "lat"), "lon"),
        P(("comp", "lat"), "lon", None, None),
        P(),
        P(),
        P(),
        P(),
        P(),
    )
    return jax.shard_map(
        local,
        mesh=mesh,
        in_specs=placed,
        out_specs=(P(("comp", "lat"), "lon", None), P(("comp", "lat"), "lon")),
        check_vma=False,
    )
```

```python
import jax
import jax.numpy as jnp
from jax import lax
from jax.experimental import pallas as pl
from jax.experimental.pallas import tpu as pltpu
from jax.sharding import PartitionSpec as P
import functools

SMOOTHING = 0.2
PHYSICS = 0.5
HIGHEST = lax.Precision.HIGHEST
ROW_BLOCK = 8


def split_bf16(values):
    high = values.astype(jnp.bfloat16)
    low = (values - high.astype(jnp.float32)).astype(jnp.bfloat16)
    return high, low


def three_pass(lhs, rhs, dims):
    lhs_hi, lhs_lo = split_bf16(lhs)
    rhs_hi, rhs_lo = split_bf16(rhs)

    def one(a, b):
        return lax.dot_general(a, b, (dims, ((), ())), preferred_element_type=jnp.float32)

    return one(lhs_hi, rhs_hi) + (one(lhs_hi, rhs_lo) + one(lhs_lo, rhs_hi))


def substep_kernel(with_flux, x_ref, top_ref, bottom_ref, west_ref, east_ref, mix_ref, *rest):
    if with_flux:
        fluxes_ref, out_ref, flux_out_ref = rest
    else:
        (out_ref,) = rest
    rows, cols, levels = x_ref.shape
    centre = x_ref[...]
    up = jnp.concatenate([top_ref[...], centre[:-1]], axis=0)
    down = jnp.concatenate([centre[1:], bottom_ref[...]], axis=0)
    column = lax.broadcasted_iota(jnp.int32, centre.shape, 1)
    west = jnp.where(column == 0, west_ref[...], pltpu.roll(centre, 1, 1))
    east = jnp.where(column == cols - 1, east_ref[...], pltpu.roll(centre, cols - 1, 1))
    smooth = centre + SMOOTHING * (up + down + west + east - 4.0 * centre)
    flat = smooth.reshape(rows * cols, levels)
    mixed = three_pass(flat, mix_ref[...], ((1,), (0,)))
    moved = flat + PHYSICS * jnp.tanh(mixed)
    out_ref[...] = moved.reshape(rows, cols, levels)
    if with_flux:
        total = centre.reshape(rows * cols, levels) + moved
        flux_out_ref[...] = three_pass(fluxes_ref[...], total, ((1,), (1,)))


def substep(values, top, bottom, west, east, mixing, fluxes_t=None):
    rows, cols, levels = values.shape
    blocks = rows // ROW_BLOCK
    top_rows = jnp.concatenate([top, values[ROW_BLOCK - 1 : rows - 1 : ROW_BLOCK]], axis=0)
    bottom_rows = jnp.concatenate([values[ROW_BLOCK:rows:ROW_BLOCK], bottom], axis=0)
    with_flux = fluxes_t is not None
    in_specs = [
        pl.BlockSpec((ROW_BLOCK, cols, levels), lambda i: (i, 0, 0)),
        pl.BlockSpec((1, cols, levels), lambda i: (i, 0, 0)),
        pl.BlockSpec((1, cols, levels), lambda i: (i, 0, 0)),
        pl.BlockSpec((ROW_BLOCK, 1, levels), lambda i: (i, 0, 0)),
        pl.BlockSpec((ROW_BLOCK, 1, levels), lambda i: (i, 0, 0)),
        pl.BlockSpec((levels, levels), lambda i: (0, 0)),
    ]
    operands = [values, top_rows, bottom_rows, west, east, mixing]
    out_shape = [jax.ShapeDtypeStruct(values.shape, jnp.float32)]
    out_specs = [pl.BlockSpec((ROW_BLOCK, cols, levels), lambda i: (i, 0, 0))]
    if with_flux:
        flux_count = fluxes_t.shape[0]
        in_specs.append(pl.BlockSpec((flux_count, levels), lambda i: (0, 0)))
        operands.append(fluxes_t)
        out_shape.append(jax.ShapeDtypeStruct((flux_count, rows * cols), jnp.float32))
        out_specs.append(pl.BlockSpec((flux_count, ROW_BLOCK * cols), lambda i: (0, i)))
    cells = rows * cols
    flops = 6 * cells * levels * levels + (6 * cells * levels * 8 if with_flux else 0)
    result = pl.pallas_call(
        functools.partial(substep_kernel, with_flux),
        grid=(blocks,),
        in_specs=in_specs,
        out_specs=out_specs,
        out_shape=out_shape,
        cost_estimate=pl.CostEstimate(
            flops=flops, transcendentals=cells * levels, bytes_accessed=8 * cells * levels
        ),
    )(*operands)
    return result


def from_behind(value, axis, steps):
    count = lax.axis_size(axis)
    pairs = [(source, (source + steps) % count) for source in range(count)]
    return lax.ppermute(value, axis, pairs)


def shortened(shard):
    return jax.tree.map(lambda a: a.astype(jnp.bfloat16) if a.dtype == jnp.float32 else a, shard)


def column_physics(values, mixing):
    return jnp.tanh(jnp.einsum("rck,kj->rcj", values, mixing, precision=HIGHEST))


def earlier_same(owners, usable):
    positions = jnp.arange(owners.shape[0], dtype=jnp.int32)
    before = (
        (owners[None, :] == owners[:, None])
        & (positions[None, :] < positions[:, None])
        & usable[None, :]
    )
    return jnp.sum(before.astype(jnp.int32), axis=1)


def pack_rows(blocks, owners, labels, usable, slots_each, owner_total):
    ranks = earlier_same(owners, usable)
    target_slot = owners * slots_each + ranks
    slot_ids = jnp.arange(owner_total * slots_each, dtype=jnp.int32)
    placing = (slot_ids[:, None] == target_slot[None, :]) & usable[None, :]
    packed = jnp.dot(
        placing.astype(jnp.bfloat16), blocks, preferred_element_type=jnp.float32
    ).astype(jnp.bfloat16)
    placed_labels = jnp.sum(jnp.where(placing, labels[None, :] + 1, 0), axis=1) - 1
    return (
        packed.reshape(owner_total, slots_each, blocks.shape[1]),
        placed_labels.reshape(owner_total, slots_each),
    )


def edge_rows(values, lower_valid, upper_valid):
    bands = lax.axis_size("comp") * lax.axis_size("lat")
    up = [(i, i + 1) for i in range(bands - 1)]
    down = [(j, i) for i, j in up]
    before = lax.ppermute(values[-1:], ("comp", "lat"), up)
    after = lax.ppermute(values[:1], ("comp", "lat"), down)
    return (jnp.where(lower_valid, before, 0.0), jnp.where(upper_valid, after, 0.0))


def edge_columns(values):
    size = lax.axis_size("lon")
    up = [(i, (i + 1) % size) for i in range(size)]
    down = [(j, i) for i, j in up]
    before = lax.ppermute(values[:, -1:], "lon", up)
    after = lax.ppermute(values[:, :1], "lon", down)
    return before, after


def local(
    state, land_mask, intersection_list, mix_atm, mix_ocn, flux_map, ocean_map, regrid_weights
):
    tile_rows, block_len, levels = state.shape
    flux_count = flux_map.shape[1]
    weight_count = regrid_weights.shape[0]
    intersections = intersection_list.shape[2]
    comp_count = lax.axis_size("comp")
    lat_count = lax.axis_size("lat")
    lon_count = lax.axis_size("lon")
    tile_count = lat_count * lon_count
    reach = min(4, lon_count)
    neighbour_count = 2 * reach
    capacity = intersections * tile_rows // neighbour_count
    quarter = capacity // comp_count
    width = flux_count * block_len
    comp_index = lax.axis_index("comp")
    tile_index = lax.axis_index("lat") * lon_count + lax.axis_index("lon")
    band = comp_index * lat_count + lax.axis_index("lat")
    ocean_band = (comp_count - 1) * lat_count
    ocean_side = comp_index == comp_count - 1
    lower_valid = (band > 0) & ((band - 1 >= ocean_band) == (band >= ocean_band))
    upper_valid = (band < comp_count * lat_count - 1) & (
        (band + 1 >= ocean_band) == (band >= ocean_band)
    )
    sea_cells = land_mask == 1

    top, bottom = edge_rows(state, lower_valid, upper_valid)
    west, east = edge_columns(state)
    mixing = jnp.where(ocean_side, mix_ocn, mix_atm)
    (first,) = substep(state, top, bottom, west, east, mixing)
    top, bottom = edge_rows(first, lower_valid, upper_valid)
    west, east = edge_columns(first)

    def atmosphere_second(values, top, bottom, west, east):
        moved, total = substep(values, top, bottom, west, east, mix_atm, flux_map.T)
        total = total.reshape(flux_count, tile_rows, block_len)
        return moved, jnp.where(sea_cells[None], 0.5 * total, 0.0).astype(jnp.bfloat16)

    def ocean_second(values, top, bottom, west, east):
        return values, jnp.zeros((flux_count, tile_rows, block_len), jnp.bfloat16)

    second, flux_sent = lax.cond(
        ocean_side, ocean_second, atmosphere_second, first, top, bottom, west, east
    )
    entry_list = intersection_list.reshape(tile_rows * intersections, 3)
    owners = entry_list[:, 0]
    targets = entry_list[:, 1]
    weight_ids = entry_list[:, 2]
    labels = weight_ids * tile_rows + targets
    entry_blocks = jnp.repeat(flux_sent.transpose(1, 0, 2), intersections, axis=0).reshape(
        tile_rows * intersections, width
    )
    sending = jnp.broadcast_to(jnp.logical_not(ocean_side), owners.shape)
    offsets = [
        (n // reach * lon_count + n % reach - (reach - 1) // 2) % tile_count
        for n in range(neighbour_count)
    ]
    offset_table = jnp.array(offsets, jnp.int32)
    distance = (owners - tile_index + tile_count) % tile_count
    neighbour_ids = jnp.sum(
        jnp.where(
            distance[:, None] == offset_table[None, :],
            jnp.arange(neighbour_count, dtype=jnp.int32)[None, :],
            0,
        ),
        axis=1,
    )
    packed, packed_labels = pack_rows(
        entry_blocks, neighbour_ids, labels, sending, capacity, neighbour_count
    )
    moved_blocks = []
    moved_labels = []
    for neighbour in range(neighbour_count):
        if offsets[neighbour] == 0:
            one_blocks, one_labels = (packed[neighbour], packed_labels[neighbour])
        else:
            one_blocks, one_labels = from_behind(
                (packed[neighbour], packed_labels[neighbour]), ("lat", "lon"), offsets[neighbour]
            )
        moved_blocks.append(one_blocks)
        moved_labels.append(one_labels)
    stacked_blocks = jnp.stack(moved_blocks).reshape(neighbour_count, comp_count, quarter, width)
    stacked_labels = jnp.stack(moved_labels).reshape(neighbour_count, comp_count, quarter)
    arrived, arrived_labels = (
        lax.all_to_all(stacked_blocks, "comp", split_axis=1, concat_axis=1, tiled=True),
        lax.all_to_all(
            shortened(stacked_labels), "comp", split_axis=1, concat_axis=1, tiled=True
        ).astype(stacked_labels.dtype),
    )
    weights_wide = regrid_weights.astype(jnp.float32)
    label_ids = jnp.arange(weight_count * tile_rows, dtype=jnp.int32)
    flat_labels = arrived_labels.reshape(-1)
    selector = (flat_labels[:, None] == label_ids[None, :]).astype(jnp.bfloat16)
    binned = lax.dot_general(
        selector,
        arrived.reshape(flat_labels.shape[0], width),
        (((0,), (0,)), ((), ())),
        preferred_element_type=jnp.float32,
    )
    binned = binned.reshape(weight_count, tile_rows, flux_count, block_len)
    partial_forcing = jnp.einsum("wdfa,wab->fdb", binned, weights_wide, precision=HIGHEST)
    forcing = lax.psum(partial_forcing, "comp")

    def ocean_final(values):
        moved = values + jnp.einsum("frc,fk->rck", forcing, ocean_map, precision=HIGHEST)
        return jnp.where(sea_cells[:, :, None], moved, state)

    final_state = lax.cond(ocean_side, ocean_final, lambda values: values, second)
    surface = final_state[:, :, 0]
    ocean_only = lax.psum(jnp.where(ocean_side, surface, 0.0), "comp")
    ocean_surface = lax.all_gather(ocean_only, ("lat", "lon"), axis=0, tiled=True)
    picked = jnp.take(ocean_surface, owners * tile_rows + targets, axis=0)
    images = jnp.einsum("eb,wab->ewa", picked, weights_wide, precision=HIGHEST)
    which_block = weight_ids[:, None] == jnp.arange(weight_count, dtype=jnp.int32)[None, :]
    chosen = jnp.sum(jnp.where(which_block[:, :, None], images, 0.0), axis=1)
    returned = chosen.reshape(tile_rows, intersections, block_len).sum(axis=1)
    surface_out = jnp.where(ocean_side, surface, jnp.where(sea_cells, returned, surface))
    return (final_state, surface_out)


def solution(mesh):
    placed = (
        P(("comp", "lat"), "lon", None),
        P(("comp", "lat"), "lon"),
        P(("comp", "lat"), "lon", None, None),
        P(),
        P(),
        P(),
        P(),
        P(),
    )
    return jax.shard_map(
        local,
        mesh=mesh,
        in_specs=placed,
        out_specs=(P(("comp", "lat"), "lon", None), P(("comp", "lat"), "lon")),
        check_vma=False,
    )
```

```python
import jax
import jax.numpy as jnp
from jax import lax
from jax.experimental import pallas as pl
from jax.experimental.pallas import tpu as pltpu
from jax.sharding import PartitionSpec as P
import functools

SMOOTHING = 0.2
PHYSICS = 0.5
HIGHEST = lax.Precision.HIGHEST
ROW_BLOCK = 8


def split_bf16(values):
    high = values.astype(jnp.bfloat16)
    low = (values - high.astype(jnp.float32)).astype(jnp.bfloat16)
    return high, low


def three_pass(lhs, rhs, dims):
    lhs_hi, lhs_lo = split_bf16(lhs)
    rhs_hi, rhs_lo = split_bf16(rhs)

    def one(a, b):
        return lax.dot_general(a, b, (dims, ((), ())), preferred_element_type=jnp.float32)

    return one(lhs_hi, rhs_hi) + (one(lhs_hi, rhs_lo) + one(lhs_lo, rhs_hi))


def substep_kernel(with_flux, x_ref, top_ref, bottom_ref, west_ref, east_ref, mix_ref, *rest):
    if with_flux:
        fluxes_ref, out_ref, flux_out_ref = rest
    else:
        (out_ref,) = rest
    rows, cols, levels = x_ref.shape
    centre = x_ref[...]
    up = jnp.concatenate([top_ref[...], centre[:-1]], axis=0)
    down = jnp.concatenate([centre[1:], bottom_ref[...]], axis=0)
    column = lax.broadcasted_iota(jnp.int32, centre.shape, 1)
    west = jnp.where(column == 0, west_ref[...], pltpu.roll(centre, 1, 1))
    east = jnp.where(column == cols - 1, east_ref[...], pltpu.roll(centre, cols - 1, 1))
    smooth = centre + SMOOTHING * (up + down + west + east - 4.0 * centre)
    flat = smooth.reshape(rows * cols, levels)
    mixed = three_pass(flat, mix_ref[...], ((1,), (0,)))
    moved = flat + PHYSICS * jnp.tanh(mixed)
    out_ref[...] = moved.reshape(rows, cols, levels)
    if with_flux:
        total = centre.reshape(rows * cols, levels) + moved
        flux_out_ref[...] = three_pass(fluxes_ref[...], total, ((1,), (1,)))


def substep(values, top, bottom, west, east, mixing, fluxes_t=None):
    rows, cols, levels = values.shape
    blocks = rows // ROW_BLOCK
    top_rows = jnp.concatenate([top, values[ROW_BLOCK - 1 : rows - 1 : ROW_BLOCK]], axis=0)
    bottom_rows = jnp.concatenate([values[ROW_BLOCK:rows:ROW_BLOCK], bottom], axis=0)
    with_flux = fluxes_t is not None
    in_specs = [
        pl.BlockSpec((ROW_BLOCK, cols, levels), lambda i: (i, 0, 0)),
        pl.BlockSpec((1, cols, levels), lambda i: (i, 0, 0)),
        pl.BlockSpec((1, cols, levels), lambda i: (i, 0, 0)),
        pl.BlockSpec((ROW_BLOCK, 1, levels), lambda i: (i, 0, 0)),
        pl.BlockSpec((ROW_BLOCK, 1, levels), lambda i: (i, 0, 0)),
        pl.BlockSpec((levels, levels), lambda i: (0, 0)),
    ]
    operands = [values, top_rows, bottom_rows, west, east, mixing]
    out_shape = [jax.ShapeDtypeStruct(values.shape, jnp.float32)]
    out_specs = [pl.BlockSpec((ROW_BLOCK, cols, levels), lambda i: (i, 0, 0))]
    if with_flux:
        flux_count = fluxes_t.shape[0]
        in_specs.append(pl.BlockSpec((flux_count, levels), lambda i: (0, 0)))
        operands.append(fluxes_t)
        out_shape.append(jax.ShapeDtypeStruct((flux_count, rows * cols), jnp.float32))
        out_specs.append(pl.BlockSpec((flux_count, ROW_BLOCK * cols), lambda i: (0, i)))
    cells = rows * cols
    flops = 6 * cells * levels * levels + (6 * cells * levels * 8 if with_flux else 0)
    result = pl.pallas_call(
        functools.partial(substep_kernel, with_flux),
        grid=(blocks,),
        in_specs=in_specs,
        out_specs=out_specs,
        out_shape=out_shape,
        cost_estimate=pl.CostEstimate(
            flops=flops, transcendentals=cells * levels, bytes_accessed=8 * cells * levels
        ),
    )(*operands)
    return result


def column_physics(values, mixing):
    return jnp.tanh(jnp.einsum("rck,kj->rcj", values, mixing, precision=HIGHEST))


def earlier_same(owners, usable):
    positions = jnp.arange(owners.shape[0], dtype=jnp.int32)
    before = (
        (owners[None, :] == owners[:, None])
        & (positions[None, :] < positions[:, None])
        & usable[None, :]
    )
    return jnp.sum(before.astype(jnp.int32), axis=1)


def pack_rows(blocks, owners, labels, usable, slots_each, owner_total):
    ranks = earlier_same(owners, usable)
    target_slot = owners * slots_each + ranks
    slot_ids = jnp.arange(owner_total * slots_each, dtype=jnp.int32)
    placing = (slot_ids[:, None] == target_slot[None, :]) & usable[None, :]
    packed = jnp.dot(
        placing.astype(jnp.bfloat16), blocks, preferred_element_type=jnp.float32
    ).astype(jnp.bfloat16)
    placed_labels = jnp.sum(jnp.where(placing, labels[None, :] + 1, 0), axis=1) - 1
    return (
        packed.reshape(owner_total, slots_each, blocks.shape[1]),
        placed_labels.reshape(owner_total, slots_each),
    )


def edge_rows(values, lower_valid, upper_valid):
    bands = lax.axis_size("comp") * lax.axis_size("lat")
    up = [(i, i + 1) for i in range(bands - 1)]
    down = [(j, i) for i, j in up]
    before = lax.ppermute(values[-1:], ("comp", "lat"), up)
    after = lax.ppermute(values[:1], ("comp", "lat"), down)
    return (jnp.where(lower_valid, before, 0.0), jnp.where(upper_valid, after, 0.0))


def edge_columns(values):
    size = lax.axis_size("lon")
    up = [(i, (i + 1) % size) for i in range(size)]
    down = [(j, i) for i, j in up]
    before = lax.ppermute(values[:, -1:], "lon", up)
    after = lax.ppermute(values[:, :1], "lon", down)
    return before, after


MESH_IDS = pl.DeviceIdType.MESH


def tile_device(comp, tile, lon_total):
    return (comp, tile // lon_total, tile % lon_total)


def gather_kernel(offsets, shape, send_ref, out_ref, land, send_sems, recv_sems):
    comp_total, lat_total, lon_total = shape
    comp = lax.axis_index("comp")
    tiles = lat_total * lon_total
    tile = lax.axis_index("lat") * lon_total + lax.axis_index("lon")
    ocean = comp_total - 1
    count = len(offsets)
    barrier = pltpu.get_barrier_semaphore()

    @pl.when(comp != ocean)
    def _():
        for off in offsets:
            target = tile_device(ocean, (tile + off) % tiles, lon_total)
            pl.semaphore_signal(barrier, 1, device_id=target, device_id_type=MESH_IDS)
        pl.semaphore_wait(barrier, count)
        copies = []
        for k, off in enumerate(offsets):
            target = tile_device(ocean, (tile + off) % tiles, lon_total)
            copy = pltpu.make_async_remote_copy(
                src_ref=send_ref.at[k],
                dst_ref=land.at[comp * count + k],
                send_sem=send_sems.at[k],
                recv_sem=recv_sems.at[comp * count + k],
                device_id=target,
                device_id_type=MESH_IDS,
            )
            copy.start()
            copies.append(copy)
        for copy in copies:
            copy.wait_send()
        out_ref[...] = jnp.zeros_like(out_ref)

    @pl.when(comp == ocean)
    def _():
        for source_comp in range(ocean):
            for off in offsets:
                source = tile_device(source_comp, (tile + tiles - off) % tiles, lon_total)
                pl.semaphore_signal(barrier, 1, device_id=source, device_id_type=MESH_IDS)
        pl.semaphore_wait(barrier, count * ocean)
        for source_comp in range(ocean):
            for k, off in enumerate(offsets):
                source = tile_device(source_comp, (tile + tiles - off) % tiles, lon_total)
                slot = source_comp * count + k
                pltpu.make_async_remote_copy(
                    src_ref=send_ref.at[k],
                    dst_ref=land.at[slot],
                    send_sem=send_sems.at[k],
                    recv_sem=recv_sems.at[slot],
                    device_id=source,
                    device_id_type=MESH_IDS,
                ).wait_recv()
        out_ref[...] = land[...]


def gather_to_ocean(blocks, offsets, shape):
    count = len(offsets)
    senders = (shape[0] - 1) * count
    slot_shape = blocks.shape[1:]
    return pl.pallas_call(
        functools.partial(gather_kernel, tuple(offsets), tuple(shape)),
        out_shape=jax.ShapeDtypeStruct((senders,) + slot_shape, blocks.dtype),
        in_specs=[pl.BlockSpec(memory_space=pltpu.VMEM)],
        out_specs=pl.BlockSpec(memory_space=pltpu.VMEM),
        scratch_shapes=[
            pltpu.VMEM((senders,) + slot_shape, blocks.dtype),
            pltpu.SemaphoreType.DMA((count,)),
            pltpu.SemaphoreType.DMA((senders,)),
        ],
        compiler_params=pltpu.CompilerParams(collective_id=0, has_side_effects=True),
    )(blocks)


def spread_kernel(offsets, shape, surface_ref, out_ref, land, send_sems, recv_sems):
    comp_total, lat_total, lon_total = shape
    comp = lax.axis_index("comp")
    tiles = lat_total * lon_total
    tile = lax.axis_index("lat") * lon_total + lax.axis_index("lon")
    ocean = comp_total - 1
    count = len(offsets)
    barrier = pltpu.get_barrier_semaphore()

    @pl.when(comp == ocean)
    def _():
        for target_comp in range(ocean):
            for off in offsets:
                target = tile_device(target_comp, (tile + tiles - off) % tiles, lon_total)
                pl.semaphore_signal(barrier, 1, device_id=target, device_id_type=MESH_IDS)
        pl.semaphore_wait(barrier, count * ocean)
        copies = []
        for target_comp in range(ocean):
            for k, off in enumerate(offsets):
                target = tile_device(target_comp, (tile + tiles - off) % tiles, lon_total)
                copy = pltpu.make_async_remote_copy(
                    src_ref=surface_ref,
                    dst_ref=land.at[k],
                    send_sem=send_sems.at[target_comp * count + k],
                    recv_sem=recv_sems.at[k],
                    device_id=target,
                    device_id_type=MESH_IDS,
                )
                copy.start()
                copies.append(copy)
        for copy in copies:
            copy.wait_send()
        out_ref[...] = jnp.zeros_like(out_ref)

    @pl.when(comp != ocean)
    def _():
        for off in offsets:
            source = tile_device(ocean, (tile + off) % tiles, lon_total)
            pl.semaphore_signal(barrier, 1, device_id=source, device_id_type=MESH_IDS)
        pl.semaphore_wait(barrier, count)
        for k, off in enumerate(offsets):
            source = tile_device(ocean, (tile + off) % tiles, lon_total)
            pltpu.make_async_remote_copy(
                src_ref=surface_ref,
                dst_ref=land.at[k],
                send_sem=send_sems.at[k],
                recv_sem=recv_sems.at[k],
                device_id=source,
                device_id_type=MESH_IDS,
            ).wait_recv()
        out_ref[...] = land[...]


def spread_from_ocean(surface, offsets, shape):
    count = len(offsets)
    senders = (shape[0] - 1) * count
    return pl.pallas_call(
        functools.partial(spread_kernel, tuple(offsets), tuple(shape)),
        out_shape=jax.ShapeDtypeStruct((count,) + surface.shape, surface.dtype),
        in_specs=[pl.BlockSpec(memory_space=pltpu.VMEM)],
        out_specs=pl.BlockSpec(memory_space=pltpu.VMEM),
        scratch_shapes=[
            pltpu.VMEM((count,) + surface.shape, surface.dtype),
            pltpu.SemaphoreType.DMA((senders,)),
            pltpu.SemaphoreType.DMA((count,)),
        ],
        compiler_params=pltpu.CompilerParams(collective_id=1, has_side_effects=True),
    )(surface)


def local(
    state, land_mask, intersection_list, mix_atm, mix_ocn, flux_map, ocean_map, regrid_weights
):
    tile_rows, block_len, levels = state.shape
    flux_count = flux_map.shape[1]
    weight_count = regrid_weights.shape[0]
    intersections = intersection_list.shape[2]
    comp_count = lax.axis_size("comp")
    lat_count = lax.axis_size("lat")
    lon_count = lax.axis_size("lon")
    tile_count = lat_count * lon_count
    reach = min(4, lon_count)
    neighbour_count = 2 * reach
    capacity = intersections * tile_rows // neighbour_count
    width = flux_count * block_len
    comp_index = lax.axis_index("comp")
    tile_index = lax.axis_index("lat") * lon_count + lax.axis_index("lon")
    band = comp_index * lat_count + lax.axis_index("lat")
    ocean_band = (comp_count - 1) * lat_count
    ocean_side = comp_index == comp_count - 1
    lower_valid = (band > 0) & ((band - 1 >= ocean_band) == (band >= ocean_band))
    upper_valid = (band < comp_count * lat_count - 1) & (
        (band + 1 >= ocean_band) == (band >= ocean_band)
    )
    sea_cells = land_mask == 1

    top, bottom = edge_rows(state, lower_valid, upper_valid)
    west, east = edge_columns(state)
    mixing = jnp.where(ocean_side, mix_ocn, mix_atm)
    (first,) = substep(state, top, bottom, west, east, mixing)
    top, bottom = edge_rows(first, lower_valid, upper_valid)
    west, east = edge_columns(first)

    def atmosphere_second(values, top, bottom, west, east):
        moved, total = substep(values, top, bottom, west, east, mix_atm, flux_map.T)
        total = total.reshape(flux_count, tile_rows, block_len)
        return moved, jnp.where(sea_cells[None], 0.5 * total, 0.0).astype(jnp.bfloat16)

    def ocean_second(values, top, bottom, west, east):
        return values, jnp.zeros((flux_count, tile_rows, block_len), jnp.bfloat16)

    second, flux_sent = lax.cond(
        ocean_side, ocean_second, atmosphere_second, first, top, bottom, west, east
    )
    entry_list = intersection_list.reshape(tile_rows * intersections, 3)
    owners = entry_list[:, 0]
    targets = entry_list[:, 1]
    weight_ids = entry_list[:, 2]
    labels = weight_ids * tile_rows + targets
    entry_blocks = jnp.repeat(flux_sent.transpose(1, 0, 2), intersections, axis=0).reshape(
        tile_rows * intersections, width
    )
    lane = jnp.arange(128, dtype=jnp.int32)[None, :]
    label_lanes = jnp.where(
        lane == 0, weight_ids[:, None], jnp.where(lane == 1, targets[:, None], 0)
    ).astype(jnp.bfloat16)
    entry_blocks = jnp.concatenate([entry_blocks, label_lanes], axis=1)
    sending = jnp.broadcast_to(jnp.logical_not(ocean_side), owners.shape)
    offsets = [
        (n // reach * lon_count + n % reach - (reach - 1) // 2) % tile_count
        for n in range(neighbour_count)
    ]
    offset_table = jnp.array(offsets, jnp.int32)
    distance = (owners - tile_index + tile_count) % tile_count
    neighbour_ids = jnp.sum(
        jnp.where(
            distance[:, None] == offset_table[None, :],
            jnp.arange(neighbour_count, dtype=jnp.int32)[None, :],
            0,
        ),
        axis=1,
    )
    packed, _ = pack_rows(entry_blocks, neighbour_ids, labels, sending, capacity, neighbour_count)
    mesh_shape = (comp_count, lat_count, lon_count)
    arrived = gather_to_ocean(packed, offsets, mesh_shape)
    weights_low = regrid_weights

    def ocean_final(values, arrived):
        flat = arrived.reshape(-1, width + 128)
        fluxes = flat[:, :width]
        arrived_labels = flat[:, width].astype(jnp.int32) * tile_rows + flat[:, width + 1].astype(
            jnp.int32
        )
        label_ids = jnp.arange(weight_count * tile_rows, dtype=jnp.int32)
        selector = (arrived_labels[:, None] == label_ids[None, :]).astype(jnp.bfloat16)
        binned = lax.dot_general(
            selector, fluxes, (((0,), (0,)), ((), ())), preferred_element_type=jnp.float32
        )
        binned = binned.reshape(weight_count, tile_rows, flux_count, block_len)
        binned_hi = binned.astype(jnp.bfloat16)
        binned_lo = (binned - binned_hi.astype(jnp.float32)).astype(jnp.bfloat16)
        forcing = jnp.einsum(
            "wdfa,wab->fdb", binned_hi, weights_low, preferred_element_type=jnp.float32
        ) + jnp.einsum("wdfa,wab->fdb", binned_lo, weights_low, preferred_element_type=jnp.float32)
        moved = values + jnp.einsum("frc,fk->rck", forcing, ocean_map, precision=HIGHEST)
        return jnp.where(sea_cells[:, :, None], moved, state)

    final_state = lax.cond(ocean_side, ocean_final, lambda values, arrived: values, second, arrived)
    surface = final_state[:, :, 0]
    around = spread_from_ocean(surface, offsets, mesh_shape)
    picked = jnp.take(
        around.reshape(neighbour_count * tile_rows, block_len),
        neighbour_ids * tile_rows + targets,
        axis=0,
    )
    weights_wide = regrid_weights.astype(jnp.float32)
    images = jnp.einsum("eb,wab->ewa", picked, weights_wide, precision=HIGHEST)
    which_block = weight_ids[:, None] == jnp.arange(weight_count, dtype=jnp.int32)[None, :]
    chosen = jnp.sum(jnp.where(which_block[:, :, None], images, 0.0), axis=1)
    returned = chosen.reshape(tile_rows, intersections, block_len).sum(axis=1)
    surface_out = jnp.where(ocean_side, surface, jnp.where(sea_cells, returned, surface))
    return (final_state, surface_out)


def solution(mesh):
    placed = (
        P(("comp", "lat"), "lon", None),
        P(("comp", "lat"), "lon"),
        P(("comp", "lat"), "lon", None, None),
        P(),
        P(),
        P(),
        P(),
        P(),
    )
    return jax.shard_map(
        local,
        mesh=mesh,
        in_specs=placed,
        out_specs=(P(("comp", "lat"), "lon", None), P(("comp", "lat"), "lon")),
        check_vma=False,
    )
```

```python
import jax
import jax.numpy as jnp
from jax import lax
from jax.experimental import pallas as pl
from jax.experimental.pallas import tpu as pltpu
from jax.sharding import PartitionSpec as P
import functools

SMOOTHING = 0.2
PHYSICS = 0.5
HIGHEST = lax.Precision.HIGHEST
ROW_BLOCK = 8


def split_bf16(values):
    high = values.astype(jnp.bfloat16)
    low = (values - high.astype(jnp.float32)).astype(jnp.bfloat16)
    return high, low


def three_pass(lhs, rhs, dims):
    lhs_hi, lhs_lo = split_bf16(lhs)
    rhs_hi, rhs_lo = split_bf16(rhs)

    def one(a, b):
        return lax.dot_general(a, b, (dims, ((), ())), preferred_element_type=jnp.float32)

    return one(lhs_hi, rhs_hi) + (one(lhs_hi, rhs_lo) + one(lhs_lo, rhs_hi))


def substep_kernel(with_flux, x_ref, top_ref, bottom_ref, west_ref, east_ref, mix_ref, *rest):
    if with_flux:
        fluxes_ref, out_ref, flux_out_ref = rest
    else:
        (out_ref,) = rest
    rows, cols, levels = x_ref.shape
    centre = x_ref[...]
    up = jnp.concatenate([top_ref[...], centre[:-1]], axis=0)
    down = jnp.concatenate([centre[1:], bottom_ref[...]], axis=0)
    column = lax.broadcasted_iota(jnp.int32, centre.shape, 1)
    west = jnp.where(column == 0, west_ref[...], pltpu.roll(centre, 1, 1))
    east = jnp.where(column == cols - 1, east_ref[...], pltpu.roll(centre, cols - 1, 1))
    smooth = centre + SMOOTHING * (up + down + west + east - 4.0 * centre)
    flat = smooth.reshape(rows * cols, levels)
    mixed = three_pass(flat, mix_ref[...], ((1,), (0,)))
    moved = flat + PHYSICS * jnp.tanh(mixed)
    out_ref[...] = moved.reshape(rows, cols, levels)
    if with_flux:
        total = centre.reshape(rows * cols, levels) + moved
        flux_out_ref[...] = three_pass(fluxes_ref[...], total, ((1,), (1,)))


def substep(values, top, bottom, west, east, mixing, fluxes_t=None):
    rows, cols, levels = values.shape
    blocks = rows // ROW_BLOCK
    top_rows = jnp.concatenate([top, values[ROW_BLOCK - 1 : rows - 1 : ROW_BLOCK]], axis=0)
    bottom_rows = jnp.concatenate([values[ROW_BLOCK:rows:ROW_BLOCK], bottom], axis=0)
    with_flux = fluxes_t is not None
    in_specs = [
        pl.BlockSpec((ROW_BLOCK, cols, levels), lambda i: (i, 0, 0)),
        pl.BlockSpec((1, cols, levels), lambda i: (i, 0, 0)),
        pl.BlockSpec((1, cols, levels), lambda i: (i, 0, 0)),
        pl.BlockSpec((ROW_BLOCK, 1, levels), lambda i: (i, 0, 0)),
        pl.BlockSpec((ROW_BLOCK, 1, levels), lambda i: (i, 0, 0)),
        pl.BlockSpec((levels, levels), lambda i: (0, 0)),
    ]
    operands = [values, top_rows, bottom_rows, west, east, mixing]
    out_shape = [jax.ShapeDtypeStruct(values.shape, jnp.float32)]
    out_specs = [pl.BlockSpec((ROW_BLOCK, cols, levels), lambda i: (i, 0, 0))]
    if with_flux:
        flux_count = fluxes_t.shape[0]
        in_specs.append(pl.BlockSpec((flux_count, levels), lambda i: (0, 0)))
        operands.append(fluxes_t)
        out_shape.append(jax.ShapeDtypeStruct((flux_count, rows * cols), jnp.float32))
        out_specs.append(pl.BlockSpec((flux_count, ROW_BLOCK * cols), lambda i: (0, i)))
    cells = rows * cols
    flops = 6 * cells * levels * levels + (6 * cells * levels * 8 if with_flux else 0)
    result = pl.pallas_call(
        functools.partial(substep_kernel, with_flux),
        grid=(blocks,),
        in_specs=in_specs,
        out_specs=out_specs,
        out_shape=out_shape,
        cost_estimate=pl.CostEstimate(
            flops=flops, transcendentals=cells * levels, bytes_accessed=8 * cells * levels
        ),
    )(*operands)
    return result


def column_physics(values, mixing):
    return jnp.tanh(jnp.einsum("rck,kj->rcj", values, mixing, precision=HIGHEST))


def earlier_same(owners, usable):
    positions = jnp.arange(owners.shape[0], dtype=jnp.int32)
    before = (
        (owners[None, :] == owners[:, None])
        & (positions[None, :] < positions[:, None])
        & usable[None, :]
    )
    return jnp.sum(before.astype(jnp.int32), axis=1)


def pack_rows(blocks, owners, labels, usable, slots_each, owner_total):
    ranks = earlier_same(owners, usable)
    target_slot = owners * slots_each + ranks
    slot_ids = jnp.arange(owner_total * slots_each, dtype=jnp.int32)
    placing = (slot_ids[:, None] == target_slot[None, :]) & usable[None, :]
    packed = jnp.dot(
        placing.astype(jnp.bfloat16), blocks, preferred_element_type=jnp.float32
    ).astype(jnp.bfloat16)
    placed_labels = jnp.sum(jnp.where(placing, labels[None, :] + 1, 0), axis=1) - 1
    return (
        packed.reshape(owner_total, slots_each, blocks.shape[1]),
        placed_labels.reshape(owner_total, slots_each),
        target_slot,
    )


def edge_rows(values, lower_valid, upper_valid):
    bands = lax.axis_size("comp") * lax.axis_size("lat")
    up = [(i, i + 1) for i in range(bands - 1)]
    down = [(j, i) for i, j in up]
    before = lax.ppermute(values[-1:], ("comp", "lat"), up)
    after = lax.ppermute(values[:1], ("comp", "lat"), down)
    return (jnp.where(lower_valid, before, 0.0), jnp.where(upper_valid, after, 0.0))


def edge_columns(values):
    size = lax.axis_size("lon")
    up = [(i, (i + 1) % size) for i in range(size)]
    down = [(j, i) for i, j in up]
    before = lax.ppermute(values[:, -1:], "lon", up)
    after = lax.ppermute(values[:, :1], "lon", down)
    return before, after


MESH_IDS = pl.DeviceIdType.MESH


def tile_device(comp, tile, lon_total):
    return (comp, tile // lon_total, tile % lon_total)


def gather_kernel(offsets, shape, send_ref, out_ref, land, send_sems, recv_sems):
    comp_total, lat_total, lon_total = shape
    comp = lax.axis_index("comp")
    tiles = lat_total * lon_total
    tile = lax.axis_index("lat") * lon_total + lax.axis_index("lon")
    ocean = comp_total - 1
    count = len(offsets)
    barrier = pltpu.get_barrier_semaphore()

    @pl.when(comp != ocean)
    def _():
        for off in offsets:
            target = tile_device(ocean, (tile + off) % tiles, lon_total)
            pl.semaphore_signal(barrier, 1, device_id=target, device_id_type=MESH_IDS)
        pl.semaphore_wait(barrier, count)
        copies = []
        for k, off in enumerate(offsets):
            target = tile_device(ocean, (tile + off) % tiles, lon_total)
            copy = pltpu.make_async_remote_copy(
                src_ref=send_ref.at[k],
                dst_ref=land.at[comp * count + k],
                send_sem=send_sems.at[k],
                recv_sem=recv_sems.at[comp * count + k],
                device_id=target,
                device_id_type=MESH_IDS,
            )
            copy.start()
            copies.append(copy)
        for copy in copies:
            copy.wait_send()
        out_ref[...] = jnp.zeros_like(out_ref)

    @pl.when(comp == ocean)
    def _():
        for source_comp in range(ocean):
            for off in offsets:
                source = tile_device(source_comp, (tile + tiles - off) % tiles, lon_total)
                pl.semaphore_signal(barrier, 1, device_id=source, device_id_type=MESH_IDS)
        pl.semaphore_wait(barrier, count * ocean)
        for source_comp in range(ocean):
            for k, off in enumerate(offsets):
                source = tile_device(source_comp, (tile + tiles - off) % tiles, lon_total)
                slot = source_comp * count + k
                pltpu.make_async_remote_copy(
                    src_ref=send_ref.at[k],
                    dst_ref=land.at[slot],
                    send_sem=send_sems.at[k],
                    recv_sem=recv_sems.at[slot],
                    device_id=source,
                    device_id_type=MESH_IDS,
                ).wait_recv()
        out_ref[...] = land[...]


def gather_to_ocean(blocks, offsets, shape):
    count = len(offsets)
    senders = (shape[0] - 1) * count
    slot_shape = blocks.shape[1:]
    return pl.pallas_call(
        functools.partial(gather_kernel, tuple(offsets), tuple(shape)),
        out_shape=jax.ShapeDtypeStruct((senders,) + slot_shape, blocks.dtype),
        in_specs=[pl.BlockSpec(memory_space=pltpu.VMEM)],
        out_specs=pl.BlockSpec(memory_space=pltpu.VMEM),
        scratch_shapes=[
            pltpu.VMEM((senders,) + slot_shape, blocks.dtype),
            pltpu.SemaphoreType.DMA((count,)),
            pltpu.SemaphoreType.DMA((senders,)),
        ],
        compiler_params=pltpu.CompilerParams(collective_id=0, has_side_effects=True),
    )(blocks)


def spread_kernel(offsets, shape, surface_ref, out_ref, land, send_sems, recv_sems):
    comp_total, lat_total, lon_total = shape
    comp = lax.axis_index("comp")
    tiles = lat_total * lon_total
    tile = lax.axis_index("lat") * lon_total + lax.axis_index("lon")
    ocean = comp_total - 1
    count = len(offsets)
    barrier = pltpu.get_barrier_semaphore()

    @pl.when(comp == ocean)
    def _():
        for target_comp in range(ocean):
            for off in offsets:
                target = tile_device(target_comp, (tile + tiles - off) % tiles, lon_total)
                pl.semaphore_signal(barrier, 1, device_id=target, device_id_type=MESH_IDS)
        pl.semaphore_wait(barrier, count * ocean)
        copies = []
        for target_comp in range(ocean):
            for k, off in enumerate(offsets):
                target = tile_device(target_comp, (tile + tiles - off) % tiles, lon_total)
                copy = pltpu.make_async_remote_copy(
                    src_ref=surface_ref.at[target_comp * count + k],
                    dst_ref=land.at[k],
                    send_sem=send_sems.at[target_comp * count + k],
                    recv_sem=recv_sems.at[k],
                    device_id=target,
                    device_id_type=MESH_IDS,
                )
                copy.start()
                copies.append(copy)
        for copy in copies:
            copy.wait_send()
        out_ref[...] = jnp.zeros_like(out_ref)

    @pl.when(comp != ocean)
    def _():
        for off in offsets:
            source = tile_device(ocean, (tile + off) % tiles, lon_total)
            pl.semaphore_signal(barrier, 1, device_id=source, device_id_type=MESH_IDS)
        pl.semaphore_wait(barrier, count)
        for k, off in enumerate(offsets):
            source = tile_device(ocean, (tile + off) % tiles, lon_total)
            pltpu.make_async_remote_copy(
                src_ref=surface_ref.at[k],
                dst_ref=land.at[k],
                send_sem=send_sems.at[k],
                recv_sem=recv_sems.at[k],
                device_id=source,
                device_id_type=MESH_IDS,
            ).wait_recv()
        out_ref[...] = land[...]


def spread_from_ocean(replies, offsets, shape):
    count = len(offsets)
    senders = (shape[0] - 1) * count
    slot_shape = replies.shape[1:]
    return pl.pallas_call(
        functools.partial(spread_kernel, tuple(offsets), tuple(shape)),
        out_shape=jax.ShapeDtypeStruct((count,) + slot_shape, replies.dtype),
        in_specs=[pl.BlockSpec(memory_space=pltpu.VMEM)],
        out_specs=pl.BlockSpec(memory_space=pltpu.VMEM),
        scratch_shapes=[
            pltpu.VMEM((count,) + slot_shape, replies.dtype),
            pltpu.SemaphoreType.DMA((senders,)),
            pltpu.SemaphoreType.DMA((count,)),
        ],
        compiler_params=pltpu.CompilerParams(collective_id=1, has_side_effects=True),
    )(replies)


def local(
    state, land_mask, intersection_list, mix_atm, mix_ocn, flux_map, ocean_map, regrid_weights
):
    tile_rows, block_len, levels = state.shape
    flux_count = flux_map.shape[1]
    weight_count = regrid_weights.shape[0]
    intersections = intersection_list.shape[2]
    comp_count = lax.axis_size("comp")
    lat_count = lax.axis_size("lat")
    lon_count = lax.axis_size("lon")
    tile_count = lat_count * lon_count
    reach = min(4, lon_count)
    neighbour_count = 2 * reach
    capacity = intersections * tile_rows // neighbour_count
    width = flux_count * block_len
    comp_index = lax.axis_index("comp")
    tile_index = lax.axis_index("lat") * lon_count + lax.axis_index("lon")
    band = comp_index * lat_count + lax.axis_index("lat")
    ocean_band = (comp_count - 1) * lat_count
    ocean_side = comp_index == comp_count - 1
    lower_valid = (band > 0) & ((band - 1 >= ocean_band) == (band >= ocean_band))
    upper_valid = (band < comp_count * lat_count - 1) & (
        (band + 1 >= ocean_band) == (band >= ocean_band)
    )
    sea_cells = land_mask == 1

    top, bottom = edge_rows(state, lower_valid, upper_valid)
    west, east = edge_columns(state)
    mixing = jnp.where(ocean_side, mix_ocn, mix_atm)
    (first,) = substep(state, top, bottom, west, east, mixing)
    top, bottom = edge_rows(first, lower_valid, upper_valid)
    west, east = edge_columns(first)

    def atmosphere_second(values, top, bottom, west, east):
        moved, total = substep(values, top, bottom, west, east, mix_atm, flux_map.T)
        total = total.reshape(flux_count, tile_rows, block_len)
        return moved, jnp.where(sea_cells[None], 0.5 * total, 0.0).astype(jnp.bfloat16)

    def ocean_second(values, top, bottom, west, east):
        return values, jnp.zeros((flux_count, tile_rows, block_len), jnp.bfloat16)

    second, flux_sent = lax.cond(
        ocean_side, ocean_second, atmosphere_second, first, top, bottom, west, east
    )
    entry_list = intersection_list.reshape(tile_rows * intersections, 3)
    owners = entry_list[:, 0]
    targets = entry_list[:, 1]
    weight_ids = entry_list[:, 2]
    labels = weight_ids * tile_rows + targets
    entry_blocks = jnp.repeat(flux_sent.transpose(1, 0, 2), intersections, axis=0).reshape(
        tile_rows * intersections, width
    )
    lane = jnp.arange(128, dtype=jnp.int32)[None, :]
    label_lanes = jnp.where(
        lane == 0, weight_ids[:, None], jnp.where(lane == 1, targets[:, None], 0)
    ).astype(jnp.bfloat16)
    entry_blocks = jnp.concatenate([entry_blocks, label_lanes], axis=1)
    sending = jnp.broadcast_to(jnp.logical_not(ocean_side), owners.shape)
    offsets = [
        (n // reach * lon_count + n % reach - (reach - 1) // 2) % tile_count
        for n in range(neighbour_count)
    ]
    offset_table = jnp.array(offsets, jnp.int32)
    distance = (owners - tile_index + tile_count) % tile_count
    neighbour_ids = jnp.sum(
        jnp.where(
            distance[:, None] == offset_table[None, :],
            jnp.arange(neighbour_count, dtype=jnp.int32)[None, :],
            0,
        ),
        axis=1,
    )
    packed, _, entry_slots = pack_rows(entry_blocks, neighbour_ids, labels, sending, capacity, neighbour_count)
    mesh_shape = (comp_count, lat_count, lon_count)
    arrived = gather_to_ocean(packed, offsets, mesh_shape)
    weights_low = regrid_weights
    weights_wide = regrid_weights.astype(jnp.float32)
    senders = (comp_count - 1) * neighbour_count

    def ocean_reply(values, arrived):
        flat = arrived.reshape(-1, width + 128)
        fluxes = flat[:, :width]
        arrived_labels = flat[:, width].astype(jnp.int32) * tile_rows + flat[:, width + 1].astype(
            jnp.int32
        )
        label_ids = jnp.arange(weight_count * tile_rows, dtype=jnp.int32)
        selector = (arrived_labels[:, None] == label_ids[None, :]).astype(jnp.bfloat16)
        binned = lax.dot_general(
            selector, fluxes, (((0,), (0,)), ((), ())), preferred_element_type=jnp.float32
        )
        binned = binned.reshape(weight_count, tile_rows, flux_count, block_len)
        binned_hi = lax.reduce_precision(binned, exponent_bits=8, mantissa_bits=7)
        binned_lo = (binned - binned_hi).astype(jnp.bfloat16)
        forcing = jnp.einsum(
            "wdfa,wab->fdb",
            binned_hi.astype(jnp.bfloat16),
            weights_low,
            preferred_element_type=jnp.float32,
        ) + jnp.einsum("wdfa,wab->fdb", binned_lo, weights_low, preferred_element_type=jnp.float32)
        lifted = jnp.sum(forcing * ocean_map[:, 0][:, None, None], axis=0)
        top_level = jnp.where(sea_cells, values[:, :, 0] + lifted, state[:, :, 0])
        table = jnp.einsum("db,wab->wda", top_level, weights_wide, precision=HIGHEST)
        replies = jnp.take(table.reshape(weight_count * tile_rows, block_len), arrived_labels, axis=0)
        return forcing, replies.reshape(senders, capacity, block_len)

    def atmosphere_reply(values, arrived):
        return (
            jnp.zeros((flux_count, tile_rows, block_len), jnp.float32),
            jnp.zeros((senders, capacity, block_len), jnp.float32),
        )

    forcing, replies = lax.cond(ocean_side, ocean_reply, atmosphere_reply, first, arrived)
    answers = spread_from_ocean(replies, offsets, mesh_shape)
    per_entry = jnp.take(
        answers.reshape(neighbour_count * capacity, block_len), entry_slots, axis=0
    )
    returned = per_entry.reshape(tile_rows, intersections, block_len).sum(axis=1)
    first, forcing, answers = lax.optimization_barrier((first, forcing, answers))

    def ocean_final(values, forcing):
        moved = values + jnp.einsum("frc,fk->rck", forcing, ocean_map, precision=HIGHEST)
        return jnp.where(sea_cells[:, :, None], moved, state)

    final_state = lax.cond(ocean_side, ocean_final, lambda values, forcing: second, first, forcing)
    surface = final_state[:, :, 0]
    surface_out = jnp.where(ocean_side, surface, jnp.where(sea_cells, returned, surface))
    return (final_state, surface_out)


def solution(mesh):
    placed = (
        P(("comp", "lat"), "lon", None),
        P(("comp", "lat"), "lon"),
        P(("comp", "lat"), "lon", None, None),
        P(),
        P(),
        P(),
        P(),
        P(),
    )
    return jax.shard_map(
        local,
        mesh=mesh,
        in_specs=placed,
        out_specs=(P(("comp", "lat"), "lon", None), P(("comp", "lat"), "lon")),
        check_vma=False,
    )
```

```python
import jax
import jax.numpy as jnp
from jax import lax
from jax.experimental import pallas as pl
from jax.experimental.pallas import tpu as pltpu
from jax.sharding import PartitionSpec as P
import functools

SMOOTHING = 0.2
PHYSICS = 0.5
HIGHEST = lax.Precision.HIGHEST
ROW_BLOCK = 8


def split_bf16(values):
    high = values.astype(jnp.bfloat16)
    low = (values - high.astype(jnp.float32)).astype(jnp.bfloat16)
    return high, low


def three_pass(lhs, rhs, dims):
    lhs_hi, lhs_lo = split_bf16(lhs)
    rhs_hi, rhs_lo = split_bf16(rhs)

    def one(a, b):
        return lax.dot_general(a, b, (dims, ((), ())), preferred_element_type=jnp.float32)

    return one(lhs_hi, rhs_hi) + (one(lhs_hi, rhs_lo) + one(lhs_lo, rhs_hi))


def exact_rows(picker, values):
    high = values.astype(jnp.bfloat16)
    rest = values - high.astype(jnp.float32)
    middle = rest.astype(jnp.bfloat16)
    low = (rest - middle.astype(jnp.float32)).astype(jnp.bfloat16)

    def one(piece):
        return lax.dot_general(
            picker, piece, (((1,), (1,)), ((), ())), preferred_element_type=jnp.float32
        )

    return one(high) + one(middle) + one(low)


def substep_kernel(with_flux, x_ref, top_ref, bottom_ref, west_ref, east_ref, mix_ref, *rest):
    if with_flux:
        fluxes_ref, out_ref, planes_ref, flux_out_ref = rest
    else:
        out_ref, planes_ref = rest
    rows, cols, levels = x_ref.shape
    centre = x_ref[...]
    up = jnp.concatenate([top_ref[...], centre[:-1]], axis=0)
    down = jnp.concatenate([centre[1:], bottom_ref[...]], axis=0)
    column = lax.broadcasted_iota(jnp.int32, centre.shape, 1)
    west = jnp.where(column == 0, west_ref[...], pltpu.roll(centre, 1, 1))
    east = jnp.where(column == cols - 1, east_ref[...], pltpu.roll(centre, cols - 1, 1))
    smooth = centre + SMOOTHING * (up + down + west + east - 4.0 * centre)
    flat = smooth.reshape(rows * cols, levels)
    mixed = three_pass(flat, mix_ref[...], ((1,), (0,)))
    moved = flat + PHYSICS * jnp.tanh(mixed)
    out_ref[...] = moved.reshape(rows, cols, levels)
    plane_row = lax.broadcasted_iota(jnp.int32, (8, levels), 0)
    plane_lane = lax.broadcasted_iota(jnp.int32, (8, levels), 1)
    pick_out = ((plane_row == 0) & (plane_lane == 0)).astype(jnp.bfloat16)
    pick_in = ((plane_row == 1) & (plane_lane == 0)).astype(jnp.bfloat16)
    planes_ref[...] = exact_rows(pick_out, moved) + exact_rows(
        pick_in, centre.reshape(rows * cols, levels)
    )
    if with_flux:
        total = centre.reshape(rows * cols, levels) + moved
        flux_out_ref[...] = three_pass(fluxes_ref[...], total, ((1,), (1,)))


def substep(values, top, bottom, west, east, mixing, fluxes_t=None):
    rows, cols, levels = values.shape
    blocks = rows // ROW_BLOCK
    top_rows = jnp.concatenate([top, values[ROW_BLOCK - 1 : rows - 1 : ROW_BLOCK]], axis=0)
    bottom_rows = jnp.concatenate([values[ROW_BLOCK:rows:ROW_BLOCK], bottom], axis=0)
    with_flux = fluxes_t is not None
    in_specs = [
        pl.BlockSpec((ROW_BLOCK, cols, levels), lambda i: (i, 0, 0)),
        pl.BlockSpec((1, cols, levels), lambda i: (i, 0, 0)),
        pl.BlockSpec((1, cols, levels), lambda i: (i, 0, 0)),
        pl.BlockSpec((ROW_BLOCK, 1, levels), lambda i: (i, 0, 0)),
        pl.BlockSpec((ROW_BLOCK, 1, levels), lambda i: (i, 0, 0)),
        pl.BlockSpec((levels, levels), lambda i: (0, 0)),
    ]
    operands = [values, top_rows, bottom_rows, west, east, mixing]
    out_shape = [
        jax.ShapeDtypeStruct(values.shape, jnp.float32),
        jax.ShapeDtypeStruct((8, rows * cols), jnp.float32),
    ]
    out_specs = [
        pl.BlockSpec((ROW_BLOCK, cols, levels), lambda i: (i, 0, 0)),
        pl.BlockSpec((8, ROW_BLOCK * cols), lambda i: (0, i)),
    ]
    if with_flux:
        flux_count = fluxes_t.shape[0]
        in_specs.append(pl.BlockSpec((flux_count, levels), lambda i: (0, 0)))
        operands.append(fluxes_t)
        out_shape.append(jax.ShapeDtypeStruct((flux_count, rows * cols), jnp.float32))
        out_specs.append(pl.BlockSpec((flux_count, ROW_BLOCK * cols), lambda i: (0, i)))
    cells = rows * cols
    flops = 6 * cells * levels * levels + (6 * cells * levels * 8 if with_flux else 0)
    result = pl.pallas_call(
        functools.partial(substep_kernel, with_flux),
        grid=(blocks,),
        in_specs=in_specs,
        out_specs=out_specs,
        out_shape=out_shape,
        cost_estimate=pl.CostEstimate(
            flops=flops, transcendentals=cells * levels, bytes_accessed=8 * cells * levels
        ),
    )(*operands)
    return result


def column_physics(values, mixing):
    return jnp.tanh(jnp.einsum("rck,kj->rcj", values, mixing, precision=HIGHEST))


def earlier_same(owners, usable):
    positions = jnp.arange(owners.shape[0], dtype=jnp.int32)
    before = (
        (owners[None, :] == owners[:, None])
        & (positions[None, :] < positions[:, None])
        & usable[None, :]
    )
    return jnp.sum(before.astype(jnp.int32), axis=1)


def pack_rows(blocks, owners, labels, usable, slots_each, owner_total):
    ranks = earlier_same(owners, usable)
    target_slot = owners * slots_each + ranks
    slot_ids = jnp.arange(owner_total * slots_each, dtype=jnp.int32)
    placing = (slot_ids[:, None] == target_slot[None, :]) & usable[None, :]
    packed = jnp.dot(
        placing.astype(jnp.bfloat16), blocks, preferred_element_type=jnp.float32
    ).astype(jnp.bfloat16)
    placed_labels = jnp.sum(jnp.where(placing, labels[None, :] + 1, 0), axis=1) - 1
    return (
        packed.reshape(owner_total, slots_each, blocks.shape[1]),
        placed_labels.reshape(owner_total, slots_each),
        target_slot,
    )


def edge_rows(values, lower_valid, upper_valid):
    bands = lax.axis_size("comp") * lax.axis_size("lat")
    up = [(i, i + 1) for i in range(bands - 1)]
    down = [(j, i) for i, j in up]
    before = lax.ppermute(values[-1:], ("comp", "lat"), up)
    after = lax.ppermute(values[:1], ("comp", "lat"), down)
    return (jnp.where(lower_valid, before, 0.0), jnp.where(upper_valid, after, 0.0))


def edge_columns(values):
    size = lax.axis_size("lon")
    up = [(i, (i + 1) % size) for i in range(size)]
    down = [(j, i) for i, j in up]
    before = lax.ppermute(values[:, -1:], "lon", up)
    after = lax.ppermute(values[:, :1], "lon", down)
    return before, after


MESH_IDS = pl.DeviceIdType.MESH


def tile_device(comp, tile, lon_total):
    return (comp, tile // lon_total, tile % lon_total)


def gather_kernel(offsets, shape, send_ref, out_ref, land, send_sems, recv_sems):
    comp_total, lat_total, lon_total = shape
    comp = lax.axis_index("comp")
    tiles = lat_total * lon_total
    tile = lax.axis_index("lat") * lon_total + lax.axis_index("lon")
    ocean = comp_total - 1
    count = len(offsets)
    barrier = pltpu.get_barrier_semaphore()

    @pl.when(comp != ocean)
    def _():
        for off in offsets:
            target = tile_device(ocean, (tile + off) % tiles, lon_total)
            pl.semaphore_signal(barrier, 1, device_id=target, device_id_type=MESH_IDS)
        pl.semaphore_wait(barrier, count)
        copies = []
        for k, off in enumerate(offsets):
            target = tile_device(ocean, (tile + off) % tiles, lon_total)
            copy = pltpu.make_async_remote_copy(
                src_ref=send_ref.at[k],
                dst_ref=land.at[comp * count + k],
                send_sem=send_sems.at[k],
                recv_sem=recv_sems.at[comp * count + k],
                device_id=target,
                device_id_type=MESH_IDS,
            )
            copy.start()
            copies.append(copy)
        for copy in copies:
            copy.wait_send()
        out_ref[...] = jnp.zeros_like(out_ref)

    @pl.when(comp == ocean)
    def _():
        for source_comp in range(ocean):
            for off in offsets:
                source = tile_device(source_comp, (tile + tiles - off) % tiles, lon_total)
                pl.semaphore_signal(barrier, 1, device_id=source, device_id_type=MESH_IDS)
        pl.semaphore_wait(barrier, count * ocean)
        for source_comp in range(ocean):
            for k, off in enumerate(offsets):
                source = tile_device(source_comp, (tile + tiles - off) % tiles, lon_total)
                slot = source_comp * count + k
                pltpu.make_async_remote_copy(
                    src_ref=send_ref.at[k],
                    dst_ref=land.at[slot],
                    send_sem=send_sems.at[k],
                    recv_sem=recv_sems.at[slot],
                    device_id=source,
                    device_id_type=MESH_IDS,
                ).wait_recv()
        out_ref[...] = land[...]


def gather_to_ocean(blocks, offsets, shape):
    count = len(offsets)
    senders = (shape[0] - 1) * count
    slot_shape = blocks.shape[1:]
    return pl.pallas_call(
        functools.partial(gather_kernel, tuple(offsets), tuple(shape)),
        out_shape=jax.ShapeDtypeStruct((senders,) + slot_shape, blocks.dtype),
        in_specs=[pl.BlockSpec(memory_space=pltpu.VMEM)],
        out_specs=pl.BlockSpec(memory_space=pltpu.VMEM),
        scratch_shapes=[
            pltpu.VMEM((senders,) + slot_shape, blocks.dtype),
            pltpu.SemaphoreType.DMA((count,)),
            pltpu.SemaphoreType.DMA((senders,)),
        ],
        compiler_params=pltpu.CompilerParams(collective_id=0, has_side_effects=True),
    )(blocks)


def spread_kernel(offsets, shape, surface_ref, out_ref, land, send_sems, recv_sems):
    comp_total, lat_total, lon_total = shape
    comp = lax.axis_index("comp")
    tiles = lat_total * lon_total
    tile = lax.axis_index("lat") * lon_total + lax.axis_index("lon")
    ocean = comp_total - 1
    count = len(offsets)
    barrier = pltpu.get_barrier_semaphore()

    @pl.when(comp == ocean)
    def _():
        for target_comp in range(ocean):
            for off in offsets:
                target = tile_device(target_comp, (tile + tiles - off) % tiles, lon_total)
                pl.semaphore_signal(barrier, 1, device_id=target, device_id_type=MESH_IDS)
        pl.semaphore_wait(barrier, count * ocean)
        copies = []
        for target_comp in range(ocean):
            for k, off in enumerate(offsets):
                target = tile_device(target_comp, (tile + tiles - off) % tiles, lon_total)
                copy = pltpu.make_async_remote_copy(
                    src_ref=surface_ref.at[target_comp * count + k],
                    dst_ref=land.at[k],
                    send_sem=send_sems.at[target_comp * count + k],
                    recv_sem=recv_sems.at[k],
                    device_id=target,
                    device_id_type=MESH_IDS,
                )
                copy.start()
                copies.append(copy)
        for copy in copies:
            copy.wait_send()
        out_ref[...] = jnp.zeros_like(out_ref)

    @pl.when(comp != ocean)
    def _():
        for off in offsets:
            source = tile_device(ocean, (tile + off) % tiles, lon_total)
            pl.semaphore_signal(barrier, 1, device_id=source, device_id_type=MESH_IDS)
        pl.semaphore_wait(barrier, count)
        for k, off in enumerate(offsets):
            source = tile_device(ocean, (tile + off) % tiles, lon_total)
            pltpu.make_async_remote_copy(
                src_ref=surface_ref.at[k],
                dst_ref=land.at[k],
                send_sem=send_sems.at[k],
                recv_sem=recv_sems.at[k],
                device_id=source,
                device_id_type=MESH_IDS,
            ).wait_recv()
        out_ref[...] = land[...]


def spread_from_ocean(replies, offsets, shape):
    count = len(offsets)
    senders = (shape[0] - 1) * count
    slot_shape = replies.shape[1:]
    return pl.pallas_call(
        functools.partial(spread_kernel, tuple(offsets), tuple(shape)),
        out_shape=jax.ShapeDtypeStruct((count,) + slot_shape, replies.dtype),
        in_specs=[pl.BlockSpec(memory_space=pltpu.VMEM)],
        out_specs=pl.BlockSpec(memory_space=pltpu.VMEM),
        scratch_shapes=[
            pltpu.VMEM((count,) + slot_shape, replies.dtype),
            pltpu.SemaphoreType.DMA((senders,)),
            pltpu.SemaphoreType.DMA((count,)),
        ],
        compiler_params=pltpu.CompilerParams(collective_id=1, has_side_effects=True),
    )(replies)


def local(
    state, land_mask, intersection_list, mix_atm, mix_ocn, flux_map, ocean_map, regrid_weights
):
    tile_rows, block_len, levels = state.shape
    flux_count = flux_map.shape[1]
    weight_count = regrid_weights.shape[0]
    intersections = intersection_list.shape[2]
    comp_count = lax.axis_size("comp")
    lat_count = lax.axis_size("lat")
    lon_count = lax.axis_size("lon")
    tile_count = lat_count * lon_count
    reach = min(4, lon_count)
    neighbour_count = 2 * reach
    capacity = intersections * tile_rows // neighbour_count
    width = flux_count * block_len
    comp_index = lax.axis_index("comp")
    tile_index = lax.axis_index("lat") * lon_count + lax.axis_index("lon")
    band = comp_index * lat_count + lax.axis_index("lat")
    ocean_band = (comp_count - 1) * lat_count
    ocean_side = comp_index == comp_count - 1
    lower_valid = (band > 0) & ((band - 1 >= ocean_band) == (band >= ocean_band))
    upper_valid = (band < comp_count * lat_count - 1) & (
        (band + 1 >= ocean_band) == (band >= ocean_band)
    )
    sea_cells = land_mask == 1

    top, bottom = edge_rows(state, lower_valid, upper_valid)
    west, east = edge_columns(state)
    mixing = jnp.where(ocean_side, mix_ocn, mix_atm)
    first, first_planes = substep(state, top, bottom, west, east, mixing)
    first_top = first_planes[0].reshape(tile_rows, block_len)
    state_top = first_planes[1].reshape(tile_rows, block_len)
    top, bottom = edge_rows(first, lower_valid, upper_valid)
    west, east = edge_columns(first)

    def atmosphere_second(values, top, bottom, west, east):
        moved, planes, total = substep(values, top, bottom, west, east, mix_atm, flux_map.T)
        total = total.reshape(flux_count, tile_rows, block_len)
        sent = jnp.where(sea_cells[None], 0.5 * total, 0.0).astype(jnp.bfloat16)
        return moved, planes[0].reshape(tile_rows, block_len), sent

    def ocean_second(values, top, bottom, west, east):
        return (
            values,
            jnp.zeros((tile_rows, block_len), jnp.float32),
            jnp.zeros((flux_count, tile_rows, block_len), jnp.bfloat16),
        )

    second, second_top, flux_sent = lax.cond(
        ocean_side, ocean_second, atmosphere_second, first, top, bottom, west, east
    )
    entry_list = intersection_list.reshape(tile_rows * intersections, 3)
    owners = entry_list[:, 0]
    targets = entry_list[:, 1]
    weight_ids = entry_list[:, 2]
    labels = weight_ids * tile_rows + targets
    entry_blocks = jnp.repeat(flux_sent.transpose(1, 0, 2), intersections, axis=0).reshape(
        tile_rows * intersections, width
    )
    lane = jnp.arange(128, dtype=jnp.int32)[None, :]
    label_lanes = jnp.where(
        lane == 0, weight_ids[:, None], jnp.where(lane == 1, targets[:, None], 0)
    ).astype(jnp.bfloat16)
    entry_blocks = jnp.concatenate([entry_blocks, label_lanes], axis=1)
    sending = jnp.broadcast_to(jnp.logical_not(ocean_side), owners.shape)
    offsets = [
        (n // reach * lon_count + n % reach - (reach - 1) // 2) % tile_count
        for n in range(neighbour_count)
    ]
    offset_table = jnp.array(offsets, jnp.int32)
    distance = (owners - tile_index + tile_count) % tile_count
    neighbour_ids = jnp.sum(
        jnp.where(
            distance[:, None] == offset_table[None, :],
            jnp.arange(neighbour_count, dtype=jnp.int32)[None, :],
            0,
        ),
        axis=1,
    )
    packed, _, entry_slots = pack_rows(entry_blocks, neighbour_ids, labels, sending, capacity, neighbour_count)
    mesh_shape = (comp_count, lat_count, lon_count)
    arrived = gather_to_ocean(packed, offsets, mesh_shape)
    weights_low = regrid_weights
    weights_wide = regrid_weights.astype(jnp.float32)
    senders = (comp_count - 1) * neighbour_count

    def ocean_reply(values_top, arrived):
        flat = arrived.reshape(-1, width + 128)
        fluxes = flat[:, :width]
        arrived_labels = flat[:, width].astype(jnp.int32) * tile_rows + flat[:, width + 1].astype(
            jnp.int32
        )
        label_ids = jnp.arange(weight_count * tile_rows, dtype=jnp.int32)
        selector = (arrived_labels[:, None] == label_ids[None, :]).astype(jnp.bfloat16)
        binned = lax.dot_general(
            selector, fluxes, (((0,), (0,)), ((), ())), preferred_element_type=jnp.float32
        )
        binned = binned.reshape(weight_count, tile_rows, flux_count, block_len)
        binned_hi = lax.reduce_precision(binned, exponent_bits=8, mantissa_bits=7)
        binned_lo = (binned - binned_hi).astype(jnp.bfloat16)
        forcing = jnp.einsum(
            "wdfa,wab->fdb",
            binned_hi.astype(jnp.bfloat16),
            weights_low,
            preferred_element_type=jnp.float32,
        ) + jnp.einsum("wdfa,wab->fdb", binned_lo, weights_low, preferred_element_type=jnp.float32)
        lifted = jnp.sum(forcing * ocean_map[:, 0][:, None, None], axis=0)
        top_level = jnp.where(sea_cells, values_top + lifted, state_top)
        table = jnp.einsum("db,wab->wda", top_level, weights_wide, precision=HIGHEST)
        replies = jnp.take(table.reshape(weight_count * tile_rows, block_len), arrived_labels, axis=0)
        return forcing, replies.reshape(senders, capacity, block_len), top_level

    def atmosphere_reply(values_top, arrived):
        return (
            jnp.zeros((flux_count, tile_rows, block_len), jnp.float32),
            jnp.zeros((senders, capacity, block_len), jnp.float32),
            values_top,
        )

    forcing, replies, ocean_top = lax.cond(
        ocean_side, ocean_reply, atmosphere_reply, first_top, arrived
    )
    answers = spread_from_ocean(replies, offsets, mesh_shape)
    per_entry = jnp.take(
        answers.reshape(neighbour_count * capacity, block_len), entry_slots, axis=0
    )
    returned = per_entry.reshape(tile_rows, intersections, block_len).sum(axis=1)
    first, forcing, answers = lax.optimization_barrier((first, forcing, answers))

    def ocean_final(values, forcing):
        moved = values + jnp.einsum("frc,fk->rck", forcing, ocean_map, precision=HIGHEST)
        return jnp.where(sea_cells[:, :, None], moved, state)

    final_state = lax.cond(ocean_side, ocean_final, lambda values, forcing: second, first, forcing)
    surface_out = jnp.where(ocean_side, ocean_top, jnp.where(sea_cells, returned, second_top))
    return (final_state, surface_out)


def solution(mesh):
    placed = (
        P(("comp", "lat"), "lon", None),
        P(("comp", "lat"), "lon"),
        P(("comp", "lat"), "lon", None, None),
        P(),
        P(),
        P(),
        P(),
        P(),
    )
    return jax.shard_map(
        local,
        mesh=mesh,
        in_specs=placed,
        out_specs=(P(("comp", "lat"), "lon", None), P(("comp", "lat"), "lon")),
        check_vma=False,
    )
```

```python
import jax
import jax.numpy as jnp
from jax import lax
from jax.experimental import pallas as pl
from jax.experimental.pallas import tpu as pltpu
from jax.sharding import PartitionSpec as P
import functools

SMOOTHING = 0.2
PHYSICS = 0.5
HIGHEST = lax.Precision.HIGHEST
ROW_BLOCK = 8


def split_bf16(values):
    high = values.astype(jnp.bfloat16)
    low = (values - high.astype(jnp.float32)).astype(jnp.bfloat16)
    return high, low


def three_pass(lhs, rhs, dims):
    lhs_hi, lhs_lo = split_bf16(lhs)
    rhs_hi, rhs_lo = split_bf16(rhs)

    def one(a, b):
        return lax.dot_general(a, b, (dims, ((), ())), preferred_element_type=jnp.float32)

    return one(lhs_hi, rhs_hi) + (one(lhs_hi, rhs_lo) + one(lhs_lo, rhs_hi))


def exact_rows(picker, values):
    high = values.astype(jnp.bfloat16)
    rest = values - high.astype(jnp.float32)
    middle = rest.astype(jnp.bfloat16)
    low = (rest - middle.astype(jnp.float32)).astype(jnp.bfloat16)

    def one(piece):
        return lax.dot_general(
            picker, piece, (((1,), (1,)), ((), ())), preferred_element_type=jnp.float32
        )

    return one(high) + one(middle) + one(low)


def substep_kernel(with_flux, comp_total, x_ref, top_ref, bottom_ref, west_ref, east_ref, mix_ref, *rest):
    if with_flux:
        fluxes_ref, out_ref, flux_out_ref = rest
    else:
        out_ref, planes_ref = rest
    rows, cols, levels = x_ref.shape
    centre = x_ref[...]
    up = jnp.concatenate([top_ref[...], centre[:-1]], axis=0)
    down = jnp.concatenate([centre[1:], bottom_ref[...]], axis=0)
    column = lax.broadcasted_iota(jnp.int32, centre.shape, 1)
    west = jnp.where(column == 0, west_ref[...], pltpu.roll(centre, 1, 1))
    east = jnp.where(column == cols - 1, east_ref[...], pltpu.roll(centre, cols - 1, 1))
    smooth = centre + SMOOTHING * (up + down + west + east - 4.0 * centre)
    flat = smooth.reshape(rows * cols, levels)
    mixed = three_pass(flat, mix_ref[...], ((1,), (0,)))
    moved = flat + PHYSICS * jnp.tanh(mixed)
    out_ref[...] = moved.reshape(rows, cols, levels)
    if not with_flux:
        ocean = lax.axis_index("comp") == comp_total - 1

        @pl.when(ocean)
        def _():
            plane_row = lax.broadcasted_iota(jnp.int32, (8, levels), 0)
            plane_lane = lax.broadcasted_iota(jnp.int32, (8, levels), 1)
            pick_out = ((plane_row == 0) & (plane_lane == 0)).astype(jnp.bfloat16)
            pick_in = ((plane_row == 1) & (plane_lane == 0)).astype(jnp.bfloat16)
            planes_ref[...] = exact_rows(pick_out, moved) + exact_rows(
                pick_in, centre.reshape(rows * cols, levels)
            )

        @pl.when(jnp.logical_not(ocean))
        def _():
            planes_ref[...] = jnp.zeros_like(planes_ref)

    else:
        total = centre.reshape(rows * cols, levels) + moved
        flux_out_ref[...] = three_pass(fluxes_ref[...], total, ((1,), (1,)))


def substep(values, top, bottom, west, east, mixing, comp_total, fluxes_t=None):
    rows, cols, levels = values.shape
    blocks = rows // ROW_BLOCK
    top_rows = jnp.concatenate([top, values[ROW_BLOCK - 1 : rows - 1 : ROW_BLOCK]], axis=0)
    bottom_rows = jnp.concatenate([values[ROW_BLOCK:rows:ROW_BLOCK], bottom], axis=0)
    with_flux = fluxes_t is not None
    in_specs = [
        pl.BlockSpec((ROW_BLOCK, cols, levels), lambda i: (i, 0, 0)),
        pl.BlockSpec((1, cols, levels), lambda i: (i, 0, 0)),
        pl.BlockSpec((1, cols, levels), lambda i: (i, 0, 0)),
        pl.BlockSpec((ROW_BLOCK, 1, levels), lambda i: (i, 0, 0)),
        pl.BlockSpec((ROW_BLOCK, 1, levels), lambda i: (i, 0, 0)),
        pl.BlockSpec((levels, levels), lambda i: (0, 0)),
    ]
    operands = [values, top_rows, bottom_rows, west, east, mixing]
    out_shape = [jax.ShapeDtypeStruct(values.shape, jnp.float32)]
    out_specs = [pl.BlockSpec((ROW_BLOCK, cols, levels), lambda i: (i, 0, 0))]
    if not with_flux:
        out_shape.append(jax.ShapeDtypeStruct((8, rows * cols), jnp.float32))
        out_specs.append(pl.BlockSpec((8, ROW_BLOCK * cols), lambda i: (0, i)))
    if with_flux:
        flux_count = fluxes_t.shape[0]
        in_specs.append(pl.BlockSpec((flux_count, levels), lambda i: (0, 0)))
        operands.append(fluxes_t)
        out_shape.append(jax.ShapeDtypeStruct((flux_count, rows * cols), jnp.float32))
        out_specs.append(pl.BlockSpec((flux_count, ROW_BLOCK * cols), lambda i: (0, i)))
    cells = rows * cols
    flops = 6 * cells * levels * levels + (6 * cells * levels * 8 if with_flux else 0)
    result = pl.pallas_call(
        functools.partial(substep_kernel, with_flux, comp_total),
        grid=(blocks,),
        in_specs=in_specs,
        out_specs=out_specs,
        out_shape=out_shape,
        cost_estimate=pl.CostEstimate(
            flops=flops, transcendentals=cells * levels, bytes_accessed=8 * cells * levels
        ),
    )(*operands)
    return result


def column_physics(values, mixing):
    return jnp.tanh(jnp.einsum("rck,kj->rcj", values, mixing, precision=HIGHEST))


def earlier_same(owners, usable):
    positions = jnp.arange(owners.shape[0], dtype=jnp.int32)
    before = (
        (owners[None, :] == owners[:, None])
        & (positions[None, :] < positions[:, None])
        & usable[None, :]
    )
    return jnp.sum(before.astype(jnp.int32), axis=1)


def pack_rows(blocks, owners, labels, usable, slots_each, owner_total):
    ranks = earlier_same(owners, usable)
    target_slot = owners * slots_each + ranks
    slot_ids = jnp.arange(owner_total * slots_each, dtype=jnp.int32)
    placing = (slot_ids[:, None] == target_slot[None, :]) & usable[None, :]
    packed = jnp.dot(
        placing.astype(jnp.bfloat16), blocks, preferred_element_type=jnp.float32
    ).astype(jnp.bfloat16)
    placed_labels = jnp.sum(jnp.where(placing, labels[None, :] + 1, 0), axis=1) - 1
    return (
        packed.reshape(owner_total, slots_each, blocks.shape[1]),
        placed_labels.reshape(owner_total, slots_each),
        target_slot,
    )


def edge_rows(values, lower_valid, upper_valid):
    bands = lax.axis_size("comp") * lax.axis_size("lat")
    up = [(i, i + 1) for i in range(bands - 1)]
    down = [(j, i) for i, j in up]
    before = lax.ppermute(values[-1:], ("comp", "lat"), up)
    after = lax.ppermute(values[:1], ("comp", "lat"), down)
    return (jnp.where(lower_valid, before, 0.0), jnp.where(upper_valid, after, 0.0))


def edge_columns(values):
    size = lax.axis_size("lon")
    up = [(i, (i + 1) % size) for i in range(size)]
    down = [(j, i) for i, j in up]
    before = lax.ppermute(values[:, -1:], "lon", up)
    after = lax.ppermute(values[:, :1], "lon", down)
    return before, after


MESH_IDS = pl.DeviceIdType.MESH


def tile_device(comp, tile, lon_total):
    return (comp, tile // lon_total, tile % lon_total)


def gather_kernel(offsets, shape, send_ref, out_ref, land, send_sems, recv_sems):
    comp_total, lat_total, lon_total = shape
    comp = lax.axis_index("comp")
    tiles = lat_total * lon_total
    tile = lax.axis_index("lat") * lon_total + lax.axis_index("lon")
    ocean = comp_total - 1
    count = len(offsets)
    barrier = pltpu.get_barrier_semaphore()

    @pl.when(comp != ocean)
    def _():
        for off in offsets:
            target = tile_device(ocean, (tile + off) % tiles, lon_total)
            pl.semaphore_signal(barrier, 1, device_id=target, device_id_type=MESH_IDS)
        pl.semaphore_wait(barrier, count)
        copies = []
        for k, off in enumerate(offsets):
            target = tile_device(ocean, (tile + off) % tiles, lon_total)
            copy = pltpu.make_async_remote_copy(
                src_ref=send_ref.at[k],
                dst_ref=land.at[comp * count + k],
                send_sem=send_sems.at[k],
                recv_sem=recv_sems.at[comp * count + k],
                device_id=target,
                device_id_type=MESH_IDS,
            )
            copy.start()
            copies.append(copy)
        for copy in copies:
            copy.wait_send()
        out_ref[...] = jnp.zeros_like(out_ref)

    @pl.when(comp == ocean)
    def _():
        for source_comp in range(ocean):
            for off in offsets:
                source = tile_device(source_comp, (tile + tiles - off) % tiles, lon_total)
                pl.semaphore_signal(barrier, 1, device_id=source, device_id_type=MESH_IDS)
        pl.semaphore_wait(barrier, count * ocean)
        for source_comp in range(ocean):
            for k, off in enumerate(offsets):
                source = tile_device(source_comp, (tile + tiles - off) % tiles, lon_total)
                slot = source_comp * count + k
                pltpu.make_async_remote_copy(
                    src_ref=send_ref.at[k],
                    dst_ref=land.at[slot],
                    send_sem=send_sems.at[k],
                    recv_sem=recv_sems.at[slot],
                    device_id=source,
                    device_id_type=MESH_IDS,
                ).wait_recv()
        out_ref[...] = land[...]


def gather_to_ocean(blocks, offsets, shape):
    count = len(offsets)
    senders = (shape[0] - 1) * count
    slot_shape = blocks.shape[1:]
    return pl.pallas_call(
        functools.partial(gather_kernel, tuple(offsets), tuple(shape)),
        out_shape=jax.ShapeDtypeStruct((senders,) + slot_shape, blocks.dtype),
        in_specs=[pl.BlockSpec(memory_space=pltpu.VMEM)],
        out_specs=pl.BlockSpec(memory_space=pltpu.VMEM),
        scratch_shapes=[
            pltpu.VMEM((senders,) + slot_shape, blocks.dtype),
            pltpu.SemaphoreType.DMA((count,)),
            pltpu.SemaphoreType.DMA((senders,)),
        ],
        compiler_params=pltpu.CompilerParams(collective_id=0, has_side_effects=True),
    )(blocks)


def spread_kernel(offsets, shape, surface_ref, out_ref, land, send_sems, recv_sems):
    comp_total, lat_total, lon_total = shape
    comp = lax.axis_index("comp")
    tiles = lat_total * lon_total
    tile = lax.axis_index("lat") * lon_total + lax.axis_index("lon")
    ocean = comp_total - 1
    count = len(offsets)
    barrier = pltpu.get_barrier_semaphore()

    @pl.when(comp == ocean)
    def _():
        for target_comp in range(ocean):
            for off in offsets:
                target = tile_device(target_comp, (tile + tiles - off) % tiles, lon_total)
                pl.semaphore_signal(barrier, 1, device_id=target, device_id_type=MESH_IDS)
        pl.semaphore_wait(barrier, count * ocean)
        copies = []
        for target_comp in range(ocean):
            for k, off in enumerate(offsets):
                target = tile_device(target_comp, (tile + tiles - off) % tiles, lon_total)
                copy = pltpu.make_async_remote_copy(
                    src_ref=surface_ref.at[target_comp * count + k],
                    dst_ref=land.at[k],
                    send_sem=send_sems.at[target_comp * count + k],
                    recv_sem=recv_sems.at[k],
                    device_id=target,
                    device_id_type=MESH_IDS,
                )
                copy.start()
                copies.append(copy)
        for copy in copies:
            copy.wait_send()
        out_ref[...] = jnp.zeros_like(out_ref)

    @pl.when(comp != ocean)
    def _():
        for off in offsets:
            source = tile_device(ocean, (tile + off) % tiles, lon_total)
            pl.semaphore_signal(barrier, 1, device_id=source, device_id_type=MESH_IDS)
        pl.semaphore_wait(barrier, count)
        for k, off in enumerate(offsets):
            source = tile_device(ocean, (tile + off) % tiles, lon_total)
            pltpu.make_async_remote_copy(
                src_ref=surface_ref.at[k],
                dst_ref=land.at[k],
                send_sem=send_sems.at[k],
                recv_sem=recv_sems.at[k],
                device_id=source,
                device_id_type=MESH_IDS,
            ).wait_recv()
        out_ref[...] = land[...]


def spread_from_ocean(replies, offsets, shape):
    count = len(offsets)
    senders = (shape[0] - 1) * count
    slot_shape = replies.shape[1:]
    return pl.pallas_call(
        functools.partial(spread_kernel, tuple(offsets), tuple(shape)),
        out_shape=jax.ShapeDtypeStruct((count,) + slot_shape, replies.dtype),
        in_specs=[pl.BlockSpec(memory_space=pltpu.VMEM)],
        out_specs=pl.BlockSpec(memory_space=pltpu.VMEM),
        scratch_shapes=[
            pltpu.VMEM((count,) + slot_shape, replies.dtype),
            pltpu.SemaphoreType.DMA((senders,)),
            pltpu.SemaphoreType.DMA((count,)),
        ],
        compiler_params=pltpu.CompilerParams(collective_id=1, has_side_effects=True),
    )(replies)


def regrid_kernel(weight_ids_ref, rows_ref, fluxes_ref, weights_ref, out_ref):
    flux_count, tile_rows, block_len = out_ref.shape
    entries = fluxes_ref.shape[0]
    weight_count = weights_ref.shape[0]
    out_ref[...] = jnp.zeros_like(out_ref)
    row_ids = lax.broadcasted_iota(jnp.int32, (tile_rows, entries), 0)
    row_hits = row_ids == rows_ref[...]

    def one_weight(w, carry):
        picker = (row_hits & (weight_ids_ref[...] == w)).astype(jnp.bfloat16)
        weight = weights_ref[w]
        for f in range(flux_count):
            binned = jnp.dot(
                picker,
                fluxes_ref[:, f * block_len : (f + 1) * block_len],
                preferred_element_type=jnp.float32,
            )
            high = binned.astype(jnp.bfloat16)
            low = (binned - high.astype(jnp.float32)).astype(jnp.bfloat16)
            out_ref[f] += jnp.dot(high, weight, preferred_element_type=jnp.float32) + jnp.dot(
                low, weight, preferred_element_type=jnp.float32
            )
        return carry

    lax.fori_loop(0, weight_count, one_weight, 0)


def regrid_arrivals(weight_ids, rows, fluxes, weights, flux_count):
    entries, width = fluxes.shape
    weight_count, block_len, _ = weights.shape
    tile_rows = block_len
    cells = flux_count * tile_rows * block_len
    return pl.pallas_call(
        regrid_kernel,
        out_shape=jax.ShapeDtypeStruct((flux_count, tile_rows, block_len), jnp.float32),
        in_specs=[pl.BlockSpec(memory_space=pltpu.VMEM)] * 4,
        out_specs=pl.BlockSpec(memory_space=pltpu.VMEM),
        cost_estimate=pl.CostEstimate(
            flops=2 * weight_count * flux_count * (tile_rows * entries * block_len + 2 * tile_rows * block_len * block_len),
            transcendentals=0,
            bytes_accessed=entries * width * 2 + weight_count * block_len * block_len * 2 + cells * 4,
        ),
    )(weight_ids, rows, fluxes, weights)


def local(
    state, land_mask, intersection_list, mix_atm, mix_ocn, flux_map, ocean_map, regrid_weights
):
    tile_rows, block_len, levels = state.shape
    flux_count = flux_map.shape[1]
    weight_count = regrid_weights.shape[0]
    intersections = intersection_list.shape[2]
    comp_count = lax.axis_size("comp")
    lat_count = lax.axis_size("lat")
    lon_count = lax.axis_size("lon")
    tile_count = lat_count * lon_count
    reach = min(4, lon_count)
    neighbour_count = 2 * reach
    capacity = intersections * tile_rows // neighbour_count
    width = flux_count * block_len
    comp_index = lax.axis_index("comp")
    tile_index = lax.axis_index("lat") * lon_count + lax.axis_index("lon")
    band = comp_index * lat_count + lax.axis_index("lat")
    ocean_band = (comp_count - 1) * lat_count
    ocean_side = comp_index == comp_count - 1
    lower_valid = (band > 0) & ((band - 1 >= ocean_band) == (band >= ocean_band))
    upper_valid = (band < comp_count * lat_count - 1) & (
        (band + 1 >= ocean_band) == (band >= ocean_band)
    )
    sea_cells = land_mask == 1

    top, bottom = edge_rows(state, lower_valid, upper_valid)
    west, east = edge_columns(state)
    mixing = jnp.where(ocean_side, mix_ocn, mix_atm)
    first, first_planes = substep(state, top, bottom, west, east, mixing, comp_count)
    first_top = first_planes[0].reshape(tile_rows, block_len)
    state_top = first_planes[1].reshape(tile_rows, block_len)
    top, bottom = edge_rows(first, lower_valid, upper_valid)
    west, east = edge_columns(first)

    def atmosphere_second(values, top, bottom, west, east):
        moved, total = substep(values, top, bottom, west, east, mix_atm, comp_count, flux_map.T)
        total = total.reshape(flux_count, tile_rows, block_len)
        sent = jnp.where(sea_cells[None], 0.5 * total, 0.0).astype(jnp.bfloat16)
        return moved, sent

    def ocean_second(values, top, bottom, west, east):
        return values, jnp.zeros((flux_count, tile_rows, block_len), jnp.bfloat16)

    second, flux_sent = lax.cond(
        ocean_side, ocean_second, atmosphere_second, first, top, bottom, west, east
    )
    entry_list = intersection_list.reshape(tile_rows * intersections, 3)
    owners = entry_list[:, 0]
    targets = entry_list[:, 1]
    weight_ids = entry_list[:, 2]
    labels = weight_ids * tile_rows + targets
    entry_blocks = jnp.repeat(flux_sent.transpose(1, 0, 2), intersections, axis=0).reshape(
        tile_rows * intersections, width
    )
    lane = jnp.arange(128, dtype=jnp.int32)[None, :]
    label_lanes = jnp.where(
        lane == 0, weight_ids[:, None], jnp.where(lane == 1, targets[:, None], 0)
    ).astype(jnp.bfloat16)
    entry_blocks = jnp.concatenate([entry_blocks, label_lanes], axis=1)
    sending = jnp.broadcast_to(jnp.logical_not(ocean_side), owners.shape)
    offsets = [
        (n // reach * lon_count + n % reach - (reach - 1) // 2) % tile_count
        for n in range(neighbour_count)
    ]
    offset_table = jnp.array(offsets, jnp.int32)
    distance = (owners - tile_index + tile_count) % tile_count
    neighbour_ids = jnp.sum(
        jnp.where(
            distance[:, None] == offset_table[None, :],
            jnp.arange(neighbour_count, dtype=jnp.int32)[None, :],
            0,
        ),
        axis=1,
    )
    packed, _, entry_slots = pack_rows(entry_blocks, neighbour_ids, labels, sending, capacity, neighbour_count)
    mesh_shape = (comp_count, lat_count, lon_count)
    arrived = gather_to_ocean(packed, offsets, mesh_shape)
    weights_low = regrid_weights
    weights_wide = regrid_weights.astype(jnp.float32)
    senders = (comp_count - 1) * neighbour_count

    def ocean_reply(values_top, arrived):
        flat = arrived.reshape(-1, width + 128)
        arrived_labels = flat[:, width].astype(jnp.int32) * tile_rows + flat[:, width + 1].astype(
            jnp.int32
        )
        forcing = regrid_arrivals(
            flat[:, width].astype(jnp.int32)[None],
            flat[:, width + 1].astype(jnp.int32)[None],
            flat,
            weights_low,
            flux_count,
        )
        lifted = jnp.sum(forcing * ocean_map[:, 0][:, None, None], axis=0)
        top_level = jnp.where(sea_cells, values_top + lifted, state_top)
        table = jnp.einsum("db,wab->wda", top_level, weights_wide, precision=HIGHEST)
        replies = jnp.take(table.reshape(weight_count * tile_rows, block_len), arrived_labels, axis=0)
        return forcing, replies.reshape(senders, capacity, block_len), top_level

    def atmosphere_reply(values_top, arrived):
        return (
            jnp.zeros((flux_count, tile_rows, block_len), jnp.float32),
            jnp.zeros((senders, capacity, block_len), jnp.float32),
            values_top,
        )

    forcing, replies, ocean_top = lax.cond(
        ocean_side, ocean_reply, atmosphere_reply, first_top, arrived
    )
    answers = spread_from_ocean(replies, offsets, mesh_shape)
    per_entry = jnp.take(
        answers.reshape(neighbour_count * capacity, block_len), entry_slots, axis=0
    )
    returned = per_entry.reshape(tile_rows, intersections, block_len).sum(axis=1)
    first, forcing, answers = lax.optimization_barrier((first, forcing, answers))

    def ocean_final(values, forcing):
        moved = values + jnp.einsum("frc,fk->rck", forcing, ocean_map, precision=HIGHEST)
        return jnp.where(sea_cells[:, :, None], moved, state)

    final_state = lax.cond(ocean_side, ocean_final, lambda values, forcing: second, first, forcing)
    surface_out = jnp.where(
        ocean_side, ocean_top, jnp.where(sea_cells, returned, final_state[:, :, 0])
    )
    return (final_state, surface_out)


def solution(mesh):
    placed = (
        P(("comp", "lat"), "lon", None),
        P(("comp", "lat"), "lon"),
        P(("comp", "lat"), "lon", None, None),
        P(),
        P(),
        P(),
        P(),
        P(),
    )
    return jax.shard_map(
        local,
        mesh=mesh,
        in_specs=placed,
        out_specs=(P(("comp", "lat"), "lon", None), P(("comp", "lat"), "lon")),
        check_vma=False,
    )
```

```python
import jax
import jax.numpy as jnp
from jax import lax
from jax.experimental import pallas as pl
from jax.experimental.pallas import tpu as pltpu
from jax.sharding import PartitionSpec as P
import functools

SMOOTHING = 0.2
PHYSICS = 0.5
HIGHEST = lax.Precision.HIGHEST
ROW_BLOCK = 8


def split_bf16(values):
    high = values.astype(jnp.bfloat16)
    low = (values - high.astype(jnp.float32)).astype(jnp.bfloat16)
    return high, low


def three_pass(lhs, rhs, dims):
    lhs_hi, lhs_lo = split_bf16(lhs)
    rhs_hi, rhs_lo = split_bf16(rhs)

    def one(a, b):
        return lax.dot_general(a, b, (dims, ((), ())), preferred_element_type=jnp.float32)

    return one(lhs_hi, rhs_hi) + (one(lhs_hi, rhs_lo) + one(lhs_lo, rhs_hi))


def exact_rows(picker, values):
    high = values.astype(jnp.bfloat16)
    rest = values - high.astype(jnp.float32)
    middle = rest.astype(jnp.bfloat16)
    low = (rest - middle.astype(jnp.float32)).astype(jnp.bfloat16)

    def one(piece):
        return lax.dot_general(
            picker, piece, (((1,), (1,)), ((), ())), preferred_element_type=jnp.float32
        )

    return one(high) + one(middle) + one(low)


def substep_kernel(with_flux, comp_total, x_ref, top_ref, bottom_ref, west_ref, east_ref, mix_ref, *rest):
    if with_flux:
        fluxes_ref, out_ref, flux_out_ref = rest
    else:
        out_ref, planes_ref = rest
    rows, cols, levels = x_ref.shape
    centre = x_ref[...]
    up = jnp.concatenate([top_ref[...], centre[:-1]], axis=0)
    down = jnp.concatenate([centre[1:], bottom_ref[...]], axis=0)
    column = lax.broadcasted_iota(jnp.int32, centre.shape, 1)
    west = jnp.where(column == 0, west_ref[...], pltpu.roll(centre, 1, 1))
    east = jnp.where(column == cols - 1, east_ref[...], pltpu.roll(centre, cols - 1, 1))
    smooth = centre + SMOOTHING * (up + down + west + east - 4.0 * centre)
    flat = smooth.reshape(rows * cols, levels)
    mixed = three_pass(flat, mix_ref[...], ((1,), (0,)))
    moved = flat + PHYSICS * jnp.tanh(mixed)
    out_ref[...] = moved.reshape(rows, cols, levels)
    if not with_flux:
        ocean = lax.axis_index("comp") == comp_total - 1

        @pl.when(ocean)
        def _():
            plane_row = lax.broadcasted_iota(jnp.int32, (8, levels), 0)
            plane_lane = lax.broadcasted_iota(jnp.int32, (8, levels), 1)
            pick_out = ((plane_row == 0) & (plane_lane == 0)).astype(jnp.bfloat16)
            pick_in = ((plane_row == 1) & (plane_lane == 0)).astype(jnp.bfloat16)
            planes_ref[...] = exact_rows(pick_out, moved) + exact_rows(
                pick_in, centre.reshape(rows * cols, levels)
            )

        @pl.when(jnp.logical_not(ocean))
        def _():
            planes_ref[...] = jnp.zeros_like(planes_ref)

    else:
        total = centre.reshape(rows * cols, levels) + moved
        flux_out_ref[...] = three_pass(fluxes_ref[...], total, ((1,), (1,)))


def substep(values, top, bottom, west, east, mixing, comp_total, fluxes_t=None):
    rows, cols, levels = values.shape
    blocks = rows // ROW_BLOCK
    top_rows = jnp.concatenate([top, values[ROW_BLOCK - 1 : rows - 1 : ROW_BLOCK]], axis=0)
    bottom_rows = jnp.concatenate([values[ROW_BLOCK:rows:ROW_BLOCK], bottom], axis=0)
    with_flux = fluxes_t is not None
    in_specs = [
        pl.BlockSpec((ROW_BLOCK, cols, levels), lambda i: (i, 0, 0)),
        pl.BlockSpec((1, cols, levels), lambda i: (i, 0, 0)),
        pl.BlockSpec((1, cols, levels), lambda i: (i, 0, 0)),
        pl.BlockSpec((ROW_BLOCK, 1, levels), lambda i: (i, 0, 0)),
        pl.BlockSpec((ROW_BLOCK, 1, levels), lambda i: (i, 0, 0)),
        pl.BlockSpec((levels, levels), lambda i: (0, 0)),
    ]
    operands = [values, top_rows, bottom_rows, west, east, mixing]
    out_shape = [jax.ShapeDtypeStruct(values.shape, jnp.float32)]
    out_specs = [pl.BlockSpec((ROW_BLOCK, cols, levels), lambda i: (i, 0, 0))]
    if not with_flux:
        out_shape.append(jax.ShapeDtypeStruct((8, rows * cols), jnp.float32))
        out_specs.append(pl.BlockSpec((8, ROW_BLOCK * cols), lambda i: (0, i)))
    if with_flux:
        flux_count = fluxes_t.shape[0]
        in_specs.append(pl.BlockSpec((flux_count, levels), lambda i: (0, 0)))
        operands.append(fluxes_t)
        out_shape.append(jax.ShapeDtypeStruct((flux_count, rows * cols), jnp.float32))
        out_specs.append(pl.BlockSpec((flux_count, ROW_BLOCK * cols), lambda i: (0, i)))
    cells = rows * cols
    flops = 6 * cells * levels * levels + (6 * cells * levels * 8 if with_flux else 0)
    result = pl.pallas_call(
        functools.partial(substep_kernel, with_flux, comp_total),
        grid=(blocks,),
        in_specs=in_specs,
        out_specs=out_specs,
        out_shape=out_shape,
        cost_estimate=pl.CostEstimate(
            flops=flops, transcendentals=cells * levels, bytes_accessed=8 * cells * levels
        ),
    )(*operands)
    return result


def column_physics(values, mixing):
    return jnp.tanh(jnp.einsum("rck,kj->rcj", values, mixing, precision=HIGHEST))


def earlier_same(owners, usable):
    positions = jnp.arange(owners.shape[0], dtype=jnp.int32)
    before = (
        (owners[None, :] == owners[:, None])
        & (positions[None, :] < positions[:, None])
        & usable[None, :]
    )
    return jnp.sum(before.astype(jnp.int32), axis=1)


def pack_rows(blocks, owners, labels, usable, slots_each, owner_total):
    ranks = earlier_same(owners, usable)
    target_slot = owners * slots_each + ranks
    slot_ids = jnp.arange(owner_total * slots_each, dtype=jnp.int32)
    placing = (slot_ids[:, None] == target_slot[None, :]) & usable[None, :]
    packed = jnp.dot(
        placing.astype(jnp.bfloat16), blocks, preferred_element_type=jnp.float32
    ).astype(jnp.bfloat16)
    placed_labels = jnp.sum(jnp.where(placing, labels[None, :] + 1, 0), axis=1) - 1
    return (
        packed.reshape(owner_total, slots_each, blocks.shape[1]),
        placed_labels.reshape(owner_total, slots_each),
        target_slot,
    )


def edge_rows(values, lower_valid, upper_valid):
    bands = lax.axis_size("comp") * lax.axis_size("lat")
    up = [(i, i + 1) for i in range(bands - 1)]
    down = [(j, i) for i, j in up]
    before = lax.ppermute(values[-1:], ("comp", "lat"), up)
    after = lax.ppermute(values[:1], ("comp", "lat"), down)
    return (jnp.where(lower_valid, before, 0.0), jnp.where(upper_valid, after, 0.0))


def edge_columns(values):
    size = lax.axis_size("lon")
    up = [(i, (i + 1) % size) for i in range(size)]
    down = [(j, i) for i, j in up]
    before = lax.ppermute(values[:, -1:], "lon", up)
    after = lax.ppermute(values[:, :1], "lon", down)
    return before, after


MESH_IDS = pl.DeviceIdType.MESH


def tile_device(comp, tile, lon_total):
    return (comp, tile // lon_total, tile % lon_total)


def gather_kernel(offsets, shape, send_ref, out_ref, land, send_sems, recv_sems):
    comp_total, lat_total, lon_total = shape
    comp = lax.axis_index("comp")
    tiles = lat_total * lon_total
    tile = lax.axis_index("lat") * lon_total + lax.axis_index("lon")
    ocean = comp_total - 1
    count = len(offsets)
    barrier = pltpu.get_barrier_semaphore()

    @pl.when(comp != ocean)
    def _():
        for off in offsets:
            target = tile_device(ocean, (tile + off) % tiles, lon_total)
            pl.semaphore_signal(barrier, 1, device_id=target, device_id_type=MESH_IDS)
        pl.semaphore_wait(barrier, count)
        copies = []
        for k, off in enumerate(offsets):
            target = tile_device(ocean, (tile + off) % tiles, lon_total)
            copy = pltpu.make_async_remote_copy(
                src_ref=send_ref.at[k],
                dst_ref=land.at[comp * count + k],
                send_sem=send_sems.at[k],
                recv_sem=recv_sems.at[comp * count + k],
                device_id=target,
                device_id_type=MESH_IDS,
            )
            copy.start()
            copies.append(copy)
        for copy in copies:
            copy.wait_send()
        out_ref[...] = jnp.zeros_like(out_ref)

    @pl.when(comp == ocean)
    def _():
        for source_comp in range(ocean):
            for off in offsets:
                source = tile_device(source_comp, (tile + tiles - off) % tiles, lon_total)
                pl.semaphore_signal(barrier, 1, device_id=source, device_id_type=MESH_IDS)
        pl.semaphore_wait(barrier, count * ocean)
        for source_comp in range(ocean):
            for k, off in enumerate(offsets):
                source = tile_device(source_comp, (tile + tiles - off) % tiles, lon_total)
                slot = source_comp * count + k
                pltpu.make_async_remote_copy(
                    src_ref=send_ref.at[k],
                    dst_ref=land.at[slot],
                    send_sem=send_sems.at[k],
                    recv_sem=recv_sems.at[slot],
                    device_id=source,
                    device_id_type=MESH_IDS,
                ).wait_recv()
        out_ref[...] = land[...]


def gather_to_ocean(blocks, offsets, shape):
    count = len(offsets)
    senders = (shape[0] - 1) * count
    slot_shape = blocks.shape[1:]
    return pl.pallas_call(
        functools.partial(gather_kernel, tuple(offsets), tuple(shape)),
        out_shape=jax.ShapeDtypeStruct((senders,) + slot_shape, blocks.dtype),
        in_specs=[pl.BlockSpec(memory_space=pltpu.VMEM)],
        out_specs=pl.BlockSpec(memory_space=pltpu.VMEM),
        scratch_shapes=[
            pltpu.VMEM((senders,) + slot_shape, blocks.dtype),
            pltpu.SemaphoreType.DMA((count,)),
            pltpu.SemaphoreType.DMA((senders,)),
        ],
        compiler_params=pltpu.CompilerParams(collective_id=0, has_side_effects=True),
    )(blocks)


def spread_kernel(offsets, shape, surface_ref, out_ref, land, send_sems, recv_sems):
    comp_total, lat_total, lon_total = shape
    comp = lax.axis_index("comp")
    tiles = lat_total * lon_total
    tile = lax.axis_index("lat") * lon_total + lax.axis_index("lon")
    ocean = comp_total - 1
    count = len(offsets)
    barrier = pltpu.get_barrier_semaphore()

    @pl.when(comp == ocean)
    def _():
        for target_comp in range(ocean):
            for off in offsets:
                target = tile_device(target_comp, (tile + tiles - off) % tiles, lon_total)
                pl.semaphore_signal(barrier, 1, device_id=target, device_id_type=MESH_IDS)
        pl.semaphore_wait(barrier, count * ocean)
        copies = []
        for target_comp in range(ocean):
            for k, off in enumerate(offsets):
                target = tile_device(target_comp, (tile + tiles - off) % tiles, lon_total)
                copy = pltpu.make_async_remote_copy(
                    src_ref=surface_ref.at[target_comp * count + k],
                    dst_ref=land.at[k],
                    send_sem=send_sems.at[target_comp * count + k],
                    recv_sem=recv_sems.at[k],
                    device_id=target,
                    device_id_type=MESH_IDS,
                )
                copy.start()
                copies.append(copy)
        for copy in copies:
            copy.wait_send()
        out_ref[...] = jnp.zeros_like(out_ref)

    @pl.when(comp != ocean)
    def _():
        for off in offsets:
            source = tile_device(ocean, (tile + off) % tiles, lon_total)
            pl.semaphore_signal(barrier, 1, device_id=source, device_id_type=MESH_IDS)
        pl.semaphore_wait(barrier, count)
        for k, off in enumerate(offsets):
            source = tile_device(ocean, (tile + off) % tiles, lon_total)
            pltpu.make_async_remote_copy(
                src_ref=surface_ref.at[k],
                dst_ref=land.at[k],
                send_sem=send_sems.at[k],
                recv_sem=recv_sems.at[k],
                device_id=source,
                device_id_type=MESH_IDS,
            ).wait_recv()
        out_ref[...] = land[...]


def spread_from_ocean(replies, offsets, shape):
    count = len(offsets)
    senders = (shape[0] - 1) * count
    slot_shape = replies.shape[1:]
    return pl.pallas_call(
        functools.partial(spread_kernel, tuple(offsets), tuple(shape)),
        out_shape=jax.ShapeDtypeStruct((count,) + slot_shape, replies.dtype),
        in_specs=[pl.BlockSpec(memory_space=pltpu.VMEM)],
        out_specs=pl.BlockSpec(memory_space=pltpu.VMEM),
        scratch_shapes=[
            pltpu.VMEM((count,) + slot_shape, replies.dtype),
            pltpu.SemaphoreType.DMA((senders,)),
            pltpu.SemaphoreType.DMA((count,)),
        ],
        compiler_params=pltpu.CompilerParams(collective_id=1, has_side_effects=True),
    )(replies)


def ocean_update_kernel(first_ref, state_ref, sea_ref, forcing_ref, spread_ref, out_ref):
    rows, cols, levels = first_ref.shape
    forcing = forcing_ref[...]
    spread = spread_ref[...]
    forcing_hi = forcing.astype(jnp.bfloat16)
    forcing_lo = (forcing - forcing_hi.astype(jnp.float32)).astype(jnp.bfloat16)
    spread_hi = spread.astype(jnp.bfloat16)
    spread_lo = (spread - spread_hi.astype(jnp.float32)).astype(jnp.bfloat16)

    def one(a, b):
        return lax.dot_general(a, b, (((0,), (0,)), ((), ())), preferred_element_type=jnp.float32)

    added = one(forcing_hi, spread_hi) + (one(forcing_hi, spread_lo) + one(forcing_lo, spread_hi))
    lane_row = lax.broadcasted_iota(jnp.int32, (8, levels), 0)
    ones = (lane_row == 0).astype(jnp.bfloat16)
    picks = jnp.where(lax.broadcasted_iota(jnp.int32, sea_ref.shape, 0) == 0, sea_ref[...], 0)
    mask = one(picks.astype(jnp.bfloat16), ones)
    moved = first_ref[...].reshape(rows * cols, levels) + added
    kept = jnp.where(mask > 0.5, moved, state_ref[...].reshape(rows * cols, levels))
    out_ref[...] = kept.reshape(rows, cols, levels)


def ocean_update(first, state, sea_rows, forcing, ocean_map):
    rows, cols, levels = first.shape
    flux_count = forcing.shape[0]
    cells = rows * cols
    return pl.pallas_call(
        ocean_update_kernel,
        grid=(rows // ROW_BLOCK,),
        in_specs=[
            pl.BlockSpec((ROW_BLOCK, cols, levels), lambda i: (i, 0, 0)),
            pl.BlockSpec((ROW_BLOCK, cols, levels), lambda i: (i, 0, 0)),
            pl.BlockSpec((8, ROW_BLOCK * cols), lambda i: (0, i)),
            pl.BlockSpec((flux_count, ROW_BLOCK * cols), lambda i: (0, i)),
            pl.BlockSpec((flux_count, levels), lambda i: (0, 0)),
        ],
        out_specs=pl.BlockSpec((ROW_BLOCK, cols, levels), lambda i: (i, 0, 0)),
        out_shape=jax.ShapeDtypeStruct(first.shape, jnp.float32),
        cost_estimate=pl.CostEstimate(
            flops=8 * cells * levels * flux_count, transcendentals=0, bytes_accessed=12 * cells * levels
        ),
    )(first, state, sea_rows, forcing, ocean_map)


def local(
    state, land_mask, intersection_list, mix_atm, mix_ocn, flux_map, ocean_map, regrid_weights
):
    tile_rows, block_len, levels = state.shape
    flux_count = flux_map.shape[1]
    weight_count = regrid_weights.shape[0]
    intersections = intersection_list.shape[2]
    comp_count = lax.axis_size("comp")
    lat_count = lax.axis_size("lat")
    lon_count = lax.axis_size("lon")
    tile_count = lat_count * lon_count
    reach = min(4, lon_count)
    neighbour_count = 2 * reach
    capacity = intersections * tile_rows // neighbour_count
    width = flux_count * block_len
    comp_index = lax.axis_index("comp")
    tile_index = lax.axis_index("lat") * lon_count + lax.axis_index("lon")
    band = comp_index * lat_count + lax.axis_index("lat")
    ocean_band = (comp_count - 1) * lat_count
    ocean_side = comp_index == comp_count - 1
    lower_valid = (band > 0) & ((band - 1 >= ocean_band) == (band >= ocean_band))
    upper_valid = (band < comp_count * lat_count - 1) & (
        (band + 1 >= ocean_band) == (band >= ocean_band)
    )
    sea_cells = land_mask == 1

    top, bottom = edge_rows(state, lower_valid, upper_valid)
    west, east = edge_columns(state)
    mixing = jnp.where(ocean_side, mix_ocn, mix_atm)
    first, first_planes = substep(state, top, bottom, west, east, mixing, comp_count)
    first_top = first_planes[0].reshape(tile_rows, block_len)
    state_top = first_planes[1].reshape(tile_rows, block_len)
    top, bottom = edge_rows(first, lower_valid, upper_valid)
    west, east = edge_columns(first)

    def atmosphere_second(values, top, bottom, west, east):
        moved, total = substep(values, top, bottom, west, east, mix_atm, comp_count, flux_map.T)
        total = total.reshape(flux_count, tile_rows, block_len)
        sent = jnp.where(sea_cells[None], 0.5 * total, 0.0).astype(jnp.bfloat16)
        return moved, sent

    def ocean_second(values, top, bottom, west, east):
        return values, jnp.zeros((flux_count, tile_rows, block_len), jnp.bfloat16)

    second, flux_sent = lax.cond(
        ocean_side, ocean_second, atmosphere_second, first, top, bottom, west, east
    )
    entry_list = intersection_list.reshape(tile_rows * intersections, 3)
    owners = entry_list[:, 0]
    targets = entry_list[:, 1]
    weight_ids = entry_list[:, 2]
    labels = weight_ids * tile_rows + targets
    entry_blocks = jnp.repeat(flux_sent.transpose(1, 0, 2), intersections, axis=0).reshape(
        tile_rows * intersections, width
    )
    lane = jnp.arange(128, dtype=jnp.int32)[None, :]
    label_lanes = jnp.where(
        lane == 0, weight_ids[:, None], jnp.where(lane == 1, targets[:, None], 0)
    ).astype(jnp.bfloat16)
    entry_blocks = jnp.concatenate([entry_blocks, label_lanes], axis=1)
    sending = jnp.broadcast_to(jnp.logical_not(ocean_side), owners.shape)
    offsets = [
        (n // reach * lon_count + n % reach - (reach - 1) // 2) % tile_count
        for n in range(neighbour_count)
    ]
    offset_table = jnp.array(offsets, jnp.int32)
    distance = (owners - tile_index + tile_count) % tile_count
    neighbour_ids = jnp.sum(
        jnp.where(
            distance[:, None] == offset_table[None, :],
            jnp.arange(neighbour_count, dtype=jnp.int32)[None, :],
            0,
        ),
        axis=1,
    )
    packed, _, entry_slots = pack_rows(entry_blocks, neighbour_ids, labels, sending, capacity, neighbour_count)
    mesh_shape = (comp_count, lat_count, lon_count)
    arrived = gather_to_ocean(packed, offsets, mesh_shape)
    weights_low = regrid_weights
    weights_wide = regrid_weights.astype(jnp.float32)
    senders = (comp_count - 1) * neighbour_count

    def ocean_reply(values_top, arrived):
        flat = arrived.reshape(-1, width + 128)
        arrived_labels = flat[:, width].astype(jnp.int32) * tile_rows + flat[:, width + 1].astype(
            jnp.int32
        )
        fluxes = flat[:, :width]
        label_ids = jnp.arange(weight_count * tile_rows, dtype=jnp.int32)
        selector = (arrived_labels[:, None] == label_ids[None, :]).astype(jnp.bfloat16)
        binned = lax.dot_general(
            selector, fluxes, (((0,), (0,)), ((), ())), preferred_element_type=jnp.float32
        )
        binned = binned.reshape(weight_count, tile_rows, flux_count, block_len)
        binned_hi = lax.reduce_precision(binned, exponent_bits=8, mantissa_bits=7)
        binned_lo = (binned - binned_hi).astype(jnp.bfloat16)
        forcing = jnp.einsum(
            "wdfa,wab->fdb",
            binned_hi.astype(jnp.bfloat16),
            weights_low,
            preferred_element_type=jnp.float32,
        ) + jnp.einsum("wdfa,wab->fdb", binned_lo, weights_low, preferred_element_type=jnp.float32)
        lifted = jnp.sum(forcing * ocean_map[:, 0][:, None, None], axis=0)
        top_level = jnp.where(sea_cells, values_top + lifted, state_top)
        table = jnp.einsum("db,wab->wda", top_level, weights_wide, precision=HIGHEST)
        replies = jnp.take(table.reshape(weight_count * tile_rows, block_len), arrived_labels, axis=0)
        return forcing, replies.reshape(senders, capacity, block_len), top_level

    def atmosphere_reply(values_top, arrived):
        return (
            jnp.zeros((flux_count, tile_rows, block_len), jnp.float32),
            jnp.zeros((senders, capacity, block_len), jnp.float32),
            values_top,
        )

    forcing, replies, ocean_top = lax.cond(
        ocean_side, ocean_reply, atmosphere_reply, first_top, arrived
    )
    answers = spread_from_ocean(replies, offsets, mesh_shape)
    per_entry = jnp.take(
        answers.reshape(neighbour_count * capacity, block_len), entry_slots, axis=0
    )
    returned = per_entry.reshape(tile_rows, intersections, block_len).sum(axis=1)
    first, forcing, answers = lax.optimization_barrier((first, forcing, answers))

    def ocean_final(values, forcing):
        sea_rows = jnp.broadcast_to(
            (land_mask == 1).astype(jnp.int32).reshape(1, tile_rows * block_len),
            (8, tile_rows * block_len),
        )
        return ocean_update(
            values, state, sea_rows, forcing.reshape(flux_count, tile_rows * block_len), ocean_map
        )

    final_state = lax.cond(ocean_side, ocean_final, lambda values, forcing: second, first, forcing)
    surface_out = jnp.where(
        ocean_side, ocean_top, jnp.where(sea_cells, returned, final_state[:, :, 0])
    )
    return (final_state, surface_out)


def solution(mesh):
    placed = (
        P(("comp", "lat"), "lon", None),
        P(("comp", "lat"), "lon"),
        P(("comp", "lat"), "lon", None, None),
        P(),
        P(),
        P(),
        P(),
        P(),
    )
    return jax.shard_map(
        local,
        mesh=mesh,
        in_specs=placed,
        out_specs=(P(("comp", "lat"), "lon", None), P(("comp", "lat"), "lon")),
        check_vma=False,
    )
```

```python
import jax
import jax.numpy as jnp
from jax import lax
from jax.experimental import pallas as pl
from jax.experimental.pallas import tpu as pltpu
from jax.sharding import PartitionSpec as P
import functools

SMOOTHING = 0.2
PHYSICS = 0.5
HIGHEST = lax.Precision.HIGHEST
ROW_BLOCK = 8


def split_bf16(values):
    high = values.astype(jnp.bfloat16)
    low = (values - high.astype(jnp.float32)).astype(jnp.bfloat16)
    return high, low


def three_pass(lhs, rhs, dims):
    lhs_hi, lhs_lo = split_bf16(lhs)
    rhs_hi, rhs_lo = split_bf16(rhs)

    def one(a, b):
        return lax.dot_general(a, b, (dims, ((), ())), preferred_element_type=jnp.float32)

    return one(lhs_hi, rhs_hi) + (one(lhs_hi, rhs_lo) + one(lhs_lo, rhs_hi))


def exact_rows(picker, values):
    high = values.astype(jnp.bfloat16)
    rest = values - high.astype(jnp.float32)
    middle = rest.astype(jnp.bfloat16)
    low = (rest - middle.astype(jnp.float32)).astype(jnp.bfloat16)

    def one(piece):
        return lax.dot_general(
            picker, piece, (((1,), (1,)), ((), ())), preferred_element_type=jnp.float32
        )

    return one(high) + one(middle) + one(low)


def substep_kernel(with_flux, comp_total, x_ref, top_ref, bottom_ref, west_ref, east_ref, mix_ref, *rest):
    if with_flux:
        fluxes_ref, out_ref, flux_out_ref = rest
    else:
        out_ref, planes_ref = rest
    rows, cols, levels = x_ref.shape
    centre = x_ref[...]
    up = jnp.concatenate([top_ref[...], centre[:-1]], axis=0)
    down = jnp.concatenate([centre[1:], bottom_ref[...]], axis=0)
    column = lax.broadcasted_iota(jnp.int32, centre.shape, 1)
    west = jnp.where(column == 0, west_ref[...], pltpu.roll(centre, 1, 1))
    east = jnp.where(column == cols - 1, east_ref[...], pltpu.roll(centre, cols - 1, 1))
    smooth = centre + SMOOTHING * (up + down + west + east - 4.0 * centre)
    flat = smooth.reshape(rows * cols, levels)
    mixed = three_pass(flat, mix_ref[...], ((1,), (0,)))
    moved = flat + PHYSICS * jnp.tanh(mixed)
    out_ref[...] = moved.reshape(rows, cols, levels)
    if not with_flux:
        ocean = lax.axis_index("comp") == comp_total - 1

        @pl.when(ocean)
        def _():
            plane_row = lax.broadcasted_iota(jnp.int32, (8, levels), 0)
            plane_lane = lax.broadcasted_iota(jnp.int32, (8, levels), 1)
            pick_out = ((plane_row == 0) & (plane_lane == 0)).astype(jnp.bfloat16)
            pick_in = ((plane_row == 1) & (plane_lane == 0)).astype(jnp.bfloat16)
            planes_ref[...] = exact_rows(pick_out, moved) + exact_rows(
                pick_in, centre.reshape(rows * cols, levels)
            )

        @pl.when(jnp.logical_not(ocean))
        def _():
            planes_ref[...] = jnp.zeros_like(planes_ref)

    else:
        total = centre.reshape(rows * cols, levels) + moved
        flux_out_ref[...] = three_pass(fluxes_ref[...], total, ((1,), (1,)))


def substep(values, top, bottom, west, east, mixing, comp_total, fluxes_t=None):
    rows, cols, levels = values.shape
    blocks = rows // ROW_BLOCK
    top_rows = jnp.concatenate([top, values[ROW_BLOCK - 1 : rows - 1 : ROW_BLOCK]], axis=0)
    bottom_rows = jnp.concatenate([values[ROW_BLOCK:rows:ROW_BLOCK], bottom], axis=0)
    with_flux = fluxes_t is not None
    in_specs = [
        pl.BlockSpec((ROW_BLOCK, cols, levels), lambda i: (i, 0, 0)),
        pl.BlockSpec((1, cols, levels), lambda i: (i, 0, 0)),
        pl.BlockSpec((1, cols, levels), lambda i: (i, 0, 0)),
        pl.BlockSpec((ROW_BLOCK, 1, levels), lambda i: (i, 0, 0)),
        pl.BlockSpec((ROW_BLOCK, 1, levels), lambda i: (i, 0, 0)),
        pl.BlockSpec((levels, levels), lambda i: (0, 0)),
    ]
    operands = [values, top_rows, bottom_rows, west, east, mixing]
    out_shape = [jax.ShapeDtypeStruct(values.shape, jnp.float32)]
    out_specs = [pl.BlockSpec((ROW_BLOCK, cols, levels), lambda i: (i, 0, 0))]
    if not with_flux:
        out_shape.append(jax.ShapeDtypeStruct((8, rows * cols), jnp.float32))
        out_specs.append(pl.BlockSpec((8, ROW_BLOCK * cols), lambda i: (0, i)))
    if with_flux:
        flux_count = fluxes_t.shape[0]
        in_specs.append(pl.BlockSpec((flux_count, levels), lambda i: (0, 0)))
        operands.append(fluxes_t)
        out_shape.append(jax.ShapeDtypeStruct((flux_count, rows * cols), jnp.float32))
        out_specs.append(pl.BlockSpec((flux_count, ROW_BLOCK * cols), lambda i: (0, i)))
    cells = rows * cols
    flops = 6 * cells * levels * levels + (6 * cells * levels * 8 if with_flux else 0)
    result = pl.pallas_call(
        functools.partial(substep_kernel, with_flux, comp_total),
        grid=(blocks,),
        in_specs=in_specs,
        out_specs=out_specs,
        out_shape=out_shape,
        cost_estimate=pl.CostEstimate(
            flops=flops, transcendentals=cells * levels, bytes_accessed=8 * cells * levels
        ),
    )(*operands)
    return result


def column_physics(values, mixing):
    return jnp.tanh(jnp.einsum("rck,kj->rcj", values, mixing, precision=HIGHEST))


def earlier_same(owners, usable):
    positions = jnp.arange(owners.shape[0], dtype=jnp.int32)
    before = (
        (owners[None, :] == owners[:, None])
        & (positions[None, :] < positions[:, None])
        & usable[None, :]
    )
    return jnp.sum(before.astype(jnp.int32), axis=1)


def pack_rows(blocks, owners, labels, usable, slots_each, owner_total):
    ranks = earlier_same(owners, usable)
    target_slot = owners * slots_each + ranks
    slot_ids = jnp.arange(owner_total * slots_each, dtype=jnp.int32)
    placing = (slot_ids[:, None] == target_slot[None, :]) & usable[None, :]
    packed = jnp.dot(
        placing.astype(jnp.bfloat16), blocks, preferred_element_type=jnp.float32
    ).astype(jnp.bfloat16)
    placed_labels = jnp.sum(jnp.where(placing, labels[None, :] + 1, 0), axis=1) - 1
    return (
        packed.reshape(owner_total, slots_each, blocks.shape[1]),
        placed_labels.reshape(owner_total, slots_each),
        target_slot,
    )


def edge_rows(values, lower_valid, upper_valid):
    bands = lax.axis_size("comp") * lax.axis_size("lat")
    up = [(i, i + 1) for i in range(bands - 1)]
    down = [(j, i) for i, j in up]
    before = lax.ppermute(values[-1:], ("comp", "lat"), up)
    after = lax.ppermute(values[:1], ("comp", "lat"), down)
    return (jnp.where(lower_valid, before, 0.0), jnp.where(upper_valid, after, 0.0))


def edge_columns(values):
    size = lax.axis_size("lon")
    up = [(i, (i + 1) % size) for i in range(size)]
    down = [(j, i) for i, j in up]
    before = lax.ppermute(values[:, -1:], "lon", up)
    after = lax.ppermute(values[:, :1], "lon", down)
    return before, after


MESH_IDS = pl.DeviceIdType.MESH


def tile_device(comp, tile, lon_total):
    return (comp, tile // lon_total, tile % lon_total)


def gather_kernel(offsets, shape, send_ref, out_ref, land, send_sems, recv_sems):
    comp_total, lat_total, lon_total = shape
    comp = lax.axis_index("comp")
    tiles = lat_total * lon_total
    tile = lax.axis_index("lat") * lon_total + lax.axis_index("lon")
    ocean = comp_total - 1
    count = len(offsets)
    barrier = pltpu.get_barrier_semaphore()

    @pl.when(comp != ocean)
    def _():
        for off in offsets:
            target = tile_device(ocean, (tile + off) % tiles, lon_total)
            pl.semaphore_signal(barrier, 1, device_id=target, device_id_type=MESH_IDS)
        pl.semaphore_wait(barrier, count)
        copies = []
        for k, off in enumerate(offsets):
            target = tile_device(ocean, (tile + off) % tiles, lon_total)
            copy = pltpu.make_async_remote_copy(
                src_ref=send_ref.at[k],
                dst_ref=land.at[comp * count + k],
                send_sem=send_sems.at[k],
                recv_sem=recv_sems.at[comp * count + k],
                device_id=target,
                device_id_type=MESH_IDS,
            )
            copy.start()
            copies.append(copy)
        for copy in copies:
            copy.wait_send()
        out_ref[...] = jnp.zeros_like(out_ref)

    @pl.when(comp == ocean)
    def _():
        for source_comp in range(ocean):
            for off in offsets:
                source = tile_device(source_comp, (tile + tiles - off) % tiles, lon_total)
                pl.semaphore_signal(barrier, 1, device_id=source, device_id_type=MESH_IDS)
        pl.semaphore_wait(barrier, count * ocean)
        for source_comp in range(ocean):
            for k, off in enumerate(offsets):
                source = tile_device(source_comp, (tile + tiles - off) % tiles, lon_total)
                slot = source_comp * count + k
                pltpu.make_async_remote_copy(
                    src_ref=send_ref.at[k],
                    dst_ref=land.at[slot],
                    send_sem=send_sems.at[k],
                    recv_sem=recv_sems.at[slot],
                    device_id=source,
                    device_id_type=MESH_IDS,
                ).wait_recv()
        out_ref[...] = land[...]


def gather_to_ocean(blocks, offsets, shape):
    count = len(offsets)
    senders = (shape[0] - 1) * count
    slot_shape = blocks.shape[1:]
    return pl.pallas_call(
        functools.partial(gather_kernel, tuple(offsets), tuple(shape)),
        out_shape=jax.ShapeDtypeStruct((senders,) + slot_shape, blocks.dtype),
        in_specs=[pl.BlockSpec(memory_space=pltpu.VMEM)],
        out_specs=pl.BlockSpec(memory_space=pltpu.VMEM),
        scratch_shapes=[
            pltpu.VMEM((senders,) + slot_shape, blocks.dtype),
            pltpu.SemaphoreType.DMA((count,)),
            pltpu.SemaphoreType.DMA((senders,)),
        ],
        compiler_params=pltpu.CompilerParams(collective_id=0, has_side_effects=True),
    )(blocks)


def spread_kernel(offsets, shape, surface_ref, out_ref, land, send_sems, recv_sems):
    comp_total, lat_total, lon_total = shape
    comp = lax.axis_index("comp")
    tiles = lat_total * lon_total
    tile = lax.axis_index("lat") * lon_total + lax.axis_index("lon")
    ocean = comp_total - 1
    count = len(offsets)
    barrier = pltpu.get_barrier_semaphore()

    @pl.when(comp == ocean)
    def _():
        for target_comp in range(ocean):
            for off in offsets:
                target = tile_device(target_comp, (tile + tiles - off) % tiles, lon_total)
                pl.semaphore_signal(barrier, 1, device_id=target, device_id_type=MESH_IDS)
        pl.semaphore_wait(barrier, count * ocean)
        copies = []
        for target_comp in range(ocean):
            for k, off in enumerate(offsets):
                target = tile_device(target_comp, (tile + tiles - off) % tiles, lon_total)
                copy = pltpu.make_async_remote_copy(
                    src_ref=surface_ref.at[target_comp * count + k],
                    dst_ref=land.at[k],
                    send_sem=send_sems.at[target_comp * count + k],
                    recv_sem=recv_sems.at[k],
                    device_id=target,
                    device_id_type=MESH_IDS,
                )
                copy.start()
                copies.append(copy)
        for copy in copies:
            copy.wait_send()
        out_ref[...] = jnp.zeros_like(out_ref)

    @pl.when(comp != ocean)
    def _():
        for off in offsets:
            source = tile_device(ocean, (tile + off) % tiles, lon_total)
            pl.semaphore_signal(barrier, 1, device_id=source, device_id_type=MESH_IDS)
        pl.semaphore_wait(barrier, count)
        for k, off in enumerate(offsets):
            source = tile_device(ocean, (tile + off) % tiles, lon_total)
            pltpu.make_async_remote_copy(
                src_ref=surface_ref.at[k],
                dst_ref=land.at[k],
                send_sem=send_sems.at[k],
                recv_sem=recv_sems.at[k],
                device_id=source,
                device_id_type=MESH_IDS,
            ).wait_recv()
        out_ref[...] = land[...]


def spread_from_ocean(replies, offsets, shape):
    count = len(offsets)
    senders = (shape[0] - 1) * count
    slot_shape = replies.shape[1:]
    return pl.pallas_call(
        functools.partial(spread_kernel, tuple(offsets), tuple(shape)),
        out_shape=jax.ShapeDtypeStruct((count,) + slot_shape, replies.dtype),
        in_specs=[pl.BlockSpec(memory_space=pltpu.VMEM)],
        out_specs=pl.BlockSpec(memory_space=pltpu.VMEM),
        scratch_shapes=[
            pltpu.VMEM((count,) + slot_shape, replies.dtype),
            pltpu.SemaphoreType.DMA((senders,)),
            pltpu.SemaphoreType.DMA((count,)),
        ],
        compiler_params=pltpu.CompilerParams(collective_id=1, has_side_effects=True),
    )(replies)


def ocean_update_kernel(comp_total, first_ref, state_ref, sea_ref, forcing_ref, spread_ref, out_ref):
    ocean = lax.axis_index("comp") == comp_total - 1

    @pl.when(ocean)
    def _():
        ocean_block(first_ref, state_ref, sea_ref, forcing_ref, spread_ref, out_ref)

    @pl.when(jnp.logical_not(ocean))
    def _():
        out_ref[...] = first_ref[...]


def ocean_block(first_ref, state_ref, sea_ref, forcing_ref, spread_ref, out_ref):
    rows, cols, levels = first_ref.shape
    forcing = forcing_ref[...]
    spread = spread_ref[...]
    forcing_hi = forcing.astype(jnp.bfloat16)
    forcing_lo = (forcing - forcing_hi.astype(jnp.float32)).astype(jnp.bfloat16)
    spread_hi = spread.astype(jnp.bfloat16)
    spread_lo = (spread - spread_hi.astype(jnp.float32)).astype(jnp.bfloat16)

    def one(a, b):
        return lax.dot_general(a, b, (((0,), (0,)), ((), ())), preferred_element_type=jnp.float32)

    added = one(forcing_hi, spread_hi) + (one(forcing_hi, spread_lo) + one(forcing_lo, spread_hi))
    lane_row = lax.broadcasted_iota(jnp.int32, (8, levels), 0)
    ones = (lane_row == 0).astype(jnp.bfloat16)
    picks = jnp.where(lax.broadcasted_iota(jnp.int32, sea_ref.shape, 0) == 0, sea_ref[...], 0)
    mask = one(picks.astype(jnp.bfloat16), ones)
    moved = first_ref[...].reshape(rows * cols, levels) + added
    kept = jnp.where(mask > 0.5, moved, state_ref[...].reshape(rows * cols, levels))
    out_ref[...] = kept.reshape(rows, cols, levels)


def ocean_update(first, state, sea_rows, forcing, ocean_map, comp_total):
    rows, cols, levels = first.shape
    flux_count = forcing.shape[0]
    cells = rows * cols
    return pl.pallas_call(
        functools.partial(ocean_update_kernel, comp_total),
        grid=(rows // ROW_BLOCK,),
        in_specs=[
            pl.BlockSpec((ROW_BLOCK, cols, levels), lambda i: (i, 0, 0)),
            pl.BlockSpec((ROW_BLOCK, cols, levels), lambda i: (i, 0, 0)),
            pl.BlockSpec((8, ROW_BLOCK * cols), lambda i: (0, i)),
            pl.BlockSpec((flux_count, ROW_BLOCK * cols), lambda i: (0, i)),
            pl.BlockSpec((flux_count, levels), lambda i: (0, 0)),
        ],
        out_specs=pl.BlockSpec((ROW_BLOCK, cols, levels), lambda i: (i, 0, 0)),
        out_shape=jax.ShapeDtypeStruct(first.shape, jnp.float32),
        cost_estimate=pl.CostEstimate(
            flops=8 * cells * levels * flux_count, transcendentals=0, bytes_accessed=12 * cells * levels
        ),
    )(first, state, sea_rows, forcing, ocean_map)


def local(
    state, land_mask, intersection_list, mix_atm, mix_ocn, flux_map, ocean_map, regrid_weights
):
    tile_rows, block_len, levels = state.shape
    flux_count = flux_map.shape[1]
    weight_count = regrid_weights.shape[0]
    intersections = intersection_list.shape[2]
    comp_count = lax.axis_size("comp")
    lat_count = lax.axis_size("lat")
    lon_count = lax.axis_size("lon")
    tile_count = lat_count * lon_count
    reach = min(4, lon_count)
    neighbour_count = 2 * reach
    capacity = intersections * tile_rows // neighbour_count
    width = flux_count * block_len
    comp_index = lax.axis_index("comp")
    tile_index = lax.axis_index("lat") * lon_count + lax.axis_index("lon")
    band = comp_index * lat_count + lax.axis_index("lat")
    ocean_band = (comp_count - 1) * lat_count
    ocean_side = comp_index == comp_count - 1
    lower_valid = (band > 0) & ((band - 1 >= ocean_band) == (band >= ocean_band))
    upper_valid = (band < comp_count * lat_count - 1) & (
        (band + 1 >= ocean_band) == (band >= ocean_band)
    )
    sea_cells = land_mask == 1

    top, bottom = edge_rows(state, lower_valid, upper_valid)
    west, east = edge_columns(state)
    mixing = jnp.where(ocean_side, mix_ocn, mix_atm)
    first, first_planes = substep(state, top, bottom, west, east, mixing, comp_count)
    first_top = first_planes[0].reshape(tile_rows, block_len)
    state_top = first_planes[1].reshape(tile_rows, block_len)
    top, bottom = edge_rows(first, lower_valid, upper_valid)
    west, east = edge_columns(first)

    def atmosphere_second(values, top, bottom, west, east):
        moved, total = substep(values, top, bottom, west, east, mix_atm, comp_count, flux_map.T)
        total = total.reshape(flux_count, tile_rows, block_len)
        sent = jnp.where(sea_cells[None], 0.5 * total, 0.0).astype(jnp.bfloat16)
        return moved, sent

    def ocean_second(values, top, bottom, west, east):
        return values, jnp.zeros((flux_count, tile_rows, block_len), jnp.bfloat16)

    second, flux_sent = lax.cond(
        ocean_side, ocean_second, atmosphere_second, first, top, bottom, west, east
    )
    entry_list = intersection_list.reshape(tile_rows * intersections, 3)
    owners = entry_list[:, 0]
    targets = entry_list[:, 1]
    weight_ids = entry_list[:, 2]
    labels = weight_ids * tile_rows + targets
    entry_blocks = jnp.repeat(flux_sent.transpose(1, 0, 2), intersections, axis=0).reshape(
        tile_rows * intersections, width
    )
    lane = jnp.arange(128, dtype=jnp.int32)[None, :]
    label_lanes = jnp.where(
        lane == 0, weight_ids[:, None], jnp.where(lane == 1, targets[:, None], 0)
    ).astype(jnp.bfloat16)
    entry_blocks = jnp.concatenate([entry_blocks, label_lanes], axis=1)
    sending = jnp.broadcast_to(jnp.logical_not(ocean_side), owners.shape)
    offsets = [
        (n // reach * lon_count + n % reach - (reach - 1) // 2) % tile_count
        for n in range(neighbour_count)
    ]
    offset_table = jnp.array(offsets, jnp.int32)
    distance = (owners - tile_index + tile_count) % tile_count
    neighbour_ids = jnp.sum(
        jnp.where(
            distance[:, None] == offset_table[None, :],
            jnp.arange(neighbour_count, dtype=jnp.int32)[None, :],
            0,
        ),
        axis=1,
    )
    packed, _, entry_slots = pack_rows(entry_blocks, neighbour_ids, labels, sending, capacity, neighbour_count)
    mesh_shape = (comp_count, lat_count, lon_count)
    arrived = gather_to_ocean(packed, offsets, mesh_shape)
    weights_low = regrid_weights
    weights_wide = regrid_weights.astype(jnp.float32)
    senders = (comp_count - 1) * neighbour_count

    def ocean_reply(values_top, arrived):
        flat = arrived.reshape(-1, width + 128)
        arrived_labels = flat[:, width].astype(jnp.int32) * tile_rows + flat[:, width + 1].astype(
            jnp.int32
        )
        fluxes = flat[:, :width]
        label_ids = jnp.arange(weight_count * tile_rows, dtype=jnp.int32)
        selector = (arrived_labels[:, None] == label_ids[None, :]).astype(jnp.bfloat16)
        binned = lax.dot_general(
            selector, fluxes, (((0,), (0,)), ((), ())), preferred_element_type=jnp.float32
        )
        binned = binned.reshape(weight_count, tile_rows, flux_count, block_len)
        binned_hi = lax.reduce_precision(binned, exponent_bits=8, mantissa_bits=7)
        binned_lo = (binned - binned_hi).astype(jnp.bfloat16)
        forcing = jnp.einsum(
            "wdfa,wab->fdb",
            binned_hi.astype(jnp.bfloat16),
            weights_low,
            preferred_element_type=jnp.float32,
        ) + jnp.einsum("wdfa,wab->fdb", binned_lo, weights_low, preferred_element_type=jnp.float32)
        lifted = jnp.sum(forcing * ocean_map[:, 0][:, None, None], axis=0)
        top_level = jnp.where(sea_cells, values_top + lifted, state_top)
        table = jnp.einsum("db,wab->wda", top_level, weights_wide, precision=HIGHEST)
        replies = jnp.take(table.reshape(weight_count * tile_rows, block_len), arrived_labels, axis=0)
        return forcing, replies.reshape(senders, capacity, block_len), top_level

    def atmosphere_reply(values_top, arrived):
        return (
            jnp.zeros((flux_count, tile_rows, block_len), jnp.float32),
            jnp.zeros((senders, capacity, block_len), jnp.float32),
            values_top,
        )

    forcing, replies, ocean_top = lax.cond(
        ocean_side, ocean_reply, atmosphere_reply, first_top, arrived
    )
    answers = spread_from_ocean(replies, offsets, mesh_shape)
    per_entry = jnp.take(
        answers.reshape(neighbour_count * capacity, block_len), entry_slots, axis=0
    )
    returned = per_entry.reshape(tile_rows, intersections, block_len).sum(axis=1)
    second, forcing, answers = lax.optimization_barrier((second, forcing, answers))
    sea_rows = jnp.broadcast_to(
        sea_cells.astype(jnp.int32).reshape(1, tile_rows * block_len), (8, tile_rows * block_len)
    )
    final_state = ocean_update(
        second,
        state,
        sea_rows,
        forcing.reshape(flux_count, tile_rows * block_len),
        ocean_map,
        comp_count,
    )
    top_plane = lax.cond(
        ocean_side, lambda values: ocean_top, lambda values: values[:, :, 0], final_state
    )
    surface_out = jnp.where(ocean_side, ocean_top, jnp.where(sea_cells, returned, top_plane))
    return (final_state, surface_out)


def solution(mesh):
    placed = (
        P(("comp", "lat"), "lon", None),
        P(("comp", "lat"), "lon"),
        P(("comp", "lat"), "lon", None, None),
        P(),
        P(),
        P(),
        P(),
        P(),
    )
    return jax.shard_map(
        local,
        mesh=mesh,
        in_specs=placed,
        out_specs=(P(("comp", "lat"), "lon", None), P(("comp", "lat"), "lon")),
        check_vma=False,
    )
```

```python
import jax
import jax.numpy as jnp
from jax import lax
from jax.experimental import pallas as pl
from jax.experimental.pallas import tpu as pltpu
from jax.sharding import PartitionSpec as P
import functools

SMOOTHING = 0.2
PHYSICS = 0.5
HIGHEST = lax.Precision.HIGHEST
ROW_BLOCK = 8


def split_bf16(values):
    high = values.astype(jnp.bfloat16)
    low = (values - high.astype(jnp.float32)).astype(jnp.bfloat16)
    return high, low


def three_pass(lhs, rhs, dims):
    lhs_hi, lhs_lo = split_bf16(lhs)
    rhs_hi, rhs_lo = split_bf16(rhs)

    def one(a, b):
        return lax.dot_general(a, b, (dims, ((), ())), preferred_element_type=jnp.float32)

    return one(lhs_hi, rhs_hi) + (one(lhs_hi, rhs_lo) + one(lhs_lo, rhs_hi))


def exact_rows(picker, values):
    high = values.astype(jnp.bfloat16)
    rest = values - high.astype(jnp.float32)
    middle = rest.astype(jnp.bfloat16)
    low = (rest - middle.astype(jnp.float32)).astype(jnp.bfloat16)

    def one(piece):
        return lax.dot_general(
            picker, piece, (((1,), (1,)), ((), ())), preferred_element_type=jnp.float32
        )

    return one(high) + one(middle) + one(low)


def substep_kernel(with_flux, comp_total, x_ref, top_ref, bottom_ref, west_ref, east_ref, mix_ref, *rest):
    if with_flux:
        fluxes_ref, out_ref, flux_out_ref = rest
    else:
        out_ref, planes_ref = rest
    rows, cols, levels = x_ref.shape
    centre = x_ref[...]
    up = jnp.concatenate([top_ref[...], centre[:-1]], axis=0)
    down = jnp.concatenate([centre[1:], bottom_ref[...]], axis=0)
    column = lax.broadcasted_iota(jnp.int32, centre.shape, 1)
    west = jnp.where(column == 0, west_ref[...], pltpu.roll(centre, 1, 1))
    east = jnp.where(column == cols - 1, east_ref[...], pltpu.roll(centre, cols - 1, 1))
    smooth = centre + SMOOTHING * (up + down + west + east - 4.0 * centre)
    flat = smooth.reshape(rows * cols, levels)
    mixed = three_pass(flat, mix_ref[...], ((1,), (0,)))
    moved = flat + PHYSICS * jnp.tanh(mixed)
    out_ref[...] = moved.reshape(rows, cols, levels)
    if not with_flux:
        ocean = lax.axis_index("comp") == comp_total - 1

        @pl.when(ocean)
        def _():
            plane_row = lax.broadcasted_iota(jnp.int32, (8, levels), 0)
            plane_lane = lax.broadcasted_iota(jnp.int32, (8, levels), 1)
            pick_out = ((plane_row == 0) & (plane_lane == 0)).astype(jnp.bfloat16)
            pick_in = ((plane_row == 1) & (plane_lane == 0)).astype(jnp.bfloat16)
            planes_ref[...] = exact_rows(pick_out, moved) + exact_rows(
                pick_in, centre.reshape(rows * cols, levels)
            )

        @pl.when(jnp.logical_not(ocean))
        def _():
            planes_ref[...] = jnp.zeros_like(planes_ref)

    else:
        total = centre.reshape(rows * cols, levels) + moved
        flux_out_ref[...] = three_pass(fluxes_ref[...], total, ((1,), (1,)))


def substep(values, top, bottom, west, east, mixing, comp_total, fluxes_t=None):
    rows, cols, levels = values.shape
    blocks = rows // ROW_BLOCK
    top_rows = jnp.concatenate([top, values[ROW_BLOCK - 1 : rows - 1 : ROW_BLOCK]], axis=0)
    bottom_rows = jnp.concatenate([values[ROW_BLOCK:rows:ROW_BLOCK], bottom], axis=0)
    with_flux = fluxes_t is not None
    in_specs = [
        pl.BlockSpec((ROW_BLOCK, cols, levels), lambda i: (i, 0, 0)),
        pl.BlockSpec((1, cols, levels), lambda i: (i, 0, 0)),
        pl.BlockSpec((1, cols, levels), lambda i: (i, 0, 0)),
        pl.BlockSpec((ROW_BLOCK, 1, levels), lambda i: (i, 0, 0)),
        pl.BlockSpec((ROW_BLOCK, 1, levels), lambda i: (i, 0, 0)),
        pl.BlockSpec((levels, levels), lambda i: (0, 0)),
    ]
    operands = [values, top_rows, bottom_rows, west, east, mixing]
    out_shape = [jax.ShapeDtypeStruct(values.shape, jnp.float32)]
    out_specs = [pl.BlockSpec((ROW_BLOCK, cols, levels), lambda i: (i, 0, 0))]
    if not with_flux:
        out_shape.append(jax.ShapeDtypeStruct((8, rows * cols), jnp.float32))
        out_specs.append(pl.BlockSpec((8, ROW_BLOCK * cols), lambda i: (0, i)))
    if with_flux:
        flux_count = fluxes_t.shape[0]
        in_specs.append(pl.BlockSpec((flux_count, levels), lambda i: (0, 0)))
        operands.append(fluxes_t)
        out_shape.append(jax.ShapeDtypeStruct((flux_count, rows * cols), jnp.float32))
        out_specs.append(pl.BlockSpec((flux_count, ROW_BLOCK * cols), lambda i: (0, i)))
    cells = rows * cols
    flops = 6 * cells * levels * levels + (6 * cells * levels * 8 if with_flux else 0)
    result = pl.pallas_call(
        functools.partial(substep_kernel, with_flux, comp_total),
        grid=(blocks,),
        in_specs=in_specs,
        out_specs=out_specs,
        out_shape=out_shape,
        cost_estimate=pl.CostEstimate(
            flops=flops, transcendentals=cells * levels, bytes_accessed=8 * cells * levels
        ),
    )(*operands)
    return result


def column_physics(values, mixing):
    return jnp.tanh(jnp.einsum("rck,kj->rcj", values, mixing, precision=HIGHEST))


def earlier_same(owners, usable):
    positions = jnp.arange(owners.shape[0], dtype=jnp.int32)
    before = (
        (owners[None, :] == owners[:, None])
        & (positions[None, :] < positions[:, None])
        & usable[None, :]
    )
    return jnp.sum(before.astype(jnp.int32), axis=1)


def pack_rows(blocks, owners, labels, usable, slots_each, owner_total):
    ranks = earlier_same(owners, usable)
    target_slot = owners * slots_each + ranks
    slot_ids = jnp.arange(owner_total * slots_each, dtype=jnp.int32)
    placing = (slot_ids[:, None] == target_slot[None, :]) & usable[None, :]
    packed = jnp.dot(
        placing.astype(jnp.bfloat16), blocks, preferred_element_type=jnp.float32
    ).astype(jnp.bfloat16)
    placed_labels = jnp.sum(jnp.where(placing, labels[None, :] + 1, 0), axis=1) - 1
    return (
        packed.reshape(owner_total, slots_each, blocks.shape[1]),
        placed_labels.reshape(owner_total, slots_each),
        target_slot,
    )


def edge_rows(values, lower_valid, upper_valid):
    bands = lax.axis_size("comp") * lax.axis_size("lat")
    up = [(i, i + 1) for i in range(bands - 1)]
    down = [(j, i) for i, j in up]
    before = lax.ppermute(values[-1:], ("comp", "lat"), up)
    after = lax.ppermute(values[:1], ("comp", "lat"), down)
    return (jnp.where(lower_valid, before, 0.0), jnp.where(upper_valid, after, 0.0))


def edge_columns(values):
    size = lax.axis_size("lon")
    up = [(i, (i + 1) % size) for i in range(size)]
    down = [(j, i) for i, j in up]
    before = lax.ppermute(values[:, -1:], "lon", up)
    after = lax.ppermute(values[:, :1], "lon", down)
    return before, after


MESH_IDS = pl.DeviceIdType.MESH


def tile_device(comp, tile, lon_total):
    return (comp, tile // lon_total, tile % lon_total)


def gather_kernel(offsets, shape, send_ref, out_ref, land, send_sems, recv_sems):
    comp_total, lat_total, lon_total = shape
    comp = lax.axis_index("comp")
    tiles = lat_total * lon_total
    tile = lax.axis_index("lat") * lon_total + lax.axis_index("lon")
    ocean = comp_total - 1
    count = len(offsets)
    barrier = pltpu.get_barrier_semaphore()

    @pl.when(comp != ocean)
    def _():
        for off in offsets:
            target = tile_device(ocean, (tile + off) % tiles, lon_total)
            pl.semaphore_signal(barrier, 1, device_id=target, device_id_type=MESH_IDS)
        pl.semaphore_wait(barrier, count)
        copies = []
        for k, off in enumerate(offsets):
            target = tile_device(ocean, (tile + off) % tiles, lon_total)
            copy = pltpu.make_async_remote_copy(
                src_ref=send_ref.at[k],
                dst_ref=land.at[comp * count + k],
                send_sem=send_sems.at[k],
                recv_sem=recv_sems.at[comp * count + k],
                device_id=target,
                device_id_type=MESH_IDS,
            )
            copy.start()
            copies.append(copy)
        for copy in copies:
            copy.wait_send()
        out_ref[...] = jnp.zeros_like(out_ref)

    @pl.when(comp == ocean)
    def _():
        for source_comp in range(ocean):
            for off in offsets:
                source = tile_device(source_comp, (tile + tiles - off) % tiles, lon_total)
                pl.semaphore_signal(barrier, 1, device_id=source, device_id_type=MESH_IDS)
        pl.semaphore_wait(barrier, count * ocean)
        for source_comp in range(ocean):
            for k, off in enumerate(offsets):
                source = tile_device(source_comp, (tile + tiles - off) % tiles, lon_total)
                slot = source_comp * count + k
                pltpu.make_async_remote_copy(
                    src_ref=send_ref.at[k],
                    dst_ref=land.at[slot],
                    send_sem=send_sems.at[k],
                    recv_sem=recv_sems.at[slot],
                    device_id=source,
                    device_id_type=MESH_IDS,
                ).wait_recv()
        out_ref[...] = land[...]


def gather_to_ocean(blocks, offsets, shape):
    count = len(offsets)
    senders = (shape[0] - 1) * count
    slot_shape = blocks.shape[1:]
    return pl.pallas_call(
        functools.partial(gather_kernel, tuple(offsets), tuple(shape)),
        out_shape=jax.ShapeDtypeStruct((senders,) + slot_shape, blocks.dtype),
        in_specs=[pl.BlockSpec(memory_space=pltpu.VMEM)],
        out_specs=pl.BlockSpec(memory_space=pltpu.VMEM),
        scratch_shapes=[
            pltpu.VMEM((senders,) + slot_shape, blocks.dtype),
            pltpu.SemaphoreType.DMA((count,)),
            pltpu.SemaphoreType.DMA((senders,)),
        ],
        compiler_params=pltpu.CompilerParams(collective_id=0, has_side_effects=True),
    )(blocks)


def spread_kernel(offsets, shape, surface_ref, out_ref, land, send_sems, recv_sems):
    comp_total, lat_total, lon_total = shape
    comp = lax.axis_index("comp")
    tiles = lat_total * lon_total
    tile = lax.axis_index("lat") * lon_total + lax.axis_index("lon")
    ocean = comp_total - 1
    count = len(offsets)
    barrier = pltpu.get_barrier_semaphore()

    @pl.when(comp == ocean)
    def _():
        for target_comp in range(ocean):
            for off in offsets:
                target = tile_device(target_comp, (tile + tiles - off) % tiles, lon_total)
                pl.semaphore_signal(barrier, 1, device_id=target, device_id_type=MESH_IDS)
        pl.semaphore_wait(barrier, count * ocean)
        copies = []
        for target_comp in range(ocean):
            for k, off in enumerate(offsets):
                target = tile_device(target_comp, (tile + tiles - off) % tiles, lon_total)
                copy = pltpu.make_async_remote_copy(
                    src_ref=surface_ref.at[target_comp * count + k],
                    dst_ref=land.at[k],
                    send_sem=send_sems.at[target_comp * count + k],
                    recv_sem=recv_sems.at[k],
                    device_id=target,
                    device_id_type=MESH_IDS,
                )
                copy.start()
                copies.append(copy)
        for copy in copies:
            copy.wait_send()
        out_ref[...] = jnp.zeros_like(out_ref)

    @pl.when(comp != ocean)
    def _():
        for off in offsets:
            source = tile_device(ocean, (tile + off) % tiles, lon_total)
            pl.semaphore_signal(barrier, 1, device_id=source, device_id_type=MESH_IDS)
        pl.semaphore_wait(barrier, count)
        for k, off in enumerate(offsets):
            source = tile_device(ocean, (tile + off) % tiles, lon_total)
            pltpu.make_async_remote_copy(
                src_ref=surface_ref.at[k],
                dst_ref=land.at[k],
                send_sem=send_sems.at[k],
                recv_sem=recv_sems.at[k],
                device_id=source,
                device_id_type=MESH_IDS,
            ).wait_recv()
        out_ref[...] = land[...]


def spread_from_ocean(replies, offsets, shape):
    count = len(offsets)
    senders = (shape[0] - 1) * count
    slot_shape = replies.shape[1:]
    return pl.pallas_call(
        functools.partial(spread_kernel, tuple(offsets), tuple(shape)),
        out_shape=jax.ShapeDtypeStruct((count,) + slot_shape, replies.dtype),
        in_specs=[pl.BlockSpec(memory_space=pltpu.VMEM)],
        out_specs=pl.BlockSpec(memory_space=pltpu.VMEM),
        scratch_shapes=[
            pltpu.VMEM((count,) + slot_shape, replies.dtype),
            pltpu.SemaphoreType.DMA((senders,)),
            pltpu.SemaphoreType.DMA((count,)),
        ],
        compiler_params=pltpu.CompilerParams(collective_id=1, has_side_effects=True),
    )(replies)


def ocean_update_kernel(comp_total, first_ref, state_ref, sea_ref, forcing_ref, spread_ref, out_ref):
    ocean = lax.axis_index("comp") == comp_total - 1

    @pl.when(ocean)
    def _():
        ocean_block(first_ref, state_ref, sea_ref, forcing_ref, spread_ref, out_ref)

    @pl.when(jnp.logical_not(ocean))
    def _():
        out_ref[...] = first_ref[...]


def ocean_block(first_ref, state_ref, sea_ref, forcing_ref, spread_ref, out_ref):
    rows, cols, levels = first_ref.shape
    forcing = forcing_ref[...]
    spread = spread_ref[...]
    forcing_hi = forcing.astype(jnp.bfloat16)
    forcing_lo = (forcing - forcing_hi.astype(jnp.float32)).astype(jnp.bfloat16)
    spread_hi = spread.astype(jnp.bfloat16)
    spread_lo = (spread - spread_hi.astype(jnp.float32)).astype(jnp.bfloat16)

    def one(a, b):
        return lax.dot_general(a, b, (((0,), (0,)), ((), ())), preferred_element_type=jnp.float32)

    added = one(forcing_hi, spread_hi) + (one(forcing_hi, spread_lo) + one(forcing_lo, spread_hi))
    lane_row = lax.broadcasted_iota(jnp.int32, (8, levels), 0)
    ones = (lane_row == 0).astype(jnp.bfloat16)
    picks = jnp.where(lax.broadcasted_iota(jnp.int32, sea_ref.shape, 0) == 0, sea_ref[...], 0)
    mask = one(picks.astype(jnp.bfloat16), ones)
    moved = first_ref[...].reshape(rows * cols, levels) + added
    kept = jnp.where(mask > 0.5, moved, state_ref[...].reshape(rows * cols, levels))
    out_ref[...] = kept.reshape(rows, cols, levels)


def ocean_update(first, state, sea_rows, forcing, ocean_map, comp_total):
    rows, cols, levels = first.shape
    flux_count = forcing.shape[0]
    cells = rows * cols
    return pl.pallas_call(
        functools.partial(ocean_update_kernel, comp_total),
        grid=(rows // ROW_BLOCK,),
        in_specs=[
            pl.BlockSpec((ROW_BLOCK, cols, levels), lambda i: (i, 0, 0)),
            pl.BlockSpec((ROW_BLOCK, cols, levels), lambda i: (i, 0, 0)),
            pl.BlockSpec((8, ROW_BLOCK * cols), lambda i: (0, i)),
            pl.BlockSpec((flux_count, ROW_BLOCK * cols), lambda i: (0, i)),
            pl.BlockSpec((flux_count, levels), lambda i: (0, 0)),
        ],
        out_specs=pl.BlockSpec((ROW_BLOCK, cols, levels), lambda i: (i, 0, 0)),
        out_shape=jax.ShapeDtypeStruct(first.shape, jnp.float32),
        cost_estimate=pl.CostEstimate(
            flops=8 * cells * levels * flux_count, transcendentals=0, bytes_accessed=12 * cells * levels
        ),
    )(first, state, sea_rows, forcing, ocean_map)


def scatter_regrid_kernel(labels_ref, fluxes_ref, weights_ref, out_ref, binned_ref):
    entries = fluxes_ref.shape[0]
    weight_count, tile_rows, block_len = weights_ref.shape
    flux_count = fluxes_ref.shape[1]
    binned_ref[...] = jnp.zeros_like(binned_ref)

    def add_one(e, carry):
        label = labels_ref[e]
        binned_ref[label] = binned_ref[label] + fluxes_ref[e]
        return carry

    lax.fori_loop(0, entries, add_one, 0, unroll=8)
    out_ref[...] = jnp.zeros_like(out_ref)

    def regrid_one(w, carry):
        start = pl.multiple_of(w * tile_rows, tile_rows)
        block = binned_ref[pl.ds(start, tile_rows)].reshape(tile_rows * flux_count, block_len)
        high = block.astype(jnp.bfloat16)
        low = (block - high.astype(jnp.float32)).astype(jnp.bfloat16)
        weight = weights_ref[w]
        out_ref[...] += jnp.dot(high, weight, preferred_element_type=jnp.float32) + jnp.dot(
            low, weight, preferred_element_type=jnp.float32
        )
        return carry

    lax.fori_loop(0, weight_count, regrid_one, 0)


def scatter_regrid(labels, fluxes, weights):
    entries, flux_count, block_len = fluxes.shape
    weight_count, tile_rows, _ = weights.shape
    return pl.pallas_call(
        scatter_regrid_kernel,
        out_shape=jax.ShapeDtypeStruct((tile_rows * flux_count, block_len), jnp.float32),
        in_specs=[
            pl.BlockSpec(memory_space=pltpu.SMEM),
            pl.BlockSpec(memory_space=pltpu.VMEM),
            pl.BlockSpec(memory_space=pltpu.VMEM),
        ],
        out_specs=pl.BlockSpec(memory_space=pltpu.VMEM),
        scratch_shapes=[pltpu.VMEM((weight_count * tile_rows, flux_count, block_len), jnp.float32)],
        compiler_params=pltpu.CompilerParams(vmem_limit_bytes=48 * 1024 * 1024),
        cost_estimate=pl.CostEstimate(
            flops=4 * weight_count * tile_rows * flux_count * block_len * block_len,
            transcendentals=0,
            bytes_accessed=entries * flux_count * block_len * 4 + weight_count * tile_rows * block_len * 2,
        ),
    )(labels, fluxes, weights)


def local(
    state, land_mask, intersection_list, mix_atm, mix_ocn, flux_map, ocean_map, regrid_weights
):
    tile_rows, block_len, levels = state.shape
    flux_count = flux_map.shape[1]
    weight_count = regrid_weights.shape[0]
    intersections = intersection_list.shape[2]
    comp_count = lax.axis_size("comp")
    lat_count = lax.axis_size("lat")
    lon_count = lax.axis_size("lon")
    tile_count = lat_count * lon_count
    reach = min(4, lon_count)
    neighbour_count = 2 * reach
    capacity = intersections * tile_rows // neighbour_count
    width = flux_count * block_len
    comp_index = lax.axis_index("comp")
    tile_index = lax.axis_index("lat") * lon_count + lax.axis_index("lon")
    band = comp_index * lat_count + lax.axis_index("lat")
    ocean_band = (comp_count - 1) * lat_count
    ocean_side = comp_index == comp_count - 1
    lower_valid = (band > 0) & ((band - 1 >= ocean_band) == (band >= ocean_band))
    upper_valid = (band < comp_count * lat_count - 1) & (
        (band + 1 >= ocean_band) == (band >= ocean_band)
    )
    sea_cells = land_mask == 1

    top, bottom = edge_rows(state, lower_valid, upper_valid)
    west, east = edge_columns(state)
    mixing = jnp.where(ocean_side, mix_ocn, mix_atm)
    first, first_planes = substep(state, top, bottom, west, east, mixing, comp_count)
    first_top = first_planes[0].reshape(tile_rows, block_len)
    state_top = first_planes[1].reshape(tile_rows, block_len)
    top, bottom = edge_rows(first, lower_valid, upper_valid)
    west, east = edge_columns(first)

    def atmosphere_second(values, top, bottom, west, east):
        moved, total = substep(values, top, bottom, west, east, mix_atm, comp_count, flux_map.T)
        total = total.reshape(flux_count, tile_rows, block_len)
        sent = jnp.where(sea_cells[None], 0.5 * total, 0.0).astype(jnp.bfloat16)
        return moved, sent

    def ocean_second(values, top, bottom, west, east):
        return values, jnp.zeros((flux_count, tile_rows, block_len), jnp.bfloat16)

    second, flux_sent = lax.cond(
        ocean_side, ocean_second, atmosphere_second, first, top, bottom, west, east
    )
    entry_list = intersection_list.reshape(tile_rows * intersections, 3)
    owners = entry_list[:, 0]
    targets = entry_list[:, 1]
    weight_ids = entry_list[:, 2]
    labels = weight_ids * tile_rows + targets
    entry_blocks = jnp.repeat(flux_sent.transpose(1, 0, 2), intersections, axis=0).reshape(
        tile_rows * intersections, width
    )
    lane = jnp.arange(128, dtype=jnp.int32)[None, :]
    label_lanes = jnp.where(
        lane == 0, weight_ids[:, None], jnp.where(lane == 1, targets[:, None], 0)
    ).astype(jnp.bfloat16)
    entry_blocks = jnp.concatenate([entry_blocks, label_lanes], axis=1)
    sending = jnp.broadcast_to(jnp.logical_not(ocean_side), owners.shape)
    offsets = [
        (n // reach * lon_count + n % reach - (reach - 1) // 2) % tile_count
        for n in range(neighbour_count)
    ]
    offset_table = jnp.array(offsets, jnp.int32)
    distance = (owners - tile_index + tile_count) % tile_count
    neighbour_ids = jnp.sum(
        jnp.where(
            distance[:, None] == offset_table[None, :],
            jnp.arange(neighbour_count, dtype=jnp.int32)[None, :],
            0,
        ),
        axis=1,
    )
    packed, _, entry_slots = pack_rows(entry_blocks, neighbour_ids, labels, sending, capacity, neighbour_count)
    mesh_shape = (comp_count, lat_count, lon_count)
    arrived = gather_to_ocean(packed, offsets, mesh_shape)
    weights_low = regrid_weights
    weights_wide = regrid_weights.astype(jnp.float32)
    senders = (comp_count - 1) * neighbour_count

    def ocean_reply(values_top, arrived):
        flat = arrived.reshape(-1, width + 128)
        arrived_labels = flat[:, width].astype(jnp.int32) * tile_rows + flat[:, width + 1].astype(
            jnp.int32
        )
        fluxes = flat[:, :width].astype(jnp.float32).reshape(-1, flux_count, block_len)
        forcing = scatter_regrid(arrived_labels, fluxes, weights_low)
        forcing = forcing.reshape(tile_rows, flux_count, block_len).transpose(1, 0, 2)
        lifted = jnp.sum(forcing * ocean_map[:, 0][:, None, None], axis=0)
        top_level = jnp.where(sea_cells, values_top + lifted, state_top)
        table = jnp.einsum("db,wab->wda", top_level, weights_wide, precision=HIGHEST)
        replies = jnp.take(table.reshape(weight_count * tile_rows, block_len), arrived_labels, axis=0)
        return forcing, replies.reshape(senders, capacity, block_len), top_level

    def atmosphere_reply(values_top, arrived):
        return (
            jnp.zeros((flux_count, tile_rows, block_len), jnp.float32),
            jnp.zeros((senders, capacity, block_len), jnp.float32),
            values_top,
        )

    forcing, replies, ocean_top = lax.cond(
        ocean_side, ocean_reply, atmosphere_reply, first_top, arrived
    )
    answers = spread_from_ocean(replies, offsets, mesh_shape)
    per_entry = jnp.take(
        answers.reshape(neighbour_count * capacity, block_len), entry_slots, axis=0
    )
    returned = per_entry.reshape(tile_rows, intersections, block_len).sum(axis=1)
    second, forcing, answers = lax.optimization_barrier((second, forcing, answers))
    sea_rows = jnp.broadcast_to(
        sea_cells.astype(jnp.int32).reshape(1, tile_rows * block_len), (8, tile_rows * block_len)
    )
    final_state = ocean_update(
        second,
        state,
        sea_rows,
        forcing.reshape(flux_count, tile_rows * block_len),
        ocean_map,
        comp_count,
    )
    top_plane = lax.cond(
        ocean_side, lambda values: ocean_top, lambda values: values[:, :, 0], final_state
    )
    surface_out = jnp.where(ocean_side, ocean_top, jnp.where(sea_cells, returned, top_plane))
    return (final_state, surface_out)


def solution(mesh):
    placed = (
        P(("comp", "lat"), "lon", None),
        P(("comp", "lat"), "lon"),
        P(("comp", "lat"), "lon", None, None),
        P(),
        P(),
        P(),
        P(),
        P(),
    )
    return jax.shard_map(
        local,
        mesh=mesh,
        in_specs=placed,
        out_specs=(P(("comp", "lat"), "lon", None), P(("comp", "lat"), "lon")),
        check_vma=False,
    )
```

```python
import jax
import jax.numpy as jnp
from jax import lax
from jax.experimental import pallas as pl
from jax.experimental.pallas import tpu as pltpu
from jax.sharding import PartitionSpec as P
import functools

SMOOTHING = 0.2
PHYSICS = 0.5
HIGHEST = lax.Precision.HIGHEST
ROW_BLOCK = 8


def split_bf16(values):
    high = values.astype(jnp.bfloat16)
    low = (values - high.astype(jnp.float32)).astype(jnp.bfloat16)
    return high, low


def three_pass(lhs, rhs, dims):
    lhs_hi, lhs_lo = split_bf16(lhs)
    rhs_hi, rhs_lo = split_bf16(rhs)

    def one(a, b):
        return lax.dot_general(a, b, (dims, ((), ())), preferred_element_type=jnp.float32)

    return one(lhs_hi, rhs_hi) + (one(lhs_hi, rhs_lo) + one(lhs_lo, rhs_hi))


def exact_rows(picker, values):
    high = values.astype(jnp.bfloat16)
    rest = values - high.astype(jnp.float32)
    middle = rest.astype(jnp.bfloat16)
    low = (rest - middle.astype(jnp.float32)).astype(jnp.bfloat16)

    def one(piece):
        return lax.dot_general(
            picker, piece, (((1,), (1,)), ((), ())), preferred_element_type=jnp.float32
        )

    return one(high) + one(middle) + one(low)


def substep_kernel(with_flux, comp_total, x_ref, top_ref, bottom_ref, west_ref, east_ref, mix_ref, *rest):
    if with_flux:
        fluxes_ref, out_ref, flux_out_ref = rest
    else:
        out_ref, planes_ref = rest
    rows, cols, levels = x_ref.shape
    centre = x_ref[...]
    up = jnp.concatenate([top_ref[...], centre[:-1]], axis=0)
    down = jnp.concatenate([centre[1:], bottom_ref[...]], axis=0)
    column = lax.broadcasted_iota(jnp.int32, centre.shape, 1)
    west = jnp.where(column == 0, west_ref[...], pltpu.roll(centre, 1, 1))
    east = jnp.where(column == cols - 1, east_ref[...], pltpu.roll(centre, cols - 1, 1))
    smooth = centre + SMOOTHING * (up + down + west + east - 4.0 * centre)
    flat = smooth.reshape(rows * cols, levels)
    mixed = three_pass(flat, mix_ref[...], ((1,), (0,)))
    moved = flat + PHYSICS * jnp.tanh(mixed)
    out_ref[...] = moved.reshape(rows, cols, levels)
    if not with_flux:
        ocean = lax.axis_index("comp") == comp_total - 1

        @pl.when(ocean)
        def _():
            plane_row = lax.broadcasted_iota(jnp.int32, (8, levels), 0)
            plane_lane = lax.broadcasted_iota(jnp.int32, (8, levels), 1)
            pick_out = ((plane_row == 0) & (plane_lane == 0)).astype(jnp.bfloat16)
            pick_in = ((plane_row == 1) & (plane_lane == 0)).astype(jnp.bfloat16)
            planes_ref[...] = exact_rows(pick_out, moved) + exact_rows(
                pick_in, centre.reshape(rows * cols, levels)
            )

        @pl.when(jnp.logical_not(ocean))
        def _():
            planes_ref[...] = jnp.zeros_like(planes_ref)

    else:
        total = centre.reshape(rows * cols, levels) + moved
        flux_out_ref[...] = three_pass(fluxes_ref[...], total, ((1,), (1,)))


def substep(values, top, bottom, west, east, mixing, comp_total, fluxes_t=None):
    rows, cols, levels = values.shape
    blocks = rows // ROW_BLOCK
    top_rows = jnp.concatenate([top, values[ROW_BLOCK - 1 : rows - 1 : ROW_BLOCK]], axis=0)
    bottom_rows = jnp.concatenate([values[ROW_BLOCK:rows:ROW_BLOCK], bottom], axis=0)
    with_flux = fluxes_t is not None
    in_specs = [
        pl.BlockSpec((ROW_BLOCK, cols, levels), lambda i: (i, 0, 0)),
        pl.BlockSpec((1, cols, levels), lambda i: (i, 0, 0)),
        pl.BlockSpec((1, cols, levels), lambda i: (i, 0, 0)),
        pl.BlockSpec((ROW_BLOCK, 1, levels), lambda i: (i, 0, 0)),
        pl.BlockSpec((ROW_BLOCK, 1, levels), lambda i: (i, 0, 0)),
        pl.BlockSpec((levels, levels), lambda i: (0, 0)),
    ]
    operands = [values, top_rows, bottom_rows, west, east, mixing]
    out_shape = [jax.ShapeDtypeStruct(values.shape, jnp.float32)]
    out_specs = [pl.BlockSpec((ROW_BLOCK, cols, levels), lambda i: (i, 0, 0))]
    if not with_flux:
        out_shape.append(jax.ShapeDtypeStruct((8, rows * cols), jnp.float32))
        out_specs.append(pl.BlockSpec((8, ROW_BLOCK * cols), lambda i: (0, i)))
    if with_flux:
        flux_count = fluxes_t.shape[0]
        in_specs.append(pl.BlockSpec((flux_count, levels), lambda i: (0, 0)))
        operands.append(fluxes_t)
        out_shape.append(jax.ShapeDtypeStruct((flux_count, rows * cols), jnp.float32))
        out_specs.append(pl.BlockSpec((flux_count, ROW_BLOCK * cols), lambda i: (0, i)))
    cells = rows * cols
    flops = 6 * cells * levels * levels + (6 * cells * levels * 8 if with_flux else 0)
    result = pl.pallas_call(
        functools.partial(substep_kernel, with_flux, comp_total),
        grid=(blocks,),
        in_specs=in_specs,
        out_specs=out_specs,
        out_shape=out_shape,
        cost_estimate=pl.CostEstimate(
            flops=flops, transcendentals=cells * levels, bytes_accessed=8 * cells * levels
        ),
    )(*operands)
    return result


def column_physics(values, mixing):
    return jnp.tanh(jnp.einsum("rck,kj->rcj", values, mixing, precision=HIGHEST))


def earlier_same(owners, usable):
    positions = jnp.arange(owners.shape[0], dtype=jnp.int32)
    before = (
        (owners[None, :] == owners[:, None])
        & (positions[None, :] < positions[:, None])
        & usable[None, :]
    )
    return jnp.sum(before.astype(jnp.int32), axis=1)


def pack_rows(blocks, owners, labels, usable, slots_each, owner_total):
    ranks = earlier_same(owners, usable)
    target_slot = owners * slots_each + ranks
    slot_ids = jnp.arange(owner_total * slots_each, dtype=jnp.int32)
    placing = (slot_ids[:, None] == target_slot[None, :]) & usable[None, :]
    packed = jnp.dot(
        placing.astype(jnp.bfloat16), blocks, preferred_element_type=jnp.float32
    ).astype(jnp.bfloat16)
    placed_labels = jnp.sum(jnp.where(placing, labels[None, :] + 1, 0), axis=1) - 1
    return (
        packed.reshape(owner_total, slots_each, blocks.shape[1]),
        placed_labels.reshape(owner_total, slots_each),
        target_slot,
    )


def edge_rows(values, lower_valid, upper_valid):
    bands = lax.axis_size("comp") * lax.axis_size("lat")
    up = [(i, i + 1) for i in range(bands - 1)]
    down = [(j, i) for i, j in up]
    before = lax.ppermute(values[-1:], ("comp", "lat"), up)
    after = lax.ppermute(values[:1], ("comp", "lat"), down)
    return (jnp.where(lower_valid, before, 0.0), jnp.where(upper_valid, after, 0.0))


def edge_columns(values):
    size = lax.axis_size("lon")
    up = [(i, (i + 1) % size) for i in range(size)]
    down = [(j, i) for i, j in up]
    before = lax.ppermute(values[:, -1:], "lon", up)
    after = lax.ppermute(values[:, :1], "lon", down)
    return before, after


MESH_IDS = pl.DeviceIdType.MESH


def tile_device(comp, tile, lon_total):
    return (comp, tile // lon_total, tile % lon_total)


def gather_kernel(offsets, shape, send_ref, out_ref, land, send_sems, recv_sems):
    comp_total, lat_total, lon_total = shape
    comp = lax.axis_index("comp")
    tiles = lat_total * lon_total
    tile = lax.axis_index("lat") * lon_total + lax.axis_index("lon")
    ocean = comp_total - 1
    count = len(offsets)
    barrier = pltpu.get_barrier_semaphore()

    @pl.when(comp != ocean)
    def _():
        for off in offsets:
            target = tile_device(ocean, (tile + off) % tiles, lon_total)
            pl.semaphore_signal(barrier, 1, device_id=target, device_id_type=MESH_IDS)
        pl.semaphore_wait(barrier, count)
        copies = []
        for k, off in enumerate(offsets):
            target = tile_device(ocean, (tile + off) % tiles, lon_total)
            copy = pltpu.make_async_remote_copy(
                src_ref=send_ref.at[k],
                dst_ref=land.at[comp * count + k],
                send_sem=send_sems.at[k],
                recv_sem=recv_sems.at[comp * count + k],
                device_id=target,
                device_id_type=MESH_IDS,
            )
            copy.start()
            copies.append(copy)
        for copy in copies:
            copy.wait_send()
        out_ref[...] = jnp.zeros_like(out_ref)

    @pl.when(comp == ocean)
    def _():
        for source_comp in range(ocean):
            for off in offsets:
                source = tile_device(source_comp, (tile + tiles - off) % tiles, lon_total)
                pl.semaphore_signal(barrier, 1, device_id=source, device_id_type=MESH_IDS)
        pl.semaphore_wait(barrier, count * ocean)
        for source_comp in range(ocean):
            for k, off in enumerate(offsets):
                source = tile_device(source_comp, (tile + tiles - off) % tiles, lon_total)
                slot = source_comp * count + k
                pltpu.make_async_remote_copy(
                    src_ref=send_ref.at[k],
                    dst_ref=land.at[slot],
                    send_sem=send_sems.at[k],
                    recv_sem=recv_sems.at[slot],
                    device_id=source,
                    device_id_type=MESH_IDS,
                ).wait_recv()
        out_ref[...] = land[...]


def gather_to_ocean(blocks, offsets, shape):
    count = len(offsets)
    senders = (shape[0] - 1) * count
    slot_shape = blocks.shape[1:]
    return pl.pallas_call(
        functools.partial(gather_kernel, tuple(offsets), tuple(shape)),
        out_shape=jax.ShapeDtypeStruct((senders,) + slot_shape, blocks.dtype),
        in_specs=[pl.BlockSpec(memory_space=pltpu.VMEM)],
        out_specs=pl.BlockSpec(memory_space=pltpu.VMEM),
        scratch_shapes=[
            pltpu.VMEM((senders,) + slot_shape, blocks.dtype),
            pltpu.SemaphoreType.DMA((count,)),
            pltpu.SemaphoreType.DMA((senders,)),
        ],
        compiler_params=pltpu.CompilerParams(collective_id=0, has_side_effects=True),
    )(blocks)


def spread_kernel(offsets, shape, surface_ref, out_ref, land, send_sems, recv_sems):
    comp_total, lat_total, lon_total = shape
    comp = lax.axis_index("comp")
    tiles = lat_total * lon_total
    tile = lax.axis_index("lat") * lon_total + lax.axis_index("lon")
    ocean = comp_total - 1
    count = len(offsets)
    barrier = pltpu.get_barrier_semaphore()

    @pl.when(comp == ocean)
    def _():
        for target_comp in range(ocean):
            for off in offsets:
                target = tile_device(target_comp, (tile + tiles - off) % tiles, lon_total)
                pl.semaphore_signal(barrier, 1, device_id=target, device_id_type=MESH_IDS)
        pl.semaphore_wait(barrier, count * ocean)
        copies = []
        for target_comp in range(ocean):
            for k, off in enumerate(offsets):
                target = tile_device(target_comp, (tile + tiles - off) % tiles, lon_total)
                copy = pltpu.make_async_remote_copy(
                    src_ref=surface_ref.at[target_comp * count + k],
                    dst_ref=land.at[k],
                    send_sem=send_sems.at[target_comp * count + k],
                    recv_sem=recv_sems.at[k],
                    device_id=target,
                    device_id_type=MESH_IDS,
                )
                copy.start()
                copies.append(copy)
        for copy in copies:
            copy.wait_send()
        out_ref[...] = jnp.zeros_like(out_ref)

    @pl.when(comp != ocean)
    def _():
        for off in offsets:
            source = tile_device(ocean, (tile + off) % tiles, lon_total)
            pl.semaphore_signal(barrier, 1, device_id=source, device_id_type=MESH_IDS)
        pl.semaphore_wait(barrier, count)
        for k, off in enumerate(offsets):
            source = tile_device(ocean, (tile + off) % tiles, lon_total)
            pltpu.make_async_remote_copy(
                src_ref=surface_ref.at[k],
                dst_ref=land.at[k],
                send_sem=send_sems.at[k],
                recv_sem=recv_sems.at[k],
                device_id=source,
                device_id_type=MESH_IDS,
            ).wait_recv()
        out_ref[...] = land[...]


def spread_from_ocean(replies, offsets, shape):
    count = len(offsets)
    senders = (shape[0] - 1) * count
    slot_shape = replies.shape[1:]
    return pl.pallas_call(
        functools.partial(spread_kernel, tuple(offsets), tuple(shape)),
        out_shape=jax.ShapeDtypeStruct((count,) + slot_shape, replies.dtype),
        in_specs=[pl.BlockSpec(memory_space=pltpu.VMEM)],
        out_specs=pl.BlockSpec(memory_space=pltpu.VMEM),
        scratch_shapes=[
            pltpu.VMEM((count,) + slot_shape, replies.dtype),
            pltpu.SemaphoreType.DMA((senders,)),
            pltpu.SemaphoreType.DMA((count,)),
        ],
        compiler_params=pltpu.CompilerParams(collective_id=1, has_side_effects=True),
    )(replies)


def ocean_update_kernel(flag_ref, first_ref, state_ref, sea_ref, forcing_ref, spread_ref, out_ref):
    ocean = flag_ref[0] == 1

    @pl.when(ocean)
    def _():
        ocean_block(first_ref, state_ref, sea_ref, forcing_ref, spread_ref, out_ref)

    @pl.when(jnp.logical_not(ocean))
    def _():
        out_ref[...] = first_ref[...]


def ocean_block(first_ref, state_ref, sea_ref, forcing_ref, spread_ref, out_ref):
    rows, cols, levels = first_ref.shape
    forcing = forcing_ref[...]
    spread = spread_ref[...]
    forcing_hi = forcing.astype(jnp.bfloat16)
    forcing_lo = (forcing - forcing_hi.astype(jnp.float32)).astype(jnp.bfloat16)
    spread_hi = spread.astype(jnp.bfloat16)
    spread_lo = (spread - spread_hi.astype(jnp.float32)).astype(jnp.bfloat16)

    def one(a, b):
        return lax.dot_general(a, b, (((0,), (0,)), ((), ())), preferred_element_type=jnp.float32)

    added = one(forcing_hi, spread_hi) + (one(forcing_hi, spread_lo) + one(forcing_lo, spread_hi))
    lane_row = lax.broadcasted_iota(jnp.int32, (8, levels), 0)
    ones = (lane_row == 0).astype(jnp.bfloat16)
    picks = jnp.where(lax.broadcasted_iota(jnp.int32, sea_ref.shape, 0) == 0, sea_ref[...], 0)
    mask = one(picks.astype(jnp.bfloat16), ones)
    moved = first_ref[...].reshape(rows * cols, levels) + added
    kept = jnp.where(mask > 0.5, moved, state_ref[...].reshape(rows * cols, levels))
    out_ref[...] = kept.reshape(rows, cols, levels)


def ocean_update(first, state, sea_rows, forcing, ocean_map, comp_total):
    rows, cols, levels = first.shape
    flux_count = forcing.shape[0]
    cells = rows * cols
    flag = (lax.axis_index("comp") == comp_total - 1).astype(jnp.int32).reshape(1)
    return pl.pallas_call(
        ocean_update_kernel,
        grid_spec=pltpu.PrefetchScalarGridSpec(
            num_scalar_prefetch=1,
            grid=(rows // ROW_BLOCK,),
            in_specs=[
                pl.BlockSpec((ROW_BLOCK, cols, levels), lambda i, f: (i, 0, 0)),
                pl.BlockSpec((ROW_BLOCK, cols, levels), lambda i, f: (i * f[0], 0, 0)),
                pl.BlockSpec((8, ROW_BLOCK * cols), lambda i, f: (0, i * f[0])),
                pl.BlockSpec((flux_count, ROW_BLOCK * cols), lambda i, f: (0, i * f[0])),
                pl.BlockSpec((flux_count, levels), lambda i, f: (0, 0)),
            ],
            out_specs=pl.BlockSpec((ROW_BLOCK, cols, levels), lambda i, f: (i, 0, 0)),
        ),
        out_shape=jax.ShapeDtypeStruct(first.shape, jnp.float32),
        cost_estimate=pl.CostEstimate(
            flops=8 * cells * levels * flux_count, transcendentals=0, bytes_accessed=12 * cells * levels
        ),
    )(flag, first, state, sea_rows, forcing, ocean_map)


def scatter_regrid_kernel(labels_ref, fluxes_ref, weights_ref, out_ref, binned_ref):
    entries = fluxes_ref.shape[0]
    weight_count, tile_rows, block_len = weights_ref.shape
    flux_count = fluxes_ref.shape[1]
    binned_ref[...] = jnp.zeros_like(binned_ref)

    def add_one(e, carry):
        label = labels_ref[e]
        binned_ref[label] = binned_ref[label] + fluxes_ref[e]
        return carry

    lax.fori_loop(0, entries, add_one, 0, unroll=8)
    out_ref[...] = jnp.zeros_like(out_ref)

    def regrid_one(w, carry):
        start = pl.multiple_of(w * tile_rows, tile_rows)
        block = binned_ref[pl.ds(start, tile_rows)].reshape(tile_rows * flux_count, block_len)
        high = block.astype(jnp.bfloat16)
        low = (block - high.astype(jnp.float32)).astype(jnp.bfloat16)
        weight = weights_ref[w]
        out_ref[...] += jnp.dot(high, weight, preferred_element_type=jnp.float32) + jnp.dot(
            low, weight, preferred_element_type=jnp.float32
        )
        return carry

    lax.fori_loop(0, weight_count, regrid_one, 0)


def scatter_regrid(labels, fluxes, weights):
    entries, flux_count, block_len = fluxes.shape
    weight_count, tile_rows, _ = weights.shape
    return pl.pallas_call(
        scatter_regrid_kernel,
        out_shape=jax.ShapeDtypeStruct((tile_rows * flux_count, block_len), jnp.float32),
        in_specs=[
            pl.BlockSpec(memory_space=pltpu.SMEM),
            pl.BlockSpec(memory_space=pltpu.VMEM),
            pl.BlockSpec(memory_space=pltpu.VMEM),
        ],
        out_specs=pl.BlockSpec(memory_space=pltpu.VMEM),
        scratch_shapes=[pltpu.VMEM((weight_count * tile_rows, flux_count, block_len), jnp.float32)],
        compiler_params=pltpu.CompilerParams(vmem_limit_bytes=48 * 1024 * 1024),
        cost_estimate=pl.CostEstimate(
            flops=4 * weight_count * tile_rows * flux_count * block_len * block_len,
            transcendentals=0,
            bytes_accessed=entries * flux_count * block_len * 4 + weight_count * tile_rows * block_len * 2,
        ),
    )(labels, fluxes, weights)


def local(
    state, land_mask, intersection_list, mix_atm, mix_ocn, flux_map, ocean_map, regrid_weights
):
    tile_rows, block_len, levels = state.shape
    flux_count = flux_map.shape[1]
    weight_count = regrid_weights.shape[0]
    intersections = intersection_list.shape[2]
    comp_count = lax.axis_size("comp")
    lat_count = lax.axis_size("lat")
    lon_count = lax.axis_size("lon")
    tile_count = lat_count * lon_count
    reach = min(4, lon_count)
    neighbour_count = 2 * reach
    capacity = intersections * tile_rows // neighbour_count
    width = flux_count * block_len
    comp_index = lax.axis_index("comp")
    tile_index = lax.axis_index("lat") * lon_count + lax.axis_index("lon")
    band = comp_index * lat_count + lax.axis_index("lat")
    ocean_band = (comp_count - 1) * lat_count
    ocean_side = comp_index == comp_count - 1
    lower_valid = (band > 0) & ((band - 1 >= ocean_band) == (band >= ocean_band))
    upper_valid = (band < comp_count * lat_count - 1) & (
        (band + 1 >= ocean_band) == (band >= ocean_band)
    )
    sea_cells = land_mask == 1

    top, bottom = edge_rows(state, lower_valid, upper_valid)
    west, east = edge_columns(state)
    mixing = jnp.where(ocean_side, mix_ocn, mix_atm)
    first, first_planes = substep(state, top, bottom, west, east, mixing, comp_count)
    first_top = first_planes[0].reshape(tile_rows, block_len)
    state_top = first_planes[1].reshape(tile_rows, block_len)
    top, bottom = edge_rows(first, lower_valid, upper_valid)
    west, east = edge_columns(first)

    def atmosphere_second(values, top, bottom, west, east):
        moved, total = substep(values, top, bottom, west, east, mix_atm, comp_count, flux_map.T)
        total = total.reshape(flux_count, tile_rows, block_len)
        sent = jnp.where(sea_cells[None], 0.5 * total, 0.0).astype(jnp.bfloat16)
        return moved, sent

    def ocean_second(values, top, bottom, west, east):
        return values, jnp.zeros((flux_count, tile_rows, block_len), jnp.bfloat16)

    second, flux_sent = lax.cond(
        ocean_side, ocean_second, atmosphere_second, first, top, bottom, west, east
    )
    entry_list = intersection_list.reshape(tile_rows * intersections, 3)
    owners = entry_list[:, 0]
    targets = entry_list[:, 1]
    weight_ids = entry_list[:, 2]
    labels = weight_ids * tile_rows + targets
    entry_blocks = jnp.repeat(flux_sent.transpose(1, 0, 2), intersections, axis=0).reshape(
        tile_rows * intersections, width
    )
    lane = jnp.arange(128, dtype=jnp.int32)[None, :]
    label_lanes = jnp.where(
        lane == 0, weight_ids[:, None], jnp.where(lane == 1, targets[:, None], 0)
    ).astype(jnp.bfloat16)
    entry_blocks = jnp.concatenate([entry_blocks, label_lanes], axis=1)
    sending = jnp.broadcast_to(jnp.logical_not(ocean_side), owners.shape)
    offsets = [
        (n // reach * lon_count + n % reach - (reach - 1) // 2) % tile_count
        for n in range(neighbour_count)
    ]
    offset_table = jnp.array(offsets, jnp.int32)
    distance = (owners - tile_index + tile_count) % tile_count
    neighbour_ids = jnp.sum(
        jnp.where(
            distance[:, None] == offset_table[None, :],
            jnp.arange(neighbour_count, dtype=jnp.int32)[None, :],
            0,
        ),
        axis=1,
    )
    packed, _, entry_slots = pack_rows(entry_blocks, neighbour_ids, labels, sending, capacity, neighbour_count)
    mesh_shape = (comp_count, lat_count, lon_count)
    arrived = gather_to_ocean(packed, offsets, mesh_shape)
    weights_low = regrid_weights
    weights_wide = regrid_weights.astype(jnp.float32)
    senders = (comp_count - 1) * neighbour_count

    def ocean_reply(values_top, arrived):
        flat = arrived.reshape(-1, width + 128)
        arrived_labels = flat[:, width].astype(jnp.int32) * tile_rows + flat[:, width + 1].astype(
            jnp.int32
        )
        fluxes = flat[:, :width].astype(jnp.float32).reshape(-1, flux_count, block_len)
        forcing = scatter_regrid(arrived_labels, fluxes, weights_low)
        forcing = forcing.reshape(tile_rows, flux_count, block_len).transpose(1, 0, 2)
        lifted = jnp.sum(forcing * ocean_map[:, 0][:, None, None], axis=0)
        top_level = jnp.where(sea_cells, values_top + lifted, state_top)
        table = jnp.einsum("db,wab->wda", top_level, weights_wide, precision=HIGHEST)
        replies = jnp.take(table.reshape(weight_count * tile_rows, block_len), arrived_labels, axis=0)
        return forcing, replies.reshape(senders, capacity, block_len), top_level

    def atmosphere_reply(values_top, arrived):
        return (
            jnp.zeros((flux_count, tile_rows, block_len), jnp.float32),
            jnp.zeros((senders, capacity, block_len), jnp.float32),
            values_top,
        )

    forcing, replies, ocean_top = lax.cond(
        ocean_side, ocean_reply, atmosphere_reply, first_top, arrived
    )
    answers = spread_from_ocean(replies, offsets, mesh_shape)
    per_entry = jnp.take(
        answers.reshape(neighbour_count * capacity, block_len), entry_slots, axis=0
    )
    returned = per_entry.reshape(tile_rows, intersections, block_len).sum(axis=1)
    second, forcing, answers = lax.optimization_barrier((second, forcing, answers))
    sea_rows = jnp.broadcast_to(
        sea_cells.astype(jnp.int32).reshape(1, tile_rows * block_len), (8, tile_rows * block_len)
    )
    final_state = ocean_update(
        second,
        state,
        sea_rows,
        forcing.reshape(flux_count, tile_rows * block_len),
        ocean_map,
        comp_count,
    )
    top_plane = lax.cond(
        ocean_side, lambda values: ocean_top, lambda values: values[:, :, 0], final_state
    )
    surface_out = jnp.where(ocean_side, ocean_top, jnp.where(sea_cells, returned, top_plane))
    return (final_state, surface_out)


def solution(mesh):
    placed = (
        P(("comp", "lat"), "lon", None),
        P(("comp", "lat"), "lon"),
        P(("comp", "lat"), "lon", None, None),
        P(),
        P(),
        P(),
        P(),
        P(),
    )
    return jax.shard_map(
        local,
        mesh=mesh,
        in_specs=placed,
        out_specs=(P(("comp", "lat"), "lon", None), P(("comp", "lat"), "lon")),
        check_vma=False,
    )
```

```python
import jax
import jax.numpy as jnp
from jax import lax
from jax.experimental import pallas as pl
from jax.experimental.pallas import tpu as pltpu
from jax.sharding import PartitionSpec as P
import functools

SMOOTHING = 0.2
PHYSICS = 0.5
HIGHEST = lax.Precision.HIGHEST
ROW_BLOCK = 8


def split_bf16(values):
    high = values.astype(jnp.bfloat16)
    low = (values - high.astype(jnp.float32)).astype(jnp.bfloat16)
    return high, low


def three_pass(lhs, rhs, dims):
    lhs_hi, lhs_lo = split_bf16(lhs)
    rhs_hi, rhs_lo = split_bf16(rhs)

    def one(a, b):
        return lax.dot_general(a, b, (dims, ((), ())), preferred_element_type=jnp.float32)

    return one(lhs_hi, rhs_hi) + (one(lhs_hi, rhs_lo) + one(lhs_lo, rhs_hi))


def exact_rows(picker, values):
    high = values.astype(jnp.bfloat16)
    rest = values - high.astype(jnp.float32)
    middle = rest.astype(jnp.bfloat16)
    low = (rest - middle.astype(jnp.float32)).astype(jnp.bfloat16)

    def one(piece):
        return lax.dot_general(
            picker, piece, (((1,), (1,)), ((), ())), preferred_element_type=jnp.float32
        )

    return one(high) + one(middle) + one(low)


def substep_kernel(with_flux, comp_total, x_ref, top_ref, bottom_ref, west_ref, east_ref, mix_ref, *rest):
    if with_flux:
        fluxes_ref, out_ref, flux_out_ref = rest
    else:
        out_ref, planes_ref = rest
    rows, cols, levels = x_ref.shape
    centre = x_ref[...]
    up = jnp.concatenate([top_ref[...], centre[:-1]], axis=0)
    down = jnp.concatenate([centre[1:], bottom_ref[...]], axis=0)
    column = lax.broadcasted_iota(jnp.int32, centre.shape, 1)
    west = jnp.where(column == 0, west_ref[...], pltpu.roll(centre, 1, 1))
    east = jnp.where(column == cols - 1, east_ref[...], pltpu.roll(centre, cols - 1, 1))
    smooth = centre + SMOOTHING * (up + down + west + east - 4.0 * centre)
    flat = smooth.reshape(rows * cols, levels)
    mixed = three_pass(flat, mix_ref[...], ((1,), (0,)))
    moved = flat + PHYSICS * jnp.tanh(mixed)
    out_ref[...] = moved.reshape(rows, cols, levels)
    if not with_flux:
        ocean = lax.axis_index("comp") == comp_total - 1

        @pl.when(ocean)
        def _():
            plane_row = lax.broadcasted_iota(jnp.int32, (8, levels), 0)
            plane_lane = lax.broadcasted_iota(jnp.int32, (8, levels), 1)
            pick_out = ((plane_row == 0) & (plane_lane == 0)).astype(jnp.bfloat16)
            pick_in = ((plane_row == 1) & (plane_lane == 0)).astype(jnp.bfloat16)
            planes_ref[...] = exact_rows(pick_out, moved) + exact_rows(
                pick_in, centre.reshape(rows * cols, levels)
            )

        @pl.when(jnp.logical_not(ocean))
        def _():
            planes_ref[...] = jnp.zeros_like(planes_ref)

    else:
        total = centre.reshape(rows * cols, levels) + moved
        flux_out_ref[...] = three_pass(fluxes_ref[...], total, ((1,), (1,)))


def substep(values, top, bottom, west, east, mixing, comp_total, fluxes_t=None):
    rows, cols, levels = values.shape
    blocks = rows // ROW_BLOCK
    top_rows = jnp.concatenate([top, values[ROW_BLOCK - 1 : rows - 1 : ROW_BLOCK]], axis=0)
    bottom_rows = jnp.concatenate([values[ROW_BLOCK:rows:ROW_BLOCK], bottom], axis=0)
    with_flux = fluxes_t is not None
    in_specs = [
        pl.BlockSpec((ROW_BLOCK, cols, levels), lambda i: (i, 0, 0)),
        pl.BlockSpec((1, cols, levels), lambda i: (i, 0, 0)),
        pl.BlockSpec((1, cols, levels), lambda i: (i, 0, 0)),
        pl.BlockSpec((ROW_BLOCK, 1, levels), lambda i: (i, 0, 0)),
        pl.BlockSpec((ROW_BLOCK, 1, levels), lambda i: (i, 0, 0)),
        pl.BlockSpec((levels, levels), lambda i: (0, 0)),
    ]
    operands = [values, top_rows, bottom_rows, west, east, mixing]
    out_shape = [jax.ShapeDtypeStruct(values.shape, jnp.float32)]
    out_specs = [pl.BlockSpec((ROW_BLOCK, cols, levels), lambda i: (i, 0, 0))]
    if not with_flux:
        out_shape.append(jax.ShapeDtypeStruct((8, rows * cols), jnp.float32))
        out_specs.append(pl.BlockSpec((8, ROW_BLOCK * cols), lambda i: (0, i)))
    if with_flux:
        flux_count = fluxes_t.shape[0]
        in_specs.append(pl.BlockSpec((flux_count, levels), lambda i: (0, 0)))
        operands.append(fluxes_t)
        out_shape.append(jax.ShapeDtypeStruct((flux_count, rows * cols), jnp.float32))
        out_specs.append(pl.BlockSpec((flux_count, ROW_BLOCK * cols), lambda i: (0, i)))
    cells = rows * cols
    flops = 6 * cells * levels * levels + (6 * cells * levels * 8 if with_flux else 0)
    result = pl.pallas_call(
        functools.partial(substep_kernel, with_flux, comp_total),
        grid=(blocks,),
        in_specs=in_specs,
        out_specs=out_specs,
        out_shape=out_shape,
        cost_estimate=pl.CostEstimate(
            flops=flops, transcendentals=cells * levels, bytes_accessed=8 * cells * levels
        ),
    )(*operands)
    return result


def column_physics(values, mixing):
    return jnp.tanh(jnp.einsum("rck,kj->rcj", values, mixing, precision=HIGHEST))


def earlier_same(owners, usable):
    positions = jnp.arange(owners.shape[0], dtype=jnp.int32)
    before = (
        (owners[None, :] == owners[:, None])
        & (positions[None, :] < positions[:, None])
        & usable[None, :]
    )
    return jnp.sum(before.astype(jnp.int32), axis=1)


def pack_rows(blocks, owners, labels, usable, slots_each, owner_total):
    ranks = earlier_same(owners, usable)
    target_slot = owners * slots_each + ranks
    slot_ids = jnp.arange(owner_total * slots_each, dtype=jnp.int32)
    placing = (slot_ids[:, None] == target_slot[None, :]) & usable[None, :]
    packed = jnp.dot(
        placing.astype(jnp.bfloat16), blocks, preferred_element_type=jnp.float32
    ).astype(jnp.bfloat16)
    placed_labels = jnp.sum(jnp.where(placing, labels[None, :] + 1, 0), axis=1) - 1
    return (
        packed.reshape(owner_total, slots_each, blocks.shape[1]),
        placed_labels.reshape(owner_total, slots_each),
        target_slot,
    )


MESH_IDS = pl.DeviceIdType.MESH


def tile_device(comp, tile, lon_total):
    return (comp, tile // lon_total, tile % lon_total)


def gather_kernel(offsets, shape, send_ref, out_ref, land, send_sems, recv_sems):
    comp_total, lat_total, lon_total = shape
    comp = lax.axis_index("comp")
    tiles = lat_total * lon_total
    tile = lax.axis_index("lat") * lon_total + lax.axis_index("lon")
    ocean = comp_total - 1
    count = len(offsets)
    barrier = pltpu.get_barrier_semaphore()

    @pl.when(comp != ocean)
    def _():
        for off in offsets:
            target = tile_device(ocean, (tile + off) % tiles, lon_total)
            pl.semaphore_signal(barrier, 1, device_id=target, device_id_type=MESH_IDS)
        pl.semaphore_wait(barrier, count)
        copies = []
        for k, off in enumerate(offsets):
            target = tile_device(ocean, (tile + off) % tiles, lon_total)
            copy = pltpu.make_async_remote_copy(
                src_ref=send_ref.at[k],
                dst_ref=land.at[comp * count + k],
                send_sem=send_sems.at[k],
                recv_sem=recv_sems.at[comp * count + k],
                device_id=target,
                device_id_type=MESH_IDS,
            )
            copy.start()
            copies.append(copy)
        for copy in copies:
            copy.wait_send()
        out_ref[...] = jnp.zeros_like(out_ref)

    @pl.when(comp == ocean)
    def _():
        for source_comp in range(ocean):
            for off in offsets:
                source = tile_device(source_comp, (tile + tiles - off) % tiles, lon_total)
                pl.semaphore_signal(barrier, 1, device_id=source, device_id_type=MESH_IDS)
        pl.semaphore_wait(barrier, count * ocean)
        for source_comp in range(ocean):
            for k, off in enumerate(offsets):
                source = tile_device(source_comp, (tile + tiles - off) % tiles, lon_total)
                slot = source_comp * count + k
                pltpu.make_async_remote_copy(
                    src_ref=send_ref.at[k],
                    dst_ref=land.at[slot],
                    send_sem=send_sems.at[k],
                    recv_sem=recv_sems.at[slot],
                    device_id=source,
                    device_id_type=MESH_IDS,
                ).wait_recv()
        out_ref[...] = land[...]


def gather_to_ocean(blocks, offsets, shape):
    count = len(offsets)
    senders = (shape[0] - 1) * count
    slot_shape = blocks.shape[1:]
    return pl.pallas_call(
        functools.partial(gather_kernel, tuple(offsets), tuple(shape)),
        out_shape=jax.ShapeDtypeStruct((senders,) + slot_shape, blocks.dtype),
        in_specs=[pl.BlockSpec(memory_space=pltpu.VMEM)],
        out_specs=pl.BlockSpec(memory_space=pltpu.VMEM),
        scratch_shapes=[
            pltpu.VMEM((senders,) + slot_shape, blocks.dtype),
            pltpu.SemaphoreType.DMA((count,)),
            pltpu.SemaphoreType.DMA((senders,)),
        ],
        compiler_params=pltpu.CompilerParams(collective_id=0, has_side_effects=True),
    )(blocks)


def spread_kernel(offsets, shape, surface_ref, out_ref, land, send_sems, recv_sems):
    comp_total, lat_total, lon_total = shape
    comp = lax.axis_index("comp")
    tiles = lat_total * lon_total
    tile = lax.axis_index("lat") * lon_total + lax.axis_index("lon")
    ocean = comp_total - 1
    count = len(offsets)
    barrier = pltpu.get_barrier_semaphore()

    @pl.when(comp == ocean)
    def _():
        for target_comp in range(ocean):
            for off in offsets:
                target = tile_device(target_comp, (tile + tiles - off) % tiles, lon_total)
                pl.semaphore_signal(barrier, 1, device_id=target, device_id_type=MESH_IDS)
        pl.semaphore_wait(barrier, count * ocean)
        copies = []
        for target_comp in range(ocean):
            for k, off in enumerate(offsets):
                target = tile_device(target_comp, (tile + tiles - off) % tiles, lon_total)
                copy = pltpu.make_async_remote_copy(
                    src_ref=surface_ref.at[target_comp * count + k],
                    dst_ref=land.at[k],
                    send_sem=send_sems.at[target_comp * count + k],
                    recv_sem=recv_sems.at[k],
                    device_id=target,
                    device_id_type=MESH_IDS,
                )
                copy.start()
                copies.append(copy)
        for copy in copies:
            copy.wait_send()
        out_ref[...] = jnp.zeros_like(out_ref)

    @pl.when(comp != ocean)
    def _():
        for off in offsets:
            source = tile_device(ocean, (tile + off) % tiles, lon_total)
            pl.semaphore_signal(barrier, 1, device_id=source, device_id_type=MESH_IDS)
        pl.semaphore_wait(barrier, count)
        for k, off in enumerate(offsets):
            source = tile_device(ocean, (tile + off) % tiles, lon_total)
            pltpu.make_async_remote_copy(
                src_ref=surface_ref.at[k],
                dst_ref=land.at[k],
                send_sem=send_sems.at[k],
                recv_sem=recv_sems.at[k],
                device_id=source,
                device_id_type=MESH_IDS,
            ).wait_recv()
        out_ref[...] = land[...]


def spread_from_ocean(replies, offsets, shape):
    count = len(offsets)
    senders = (shape[0] - 1) * count
    slot_shape = replies.shape[1:]
    return pl.pallas_call(
        functools.partial(spread_kernel, tuple(offsets), tuple(shape)),
        out_shape=jax.ShapeDtypeStruct((count,) + slot_shape, replies.dtype),
        in_specs=[pl.BlockSpec(memory_space=pltpu.VMEM)],
        out_specs=pl.BlockSpec(memory_space=pltpu.VMEM),
        scratch_shapes=[
            pltpu.VMEM((count,) + slot_shape, replies.dtype),
            pltpu.SemaphoreType.DMA((senders,)),
            pltpu.SemaphoreType.DMA((count,)),
        ],
        compiler_params=pltpu.CompilerParams(collective_id=1, has_side_effects=True),
    )(replies)


def ocean_update_kernel(flag_ref, first_ref, state_ref, sea_ref, forcing_ref, spread_ref, out_ref):
    ocean = flag_ref[0] == 1

    @pl.when(ocean)
    def _():
        ocean_block(first_ref, state_ref, sea_ref, forcing_ref, spread_ref, out_ref)

    @pl.when(jnp.logical_not(ocean))
    def _():
        out_ref[...] = first_ref[...]


def ocean_block(first_ref, state_ref, sea_ref, forcing_ref, spread_ref, out_ref):
    rows, cols, levels = first_ref.shape
    forcing = forcing_ref[...]
    spread = spread_ref[...]
    forcing_hi = forcing.astype(jnp.bfloat16)
    forcing_lo = (forcing - forcing_hi.astype(jnp.float32)).astype(jnp.bfloat16)
    spread_hi = spread.astype(jnp.bfloat16)
    spread_lo = (spread - spread_hi.astype(jnp.float32)).astype(jnp.bfloat16)

    def one(a, b):
        return lax.dot_general(a, b, (((0,), (0,)), ((), ())), preferred_element_type=jnp.float32)

    added = one(forcing_hi, spread_hi) + (one(forcing_hi, spread_lo) + one(forcing_lo, spread_hi))
    lane_row = lax.broadcasted_iota(jnp.int32, (8, levels), 0)
    ones = (lane_row == 0).astype(jnp.bfloat16)
    picks = jnp.where(lax.broadcasted_iota(jnp.int32, sea_ref.shape, 0) == 0, sea_ref[...], 0)
    mask = one(picks.astype(jnp.bfloat16), ones)
    moved = first_ref[...].reshape(rows * cols, levels) + added
    kept = jnp.where(mask > 0.5, moved, state_ref[...].reshape(rows * cols, levels))
    out_ref[...] = kept.reshape(rows, cols, levels)


def ocean_update(first, state, sea_rows, forcing, ocean_map, comp_total):
    rows, cols, levels = first.shape
    flux_count = forcing.shape[0]
    cells = rows * cols
    flag = (lax.axis_index("comp") == comp_total - 1).astype(jnp.int32).reshape(1)
    return pl.pallas_call(
        ocean_update_kernel,
        grid_spec=pltpu.PrefetchScalarGridSpec(
            num_scalar_prefetch=1,
            grid=(rows // ROW_BLOCK,),
            in_specs=[
                pl.BlockSpec((ROW_BLOCK, cols, levels), lambda i, f: (i, 0, 0)),
                pl.BlockSpec((ROW_BLOCK, cols, levels), lambda i, f: (i * f[0], 0, 0)),
                pl.BlockSpec((8, ROW_BLOCK * cols), lambda i, f: (0, i * f[0])),
                pl.BlockSpec((flux_count, ROW_BLOCK * cols), lambda i, f: (0, i * f[0])),
                pl.BlockSpec((flux_count, levels), lambda i, f: (0, 0)),
            ],
            out_specs=pl.BlockSpec((ROW_BLOCK, cols, levels), lambda i, f: (i, 0, 0)),
        ),
        out_shape=jax.ShapeDtypeStruct(first.shape, jnp.float32),
        cost_estimate=pl.CostEstimate(
            flops=8 * cells * levels * flux_count, transcendentals=0, bytes_accessed=12 * cells * levels
        ),
    )(flag, first, state, sea_rows, forcing, ocean_map)


def scatter_regrid_kernel(labels_ref, fluxes_ref, weights_ref, out_ref, binned_ref):
    entries = fluxes_ref.shape[0]
    weight_count, tile_rows, block_len = weights_ref.shape
    flux_count = fluxes_ref.shape[1]
    binned_ref[...] = jnp.zeros_like(binned_ref)

    def add_one(e, carry):
        label = labels_ref[e]
        binned_ref[label] = binned_ref[label] + fluxes_ref[e]
        return carry

    lax.fori_loop(0, entries, add_one, 0, unroll=8)
    out_ref[...] = jnp.zeros_like(out_ref)

    def regrid_one(w, carry):
        start = pl.multiple_of(w * tile_rows, tile_rows)
        block = binned_ref[pl.ds(start, tile_rows)].reshape(tile_rows * flux_count, block_len)
        high = block.astype(jnp.bfloat16)
        low = (block - high.astype(jnp.float32)).astype(jnp.bfloat16)
        weight = weights_ref[w]
        out_ref[...] += jnp.dot(high, weight, preferred_element_type=jnp.float32) + jnp.dot(
            low, weight, preferred_element_type=jnp.float32
        )
        return carry

    lax.fori_loop(0, weight_count, regrid_one, 0)


def scatter_regrid(labels, fluxes, weights):
    entries, flux_count, block_len = fluxes.shape
    weight_count, tile_rows, _ = weights.shape
    return pl.pallas_call(
        scatter_regrid_kernel,
        out_shape=jax.ShapeDtypeStruct((tile_rows * flux_count, block_len), jnp.float32),
        in_specs=[
            pl.BlockSpec(memory_space=pltpu.SMEM),
            pl.BlockSpec(memory_space=pltpu.VMEM),
            pl.BlockSpec(memory_space=pltpu.VMEM),
        ],
        out_specs=pl.BlockSpec(memory_space=pltpu.VMEM),
        scratch_shapes=[pltpu.VMEM((weight_count * tile_rows, flux_count, block_len), jnp.float32)],
        compiler_params=pltpu.CompilerParams(vmem_limit_bytes=48 * 1024 * 1024),
        cost_estimate=pl.CostEstimate(
            flops=4 * weight_count * tile_rows * flux_count * block_len * block_len,
            transcendentals=0,
            bytes_accessed=entries * flux_count * block_len * 4 + weight_count * tile_rows * block_len * 2,
        ),
    )(labels, fluxes, weights)


def halo_kernel(shape, values_ref, rows_out, cols_out, rows_land, cols_land, send_sems, recv_sems):
    comp_total, lat_total, lon_total = shape
    bands = comp_total * lat_total
    band = lax.axis_index("comp") * lat_total + lax.axis_index("lat")
    lon = lax.axis_index("lon")
    rows, cols, _ = values_ref.shape
    up = (band + 1) % bands
    down = (band + bands - 1) % bands
    up_device = (up // lat_total, up % lat_total, lon)
    down_device = (down // lat_total, down % lat_total, lon)
    east_device = (band // lat_total, band % lat_total, (lon + 1) % lon_total)
    west_device = (band // lat_total, band % lat_total, (lon + lon_total - 1) % lon_total)
    barrier = pltpu.get_barrier_semaphore()
    for device in (up_device, down_device, east_device, west_device):
        pl.semaphore_signal(barrier, 1, device_id=device, device_id_type=MESH_IDS)
    pl.semaphore_wait(barrier, 4)
    plan = [
        (values_ref.at[pl.ds(rows - 1, 1)], rows_land.at[0], up_device),
        (values_ref.at[pl.ds(0, 1)], rows_land.at[1], down_device),
        (values_ref.at[:, pl.ds(cols - 1, 1)], cols_land.at[0], east_device),
        (values_ref.at[:, pl.ds(0, 1)], cols_land.at[1], west_device),
    ]
    copies = []
    for slot, (source, target, device) in enumerate(plan):
        copy = pltpu.make_async_remote_copy(
            src_ref=source,
            dst_ref=target,
            send_sem=send_sems.at[slot],
            recv_sem=recv_sems.at[slot],
            device_id=device,
            device_id_type=MESH_IDS,
        )
        copy.start()
        copies.append(copy)
    for copy in copies:
        copy.wait_send()
    for copy in copies:
        copy.wait_recv()
    rows_out[...] = rows_land[...]
    cols_out[...] = cols_land[...]


def halo_edges(values, shape, collective):
    rows, cols, levels = values.shape
    return pl.pallas_call(
        functools.partial(halo_kernel, tuple(shape)),
        out_shape=(
            jax.ShapeDtypeStruct((2, 1, cols, levels), values.dtype),
            jax.ShapeDtypeStruct((2, rows, 1, levels), values.dtype),
        ),
        in_specs=[pl.BlockSpec(memory_space=pl.ANY)],
        out_specs=(
            pl.BlockSpec(memory_space=pltpu.VMEM),
            pl.BlockSpec(memory_space=pltpu.VMEM),
        ),
        scratch_shapes=[
            pltpu.VMEM((2, 1, cols, levels), values.dtype),
            pltpu.VMEM((2, rows, 1, levels), values.dtype),
            pltpu.SemaphoreType.DMA((4,)),
            pltpu.SemaphoreType.DMA((4,)),
        ],
        compiler_params=pltpu.CompilerParams(collective_id=collective, has_side_effects=True),
    )(values)


def local(
    state, land_mask, intersection_list, mix_atm, mix_ocn, flux_map, ocean_map, regrid_weights
):
    tile_rows, block_len, levels = state.shape
    flux_count = flux_map.shape[1]
    weight_count = regrid_weights.shape[0]
    intersections = intersection_list.shape[2]
    comp_count = lax.axis_size("comp")
    lat_count = lax.axis_size("lat")
    lon_count = lax.axis_size("lon")
    tile_count = lat_count * lon_count
    reach = min(4, lon_count)
    neighbour_count = 2 * reach
    capacity = intersections * tile_rows // neighbour_count
    width = flux_count * block_len
    comp_index = lax.axis_index("comp")
    tile_index = lax.axis_index("lat") * lon_count + lax.axis_index("lon")
    band = comp_index * lat_count + lax.axis_index("lat")
    ocean_band = (comp_count - 1) * lat_count
    ocean_side = comp_index == comp_count - 1
    lower_valid = (band > 0) & ((band - 1 >= ocean_band) == (band >= ocean_band))
    upper_valid = (band < comp_count * lat_count - 1) & (
        (band + 1 >= ocean_band) == (band >= ocean_band)
    )
    sea_cells = land_mask == 1

    mesh_shape = (comp_count, lat_count, lon_count)

    def halos(values, collective):
        rows, cols = halo_edges(values, mesh_shape, collective)
        top = jnp.where(lower_valid, rows[0], 0.0)
        bottom = jnp.where(upper_valid, rows[1], 0.0)
        return top, bottom, cols[0], cols[1]

    top, bottom, west, east = halos(state, 2)
    mixing = jnp.where(ocean_side, mix_ocn, mix_atm)
    first, first_planes = substep(state, top, bottom, west, east, mixing, comp_count)
    first_top = first_planes[0].reshape(tile_rows, block_len)
    state_top = first_planes[1].reshape(tile_rows, block_len)
    top, bottom, west, east = halos(first, 3)

    def atmosphere_second(values, top, bottom, west, east):
        moved, total = substep(values, top, bottom, west, east, mix_atm, comp_count, flux_map.T)
        total = total.reshape(flux_count, tile_rows, block_len)
        sent = jnp.where(sea_cells[None], 0.5 * total, 0.0).astype(jnp.bfloat16)
        return moved, sent

    def ocean_second(values, top, bottom, west, east):
        return values, jnp.zeros((flux_count, tile_rows, block_len), jnp.bfloat16)

    second, flux_sent = lax.cond(
        ocean_side, ocean_second, atmosphere_second, first, top, bottom, west, east
    )
    entry_list = intersection_list.reshape(tile_rows * intersections, 3)
    owners = entry_list[:, 0]
    targets = entry_list[:, 1]
    weight_ids = entry_list[:, 2]
    labels = weight_ids * tile_rows + targets
    entry_blocks = jnp.repeat(flux_sent.transpose(1, 0, 2), intersections, axis=0).reshape(
        tile_rows * intersections, width
    )
    lane = jnp.arange(128, dtype=jnp.int32)[None, :]
    label_lanes = jnp.where(
        lane == 0, weight_ids[:, None], jnp.where(lane == 1, targets[:, None], 0)
    ).astype(jnp.bfloat16)
    entry_blocks = jnp.concatenate([entry_blocks, label_lanes], axis=1)
    sending = jnp.broadcast_to(jnp.logical_not(ocean_side), owners.shape)
    offsets = [
        (n // reach * lon_count + n % reach - (reach - 1) // 2) % tile_count
        for n in range(neighbour_count)
    ]
    offset_table = jnp.array(offsets, jnp.int32)
    distance = (owners - tile_index + tile_count) % tile_count
    neighbour_ids = jnp.sum(
        jnp.where(
            distance[:, None] == offset_table[None, :],
            jnp.arange(neighbour_count, dtype=jnp.int32)[None, :],
            0,
        ),
        axis=1,
    )
    packed, _, entry_slots = pack_rows(entry_blocks, neighbour_ids, labels, sending, capacity, neighbour_count)
    arrived = gather_to_ocean(packed, offsets, mesh_shape)
    weights_low = regrid_weights
    weights_wide = regrid_weights.astype(jnp.float32)
    senders = (comp_count - 1) * neighbour_count

    def ocean_reply(values_top, arrived):
        flat = arrived.reshape(-1, width + 128)
        arrived_labels = flat[:, width].astype(jnp.int32) * tile_rows + flat[:, width + 1].astype(
            jnp.int32
        )
        fluxes = flat[:, :width].astype(jnp.float32).reshape(-1, flux_count, block_len)
        forcing = scatter_regrid(arrived_labels, fluxes, weights_low)
        forcing = forcing.reshape(tile_rows, flux_count, block_len).transpose(1, 0, 2)
        lifted = jnp.sum(forcing * ocean_map[:, 0][:, None, None], axis=0)
        top_level = jnp.where(sea_cells, values_top + lifted, state_top)
        table = jnp.einsum("db,wab->wda", top_level, weights_wide, precision=HIGHEST)
        replies = jnp.take(table.reshape(weight_count * tile_rows, block_len), arrived_labels, axis=0)
        return forcing, replies.reshape(senders, capacity, block_len), top_level

    def atmosphere_reply(values_top, arrived):
        return (
            jnp.zeros((flux_count, tile_rows, block_len), jnp.float32),
            jnp.zeros((senders, capacity, block_len), jnp.float32),
            values_top,
        )

    forcing, replies, ocean_top = lax.cond(
        ocean_side, ocean_reply, atmosphere_reply, first_top, arrived
    )
    answers = spread_from_ocean(replies, offsets, mesh_shape)
    per_entry = jnp.take(
        answers.reshape(neighbour_count * capacity, block_len), entry_slots, axis=0
    )
    returned = per_entry.reshape(tile_rows, intersections, block_len).sum(axis=1)
    second, forcing, answers = lax.optimization_barrier((second, forcing, answers))
    sea_rows = jnp.broadcast_to(
        sea_cells.astype(jnp.int32).reshape(1, tile_rows * block_len), (8, tile_rows * block_len)
    )
    final_state = ocean_update(
        second,
        state,
        sea_rows,
        forcing.reshape(flux_count, tile_rows * block_len),
        ocean_map,
        comp_count,
    )
    top_plane = lax.cond(
        ocean_side, lambda values: ocean_top, lambda values: values[:, :, 0], final_state
    )
    surface_out = jnp.where(ocean_side, ocean_top, jnp.where(sea_cells, returned, top_plane))
    return (final_state, surface_out)


def solution(mesh):
    placed = (
        P(("comp", "lat"), "lon", None),
        P(("comp", "lat"), "lon"),
        P(("comp", "lat"), "lon", None, None),
        P(),
        P(),
        P(),
        P(),
        P(),
    )
    return jax.shard_map(
        local,
        mesh=mesh,
        in_specs=placed,
        out_specs=(P(("comp", "lat"), "lon", None), P(("comp", "lat"), "lon")),
        check_vma=False,
    )
```

```python
import jax
import jax.numpy as jnp
from jax import lax
from jax.experimental import pallas as pl
from jax.experimental.pallas import tpu as pltpu
from jax.sharding import PartitionSpec as P
import functools

SMOOTHING = 0.2
PHYSICS = 0.5
HIGHEST = lax.Precision.HIGHEST
ROW_BLOCK = 8


def split_bf16(values):
    high = values.astype(jnp.bfloat16)
    low = (values - high.astype(jnp.float32)).astype(jnp.bfloat16)
    return high, low


def three_pass(lhs, rhs, dims):
    lhs_hi, lhs_lo = split_bf16(lhs)
    rhs_hi, rhs_lo = split_bf16(rhs)

    def one(a, b):
        return lax.dot_general(a, b, (dims, ((), ())), preferred_element_type=jnp.float32)

    return one(lhs_hi, rhs_hi) + (one(lhs_hi, rhs_lo) + one(lhs_lo, rhs_hi))


def exact_rows(picker, values):
    high = values.astype(jnp.bfloat16)
    rest = values - high.astype(jnp.float32)
    middle = rest.astype(jnp.bfloat16)
    low = (rest - middle.astype(jnp.float32)).astype(jnp.bfloat16)

    def one(piece):
        return lax.dot_general(
            picker, piece, (((1,), (1,)), ((), ())), preferred_element_type=jnp.float32
        )

    return one(high) + one(middle) + one(low)


def substep_kernel(with_flux, comp_total, x_ref, top_ref, bottom_ref, west_ref, east_ref, mix_ref, *rest):
    if with_flux:
        fluxes_ref, out_ref, flux_out_ref = rest
    else:
        out_ref, planes_ref = rest
    rows, cols, levels = x_ref.shape
    centre = x_ref[...]
    up = jnp.concatenate([top_ref[...], centre[:-1]], axis=0)
    down = jnp.concatenate([centre[1:], bottom_ref[...]], axis=0)
    column = lax.broadcasted_iota(jnp.int32, centre.shape, 1)
    west = jnp.where(column == 0, west_ref[...], pltpu.roll(centre, 1, 1))
    east = jnp.where(column == cols - 1, east_ref[...], pltpu.roll(centre, cols - 1, 1))
    smooth = centre + SMOOTHING * (up + down + west + east - 4.0 * centre)
    flat = smooth.reshape(rows * cols, levels)
    mixed = three_pass(flat, mix_ref[...], ((1,), (0,)))
    moved = flat + PHYSICS * jnp.tanh(mixed)
    out_ref[...] = moved.reshape(rows, cols, levels)
    if not with_flux:
        ocean = lax.axis_index("comp") == comp_total - 1

        @pl.when(ocean)
        def _():
            plane_row = lax.broadcasted_iota(jnp.int32, (8, levels), 0)
            plane_lane = lax.broadcasted_iota(jnp.int32, (8, levels), 1)
            pick_out = ((plane_row == 0) & (plane_lane == 0)).astype(jnp.bfloat16)
            pick_in = ((plane_row == 1) & (plane_lane == 0)).astype(jnp.bfloat16)
            planes_ref[...] = exact_rows(pick_out, moved) + exact_rows(
                pick_in, centre.reshape(rows * cols, levels)
            )

        @pl.when(jnp.logical_not(ocean))
        def _():
            planes_ref[...] = jnp.zeros_like(planes_ref)

    else:
        total = centre.reshape(rows * cols, levels) + moved
        flux_out_ref[...] = three_pass(fluxes_ref[...], total, ((1,), (1,)))


def substep(values, top, bottom, west, east, mixing, comp_total, fluxes_t=None):
    rows, cols, levels = values.shape
    blocks = rows // ROW_BLOCK
    top_rows = jnp.concatenate([top, values[ROW_BLOCK - 1 : rows - 1 : ROW_BLOCK]], axis=0)
    bottom_rows = jnp.concatenate([values[ROW_BLOCK:rows:ROW_BLOCK], bottom], axis=0)
    with_flux = fluxes_t is not None
    in_specs = [
        pl.BlockSpec((ROW_BLOCK, cols, levels), lambda i: (i, 0, 0)),
        pl.BlockSpec((1, cols, levels), lambda i: (i, 0, 0)),
        pl.BlockSpec((1, cols, levels), lambda i: (i, 0, 0)),
        pl.BlockSpec((ROW_BLOCK, 1, levels), lambda i: (i, 0, 0)),
        pl.BlockSpec((ROW_BLOCK, 1, levels), lambda i: (i, 0, 0)),
        pl.BlockSpec((levels, levels), lambda i: (0, 0)),
    ]
    operands = [values, top_rows, bottom_rows, west, east, mixing]
    out_shape = [jax.ShapeDtypeStruct(values.shape, jnp.float32)]
    out_specs = [pl.BlockSpec((ROW_BLOCK, cols, levels), lambda i: (i, 0, 0))]
    if not with_flux:
        out_shape.append(jax.ShapeDtypeStruct((8, rows * cols), jnp.float32))
        out_specs.append(pl.BlockSpec((8, ROW_BLOCK * cols), lambda i: (0, i)))
    if with_flux:
        flux_count = fluxes_t.shape[0]
        in_specs.append(pl.BlockSpec((flux_count, levels), lambda i: (0, 0)))
        operands.append(fluxes_t)
        out_shape.append(jax.ShapeDtypeStruct((flux_count, rows * cols), jnp.float32))
        out_specs.append(pl.BlockSpec((flux_count, ROW_BLOCK * cols), lambda i: (0, i)))
    cells = rows * cols
    flops = 6 * cells * levels * levels + (6 * cells * levels * 8 if with_flux else 0)
    result = pl.pallas_call(
        functools.partial(substep_kernel, with_flux, comp_total),
        grid=(blocks,),
        in_specs=in_specs,
        out_specs=out_specs,
        out_shape=out_shape,
        cost_estimate=pl.CostEstimate(
            flops=flops, transcendentals=cells * levels, bytes_accessed=8 * cells * levels
        ),
    )(*operands)
    return result


def column_physics(values, mixing):
    return jnp.tanh(jnp.einsum("rck,kj->rcj", values, mixing, precision=HIGHEST))


def earlier_same(owners, usable):
    positions = jnp.arange(owners.shape[0], dtype=jnp.int32)
    before = (
        (owners[None, :] == owners[:, None])
        & (positions[None, :] < positions[:, None])
        & usable[None, :]
    )
    return jnp.sum(before.astype(jnp.int32), axis=1)


def pack_rows(blocks, owners, labels, usable, slots_each, owner_total):
    ranks = earlier_same(owners, usable)
    target_slot = owners * slots_each + ranks
    slot_ids = jnp.arange(owner_total * slots_each, dtype=jnp.int32)
    placing = (slot_ids[:, None] == target_slot[None, :]) & usable[None, :]
    packed = jnp.dot(
        placing.astype(jnp.bfloat16), blocks, preferred_element_type=jnp.float32
    ).astype(jnp.bfloat16)
    placed_labels = jnp.sum(jnp.where(placing, labels[None, :] + 1, 0), axis=1) - 1
    return (
        packed.reshape(owner_total, slots_each, blocks.shape[1]),
        placed_labels.reshape(owner_total, slots_each),
        target_slot,
    )


MESH_IDS = pl.DeviceIdType.MESH


def tile_device(comp, tile, lon_total):
    return (comp, tile // lon_total, tile % lon_total)


def gather_kernel(offsets, shape, send_ref, out_ref, land, send_sems, recv_sems):
    comp_total, lat_total, lon_total = shape
    comp = lax.axis_index("comp")
    tiles = lat_total * lon_total
    tile = lax.axis_index("lat") * lon_total + lax.axis_index("lon")
    ocean = comp_total - 1
    count = len(offsets)
    barrier = pltpu.get_barrier_semaphore()

    @pl.when(comp != ocean)
    def _():
        for off in offsets:
            target = tile_device(ocean, (tile + off) % tiles, lon_total)
            pl.semaphore_signal(barrier, 1, device_id=target, device_id_type=MESH_IDS)
        pl.semaphore_wait(barrier, count)
        copies = []
        for k, off in enumerate(offsets):
            target = tile_device(ocean, (tile + off) % tiles, lon_total)
            copy = pltpu.make_async_remote_copy(
                src_ref=send_ref.at[k],
                dst_ref=land.at[comp * count + k],
                send_sem=send_sems.at[k],
                recv_sem=recv_sems.at[comp * count + k],
                device_id=target,
                device_id_type=MESH_IDS,
            )
            copy.start()
            copies.append(copy)
        for copy in copies:
            copy.wait_send()
        out_ref[...] = jnp.zeros_like(out_ref)

    @pl.when(comp == ocean)
    def _():
        for source_comp in range(ocean):
            for off in offsets:
                source = tile_device(source_comp, (tile + tiles - off) % tiles, lon_total)
                pl.semaphore_signal(barrier, 1, device_id=source, device_id_type=MESH_IDS)
        pl.semaphore_wait(barrier, count * ocean)
        for source_comp in range(ocean):
            for k, off in enumerate(offsets):
                source = tile_device(source_comp, (tile + tiles - off) % tiles, lon_total)
                slot = source_comp * count + k
                pltpu.make_async_remote_copy(
                    src_ref=send_ref.at[k],
                    dst_ref=land.at[slot],
                    send_sem=send_sems.at[k],
                    recv_sem=recv_sems.at[slot],
                    device_id=source,
                    device_id_type=MESH_IDS,
                ).wait_recv()
        out_ref[...] = land[...]


def gather_to_ocean(blocks, offsets, shape):
    count = len(offsets)
    senders = (shape[0] - 1) * count
    slot_shape = blocks.shape[1:]
    return pl.pallas_call(
        functools.partial(gather_kernel, tuple(offsets), tuple(shape)),
        out_shape=jax.ShapeDtypeStruct((senders,) + slot_shape, blocks.dtype),
        in_specs=[pl.BlockSpec(memory_space=pltpu.VMEM)],
        out_specs=pl.BlockSpec(memory_space=pltpu.VMEM),
        scratch_shapes=[
            pltpu.VMEM((senders,) + slot_shape, blocks.dtype),
            pltpu.SemaphoreType.DMA((count,)),
            pltpu.SemaphoreType.DMA((senders,)),
        ],
        compiler_params=pltpu.CompilerParams(collective_id=0, has_side_effects=True),
    )(blocks)


def spread_kernel(offsets, shape, surface_ref, out_ref, land, send_sems, recv_sems):
    comp_total, lat_total, lon_total = shape
    comp = lax.axis_index("comp")
    tiles = lat_total * lon_total
    tile = lax.axis_index("lat") * lon_total + lax.axis_index("lon")
    ocean = comp_total - 1
    count = len(offsets)
    barrier = pltpu.get_barrier_semaphore()

    @pl.when(comp == ocean)
    def _():
        for target_comp in range(ocean):
            for off in offsets:
                target = tile_device(target_comp, (tile + tiles - off) % tiles, lon_total)
                pl.semaphore_signal(barrier, 1, device_id=target, device_id_type=MESH_IDS)
        pl.semaphore_wait(barrier, count * ocean)
        copies = []
        for target_comp in range(ocean):
            for k, off in enumerate(offsets):
                target = tile_device(target_comp, (tile + tiles - off) % tiles, lon_total)
                copy = pltpu.make_async_remote_copy(
                    src_ref=surface_ref.at[target_comp * count + k],
                    dst_ref=land.at[k],
                    send_sem=send_sems.at[target_comp * count + k],
                    recv_sem=recv_sems.at[k],
                    device_id=target,
                    device_id_type=MESH_IDS,
                )
                copy.start()
                copies.append(copy)
        for copy in copies:
            copy.wait_send()
        out_ref[...] = jnp.zeros_like(out_ref)

    @pl.when(comp != ocean)
    def _():
        for off in offsets:
            source = tile_device(ocean, (tile + off) % tiles, lon_total)
            pl.semaphore_signal(barrier, 1, device_id=source, device_id_type=MESH_IDS)
        pl.semaphore_wait(barrier, count)
        for k, off in enumerate(offsets):
            source = tile_device(ocean, (tile + off) % tiles, lon_total)
            pltpu.make_async_remote_copy(
                src_ref=surface_ref.at[k],
                dst_ref=land.at[k],
                send_sem=send_sems.at[k],
                recv_sem=recv_sems.at[k],
                device_id=source,
                device_id_type=MESH_IDS,
            ).wait_recv()
        out_ref[...] = land[...]


def spread_from_ocean(replies, offsets, shape):
    count = len(offsets)
    senders = (shape[0] - 1) * count
    slot_shape = replies.shape[1:]
    return pl.pallas_call(
        functools.partial(spread_kernel, tuple(offsets), tuple(shape)),
        out_shape=jax.ShapeDtypeStruct((count,) + slot_shape, replies.dtype),
        in_specs=[pl.BlockSpec(memory_space=pltpu.VMEM)],
        out_specs=pl.BlockSpec(memory_space=pltpu.VMEM),
        scratch_shapes=[
            pltpu.VMEM((count,) + slot_shape, replies.dtype),
            pltpu.SemaphoreType.DMA((senders,)),
            pltpu.SemaphoreType.DMA((count,)),
        ],
        compiler_params=pltpu.CompilerParams(collective_id=1, has_side_effects=True),
    )(replies)


def ocean_update_kernel(
    flag_ref, first_ref, moved_ref, state_ref, sea_ref, forcing_ref, spread_ref, out_ref
):
    ocean = flag_ref[0] == 1

    @pl.when(ocean)
    def _():
        ocean_block(first_ref, state_ref, sea_ref, forcing_ref, spread_ref, out_ref)

    @pl.when(jnp.logical_not(ocean))
    def _():
        out_ref[...] = moved_ref[...]


def ocean_block(first_ref, state_ref, sea_ref, forcing_ref, spread_ref, out_ref):
    rows, cols, levels = first_ref.shape
    forcing = forcing_ref[...]
    spread = spread_ref[...]
    forcing_hi = forcing.astype(jnp.bfloat16)
    forcing_lo = (forcing - forcing_hi.astype(jnp.float32)).astype(jnp.bfloat16)
    spread_hi = spread.astype(jnp.bfloat16)
    spread_lo = (spread - spread_hi.astype(jnp.float32)).astype(jnp.bfloat16)

    def one(a, b):
        return lax.dot_general(a, b, (((0,), (0,)), ((), ())), preferred_element_type=jnp.float32)

    added = one(forcing_hi, spread_hi) + (one(forcing_hi, spread_lo) + one(forcing_lo, spread_hi))
    lane_row = lax.broadcasted_iota(jnp.int32, (8, levels), 0)
    ones = (lane_row == 0).astype(jnp.bfloat16)
    picks = jnp.where(lax.broadcasted_iota(jnp.int32, sea_ref.shape, 0) == 0, sea_ref[...], 0)
    mask = one(picks.astype(jnp.bfloat16), ones)
    moved = first_ref[...].reshape(rows * cols, levels) + added
    kept = jnp.where(mask > 0.5, moved, state_ref[...].reshape(rows * cols, levels))
    out_ref[...] = kept.reshape(rows, cols, levels)


def ocean_update(first, moved, state, sea_rows, forcing, ocean_map, comp_total):
    rows, cols, levels = first.shape
    flux_count = forcing.shape[0]
    cells = rows * cols
    flag = (lax.axis_index("comp") == comp_total - 1).astype(jnp.int32).reshape(1)
    return pl.pallas_call(
        ocean_update_kernel,
        grid_spec=pltpu.PrefetchScalarGridSpec(
            num_scalar_prefetch=1,
            grid=(rows // ROW_BLOCK,),
            in_specs=[
                pl.BlockSpec((ROW_BLOCK, cols, levels), lambda i, f: (i * f[0], 0, 0)),
                pl.BlockSpec((ROW_BLOCK, cols, levels), lambda i, f: (i * (1 - f[0]), 0, 0)),
                pl.BlockSpec((ROW_BLOCK, cols, levels), lambda i, f: (i * f[0], 0, 0)),
                pl.BlockSpec((8, ROW_BLOCK * cols), lambda i, f: (0, i * f[0])),
                pl.BlockSpec((flux_count, ROW_BLOCK * cols), lambda i, f: (0, i * f[0])),
                pl.BlockSpec((flux_count, levels), lambda i, f: (0, 0)),
            ],
            out_specs=pl.BlockSpec((ROW_BLOCK, cols, levels), lambda i, f: (i, 0, 0)),
        ),
        out_shape=jax.ShapeDtypeStruct(first.shape, jnp.float32),
        cost_estimate=pl.CostEstimate(
            flops=8 * cells * levels * flux_count, transcendentals=0, bytes_accessed=12 * cells * levels
        ),
    )(flag, first, moved, state, sea_rows, forcing, ocean_map)


def scatter_regrid_kernel(labels_ref, fluxes_ref, weights_ref, out_ref, binned_ref):
    entries = fluxes_ref.shape[0]
    weight_count, tile_rows, block_len = weights_ref.shape
    flux_count = fluxes_ref.shape[1]
    binned_ref[...] = jnp.zeros_like(binned_ref)

    def add_one(e, carry):
        label = labels_ref[e]
        binned_ref[label] = binned_ref[label] + fluxes_ref[e]
        return carry

    lax.fori_loop(0, entries, add_one, 0, unroll=8)
    out_ref[...] = jnp.zeros_like(out_ref)

    def regrid_one(w, carry):
        start = pl.multiple_of(w * tile_rows, tile_rows)
        block = binned_ref[pl.ds(start, tile_rows)].reshape(tile_rows * flux_count, block_len)
        high = block.astype(jnp.bfloat16)
        low = (block - high.astype(jnp.float32)).astype(jnp.bfloat16)
        weight = weights_ref[w]
        out_ref[...] += jnp.dot(high, weight, preferred_element_type=jnp.float32) + jnp.dot(
            low, weight, preferred_element_type=jnp.float32
        )
        return carry

    lax.fori_loop(0, weight_count, regrid_one, 0)


def scatter_regrid(labels, fluxes, weights):
    entries, flux_count, block_len = fluxes.shape
    weight_count, tile_rows, _ = weights.shape
    return pl.pallas_call(
        scatter_regrid_kernel,
        out_shape=jax.ShapeDtypeStruct((tile_rows * flux_count, block_len), jnp.float32),
        in_specs=[
            pl.BlockSpec(memory_space=pltpu.SMEM),
            pl.BlockSpec(memory_space=pltpu.VMEM),
            pl.BlockSpec(memory_space=pltpu.VMEM),
        ],
        out_specs=pl.BlockSpec(memory_space=pltpu.VMEM),
        scratch_shapes=[pltpu.VMEM((weight_count * tile_rows, flux_count, block_len), jnp.float32)],
        compiler_params=pltpu.CompilerParams(vmem_limit_bytes=48 * 1024 * 1024),
        cost_estimate=pl.CostEstimate(
            flops=4 * weight_count * tile_rows * flux_count * block_len * block_len,
            transcendentals=0,
            bytes_accessed=entries * flux_count * block_len * 4 + weight_count * tile_rows * block_len * 2,
        ),
    )(labels, fluxes, weights)


def halo_kernel(shape, values_ref, rows_out, cols_out, rows_land, cols_land, send_sems, recv_sems):
    comp_total, lat_total, lon_total = shape
    bands = comp_total * lat_total
    band = lax.axis_index("comp") * lat_total + lax.axis_index("lat")
    lon = lax.axis_index("lon")
    rows, cols, _ = values_ref.shape
    up = (band + 1) % bands
    down = (band + bands - 1) % bands
    up_device = (up // lat_total, up % lat_total, lon)
    down_device = (down // lat_total, down % lat_total, lon)
    east_device = (band // lat_total, band % lat_total, (lon + 1) % lon_total)
    west_device = (band // lat_total, band % lat_total, (lon + lon_total - 1) % lon_total)
    barrier = pltpu.get_barrier_semaphore()
    for device in (up_device, down_device, east_device, west_device):
        pl.semaphore_signal(barrier, 1, device_id=device, device_id_type=MESH_IDS)
    pl.semaphore_wait(barrier, 4)
    plan = [
        (values_ref.at[pl.ds(rows - 1, 1)], rows_land.at[0], up_device),
        (values_ref.at[pl.ds(0, 1)], rows_land.at[1], down_device),
        (values_ref.at[:, pl.ds(cols - 1, 1)], cols_land.at[0], east_device),
        (values_ref.at[:, pl.ds(0, 1)], cols_land.at[1], west_device),
    ]
    copies = []
    for slot, (source, target, device) in enumerate(plan):
        copy = pltpu.make_async_remote_copy(
            src_ref=source,
            dst_ref=target,
            send_sem=send_sems.at[slot],
            recv_sem=recv_sems.at[slot],
            device_id=device,
            device_id_type=MESH_IDS,
        )
        copy.start()
        copies.append(copy)
    for copy in copies:
        copy.wait_send()
    for copy in copies:
        copy.wait_recv()
    rows_out[...] = rows_land[...]
    cols_out[...] = cols_land[...]


def halo_edges(values, shape, collective):
    rows, cols, levels = values.shape
    return pl.pallas_call(
        functools.partial(halo_kernel, tuple(shape)),
        out_shape=(
            jax.ShapeDtypeStruct((2, 1, cols, levels), values.dtype),
            jax.ShapeDtypeStruct((2, rows, 1, levels), values.dtype),
        ),
        in_specs=[pl.BlockSpec(memory_space=pl.ANY)],
        out_specs=(
            pl.BlockSpec(memory_space=pltpu.VMEM),
            pl.BlockSpec(memory_space=pltpu.VMEM),
        ),
        scratch_shapes=[
            pltpu.VMEM((2, 1, cols, levels), values.dtype),
            pltpu.VMEM((2, rows, 1, levels), values.dtype),
            pltpu.SemaphoreType.DMA((4,)),
            pltpu.SemaphoreType.DMA((4,)),
        ],
        compiler_params=pltpu.CompilerParams(collective_id=collective, has_side_effects=True),
    )(values)


def local(
    state, land_mask, intersection_list, mix_atm, mix_ocn, flux_map, ocean_map, regrid_weights
):
    tile_rows, block_len, levels = state.shape
    flux_count = flux_map.shape[1]
    weight_count = regrid_weights.shape[0]
    intersections = intersection_list.shape[2]
    comp_count = lax.axis_size("comp")
    lat_count = lax.axis_size("lat")
    lon_count = lax.axis_size("lon")
    tile_count = lat_count * lon_count
    reach = min(4, lon_count)
    neighbour_count = 2 * reach
    capacity = intersections * tile_rows // neighbour_count
    width = flux_count * block_len
    comp_index = lax.axis_index("comp")
    tile_index = lax.axis_index("lat") * lon_count + lax.axis_index("lon")
    band = comp_index * lat_count + lax.axis_index("lat")
    ocean_band = (comp_count - 1) * lat_count
    ocean_side = comp_index == comp_count - 1
    lower_valid = (band > 0) & ((band - 1 >= ocean_band) == (band >= ocean_band))
    upper_valid = (band < comp_count * lat_count - 1) & (
        (band + 1 >= ocean_band) == (band >= ocean_band)
    )
    sea_cells = land_mask == 1

    mesh_shape = (comp_count, lat_count, lon_count)

    def halos(values, collective):
        rows, cols = halo_edges(values, mesh_shape, collective)
        top = jnp.where(lower_valid, rows[0], 0.0)
        bottom = jnp.where(upper_valid, rows[1], 0.0)
        return top, bottom, cols[0], cols[1]

    top, bottom, west, east = halos(state, 2)
    mixing = jnp.where(ocean_side, mix_ocn, mix_atm)
    first, first_planes = substep(state, top, bottom, west, east, mixing, comp_count)
    first_top = first_planes[0].reshape(tile_rows, block_len)
    state_top = first_planes[1].reshape(tile_rows, block_len)
    top, bottom, west, east = halos(first, 3)

    second, total = substep(first, top, bottom, west, east, mix_atm, comp_count, flux_map.T)
    total = total.reshape(flux_count, tile_rows, block_len)
    flux_sent = jnp.where(sea_cells[None], 0.5 * total, 0.0).astype(jnp.bfloat16)
    entry_list = intersection_list.reshape(tile_rows * intersections, 3)
    owners = entry_list[:, 0]
    targets = entry_list[:, 1]
    weight_ids = entry_list[:, 2]
    labels = weight_ids * tile_rows + targets
    entry_blocks = jnp.repeat(flux_sent.transpose(1, 0, 2), intersections, axis=0).reshape(
        tile_rows * intersections, width
    )
    lane = jnp.arange(128, dtype=jnp.int32)[None, :]
    label_lanes = jnp.where(
        lane == 0, weight_ids[:, None], jnp.where(lane == 1, targets[:, None], 0)
    ).astype(jnp.bfloat16)
    entry_blocks = jnp.concatenate([entry_blocks, label_lanes], axis=1)
    sending = jnp.broadcast_to(jnp.logical_not(ocean_side), owners.shape)
    offsets = [
        (n // reach * lon_count + n % reach - (reach - 1) // 2) % tile_count
        for n in range(neighbour_count)
    ]
    offset_table = jnp.array(offsets, jnp.int32)
    distance = (owners - tile_index + tile_count) % tile_count
    neighbour_ids = jnp.sum(
        jnp.where(
            distance[:, None] == offset_table[None, :],
            jnp.arange(neighbour_count, dtype=jnp.int32)[None, :],
            0,
        ),
        axis=1,
    )
    packed, _, entry_slots = pack_rows(entry_blocks, neighbour_ids, labels, sending, capacity, neighbour_count)
    arrived = gather_to_ocean(packed, offsets, mesh_shape)
    weights_low = regrid_weights
    weights_wide = regrid_weights.astype(jnp.float32)
    senders = (comp_count - 1) * neighbour_count

    def ocean_reply(values_top, arrived):
        flat = arrived.reshape(-1, width + 128)
        arrived_labels = flat[:, width].astype(jnp.int32) * tile_rows + flat[:, width + 1].astype(
            jnp.int32
        )
        fluxes = flat[:, :width].astype(jnp.float32).reshape(-1, flux_count, block_len)
        forcing = scatter_regrid(arrived_labels, fluxes, weights_low)
        forcing = forcing.reshape(tile_rows, flux_count, block_len).transpose(1, 0, 2)
        lifted = jnp.sum(forcing * ocean_map[:, 0][:, None, None], axis=0)
        top_level = jnp.where(sea_cells, values_top + lifted, state_top)
        table = jnp.einsum("db,wab->wda", top_level, weights_wide, precision=HIGHEST)
        replies = jnp.take(table.reshape(weight_count * tile_rows, block_len), arrived_labels, axis=0)
        return forcing, replies.reshape(senders, capacity, block_len), top_level

    def atmosphere_reply(values_top, arrived):
        return (
            jnp.zeros((flux_count, tile_rows, block_len), jnp.float32),
            jnp.zeros((senders, capacity, block_len), jnp.float32),
            values_top,
        )

    forcing, replies, ocean_top = lax.cond(
        ocean_side, ocean_reply, atmosphere_reply, first_top, arrived
    )
    answers = spread_from_ocean(replies, offsets, mesh_shape)
    per_entry = jnp.take(
        answers.reshape(neighbour_count * capacity, block_len), entry_slots, axis=0
    )
    returned = per_entry.reshape(tile_rows, intersections, block_len).sum(axis=1)
    first, second, forcing, answers = lax.optimization_barrier((first, second, forcing, answers))
    sea_rows = jnp.broadcast_to(
        sea_cells.astype(jnp.int32).reshape(1, tile_rows * block_len), (8, tile_rows * block_len)
    )
    final_state = ocean_update(
        first,
        second,
        state,
        sea_rows,
        forcing.reshape(flux_count, tile_rows * block_len),
        ocean_map,
        comp_count,
    )
    top_plane = lax.cond(
        ocean_side, lambda values: ocean_top, lambda values: values[:, :, 0], final_state
    )
    surface_out = jnp.where(ocean_side, ocean_top, jnp.where(sea_cells, returned, top_plane))
    return (final_state, surface_out)


def solution(mesh):
    placed = (
        P(("comp", "lat"), "lon", None),
        P(("comp", "lat"), "lon"),
        P(("comp", "lat"), "lon", None, None),
        P(),
        P(),
        P(),
        P(),
        P(),
    )
    return jax.shard_map(
        local,
        mesh=mesh,
        in_specs=placed,
        out_specs=(P(("comp", "lat"), "lon", None), P(("comp", "lat"), "lon")),
        check_vma=False,
    )
```

```python
import jax
import jax.numpy as jnp
from jax import lax
from jax.experimental import pallas as pl
from jax.experimental.pallas import tpu as pltpu
from jax.sharding import PartitionSpec as P
import functools

SMOOTHING = 0.2
PHYSICS = 0.5
HIGHEST = lax.Precision.HIGHEST
ROW_BLOCK = 8


def split_bf16(values):
    high = values.astype(jnp.bfloat16)
    low = (values - high.astype(jnp.float32)).astype(jnp.bfloat16)
    return high, low


def three_pass(lhs, rhs, dims):
    lhs_hi, lhs_lo = split_bf16(lhs)
    rhs_hi, rhs_lo = split_bf16(rhs)

    def one(a, b):
        return lax.dot_general(a, b, (dims, ((), ())), preferred_element_type=jnp.float32)

    return one(lhs_hi, rhs_hi) + (one(lhs_hi, rhs_lo) + one(lhs_lo, rhs_hi))


def exact_rows(picker, values):
    high = values.astype(jnp.bfloat16)
    rest = values - high.astype(jnp.float32)
    middle = rest.astype(jnp.bfloat16)
    low = (rest - middle.astype(jnp.float32)).astype(jnp.bfloat16)

    def one(piece):
        return lax.dot_general(
            picker, piece, (((1,), (1,)), ((), ())), preferred_element_type=jnp.float32
        )

    return one(high) + one(middle) + one(low)


def substep_kernel(with_flux, comp_total, x_ref, top_ref, bottom_ref, west_ref, east_ref, mix_ref, *rest):
    if with_flux:
        fluxes_ref, out_ref, flux_out_ref = rest
    else:
        out_ref, planes_ref = rest
    rows, cols, levels = x_ref.shape
    centre = x_ref[...]
    up = jnp.concatenate([top_ref[...], centre[:-1]], axis=0)
    down = jnp.concatenate([centre[1:], bottom_ref[...]], axis=0)
    column = lax.broadcasted_iota(jnp.int32, centre.shape, 1)
    west = jnp.where(column == 0, west_ref[...], pltpu.roll(centre, 1, 1))
    east = jnp.where(column == cols - 1, east_ref[...], pltpu.roll(centre, cols - 1, 1))
    smooth = centre + SMOOTHING * (up + down + west + east - 4.0 * centre)
    flat = smooth.reshape(rows * cols, levels)
    mixed = three_pass(flat, mix_ref[...], ((1,), (0,)))
    moved = flat + PHYSICS * jnp.tanh(mixed)
    out_ref[...] = moved.reshape(rows, cols, levels)
    if not with_flux:
        ocean = lax.axis_index("comp") == comp_total - 1

        @pl.when(ocean)
        def _():
            plane_row = lax.broadcasted_iota(jnp.int32, (8, levels), 0)
            plane_lane = lax.broadcasted_iota(jnp.int32, (8, levels), 1)
            pick_out = ((plane_row == 0) & (plane_lane == 0)).astype(jnp.bfloat16)
            pick_in = ((plane_row == 1) & (plane_lane == 0)).astype(jnp.bfloat16)
            planes_ref[...] = exact_rows(pick_out, moved) + exact_rows(
                pick_in, centre.reshape(rows * cols, levels)
            )

        @pl.when(jnp.logical_not(ocean))
        def _():
            planes_ref[...] = jnp.zeros_like(planes_ref)

    else:
        total = centre.reshape(rows * cols, levels) + moved
        flux_out_ref[...] = three_pass(fluxes_ref[...], total, ((1,), (1,)))


def substep(values, top, bottom, west, east, mixing, comp_total, fluxes_t=None):
    rows, cols, levels = values.shape
    blocks = rows // ROW_BLOCK
    top_rows = jnp.concatenate([top, values[ROW_BLOCK - 1 : rows - 1 : ROW_BLOCK]], axis=0)
    bottom_rows = jnp.concatenate([values[ROW_BLOCK:rows:ROW_BLOCK], bottom], axis=0)
    with_flux = fluxes_t is not None
    in_specs = [
        pl.BlockSpec((ROW_BLOCK, cols, levels), lambda i: (i, 0, 0)),
        pl.BlockSpec((1, cols, levels), lambda i: (i, 0, 0)),
        pl.BlockSpec((1, cols, levels), lambda i: (i, 0, 0)),
        pl.BlockSpec((ROW_BLOCK, 1, levels), lambda i: (i, 0, 0)),
        pl.BlockSpec((ROW_BLOCK, 1, levels), lambda i: (i, 0, 0)),
        pl.BlockSpec((levels, levels), lambda i: (0, 0)),
    ]
    operands = [values, top_rows, bottom_rows, west, east, mixing]
    out_shape = [jax.ShapeDtypeStruct(values.shape, jnp.float32)]
    out_specs = [pl.BlockSpec((ROW_BLOCK, cols, levels), lambda i: (i, 0, 0))]
    if not with_flux:
        out_shape.append(jax.ShapeDtypeStruct((8, rows * cols), jnp.float32))
        out_specs.append(pl.BlockSpec((8, ROW_BLOCK * cols), lambda i: (0, i)))
    if with_flux:
        flux_count = fluxes_t.shape[0]
        in_specs.append(pl.BlockSpec((flux_count, levels), lambda i: (0, 0)))
        operands.append(fluxes_t)
        out_shape.append(jax.ShapeDtypeStruct((flux_count, rows * cols), jnp.float32))
        out_specs.append(pl.BlockSpec((flux_count, ROW_BLOCK * cols), lambda i: (0, i)))
    cells = rows * cols
    flops = 6 * cells * levels * levels + (6 * cells * levels * 8 if with_flux else 0)
    result = pl.pallas_call(
        functools.partial(substep_kernel, with_flux, comp_total),
        grid=(blocks,),
        in_specs=in_specs,
        out_specs=out_specs,
        out_shape=out_shape,
        cost_estimate=pl.CostEstimate(
            flops=flops, transcendentals=cells * levels, bytes_accessed=8 * cells * levels
        ),
    )(*operands)
    return result


def column_physics(values, mixing):
    return jnp.tanh(jnp.einsum("rck,kj->rcj", values, mixing, precision=HIGHEST))


def earlier_same(owners, usable):
    positions = jnp.arange(owners.shape[0], dtype=jnp.int32)
    before = (
        (owners[None, :] == owners[:, None])
        & (positions[None, :] < positions[:, None])
        & usable[None, :]
    )
    return jnp.sum(before.astype(jnp.int32), axis=1)


def pack_rows(blocks, owners, labels, usable, slots_each, owner_total):
    ranks = earlier_same(owners, usable)
    target_slot = owners * slots_each + ranks
    slot_ids = jnp.arange(owner_total * slots_each, dtype=jnp.int32)
    placing = (slot_ids[:, None] == target_slot[None, :]) & usable[None, :]
    packed = jnp.dot(
        placing.astype(jnp.bfloat16), blocks, preferred_element_type=jnp.float32
    ).astype(jnp.bfloat16)
    placed_labels = jnp.sum(jnp.where(placing, labels[None, :] + 1, 0), axis=1) - 1
    return (
        packed.reshape(owner_total, slots_each, blocks.shape[1]),
        placed_labels.reshape(owner_total, slots_each),
        target_slot,
    )


MESH_IDS = pl.DeviceIdType.MESH


def tile_device(comp, tile, lon_total):
    return (comp, tile // lon_total, tile % lon_total)


def gather_kernel(offsets, shape, send_ref, out_ref, land, send_sems, recv_sems):
    comp_total, lat_total, lon_total = shape
    comp = lax.axis_index("comp")
    tiles = lat_total * lon_total
    tile = lax.axis_index("lat") * lon_total + lax.axis_index("lon")
    ocean = comp_total - 1
    count = len(offsets)
    barrier = pltpu.get_barrier_semaphore()

    @pl.when(comp != ocean)
    def _():
        for off in offsets:
            target = tile_device(ocean, (tile + off) % tiles, lon_total)
            pl.semaphore_signal(barrier, 1, device_id=target, device_id_type=MESH_IDS)
        pl.semaphore_wait(barrier, count)
        copies = []
        for k, off in enumerate(offsets):
            target = tile_device(ocean, (tile + off) % tiles, lon_total)
            copy = pltpu.make_async_remote_copy(
                src_ref=send_ref.at[k],
                dst_ref=land.at[comp * count + k],
                send_sem=send_sems.at[k],
                recv_sem=recv_sems.at[comp * count + k],
                device_id=target,
                device_id_type=MESH_IDS,
            )
            copy.start()
            copies.append(copy)
        for copy in copies:
            copy.wait_send()
        out_ref[...] = jnp.zeros_like(out_ref)

    @pl.when(comp == ocean)
    def _():
        for source_comp in range(ocean):
            for off in offsets:
                source = tile_device(source_comp, (tile + tiles - off) % tiles, lon_total)
                pl.semaphore_signal(barrier, 1, device_id=source, device_id_type=MESH_IDS)
        pl.semaphore_wait(barrier, count * ocean)
        for source_comp in range(ocean):
            for k, off in enumerate(offsets):
                source = tile_device(source_comp, (tile + tiles - off) % tiles, lon_total)
                slot = source_comp * count + k
                pltpu.make_async_remote_copy(
                    src_ref=send_ref.at[k],
                    dst_ref=land.at[slot],
                    send_sem=send_sems.at[k],
                    recv_sem=recv_sems.at[slot],
                    device_id=source,
                    device_id_type=MESH_IDS,
                ).wait_recv()
        out_ref[...] = land[...]


def gather_to_ocean(blocks, offsets, shape):
    count = len(offsets)
    senders = (shape[0] - 1) * count
    slot_shape = blocks.shape[1:]
    return pl.pallas_call(
        functools.partial(gather_kernel, tuple(offsets), tuple(shape)),
        out_shape=jax.ShapeDtypeStruct((senders,) + slot_shape, blocks.dtype),
        in_specs=[pl.BlockSpec(memory_space=pltpu.VMEM)],
        out_specs=pl.BlockSpec(memory_space=pltpu.VMEM),
        scratch_shapes=[
            pltpu.VMEM((senders,) + slot_shape, blocks.dtype),
            pltpu.SemaphoreType.DMA((count,)),
            pltpu.SemaphoreType.DMA((senders,)),
        ],
        compiler_params=pltpu.CompilerParams(collective_id=0, has_side_effects=True),
    )(blocks)


def spread_kernel(offsets, shape, surface_ref, out_ref, land, send_sems, recv_sems):
    comp_total, lat_total, lon_total = shape
    comp = lax.axis_index("comp")
    tiles = lat_total * lon_total
    tile = lax.axis_index("lat") * lon_total + lax.axis_index("lon")
    ocean = comp_total - 1
    count = len(offsets)
    barrier = pltpu.get_barrier_semaphore()

    @pl.when(comp == ocean)
    def _():
        for target_comp in range(ocean):
            for off in offsets:
                target = tile_device(target_comp, (tile + tiles - off) % tiles, lon_total)
                pl.semaphore_signal(barrier, 1, device_id=target, device_id_type=MESH_IDS)
        pl.semaphore_wait(barrier, count * ocean)
        copies = []
        for target_comp in range(ocean):
            for k, off in enumerate(offsets):
                target = tile_device(target_comp, (tile + tiles - off) % tiles, lon_total)
                copy = pltpu.make_async_remote_copy(
                    src_ref=surface_ref.at[target_comp * count + k],
                    dst_ref=land.at[k],
                    send_sem=send_sems.at[target_comp * count + k],
                    recv_sem=recv_sems.at[k],
                    device_id=target,
                    device_id_type=MESH_IDS,
                )
                copy.start()
                copies.append(copy)
        for copy in copies:
            copy.wait_send()
        out_ref[...] = jnp.zeros_like(out_ref)

    @pl.when(comp != ocean)
    def _():
        for off in offsets:
            source = tile_device(ocean, (tile + off) % tiles, lon_total)
            pl.semaphore_signal(barrier, 1, device_id=source, device_id_type=MESH_IDS)
        pl.semaphore_wait(barrier, count)
        for k, off in enumerate(offsets):
            source = tile_device(ocean, (tile + off) % tiles, lon_total)
            pltpu.make_async_remote_copy(
                src_ref=surface_ref.at[k],
                dst_ref=land.at[k],
                send_sem=send_sems.at[k],
                recv_sem=recv_sems.at[k],
                device_id=source,
                device_id_type=MESH_IDS,
            ).wait_recv()
        out_ref[...] = land[...]


def spread_from_ocean(replies, offsets, shape):
    count = len(offsets)
    senders = (shape[0] - 1) * count
    slot_shape = replies.shape[1:]
    return pl.pallas_call(
        functools.partial(spread_kernel, tuple(offsets), tuple(shape)),
        out_shape=jax.ShapeDtypeStruct((count,) + slot_shape, replies.dtype),
        in_specs=[pl.BlockSpec(memory_space=pltpu.VMEM)],
        out_specs=pl.BlockSpec(memory_space=pltpu.VMEM),
        scratch_shapes=[
            pltpu.VMEM((count,) + slot_shape, replies.dtype),
            pltpu.SemaphoreType.DMA((senders,)),
            pltpu.SemaphoreType.DMA((count,)),
        ],
        compiler_params=pltpu.CompilerParams(collective_id=1, has_side_effects=True),
    )(replies)


def ocean_update_kernel(flag_ref, base_ref, state_ref, sea_ref, forcing_ref, spread_ref, out_ref):
    rows, cols, levels = base_ref.shape
    flux_count = forcing_ref.shape[0]

    def block(base_block, state_block, sea_block, forcing_block, out_block):
        ocean_block(base_block, state_block, sea_block, forcing_block, spread_ref, out_block)

    @pl.when(flag_ref[0] == 1)
    def _():
        pltpu.emit_pipeline(
            block,
            grid=(rows // ROW_BLOCK,),
            in_specs=[
                pl.BlockSpec((ROW_BLOCK, cols, levels), lambda i: (i, 0, 0)),
                pl.BlockSpec((ROW_BLOCK, cols, levels), lambda i: (i, 0, 0)),
                pl.BlockSpec((8, ROW_BLOCK * cols), lambda i: (0, i)),
                pl.BlockSpec((flux_count, ROW_BLOCK * cols), lambda i: (0, i)),
            ],
            out_specs=[pl.BlockSpec((ROW_BLOCK, cols, levels), lambda i: (i, 0, 0))],
        )(base_ref, state_ref, sea_ref, forcing_ref, out_ref)


def ocean_block(first_ref, state_ref, sea_ref, forcing_ref, spread_ref, out_ref):
    rows, cols, levels = first_ref.shape
    forcing = forcing_ref[...]
    spread = spread_ref[...]
    forcing_hi = forcing.astype(jnp.bfloat16)
    forcing_lo = (forcing - forcing_hi.astype(jnp.float32)).astype(jnp.bfloat16)
    spread_hi = spread.astype(jnp.bfloat16)
    spread_lo = (spread - spread_hi.astype(jnp.float32)).astype(jnp.bfloat16)

    def one(a, b):
        return lax.dot_general(a, b, (((0,), (0,)), ((), ())), preferred_element_type=jnp.float32)

    added = one(forcing_hi, spread_hi) + (one(forcing_hi, spread_lo) + one(forcing_lo, spread_hi))
    lane_row = lax.broadcasted_iota(jnp.int32, (8, levels), 0)
    ones = (lane_row == 0).astype(jnp.bfloat16)
    picks = jnp.where(lax.broadcasted_iota(jnp.int32, sea_ref.shape, 0) == 0, sea_ref[...], 0)
    mask = one(picks.astype(jnp.bfloat16), ones)
    moved = first_ref[...].reshape(rows * cols, levels) + added
    kept = jnp.where(mask > 0.5, moved, state_ref[...].reshape(rows * cols, levels))
    out_ref[...] = kept.reshape(rows, cols, levels)


def ocean_update(first, state, sea_rows, forcing, ocean_map, comp_total):
    rows, cols, levels = first.shape
    flux_count = forcing.shape[0]
    cells = rows * cols
    flag = (lax.axis_index("comp") == comp_total - 1).astype(jnp.int32).reshape(1)
    return pl.pallas_call(
        ocean_update_kernel,
        out_shape=jax.ShapeDtypeStruct(first.shape, jnp.float32),
        in_specs=[
            pl.BlockSpec(memory_space=pltpu.SMEM),
            pl.BlockSpec(memory_space=pl.ANY),
            pl.BlockSpec(memory_space=pl.ANY),
            pl.BlockSpec(memory_space=pl.ANY),
            pl.BlockSpec(memory_space=pl.ANY),
            pl.BlockSpec(memory_space=pltpu.VMEM),
        ],
        out_specs=pl.BlockSpec(memory_space=pl.ANY),
        input_output_aliases={1: 0},
        cost_estimate=pl.CostEstimate(
            flops=8 * cells * levels * flux_count, transcendentals=0, bytes_accessed=12 * cells * levels
        ),
    )(flag, first, state, sea_rows, forcing, ocean_map)


def scatter_regrid_kernel(labels_ref, fluxes_ref, weights_ref, out_ref, binned_ref):
    entries = fluxes_ref.shape[0]
    weight_count, tile_rows, block_len = weights_ref.shape
    flux_count = fluxes_ref.shape[1]
    binned_ref[...] = jnp.zeros_like(binned_ref)

    def add_one(e, carry):
        label = labels_ref[e]
        binned_ref[label] = binned_ref[label] + fluxes_ref[e]
        return carry

    lax.fori_loop(0, entries, add_one, 0, unroll=8)
    out_ref[...] = jnp.zeros_like(out_ref)

    def regrid_one(w, carry):
        start = pl.multiple_of(w * tile_rows, tile_rows)
        block = binned_ref[pl.ds(start, tile_rows)].reshape(tile_rows * flux_count, block_len)
        high = block.astype(jnp.bfloat16)
        low = (block - high.astype(jnp.float32)).astype(jnp.bfloat16)
        weight = weights_ref[w]
        out_ref[...] += jnp.dot(high, weight, preferred_element_type=jnp.float32) + jnp.dot(
            low, weight, preferred_element_type=jnp.float32
        )
        return carry

    lax.fori_loop(0, weight_count, regrid_one, 0)


def scatter_regrid(labels, fluxes, weights):
    entries, flux_count, block_len = fluxes.shape
    weight_count, tile_rows, _ = weights.shape
    return pl.pallas_call(
        scatter_regrid_kernel,
        out_shape=jax.ShapeDtypeStruct((tile_rows * flux_count, block_len), jnp.float32),
        in_specs=[
            pl.BlockSpec(memory_space=pltpu.SMEM),
            pl.BlockSpec(memory_space=pltpu.VMEM),
            pl.BlockSpec(memory_space=pltpu.VMEM),
        ],
        out_specs=pl.BlockSpec(memory_space=pltpu.VMEM),
        scratch_shapes=[pltpu.VMEM((weight_count * tile_rows, flux_count, block_len), jnp.float32)],
        compiler_params=pltpu.CompilerParams(vmem_limit_bytes=48 * 1024 * 1024),
        cost_estimate=pl.CostEstimate(
            flops=4 * weight_count * tile_rows * flux_count * block_len * block_len,
            transcendentals=0,
            bytes_accessed=entries * flux_count * block_len * 4 + weight_count * tile_rows * block_len * 2,
        ),
    )(labels, fluxes, weights)


def halo_kernel(shape, values_ref, rows_out, cols_out, rows_land, cols_land, send_sems, recv_sems):
    comp_total, lat_total, lon_total = shape
    bands = comp_total * lat_total
    band = lax.axis_index("comp") * lat_total + lax.axis_index("lat")
    lon = lax.axis_index("lon")
    rows, cols, _ = values_ref.shape
    up = (band + 1) % bands
    down = (band + bands - 1) % bands
    up_device = (up // lat_total, up % lat_total, lon)
    down_device = (down // lat_total, down % lat_total, lon)
    east_device = (band // lat_total, band % lat_total, (lon + 1) % lon_total)
    west_device = (band // lat_total, band % lat_total, (lon + lon_total - 1) % lon_total)
    barrier = pltpu.get_barrier_semaphore()
    for device in (up_device, down_device, east_device, west_device):
        pl.semaphore_signal(barrier, 1, device_id=device, device_id_type=MESH_IDS)
    pl.semaphore_wait(barrier, 4)
    plan = [
        (values_ref.at[pl.ds(rows - 1, 1)], rows_land.at[0], up_device),
        (values_ref.at[pl.ds(0, 1)], rows_land.at[1], down_device),
        (values_ref.at[:, pl.ds(cols - 1, 1)], cols_land.at[0], east_device),
        (values_ref.at[:, pl.ds(0, 1)], cols_land.at[1], west_device),
    ]
    copies = []
    for slot, (source, target, device) in enumerate(plan):
        copy = pltpu.make_async_remote_copy(
            src_ref=source,
            dst_ref=target,
            send_sem=send_sems.at[slot],
            recv_sem=recv_sems.at[slot],
            device_id=device,
            device_id_type=MESH_IDS,
        )
        copy.start()
        copies.append(copy)
    for copy in copies:
        copy.wait_send()
    for copy in copies:
        copy.wait_recv()
    rows_out[...] = rows_land[...]
    cols_out[...] = cols_land[...]


def halo_edges(values, shape, collective):
    rows, cols, levels = values.shape
    return pl.pallas_call(
        functools.partial(halo_kernel, tuple(shape)),
        out_shape=(
            jax.ShapeDtypeStruct((2, 1, cols, levels), values.dtype),
            jax.ShapeDtypeStruct((2, rows, 1, levels), values.dtype),
        ),
        in_specs=[pl.BlockSpec(memory_space=pl.ANY)],
        out_specs=(
            pl.BlockSpec(memory_space=pltpu.VMEM),
            pl.BlockSpec(memory_space=pltpu.VMEM),
        ),
        scratch_shapes=[
            pltpu.VMEM((2, 1, cols, levels), values.dtype),
            pltpu.VMEM((2, rows, 1, levels), values.dtype),
            pltpu.SemaphoreType.DMA((4,)),
            pltpu.SemaphoreType.DMA((4,)),
        ],
        compiler_params=pltpu.CompilerParams(collective_id=collective, has_side_effects=True),
    )(values)


def local(
    state, land_mask, intersection_list, mix_atm, mix_ocn, flux_map, ocean_map, regrid_weights
):
    tile_rows, block_len, levels = state.shape
    flux_count = flux_map.shape[1]
    weight_count = regrid_weights.shape[0]
    intersections = intersection_list.shape[2]
    comp_count = lax.axis_size("comp")
    lat_count = lax.axis_size("lat")
    lon_count = lax.axis_size("lon")
    tile_count = lat_count * lon_count
    reach = min(4, lon_count)
    neighbour_count = 2 * reach
    capacity = intersections * tile_rows // neighbour_count
    width = flux_count * block_len
    comp_index = lax.axis_index("comp")
    tile_index = lax.axis_index("lat") * lon_count + lax.axis_index("lon")
    band = comp_index * lat_count + lax.axis_index("lat")
    ocean_band = (comp_count - 1) * lat_count
    ocean_side = comp_index == comp_count - 1
    lower_valid = (band > 0) & ((band - 1 >= ocean_band) == (band >= ocean_band))
    upper_valid = (band < comp_count * lat_count - 1) & (
        (band + 1 >= ocean_band) == (band >= ocean_band)
    )
    sea_cells = land_mask == 1

    mesh_shape = (comp_count, lat_count, lon_count)

    def halos(values, collective):
        rows, cols = halo_edges(values, mesh_shape, collective)
        top = jnp.where(lower_valid, rows[0], 0.0)
        bottom = jnp.where(upper_valid, rows[1], 0.0)
        return top, bottom, cols[0], cols[1]

    top, bottom, west, east = halos(state, 2)
    mixing = jnp.where(ocean_side, mix_ocn, mix_atm)
    first, first_planes = substep(state, top, bottom, west, east, mixing, comp_count)
    first_top = first_planes[0].reshape(tile_rows, block_len)
    state_top = first_planes[1].reshape(tile_rows, block_len)
    top, bottom, west, east = halos(first, 3)

    def atmosphere_second(values, top, bottom, west, east):
        moved, total = substep(values, top, bottom, west, east, mix_atm, comp_count, flux_map.T)
        total = total.reshape(flux_count, tile_rows, block_len)
        sent = jnp.where(sea_cells[None], 0.5 * total, 0.0).astype(jnp.bfloat16)
        return moved, sent

    def ocean_second(values, top, bottom, west, east):
        return values, jnp.zeros((flux_count, tile_rows, block_len), jnp.bfloat16)

    second, flux_sent = lax.cond(
        ocean_side, ocean_second, atmosphere_second, first, top, bottom, west, east
    )
    entry_list = intersection_list.reshape(tile_rows * intersections, 3)
    owners = entry_list[:, 0]
    targets = entry_list[:, 1]
    weight_ids = entry_list[:, 2]
    labels = weight_ids * tile_rows + targets
    entry_blocks = jnp.repeat(flux_sent.transpose(1, 0, 2), intersections, axis=0).reshape(
        tile_rows * intersections, width
    )
    lane = jnp.arange(128, dtype=jnp.int32)[None, :]
    label_lanes = jnp.where(
        lane == 0, weight_ids[:, None], jnp.where(lane == 1, targets[:, None], 0)
    ).astype(jnp.bfloat16)
    entry_blocks = jnp.concatenate([entry_blocks, label_lanes], axis=1)
    sending = jnp.broadcast_to(jnp.logical_not(ocean_side), owners.shape)
    offsets = [
        (n // reach * lon_count + n % reach - (reach - 1) // 2) % tile_count
        for n in range(neighbour_count)
    ]
    offset_table = jnp.array(offsets, jnp.int32)
    distance = (owners - tile_index + tile_count) % tile_count
    neighbour_ids = jnp.sum(
        jnp.where(
            distance[:, None] == offset_table[None, :],
            jnp.arange(neighbour_count, dtype=jnp.int32)[None, :],
            0,
        ),
        axis=1,
    )
    packed, _, entry_slots = pack_rows(entry_blocks, neighbour_ids, labels, sending, capacity, neighbour_count)
    arrived = gather_to_ocean(packed, offsets, mesh_shape)
    weights_low = regrid_weights
    weights_wide = regrid_weights.astype(jnp.float32)
    senders = (comp_count - 1) * neighbour_count

    def ocean_reply(values_top, arrived):
        flat = arrived.reshape(-1, width + 128)
        arrived_labels = flat[:, width].astype(jnp.int32) * tile_rows + flat[:, width + 1].astype(
            jnp.int32
        )
        fluxes = flat[:, :width].astype(jnp.float32).reshape(-1, flux_count, block_len)
        forcing = scatter_regrid(arrived_labels, fluxes, weights_low)
        forcing = forcing.reshape(tile_rows, flux_count, block_len).transpose(1, 0, 2)
        lifted = jnp.sum(forcing * ocean_map[:, 0][:, None, None], axis=0)
        top_level = jnp.where(sea_cells, values_top + lifted, state_top)
        table = jnp.einsum("db,wab->wda", top_level, weights_wide, precision=HIGHEST)
        replies = jnp.take(table.reshape(weight_count * tile_rows, block_len), arrived_labels, axis=0)
        return forcing, replies.reshape(senders, capacity, block_len), top_level

    def atmosphere_reply(values_top, arrived):
        return (
            jnp.zeros((flux_count, tile_rows, block_len), jnp.float32),
            jnp.zeros((senders, capacity, block_len), jnp.float32),
            values_top,
        )

    forcing, replies, ocean_top = lax.cond(
        ocean_side, ocean_reply, atmosphere_reply, first_top, arrived
    )
    answers = spread_from_ocean(replies, offsets, mesh_shape)
    per_entry = jnp.take(
        answers.reshape(neighbour_count * capacity, block_len), entry_slots, axis=0
    )
    returned = per_entry.reshape(tile_rows, intersections, block_len).sum(axis=1)
    second, forcing, answers = lax.optimization_barrier((second, forcing, answers))
    sea_rows = jnp.broadcast_to(
        sea_cells.astype(jnp.int32).reshape(1, tile_rows * block_len), (8, tile_rows * block_len)
    )
    final_state = ocean_update(
        second,
        state,
        sea_rows,
        forcing.reshape(flux_count, tile_rows * block_len),
        ocean_map,
        comp_count,
    )
    top_plane = lax.cond(
        ocean_side, lambda values: ocean_top, lambda values: values[:, :, 0], final_state
    )
    surface_out = jnp.where(ocean_side, ocean_top, jnp.where(sea_cells, returned, top_plane))
    return (final_state, surface_out)


def solution(mesh):
    placed = (
        P(("comp", "lat"), "lon", None),
        P(("comp", "lat"), "lon"),
        P(("comp", "lat"), "lon", None, None),
        P(),
        P(),
        P(),
        P(),
        P(),
    )
    return jax.shard_map(
        local,
        mesh=mesh,
        in_specs=placed,
        out_specs=(P(("comp", "lat"), "lon", None), P(("comp", "lat"), "lon")),
        check_vma=False,
    )
```

```python
import jax
import jax.numpy as jnp
from jax import lax
from jax.experimental import pallas as pl
from jax.experimental.pallas import tpu as pltpu
from jax.sharding import PartitionSpec as P
import functools

SMOOTHING = 0.2
PHYSICS = 0.5
HIGHEST = lax.Precision.HIGHEST
ROW_BLOCK = 8


def split_bf16(values):
    high = values.astype(jnp.bfloat16)
    low = (values - high.astype(jnp.float32)).astype(jnp.bfloat16)
    return high, low


def three_pass(lhs, rhs, dims):
    lhs_hi, lhs_lo = split_bf16(lhs)
    rhs_hi, rhs_lo = split_bf16(rhs)

    def one(a, b):
        return lax.dot_general(a, b, (dims, ((), ())), preferred_element_type=jnp.float32)

    return one(lhs_hi, rhs_hi) + (one(lhs_hi, rhs_lo) + one(lhs_lo, rhs_hi))


def exact_rows(picker, values):
    high = values.astype(jnp.bfloat16)
    rest = values - high.astype(jnp.float32)
    middle = rest.astype(jnp.bfloat16)
    low = (rest - middle.astype(jnp.float32)).astype(jnp.bfloat16)

    def one(piece):
        return lax.dot_general(
            picker, piece, (((1,), (1,)), ((), ())), preferred_element_type=jnp.float32
        )

    return one(high) + one(middle) + one(low)


def substep_kernel(with_flux, comp_total, x_ref, top_ref, bottom_ref, west_ref, east_ref, mix_ref, *rest):
    if with_flux:
        fluxes_ref, out_ref, flux_out_ref = rest
    else:
        out_ref, planes_ref = rest
    rows, cols, levels = x_ref.shape
    centre = x_ref[...]
    up = jnp.concatenate([top_ref[...], centre[:-1]], axis=0)
    down = jnp.concatenate([centre[1:], bottom_ref[...]], axis=0)
    column = lax.broadcasted_iota(jnp.int32, centre.shape, 1)
    west = jnp.where(column == 0, west_ref[...], pltpu.roll(centre, 1, 1))
    east = jnp.where(column == cols - 1, east_ref[...], pltpu.roll(centre, cols - 1, 1))
    smooth = centre + SMOOTHING * (up + down + west + east - 4.0 * centre)
    flat = smooth.reshape(rows * cols, levels)
    mixed = three_pass(flat, mix_ref[...], ((1,), (0,)))
    moved = flat + PHYSICS * jnp.tanh(mixed)
    out_ref[...] = moved.reshape(rows, cols, levels)
    if not with_flux:
        ocean = lax.axis_index("comp") == comp_total - 1

        @pl.when(ocean)
        def _():
            plane_row = lax.broadcasted_iota(jnp.int32, (8, levels), 0)
            plane_lane = lax.broadcasted_iota(jnp.int32, (8, levels), 1)
            pick_out = ((plane_row == 0) & (plane_lane == 0)).astype(jnp.bfloat16)
            pick_in = ((plane_row == 1) & (plane_lane == 0)).astype(jnp.bfloat16)
            planes_ref[...] = exact_rows(pick_out, moved) + exact_rows(
                pick_in, centre.reshape(rows * cols, levels)
            )

        @pl.when(jnp.logical_not(ocean))
        def _():
            planes_ref[...] = jnp.zeros_like(planes_ref)

    else:
        total = centre.reshape(rows * cols, levels) + moved
        flux_out_ref[...] = three_pass(fluxes_ref[...], total, ((1,), (1,)))


def substep(values, top, bottom, west, east, mixing, comp_total, fluxes_t=None):
    rows, cols, levels = values.shape
    blocks = rows // ROW_BLOCK
    top_rows = jnp.concatenate([top, values[ROW_BLOCK - 1 : rows - 1 : ROW_BLOCK]], axis=0)
    bottom_rows = jnp.concatenate([values[ROW_BLOCK:rows:ROW_BLOCK], bottom], axis=0)
    with_flux = fluxes_t is not None
    in_specs = [
        pl.BlockSpec((ROW_BLOCK, cols, levels), lambda i: (i, 0, 0)),
        pl.BlockSpec((1, cols, levels), lambda i: (i, 0, 0)),
        pl.BlockSpec((1, cols, levels), lambda i: (i, 0, 0)),
        pl.BlockSpec((ROW_BLOCK, 1, levels), lambda i: (i, 0, 0)),
        pl.BlockSpec((ROW_BLOCK, 1, levels), lambda i: (i, 0, 0)),
        pl.BlockSpec((levels, levels), lambda i: (0, 0)),
    ]
    operands = [values, top_rows, bottom_rows, west, east, mixing]
    out_shape = [jax.ShapeDtypeStruct(values.shape, jnp.float32)]
    out_specs = [pl.BlockSpec((ROW_BLOCK, cols, levels), lambda i: (i, 0, 0))]
    if not with_flux:
        out_shape.append(jax.ShapeDtypeStruct((8, rows * cols), jnp.float32))
        out_specs.append(pl.BlockSpec((8, ROW_BLOCK * cols), lambda i: (0, i)))
    if with_flux:
        flux_count = fluxes_t.shape[0]
        in_specs.append(pl.BlockSpec((flux_count, levels), lambda i: (0, 0)))
        operands.append(fluxes_t)
        out_shape.append(jax.ShapeDtypeStruct((flux_count, rows * cols), jnp.float32))
        out_specs.append(pl.BlockSpec((flux_count, ROW_BLOCK * cols), lambda i: (0, i)))
    cells = rows * cols
    flops = 6 * cells * levels * levels + (6 * cells * levels * 8 if with_flux else 0)
    result = pl.pallas_call(
        functools.partial(substep_kernel, with_flux, comp_total),
        grid=(blocks,),
        in_specs=in_specs,
        out_specs=out_specs,
        out_shape=out_shape,
        cost_estimate=pl.CostEstimate(
            flops=flops, transcendentals=cells * levels, bytes_accessed=8 * cells * levels
        ),
    )(*operands)
    return result


def column_physics(values, mixing):
    return jnp.tanh(jnp.einsum("rck,kj->rcj", values, mixing, precision=HIGHEST))


def earlier_same(owners, usable):
    positions = jnp.arange(owners.shape[0], dtype=jnp.int32)
    before = (
        (owners[None, :] == owners[:, None])
        & (positions[None, :] < positions[:, None])
        & usable[None, :]
    )
    return jnp.sum(before.astype(jnp.int32), axis=1)


def pack_rows(blocks, owners, labels, usable, slots_each, owner_total):
    ranks = earlier_same(owners, usable)
    target_slot = owners * slots_each + ranks
    slot_ids = jnp.arange(owner_total * slots_each, dtype=jnp.int32)
    placing = (slot_ids[:, None] == target_slot[None, :]) & usable[None, :]
    packed = jnp.dot(
        placing.astype(jnp.bfloat16), blocks, preferred_element_type=jnp.float32
    ).astype(jnp.bfloat16)
    placed_labels = jnp.sum(jnp.where(placing, labels[None, :] + 1, 0), axis=1) - 1
    return (
        packed.reshape(owner_total, slots_each, blocks.shape[1]),
        placed_labels.reshape(owner_total, slots_each),
        target_slot,
    )


MESH_IDS = pl.DeviceIdType.MESH


def tile_device(comp, tile, lon_total):
    return (comp, tile // lon_total, tile % lon_total)


def gather_kernel(offsets, shape, send_ref, out_ref, land, send_sems, recv_sems):
    comp_total, lat_total, lon_total = shape
    comp = lax.axis_index("comp")
    tiles = lat_total * lon_total
    tile = lax.axis_index("lat") * lon_total + lax.axis_index("lon")
    ocean = comp_total - 1
    count = len(offsets)
    barrier = pltpu.get_barrier_semaphore()

    @pl.when(comp != ocean)
    def _():
        for off in offsets:
            target = tile_device(ocean, (tile + off) % tiles, lon_total)
            pl.semaphore_signal(barrier, 1, device_id=target, device_id_type=MESH_IDS)
        pl.semaphore_wait(barrier, count)
        copies = []
        for k, off in enumerate(offsets):
            target = tile_device(ocean, (tile + off) % tiles, lon_total)
            copy = pltpu.make_async_remote_copy(
                src_ref=send_ref.at[k],
                dst_ref=land.at[comp * count + k],
                send_sem=send_sems.at[k],
                recv_sem=recv_sems.at[comp * count + k],
                device_id=target,
                device_id_type=MESH_IDS,
            )
            copy.start()
            copies.append(copy)
        for copy in copies:
            copy.wait_send()
        out_ref[...] = jnp.zeros_like(out_ref)

    @pl.when(comp == ocean)
    def _():
        for source_comp in range(ocean):
            for off in offsets:
                source = tile_device(source_comp, (tile + tiles - off) % tiles, lon_total)
                pl.semaphore_signal(barrier, 1, device_id=source, device_id_type=MESH_IDS)
        pl.semaphore_wait(barrier, count * ocean)
        for source_comp in range(ocean):
            for k, off in enumerate(offsets):
                source = tile_device(source_comp, (tile + tiles - off) % tiles, lon_total)
                slot = source_comp * count + k
                pltpu.make_async_remote_copy(
                    src_ref=send_ref.at[k],
                    dst_ref=land.at[slot],
                    send_sem=send_sems.at[k],
                    recv_sem=recv_sems.at[slot],
                    device_id=source,
                    device_id_type=MESH_IDS,
                ).wait_recv()
        out_ref[...] = land[...]


def gather_to_ocean(blocks, offsets, shape):
    count = len(offsets)
    senders = (shape[0] - 1) * count
    slot_shape = blocks.shape[1:]
    return pl.pallas_call(
        functools.partial(gather_kernel, tuple(offsets), tuple(shape)),
        out_shape=jax.ShapeDtypeStruct((senders,) + slot_shape, blocks.dtype),
        in_specs=[pl.BlockSpec(memory_space=pltpu.VMEM)],
        out_specs=pl.BlockSpec(memory_space=pltpu.VMEM),
        scratch_shapes=[
            pltpu.VMEM((senders,) + slot_shape, blocks.dtype),
            pltpu.SemaphoreType.DMA((count,)),
            pltpu.SemaphoreType.DMA((senders,)),
        ],
        compiler_params=pltpu.CompilerParams(collective_id=0, has_side_effects=True),
    )(blocks)


def spread_kernel(offsets, shape, surface_ref, out_ref, land, send_sems, recv_sems):
    comp_total, lat_total, lon_total = shape
    comp = lax.axis_index("comp")
    tiles = lat_total * lon_total
    tile = lax.axis_index("lat") * lon_total + lax.axis_index("lon")
    ocean = comp_total - 1
    count = len(offsets)
    barrier = pltpu.get_barrier_semaphore()

    @pl.when(comp == ocean)
    def _():
        for target_comp in range(ocean):
            for off in offsets:
                target = tile_device(target_comp, (tile + tiles - off) % tiles, lon_total)
                pl.semaphore_signal(barrier, 1, device_id=target, device_id_type=MESH_IDS)
        pl.semaphore_wait(barrier, count * ocean)
        copies = []
        for target_comp in range(ocean):
            for k, off in enumerate(offsets):
                target = tile_device(target_comp, (tile + tiles - off) % tiles, lon_total)
                copy = pltpu.make_async_remote_copy(
                    src_ref=surface_ref.at[target_comp * count + k],
                    dst_ref=land.at[k],
                    send_sem=send_sems.at[target_comp * count + k],
                    recv_sem=recv_sems.at[k],
                    device_id=target,
                    device_id_type=MESH_IDS,
                )
                copy.start()
                copies.append(copy)
        for copy in copies:
            copy.wait_send()
        out_ref[...] = jnp.zeros_like(out_ref)

    @pl.when(comp != ocean)
    def _():
        for off in offsets:
            source = tile_device(ocean, (tile + off) % tiles, lon_total)
            pl.semaphore_signal(barrier, 1, device_id=source, device_id_type=MESH_IDS)
        pl.semaphore_wait(barrier, count)
        for k, off in enumerate(offsets):
            source = tile_device(ocean, (tile + off) % tiles, lon_total)
            pltpu.make_async_remote_copy(
                src_ref=surface_ref.at[k],
                dst_ref=land.at[k],
                send_sem=send_sems.at[k],
                recv_sem=recv_sems.at[k],
                device_id=source,
                device_id_type=MESH_IDS,
            ).wait_recv()
        out_ref[...] = land[...]


def spread_from_ocean(replies, offsets, shape):
    count = len(offsets)
    senders = (shape[0] - 1) * count
    slot_shape = replies.shape[1:]
    return pl.pallas_call(
        functools.partial(spread_kernel, tuple(offsets), tuple(shape)),
        out_shape=jax.ShapeDtypeStruct((count,) + slot_shape, replies.dtype),
        in_specs=[pl.BlockSpec(memory_space=pltpu.VMEM)],
        out_specs=pl.BlockSpec(memory_space=pltpu.VMEM),
        scratch_shapes=[
            pltpu.VMEM((count,) + slot_shape, replies.dtype),
            pltpu.SemaphoreType.DMA((senders,)),
            pltpu.SemaphoreType.DMA((count,)),
        ],
        compiler_params=pltpu.CompilerParams(collective_id=1, has_side_effects=True),
    )(replies)


def ocean_update_kernel(flag_ref, base_ref, state_ref, sea_ref, forcing_ref, spread_ref, out_ref):
    rows, cols, levels = base_ref.shape
    flux_count = forcing_ref.shape[0]

    def block(base_block, state_block, sea_block, forcing_block, out_block):
        ocean_block(base_block, state_block, sea_block, forcing_block, spread_ref, out_block)

    @pl.when(flag_ref[0] == 1)
    def _():
        pltpu.emit_pipeline(
            block,
            grid=(rows // ROW_BLOCK,),
            in_specs=[
                pl.BlockSpec((ROW_BLOCK, cols, levels), lambda i: (i, 0, 0)),
                pl.BlockSpec((ROW_BLOCK, cols, levels), lambda i: (i, 0, 0)),
                pl.BlockSpec((8, ROW_BLOCK * cols), lambda i: (0, i)),
                pl.BlockSpec((flux_count, ROW_BLOCK * cols), lambda i: (0, i)),
            ],
            out_specs=[pl.BlockSpec((ROW_BLOCK, cols, levels), lambda i: (i, 0, 0))],
        )(base_ref, state_ref, sea_ref, forcing_ref, out_ref)


def ocean_block(first_ref, state_ref, sea_ref, forcing_ref, spread_ref, out_ref):
    rows, cols, levels = first_ref.shape
    forcing = forcing_ref[...]
    spread = spread_ref[...]
    forcing_hi = forcing.astype(jnp.bfloat16)
    forcing_lo = (forcing - forcing_hi.astype(jnp.float32)).astype(jnp.bfloat16)
    spread_hi = spread.astype(jnp.bfloat16)
    spread_lo = (spread - spread_hi.astype(jnp.float32)).astype(jnp.bfloat16)

    def one(a, b):
        return lax.dot_general(a, b, (((0,), (0,)), ((), ())), preferred_element_type=jnp.float32)

    stacked = jnp.concatenate(
        [forcing_hi.astype(jnp.float32), forcing_hi.astype(jnp.float32), forcing_lo.astype(jnp.float32)],
        axis=0,
    ).astype(jnp.bfloat16)
    spread_stack = jnp.concatenate(
        [spread_hi.astype(jnp.float32), spread_lo.astype(jnp.float32), spread_hi.astype(jnp.float32)],
        axis=0,
    ).astype(jnp.bfloat16)
    added = one(stacked, spread_stack)
    lane_row = lax.broadcasted_iota(jnp.int32, (8, levels), 0)
    ones = (lane_row == 0).astype(jnp.bfloat16)
    picks = jnp.where(lax.broadcasted_iota(jnp.int32, sea_ref.shape, 0) == 0, sea_ref[...], 0)
    mask = one(picks.astype(jnp.bfloat16), ones)
    moved = first_ref[...].reshape(rows * cols, levels) + added
    kept = jnp.where(mask > 0.5, moved, state_ref[...].reshape(rows * cols, levels))
    out_ref[...] = kept.reshape(rows, cols, levels)


def ocean_update(first, state, sea_rows, forcing, ocean_map, comp_total):
    rows, cols, levels = first.shape
    flux_count = forcing.shape[0]
    cells = rows * cols
    flag = (lax.axis_index("comp") == comp_total - 1).astype(jnp.int32).reshape(1)
    return pl.pallas_call(
        ocean_update_kernel,
        out_shape=jax.ShapeDtypeStruct(first.shape, jnp.float32),
        in_specs=[
            pl.BlockSpec(memory_space=pltpu.SMEM),
            pl.BlockSpec(memory_space=pl.ANY),
            pl.BlockSpec(memory_space=pl.ANY),
            pl.BlockSpec(memory_space=pl.ANY),
            pl.BlockSpec(memory_space=pl.ANY),
            pl.BlockSpec(memory_space=pltpu.VMEM),
        ],
        out_specs=pl.BlockSpec(memory_space=pl.ANY),
        input_output_aliases={1: 0},
        cost_estimate=pl.CostEstimate(
            flops=8 * cells * levels * flux_count, transcendentals=0, bytes_accessed=12 * cells * levels
        ),
    )(flag, first, state, sea_rows, forcing, ocean_map)


def scatter_regrid_kernel(labels_ref, fluxes_ref, weights_ref, out_ref, binned_ref):
    entries = fluxes_ref.shape[0]
    weight_count, tile_rows, block_len = weights_ref.shape
    flux_count = fluxes_ref.shape[1]
    binned_ref[...] = jnp.zeros_like(binned_ref)

    def add_one(e, carry):
        label = labels_ref[e]
        binned_ref[label] = binned_ref[label] + fluxes_ref[e]
        return carry

    lax.fori_loop(0, entries, add_one, 0, unroll=8)
    out_ref[...] = jnp.zeros_like(out_ref)

    def regrid_one(w, carry):
        start = pl.multiple_of(w * tile_rows, tile_rows)
        block = binned_ref[pl.ds(start, tile_rows)].reshape(tile_rows * flux_count, block_len)
        high = block.astype(jnp.bfloat16)
        low = (block - high.astype(jnp.float32)).astype(jnp.bfloat16)
        weight = weights_ref[w]
        out_ref[...] += jnp.dot(high, weight, preferred_element_type=jnp.float32) + jnp.dot(
            low, weight, preferred_element_type=jnp.float32
        )
        return carry

    lax.fori_loop(0, weight_count, regrid_one, 0)


def scatter_regrid(labels, fluxes, weights):
    entries, flux_count, block_len = fluxes.shape
    weight_count, tile_rows, _ = weights.shape
    return pl.pallas_call(
        scatter_regrid_kernel,
        out_shape=jax.ShapeDtypeStruct((tile_rows * flux_count, block_len), jnp.float32),
        in_specs=[
            pl.BlockSpec(memory_space=pltpu.SMEM),
            pl.BlockSpec(memory_space=pltpu.VMEM),
            pl.BlockSpec(memory_space=pltpu.VMEM),
        ],
        out_specs=pl.BlockSpec(memory_space=pltpu.VMEM),
        scratch_shapes=[pltpu.VMEM((weight_count * tile_rows, flux_count, block_len), jnp.float32)],
        compiler_params=pltpu.CompilerParams(vmem_limit_bytes=48 * 1024 * 1024),
        cost_estimate=pl.CostEstimate(
            flops=4 * weight_count * tile_rows * flux_count * block_len * block_len,
            transcendentals=0,
            bytes_accessed=entries * flux_count * block_len * 4 + weight_count * tile_rows * block_len * 2,
        ),
    )(labels, fluxes, weights)


def halo_kernel(shape, values_ref, rows_out, cols_out, rows_land, cols_land, send_sems, recv_sems):
    comp_total, lat_total, lon_total = shape
    bands = comp_total * lat_total
    band = lax.axis_index("comp") * lat_total + lax.axis_index("lat")
    lon = lax.axis_index("lon")
    rows, cols, _ = values_ref.shape
    up = (band + 1) % bands
    down = (band + bands - 1) % bands
    up_device = (up // lat_total, up % lat_total, lon)
    down_device = (down // lat_total, down % lat_total, lon)
    east_device = (band // lat_total, band % lat_total, (lon + 1) % lon_total)
    west_device = (band // lat_total, band % lat_total, (lon + lon_total - 1) % lon_total)
    barrier = pltpu.get_barrier_semaphore()
    for device in (up_device, down_device, east_device, west_device):
        pl.semaphore_signal(barrier, 1, device_id=device, device_id_type=MESH_IDS)
    pl.semaphore_wait(barrier, 4)
    plan = [
        (values_ref.at[pl.ds(rows - 1, 1)], rows_land.at[0], up_device),
        (values_ref.at[pl.ds(0, 1)], rows_land.at[1], down_device),
        (values_ref.at[:, pl.ds(cols - 1, 1)], cols_land.at[0], east_device),
        (values_ref.at[:, pl.ds(0, 1)], cols_land.at[1], west_device),
    ]
    copies = []
    for slot, (source, target, device) in enumerate(plan):
        copy = pltpu.make_async_remote_copy(
            src_ref=source,
            dst_ref=target,
            send_sem=send_sems.at[slot],
            recv_sem=recv_sems.at[slot],
            device_id=device,
            device_id_type=MESH_IDS,
        )
        copy.start()
        copies.append(copy)
    for copy in copies:
        copy.wait_send()
    for copy in copies:
        copy.wait_recv()
    rows_out[...] = rows_land[...]
    cols_out[...] = cols_land[...]


def halo_edges(values, shape, collective):
    rows, cols, levels = values.shape
    return pl.pallas_call(
        functools.partial(halo_kernel, tuple(shape)),
        out_shape=(
            jax.ShapeDtypeStruct((2, 1, cols, levels), values.dtype),
            jax.ShapeDtypeStruct((2, rows, 1, levels), values.dtype),
        ),
        in_specs=[pl.BlockSpec(memory_space=pl.ANY)],
        out_specs=(
            pl.BlockSpec(memory_space=pltpu.VMEM),
            pl.BlockSpec(memory_space=pltpu.VMEM),
        ),
        scratch_shapes=[
            pltpu.VMEM((2, 1, cols, levels), values.dtype),
            pltpu.VMEM((2, rows, 1, levels), values.dtype),
            pltpu.SemaphoreType.DMA((4,)),
            pltpu.SemaphoreType.DMA((4,)),
        ],
        compiler_params=pltpu.CompilerParams(collective_id=collective, has_side_effects=True),
    )(values)


def local(
    state, land_mask, intersection_list, mix_atm, mix_ocn, flux_map, ocean_map, regrid_weights
):
    tile_rows, block_len, levels = state.shape
    flux_count = flux_map.shape[1]
    weight_count = regrid_weights.shape[0]
    intersections = intersection_list.shape[2]
    comp_count = lax.axis_size("comp")
    lat_count = lax.axis_size("lat")
    lon_count = lax.axis_size("lon")
    tile_count = lat_count * lon_count
    reach = min(4, lon_count)
    neighbour_count = 2 * reach
    capacity = intersections * tile_rows // neighbour_count
    width = flux_count * block_len
    comp_index = lax.axis_index("comp")
    tile_index = lax.axis_index("lat") * lon_count + lax.axis_index("lon")
    band = comp_index * lat_count + lax.axis_index("lat")
    ocean_band = (comp_count - 1) * lat_count
    ocean_side = comp_index == comp_count - 1
    lower_valid = (band > 0) & ((band - 1 >= ocean_band) == (band >= ocean_band))
    upper_valid = (band < comp_count * lat_count - 1) & (
        (band + 1 >= ocean_band) == (band >= ocean_band)
    )
    sea_cells = land_mask == 1

    mesh_shape = (comp_count, lat_count, lon_count)

    def halos(values, collective):
        rows, cols = halo_edges(values, mesh_shape, collective)
        top = jnp.where(lower_valid, rows[0], 0.0)
        bottom = jnp.where(upper_valid, rows[1], 0.0)
        return top, bottom, cols[0], cols[1]

    top, bottom, west, east = halos(state, 2)
    mixing = jnp.where(ocean_side, mix_ocn, mix_atm)
    first, first_planes = substep(state, top, bottom, west, east, mixing, comp_count)
    first_top = first_planes[0].reshape(tile_rows, block_len)
    state_top = first_planes[1].reshape(tile_rows, block_len)
    top, bottom, west, east = halos(first, 3)

    def atmosphere_second(values, top, bottom, west, east):
        moved, total = substep(values, top, bottom, west, east, mix_atm, comp_count, flux_map.T)
        total = total.reshape(flux_count, tile_rows, block_len)
        sent = jnp.where(sea_cells[None], 0.5 * total, 0.0).astype(jnp.bfloat16)
        return moved, sent

    def ocean_second(values, top, bottom, west, east):
        return values, jnp.zeros((flux_count, tile_rows, block_len), jnp.bfloat16)

    second, flux_sent = lax.cond(
        ocean_side, ocean_second, atmosphere_second, first, top, bottom, west, east
    )
    entry_list = intersection_list.reshape(tile_rows * intersections, 3)
    owners = entry_list[:, 0]
    targets = entry_list[:, 1]
    weight_ids = entry_list[:, 2]
    labels = weight_ids * tile_rows + targets
    entry_blocks = jnp.repeat(flux_sent.transpose(1, 0, 2), intersections, axis=0).reshape(
        tile_rows * intersections, width
    )
    lane = jnp.arange(128, dtype=jnp.int32)[None, :]
    label_lanes = jnp.where(
        lane == 0, weight_ids[:, None], jnp.where(lane == 1, targets[:, None], 0)
    ).astype(jnp.bfloat16)
    entry_blocks = jnp.concatenate([entry_blocks, label_lanes], axis=1)
    sending = jnp.broadcast_to(jnp.logical_not(ocean_side), owners.shape)
    offsets = [
        (n // reach * lon_count + n % reach - (reach - 1) // 2) % tile_count
        for n in range(neighbour_count)
    ]
    offset_table = jnp.array(offsets, jnp.int32)
    distance = (owners - tile_index + tile_count) % tile_count
    neighbour_ids = jnp.sum(
        jnp.where(
            distance[:, None] == offset_table[None, :],
            jnp.arange(neighbour_count, dtype=jnp.int32)[None, :],
            0,
        ),
        axis=1,
    )
    packed, _, entry_slots = pack_rows(entry_blocks, neighbour_ids, labels, sending, capacity, neighbour_count)
    arrived = gather_to_ocean(packed, offsets, mesh_shape)
    weights_low = regrid_weights
    weights_wide = regrid_weights.astype(jnp.float32)
    senders = (comp_count - 1) * neighbour_count

    def ocean_reply(values_top, arrived):
        flat = arrived.reshape(-1, width + 128)
        arrived_labels = flat[:, width].astype(jnp.int32) * tile_rows + flat[:, width + 1].astype(
            jnp.int32
        )
        fluxes = flat[:, :width].astype(jnp.float32).reshape(-1, flux_count, block_len)
        forcing = scatter_regrid(arrived_labels, fluxes, weights_low)
        forcing = forcing.reshape(tile_rows, flux_count, block_len).transpose(1, 0, 2)
        lifted = jnp.sum(forcing * ocean_map[:, 0][:, None, None], axis=0)
        top_level = jnp.where(sea_cells, values_top + lifted, state_top)
        table = jnp.einsum("db,wab->wda", top_level, weights_wide, precision=HIGHEST)
        replies = jnp.take(table.reshape(weight_count * tile_rows, block_len), arrived_labels, axis=0)
        return forcing, replies.reshape(senders, capacity, block_len), top_level

    def atmosphere_reply(values_top, arrived):
        return (
            jnp.zeros((flux_count, tile_rows, block_len), jnp.float32),
            jnp.zeros((senders, capacity, block_len), jnp.float32),
            values_top,
        )

    forcing, replies, ocean_top = lax.cond(
        ocean_side, ocean_reply, atmosphere_reply, first_top, arrived
    )
    answers = spread_from_ocean(replies, offsets, mesh_shape)
    per_entry = jnp.take(
        answers.reshape(neighbour_count * capacity, block_len), entry_slots, axis=0
    )
    returned = per_entry.reshape(tile_rows, intersections, block_len).sum(axis=1)
    second, forcing, answers = lax.optimization_barrier((second, forcing, answers))
    sea_rows = jnp.broadcast_to(
        sea_cells.astype(jnp.int32).reshape(1, tile_rows * block_len), (8, tile_rows * block_len)
    )
    final_state = ocean_update(
        second,
        state,
        sea_rows,
        forcing.reshape(flux_count, tile_rows * block_len),
        ocean_map,
        comp_count,
    )
    top_plane = lax.cond(
        ocean_side, lambda values: ocean_top, lambda values: values[:, :, 0], final_state
    )
    surface_out = jnp.where(ocean_side, ocean_top, jnp.where(sea_cells, returned, top_plane))
    return (final_state, surface_out)


def solution(mesh):
    placed = (
        P(("comp", "lat"), "lon", None),
        P(("comp", "lat"), "lon"),
        P(("comp", "lat"), "lon", None, None),
        P(),
        P(),
        P(),
        P(),
        P(),
    )
    return jax.shard_map(
        local,
        mesh=mesh,
        in_specs=placed,
        out_specs=(P(("comp", "lat"), "lon", None), P(("comp", "lat"), "lon")),
        check_vma=False,
    )
```

```python
import jax
import jax.numpy as jnp
from jax import lax
from jax.experimental import pallas as pl
from jax.experimental.pallas import tpu as pltpu
from jax.sharding import PartitionSpec as P
import functools

SMOOTHING = 0.2
PHYSICS = 0.5
HIGHEST = lax.Precision.HIGHEST
ROW_BLOCK = 8
UPDATE_BLOCK = 16


def split_bf16(values):
    high = values.astype(jnp.bfloat16)
    low = (values - high.astype(jnp.float32)).astype(jnp.bfloat16)
    return high, low


def three_pass(lhs, rhs, dims):
    lhs_hi, lhs_lo = split_bf16(lhs)
    rhs_hi, rhs_lo = split_bf16(rhs)

    def one(a, b):
        return lax.dot_general(a, b, (dims, ((), ())), preferred_element_type=jnp.float32)

    return one(lhs_hi, rhs_hi) + (one(lhs_hi, rhs_lo) + one(lhs_lo, rhs_hi))


def exact_rows(picker, values):
    high = values.astype(jnp.bfloat16)
    rest = values - high.astype(jnp.float32)
    middle = rest.astype(jnp.bfloat16)
    low = (rest - middle.astype(jnp.float32)).astype(jnp.bfloat16)

    def one(piece):
        return lax.dot_general(
            picker, piece, (((1,), (1,)), ((), ())), preferred_element_type=jnp.float32
        )

    return one(high) + one(middle) + one(low)


def substep_kernel(with_flux, comp_total, x_ref, top_ref, bottom_ref, west_ref, east_ref, mix_ref, *rest):
    if with_flux:
        fluxes_ref, out_ref, flux_out_ref = rest
    else:
        out_ref, planes_ref = rest
    rows, cols, levels = x_ref.shape
    centre = x_ref[...]
    up = jnp.concatenate([top_ref[...], centre[:-1]], axis=0)
    down = jnp.concatenate([centre[1:], bottom_ref[...]], axis=0)
    column = lax.broadcasted_iota(jnp.int32, centre.shape, 1)
    west = jnp.where(column == 0, west_ref[...], pltpu.roll(centre, 1, 1))
    east = jnp.where(column == cols - 1, east_ref[...], pltpu.roll(centre, cols - 1, 1))
    smooth = centre + SMOOTHING * (up + down + west + east - 4.0 * centre)
    flat = smooth.reshape(rows * cols, levels)
    mixed = three_pass(flat, mix_ref[...], ((1,), (0,)))
    moved = flat + PHYSICS * jnp.tanh(mixed)
    out_ref[...] = moved.reshape(rows, cols, levels)
    if not with_flux:
        ocean = lax.axis_index("comp") == comp_total - 1

        @pl.when(ocean)
        def _():
            plane_row = lax.broadcasted_iota(jnp.int32, (8, levels), 0)
            plane_lane = lax.broadcasted_iota(jnp.int32, (8, levels), 1)
            pick_out = ((plane_row == 0) & (plane_lane == 0)).astype(jnp.bfloat16)
            pick_in = ((plane_row == 1) & (plane_lane == 0)).astype(jnp.bfloat16)
            planes_ref[...] = exact_rows(pick_out, moved) + exact_rows(
                pick_in, centre.reshape(rows * cols, levels)
            )

        @pl.when(jnp.logical_not(ocean))
        def _():
            planes_ref[...] = jnp.zeros_like(planes_ref)

    else:
        total = centre.reshape(rows * cols, levels) + moved
        flux_out_ref[...] = three_pass(fluxes_ref[...], total, ((1,), (1,)))


def substep(values, top, bottom, west, east, mixing, comp_total, fluxes_t=None):
    rows, cols, levels = values.shape
    blocks = rows // ROW_BLOCK
    top_rows = jnp.concatenate([top, values[ROW_BLOCK - 1 : rows - 1 : ROW_BLOCK]], axis=0)
    bottom_rows = jnp.concatenate([values[ROW_BLOCK:rows:ROW_BLOCK], bottom], axis=0)
    with_flux = fluxes_t is not None
    in_specs = [
        pl.BlockSpec((ROW_BLOCK, cols, levels), lambda i: (i, 0, 0)),
        pl.BlockSpec((1, cols, levels), lambda i: (i, 0, 0)),
        pl.BlockSpec((1, cols, levels), lambda i: (i, 0, 0)),
        pl.BlockSpec((ROW_BLOCK, 1, levels), lambda i: (i, 0, 0)),
        pl.BlockSpec((ROW_BLOCK, 1, levels), lambda i: (i, 0, 0)),
        pl.BlockSpec((levels, levels), lambda i: (0, 0)),
    ]
    operands = [values, top_rows, bottom_rows, west, east, mixing]
    out_shape = [jax.ShapeDtypeStruct(values.shape, jnp.float32)]
    out_specs = [pl.BlockSpec((ROW_BLOCK, cols, levels), lambda i: (i, 0, 0))]
    if not with_flux:
        out_shape.append(jax.ShapeDtypeStruct((8, rows * cols), jnp.float32))
        out_specs.append(pl.BlockSpec((8, ROW_BLOCK * cols), lambda i: (0, i)))
    if with_flux:
        flux_count = fluxes_t.shape[0]
        in_specs.append(pl.BlockSpec((flux_count, levels), lambda i: (0, 0)))
        operands.append(fluxes_t)
        out_shape.append(jax.ShapeDtypeStruct((flux_count, rows * cols), jnp.float32))
        out_specs.append(pl.BlockSpec((flux_count, ROW_BLOCK * cols), lambda i: (0, i)))
    cells = rows * cols
    flops = 6 * cells * levels * levels + (6 * cells * levels * 8 if with_flux else 0)
    result = pl.pallas_call(
        functools.partial(substep_kernel, with_flux, comp_total),
        grid=(blocks,),
        in_specs=in_specs,
        out_specs=out_specs,
        out_shape=out_shape,
        cost_estimate=pl.CostEstimate(
            flops=flops, transcendentals=cells * levels, bytes_accessed=8 * cells * levels
        ),
    )(*operands)
    return result


def column_physics(values, mixing):
    return jnp.tanh(jnp.einsum("rck,kj->rcj", values, mixing, precision=HIGHEST))


def earlier_same(owners, usable):
    positions = jnp.arange(owners.shape[0], dtype=jnp.int32)
    before = (
        (owners[None, :] == owners[:, None])
        & (positions[None, :] < positions[:, None])
        & usable[None, :]
    )
    return jnp.sum(before.astype(jnp.int32), axis=1)


def pack_rows(blocks, owners, labels, usable, slots_each, owner_total):
    ranks = earlier_same(owners, usable)
    target_slot = owners * slots_each + ranks
    slot_ids = jnp.arange(owner_total * slots_each, dtype=jnp.int32)
    placing = (slot_ids[:, None] == target_slot[None, :]) & usable[None, :]
    packed = jnp.dot(
        placing.astype(jnp.bfloat16), blocks, preferred_element_type=jnp.float32
    ).astype(jnp.bfloat16)
    placed_labels = jnp.sum(jnp.where(placing, labels[None, :] + 1, 0), axis=1) - 1
    return (
        packed.reshape(owner_total, slots_each, blocks.shape[1]),
        placed_labels.reshape(owner_total, slots_each),
        target_slot,
    )


MESH_IDS = pl.DeviceIdType.MESH


def tile_device(comp, tile, lon_total):
    return (comp, tile // lon_total, tile % lon_total)


def gather_kernel(offsets, shape, send_ref, out_ref, land, send_sems, recv_sems):
    comp_total, lat_total, lon_total = shape
    comp = lax.axis_index("comp")
    tiles = lat_total * lon_total
    tile = lax.axis_index("lat") * lon_total + lax.axis_index("lon")
    ocean = comp_total - 1
    count = len(offsets)
    barrier = pltpu.get_barrier_semaphore()

    @pl.when(comp != ocean)
    def _():
        for off in offsets:
            target = tile_device(ocean, (tile + off) % tiles, lon_total)
            pl.semaphore_signal(barrier, 1, device_id=target, device_id_type=MESH_IDS)
        pl.semaphore_wait(barrier, count)
        copies = []
        for k, off in enumerate(offsets):
            target = tile_device(ocean, (tile + off) % tiles, lon_total)
            copy = pltpu.make_async_remote_copy(
                src_ref=send_ref.at[k],
                dst_ref=land.at[comp * count + k],
                send_sem=send_sems.at[k],
                recv_sem=recv_sems.at[comp * count + k],
                device_id=target,
                device_id_type=MESH_IDS,
            )
            copy.start()
            copies.append(copy)
        for copy in copies:
            copy.wait_send()
        out_ref[...] = jnp.zeros_like(out_ref)

    @pl.when(comp == ocean)
    def _():
        for source_comp in range(ocean):
            for off in offsets:
                source = tile_device(source_comp, (tile + tiles - off) % tiles, lon_total)
                pl.semaphore_signal(barrier, 1, device_id=source, device_id_type=MESH_IDS)
        pl.semaphore_wait(barrier, count * ocean)
        for source_comp in range(ocean):
            for k, off in enumerate(offsets):
                source = tile_device(source_comp, (tile + tiles - off) % tiles, lon_total)
                slot = source_comp * count + k
                pltpu.make_async_remote_copy(
                    src_ref=send_ref.at[k],
                    dst_ref=land.at[slot],
                    send_sem=send_sems.at[k],
                    recv_sem=recv_sems.at[slot],
                    device_id=source,
                    device_id_type=MESH_IDS,
                ).wait_recv()
        out_ref[...] = land[...]


def gather_to_ocean(blocks, offsets, shape):
    count = len(offsets)
    senders = (shape[0] - 1) * count
    slot_shape = blocks.shape[1:]
    return pl.pallas_call(
        functools.partial(gather_kernel, tuple(offsets), tuple(shape)),
        out_shape=jax.ShapeDtypeStruct((senders,) + slot_shape, blocks.dtype),
        in_specs=[pl.BlockSpec(memory_space=pltpu.VMEM)],
        out_specs=pl.BlockSpec(memory_space=pltpu.VMEM),
        scratch_shapes=[
            pltpu.VMEM((senders,) + slot_shape, blocks.dtype),
            pltpu.SemaphoreType.DMA((count,)),
            pltpu.SemaphoreType.DMA((senders,)),
        ],
        compiler_params=pltpu.CompilerParams(collective_id=0, has_side_effects=True),
    )(blocks)


def spread_kernel(offsets, shape, surface_ref, out_ref, land, send_sems, recv_sems):
    comp_total, lat_total, lon_total = shape
    comp = lax.axis_index("comp")
    tiles = lat_total * lon_total
    tile = lax.axis_index("lat") * lon_total + lax.axis_index("lon")
    ocean = comp_total - 1
    count = len(offsets)
    barrier = pltpu.get_barrier_semaphore()

    @pl.when(comp == ocean)
    def _():
        for target_comp in range(ocean):
            for off in offsets:
                target = tile_device(target_comp, (tile + tiles - off) % tiles, lon_total)
                pl.semaphore_signal(barrier, 1, device_id=target, device_id_type=MESH_IDS)
        pl.semaphore_wait(barrier, count * ocean)
        copies = []
        for target_comp in range(ocean):
            for k, off in enumerate(offsets):
                target = tile_device(target_comp, (tile + tiles - off) % tiles, lon_total)
                copy = pltpu.make_async_remote_copy(
                    src_ref=surface_ref.at[target_comp * count + k],
                    dst_ref=land.at[k],
                    send_sem=send_sems.at[target_comp * count + k],
                    recv_sem=recv_sems.at[k],
                    device_id=target,
                    device_id_type=MESH_IDS,
                )
                copy.start()
                copies.append(copy)
        for copy in copies:
            copy.wait_send()
        out_ref[...] = jnp.zeros_like(out_ref)

    @pl.when(comp != ocean)
    def _():
        for off in offsets:
            source = tile_device(ocean, (tile + off) % tiles, lon_total)
            pl.semaphore_signal(barrier, 1, device_id=source, device_id_type=MESH_IDS)
        pl.semaphore_wait(barrier, count)
        for k, off in enumerate(offsets):
            source = tile_device(ocean, (tile + off) % tiles, lon_total)
            pltpu.make_async_remote_copy(
                src_ref=surface_ref.at[k],
                dst_ref=land.at[k],
                send_sem=send_sems.at[k],
                recv_sem=recv_sems.at[k],
                device_id=source,
                device_id_type=MESH_IDS,
            ).wait_recv()
        out_ref[...] = land[...]


def spread_from_ocean(replies, offsets, shape):
    count = len(offsets)
    senders = (shape[0] - 1) * count
    slot_shape = replies.shape[1:]
    return pl.pallas_call(
        functools.partial(spread_kernel, tuple(offsets), tuple(shape)),
        out_shape=jax.ShapeDtypeStruct((count,) + slot_shape, replies.dtype),
        in_specs=[pl.BlockSpec(memory_space=pltpu.VMEM)],
        out_specs=pl.BlockSpec(memory_space=pltpu.VMEM),
        scratch_shapes=[
            pltpu.VMEM((count,) + slot_shape, replies.dtype),
            pltpu.SemaphoreType.DMA((senders,)),
            pltpu.SemaphoreType.DMA((count,)),
        ],
        compiler_params=pltpu.CompilerParams(collective_id=1, has_side_effects=True),
    )(replies)


def ocean_update_kernel(flag_ref, base_ref, state_ref, sea_ref, forcing_ref, spread_ref, out_ref):
    rows, cols, levels = base_ref.shape
    flux_count = forcing_ref.shape[0]

    def block(base_block, state_block, sea_block, forcing_block, out_block):
        ocean_block(base_block, state_block, sea_block, forcing_block, spread_ref, out_block)

    @pl.when(flag_ref[0] == 1)
    def _():
        pltpu.emit_pipeline(
            block,
            grid=(rows // UPDATE_BLOCK,),
            in_specs=[
                pl.BlockSpec((UPDATE_BLOCK, cols, levels), lambda i: (i, 0, 0)),
                pl.BlockSpec((UPDATE_BLOCK, cols, levels), lambda i: (i, 0, 0)),
                pl.BlockSpec((8, UPDATE_BLOCK * cols), lambda i: (0, i)),
                pl.BlockSpec((flux_count, UPDATE_BLOCK * cols), lambda i: (0, i)),
            ],
            out_specs=[pl.BlockSpec((UPDATE_BLOCK, cols, levels), lambda i: (i, 0, 0))],
        )(base_ref, state_ref, sea_ref, forcing_ref, out_ref)


def ocean_block(first_ref, state_ref, sea_ref, forcing_ref, spread_ref, out_ref):
    rows, cols, levels = first_ref.shape
    forcing = forcing_ref[...]
    spread = spread_ref[...]
    forcing_hi = forcing.astype(jnp.bfloat16)
    forcing_lo = (forcing - forcing_hi.astype(jnp.float32)).astype(jnp.bfloat16)
    spread_hi = spread.astype(jnp.bfloat16)
    spread_lo = (spread - spread_hi.astype(jnp.float32)).astype(jnp.bfloat16)

    def one(a, b):
        return lax.dot_general(a, b, (((0,), (0,)), ((), ())), preferred_element_type=jnp.float32)

    stacked = jnp.concatenate(
        [forcing_hi.astype(jnp.float32), forcing_hi.astype(jnp.float32), forcing_lo.astype(jnp.float32)],
        axis=0,
    ).astype(jnp.bfloat16)
    spread_stack = jnp.concatenate(
        [spread_hi.astype(jnp.float32), spread_lo.astype(jnp.float32), spread_hi.astype(jnp.float32)],
        axis=0,
    ).astype(jnp.bfloat16)
    added = one(stacked, spread_stack)
    lane_row = lax.broadcasted_iota(jnp.int32, (8, levels), 0)
    ones = (lane_row == 0).astype(jnp.bfloat16)
    picks = jnp.where(lax.broadcasted_iota(jnp.int32, sea_ref.shape, 0) == 0, sea_ref[...], 0)
    mask = one(picks.astype(jnp.bfloat16), ones)
    moved = first_ref[...].reshape(rows * cols, levels) + added
    kept = jnp.where(mask > 0.5, moved, state_ref[...].reshape(rows * cols, levels))
    out_ref[...] = kept.reshape(rows, cols, levels)


def ocean_update(first, state, sea_rows, forcing, ocean_map, comp_total):
    rows, cols, levels = first.shape
    flux_count = forcing.shape[0]
    cells = rows * cols
    flag = (lax.axis_index("comp") == comp_total - 1).astype(jnp.int32).reshape(1)
    return pl.pallas_call(
        ocean_update_kernel,
        out_shape=jax.ShapeDtypeStruct(first.shape, jnp.float32),
        in_specs=[
            pl.BlockSpec(memory_space=pltpu.SMEM),
            pl.BlockSpec(memory_space=pl.ANY),
            pl.BlockSpec(memory_space=pl.ANY),
            pl.BlockSpec(memory_space=pl.ANY),
            pl.BlockSpec(memory_space=pl.ANY),
            pl.BlockSpec(memory_space=pltpu.VMEM),
        ],
        out_specs=pl.BlockSpec(memory_space=pl.ANY),
        input_output_aliases={1: 0},
        cost_estimate=pl.CostEstimate(
            flops=8 * cells * levels * flux_count, transcendentals=0, bytes_accessed=12 * cells * levels
        ),
    )(flag, first, state, sea_rows, forcing, ocean_map)


def scatter_regrid_kernel(labels_ref, fluxes_ref, weights_ref, out_ref, binned_ref):
    entries = fluxes_ref.shape[0]
    weight_count, tile_rows, block_len = weights_ref.shape
    flux_count = fluxes_ref.shape[1]
    binned_ref[...] = jnp.zeros_like(binned_ref)

    def add_one(e, carry):
        label = labels_ref[e]
        binned_ref[label] = binned_ref[label] + fluxes_ref[e]
        return carry

    lax.fori_loop(0, entries, add_one, 0, unroll=8)
    out_ref[...] = jnp.zeros_like(out_ref)

    def regrid_one(w, carry):
        start = pl.multiple_of(w * tile_rows, tile_rows)
        block = binned_ref[pl.ds(start, tile_rows)].reshape(tile_rows * flux_count, block_len)
        high = block.astype(jnp.bfloat16)
        low = (block - high.astype(jnp.float32)).astype(jnp.bfloat16)
        weight = weights_ref[w]
        out_ref[...] += jnp.dot(high, weight, preferred_element_type=jnp.float32) + jnp.dot(
            low, weight, preferred_element_type=jnp.float32
        )
        return carry

    lax.fori_loop(0, weight_count, regrid_one, 0)


def scatter_regrid(labels, fluxes, weights):
    entries, flux_count, block_len = fluxes.shape
    weight_count, tile_rows, _ = weights.shape
    return pl.pallas_call(
        scatter_regrid_kernel,
        out_shape=jax.ShapeDtypeStruct((tile_rows * flux_count, block_len), jnp.float32),
        in_specs=[
            pl.BlockSpec(memory_space=pltpu.SMEM),
            pl.BlockSpec(memory_space=pltpu.VMEM),
            pl.BlockSpec(memory_space=pltpu.VMEM),
        ],
        out_specs=pl.BlockSpec(memory_space=pltpu.VMEM),
        scratch_shapes=[pltpu.VMEM((weight_count * tile_rows, flux_count, block_len), jnp.float32)],
        compiler_params=pltpu.CompilerParams(vmem_limit_bytes=48 * 1024 * 1024),
        cost_estimate=pl.CostEstimate(
            flops=4 * weight_count * tile_rows * flux_count * block_len * block_len,
            transcendentals=0,
            bytes_accessed=entries * flux_count * block_len * 4 + weight_count * tile_rows * block_len * 2,
        ),
    )(labels, fluxes, weights)


def halo_kernel(shape, values_ref, rows_out, cols_out, rows_land, cols_land, send_sems, recv_sems):
    comp_total, lat_total, lon_total = shape
    bands = comp_total * lat_total
    band = lax.axis_index("comp") * lat_total + lax.axis_index("lat")
    lon = lax.axis_index("lon")
    rows, cols, _ = values_ref.shape
    up = (band + 1) % bands
    down = (band + bands - 1) % bands
    up_device = (up // lat_total, up % lat_total, lon)
    down_device = (down // lat_total, down % lat_total, lon)
    east_device = (band // lat_total, band % lat_total, (lon + 1) % lon_total)
    west_device = (band // lat_total, band % lat_total, (lon + lon_total - 1) % lon_total)
    barrier = pltpu.get_barrier_semaphore()
    for device in (up_device, down_device, east_device, west_device):
        pl.semaphore_signal(barrier, 1, device_id=device, device_id_type=MESH_IDS)
    pl.semaphore_wait(barrier, 4)
    plan = [
        (values_ref.at[pl.ds(rows - 1, 1)], rows_land.at[0], up_device),
        (values_ref.at[pl.ds(0, 1)], rows_land.at[1], down_device),
        (values_ref.at[:, pl.ds(cols - 1, 1)], cols_land.at[0], east_device),
        (values_ref.at[:, pl.ds(0, 1)], cols_land.at[1], west_device),
    ]
    copies = []
    for slot, (source, target, device) in enumerate(plan):
        copy = pltpu.make_async_remote_copy(
            src_ref=source,
            dst_ref=target,
            send_sem=send_sems.at[slot],
            recv_sem=recv_sems.at[slot],
            device_id=device,
            device_id_type=MESH_IDS,
        )
        copy.start()
        copies.append(copy)
    for copy in copies:
        copy.wait_send()
    for copy in copies:
        copy.wait_recv()
    rows_out[...] = rows_land[...]
    cols_out[...] = cols_land[...]


def halo_edges(values, shape, collective):
    rows, cols, levels = values.shape
    return pl.pallas_call(
        functools.partial(halo_kernel, tuple(shape)),
        out_shape=(
            jax.ShapeDtypeStruct((2, 1, cols, levels), values.dtype),
            jax.ShapeDtypeStruct((2, rows, 1, levels), values.dtype),
        ),
        in_specs=[pl.BlockSpec(memory_space=pl.ANY)],
        out_specs=(
            pl.BlockSpec(memory_space=pltpu.VMEM),
            pl.BlockSpec(memory_space=pltpu.VMEM),
        ),
        scratch_shapes=[
            pltpu.VMEM((2, 1, cols, levels), values.dtype),
            pltpu.VMEM((2, rows, 1, levels), values.dtype),
            pltpu.SemaphoreType.DMA((4,)),
            pltpu.SemaphoreType.DMA((4,)),
        ],
        compiler_params=pltpu.CompilerParams(collective_id=collective, has_side_effects=True),
    )(values)


def local(
    state, land_mask, intersection_list, mix_atm, mix_ocn, flux_map, ocean_map, regrid_weights
):
    tile_rows, block_len, levels = state.shape
    flux_count = flux_map.shape[1]
    weight_count = regrid_weights.shape[0]
    intersections = intersection_list.shape[2]
    comp_count = lax.axis_size("comp")
    lat_count = lax.axis_size("lat")
    lon_count = lax.axis_size("lon")
    tile_count = lat_count * lon_count
    reach = min(4, lon_count)
    neighbour_count = 2 * reach
    capacity = intersections * tile_rows // neighbour_count
    width = flux_count * block_len
    comp_index = lax.axis_index("comp")
    tile_index = lax.axis_index("lat") * lon_count + lax.axis_index("lon")
    band = comp_index * lat_count + lax.axis_index("lat")
    ocean_band = (comp_count - 1) * lat_count
    ocean_side = comp_index == comp_count - 1
    lower_valid = (band > 0) & ((band - 1 >= ocean_band) == (band >= ocean_band))
    upper_valid = (band < comp_count * lat_count - 1) & (
        (band + 1 >= ocean_band) == (band >= ocean_band)
    )
    sea_cells = land_mask == 1

    mesh_shape = (comp_count, lat_count, lon_count)

    def halos(values, collective):
        rows, cols = halo_edges(values, mesh_shape, collective)
        top = jnp.where(lower_valid, rows[0], 0.0)
        bottom = jnp.where(upper_valid, rows[1], 0.0)
        return top, bottom, cols[0], cols[1]

    top, bottom, west, east = halos(state, 2)
    mixing = jnp.where(ocean_side, mix_ocn, mix_atm)
    first, first_planes = substep(state, top, bottom, west, east, mixing, comp_count)
    first_top = first_planes[0].reshape(tile_rows, block_len)
    state_top = first_planes[1].reshape(tile_rows, block_len)
    top, bottom, west, east = halos(first, 3)

    def atmosphere_second(values, top, bottom, west, east):
        moved, total = substep(values, top, bottom, west, east, mix_atm, comp_count, flux_map.T)
        total = total.reshape(flux_count, tile_rows, block_len)
        sent = jnp.where(sea_cells[None], 0.5 * total, 0.0).astype(jnp.bfloat16)
        return moved, sent

    def ocean_second(values, top, bottom, west, east):
        return values, jnp.zeros((flux_count, tile_rows, block_len), jnp.bfloat16)

    second, flux_sent = lax.cond(
        ocean_side, ocean_second, atmosphere_second, first, top, bottom, west, east
    )
    entry_list = intersection_list.reshape(tile_rows * intersections, 3)
    owners = entry_list[:, 0]
    targets = entry_list[:, 1]
    weight_ids = entry_list[:, 2]
    labels = weight_ids * tile_rows + targets
    entry_blocks = jnp.repeat(flux_sent.transpose(1, 0, 2), intersections, axis=0).reshape(
        tile_rows * intersections, width
    )
    lane = jnp.arange(128, dtype=jnp.int32)[None, :]
    label_lanes = jnp.where(
        lane == 0, weight_ids[:, None], jnp.where(lane == 1, targets[:, None], 0)
    ).astype(jnp.bfloat16)
    entry_blocks = jnp.concatenate([entry_blocks, label_lanes], axis=1)
    sending = jnp.broadcast_to(jnp.logical_not(ocean_side), owners.shape)
    offsets = [
        (n // reach * lon_count + n % reach - (reach - 1) // 2) % tile_count
        for n in range(neighbour_count)
    ]
    offset_table = jnp.array(offsets, jnp.int32)
    distance = (owners - tile_index + tile_count) % tile_count
    neighbour_ids = jnp.sum(
        jnp.where(
            distance[:, None] == offset_table[None, :],
            jnp.arange(neighbour_count, dtype=jnp.int32)[None, :],
            0,
        ),
        axis=1,
    )
    packed, _, entry_slots = pack_rows(entry_blocks, neighbour_ids, labels, sending, capacity, neighbour_count)
    arrived = gather_to_ocean(packed, offsets, mesh_shape)
    weights_low = regrid_weights
    weights_wide = regrid_weights.astype(jnp.float32)
    senders = (comp_count - 1) * neighbour_count

    def ocean_reply(values_top, arrived):
        flat = arrived.reshape(-1, width + 128)
        arrived_labels = flat[:, width].astype(jnp.int32) * tile_rows + flat[:, width + 1].astype(
            jnp.int32
        )
        fluxes = flat[:, :width].astype(jnp.float32).reshape(-1, flux_count, block_len)
        forcing = scatter_regrid(arrived_labels, fluxes, weights_low)
        forcing = forcing.reshape(tile_rows, flux_count, block_len).transpose(1, 0, 2)
        lifted = jnp.sum(forcing * ocean_map[:, 0][:, None, None], axis=0)
        top_level = jnp.where(sea_cells, values_top + lifted, state_top)
        table = jnp.einsum("db,wab->wda", top_level, weights_wide, precision=HIGHEST)
        replies = jnp.take(table.reshape(weight_count * tile_rows, block_len), arrived_labels, axis=0)
        return forcing, replies.reshape(senders, capacity, block_len), top_level

    def atmosphere_reply(values_top, arrived):
        return (
            jnp.zeros((flux_count, tile_rows, block_len), jnp.float32),
            jnp.zeros((senders, capacity, block_len), jnp.float32),
            values_top,
        )

    forcing, replies, ocean_top = lax.cond(
        ocean_side, ocean_reply, atmosphere_reply, first_top, arrived
    )
    atmosphere_top = lax.cond(
        ocean_side,
        lambda values: jnp.zeros((tile_rows, block_len), jnp.float32),
        lambda values: values[:, :, 0],
        second,
    )
    replies, atmosphere_top = lax.optimization_barrier((replies, atmosphere_top))
    answers = spread_from_ocean(replies, offsets, mesh_shape)
    per_entry = jnp.take(
        answers.reshape(neighbour_count * capacity, block_len), entry_slots, axis=0
    )
    returned = per_entry.reshape(tile_rows, intersections, block_len).sum(axis=1)
    second, forcing, answers = lax.optimization_barrier((second, forcing, answers))
    sea_rows = jnp.broadcast_to(
        sea_cells.astype(jnp.int32).reshape(1, tile_rows * block_len), (8, tile_rows * block_len)
    )
    final_state = ocean_update(
        second,
        state,
        sea_rows,
        forcing.reshape(flux_count, tile_rows * block_len),
        ocean_map,
        comp_count,
    )
    surface_out = jnp.where(
        ocean_side, ocean_top, jnp.where(sea_cells, returned, atmosphere_top)
    )
    return (final_state, surface_out)


def solution(mesh):
    placed = (
        P(("comp", "lat"), "lon", None),
        P(("comp", "lat"), "lon"),
        P(("comp", "lat"), "lon", None, None),
        P(),
        P(),
        P(),
        P(),
        P(),
    )
    return jax.shard_map(
        local,
        mesh=mesh,
        in_specs=placed,
        out_specs=(P(("comp", "lat"), "lon", None), P(("comp", "lat"), "lon")),
        check_vma=False,
    )
```

```python
import jax
import jax.numpy as jnp
from jax import lax
from jax.experimental import pallas as pl
from jax.experimental.pallas import tpu as pltpu
from jax.sharding import PartitionSpec as P
import functools

SMOOTHING = 0.2
PHYSICS = 0.5
HIGHEST = lax.Precision.HIGHEST
ROW_BLOCK = 16
UPDATE_BLOCK = 32


def split_bf16(values):
    high = values.astype(jnp.bfloat16)
    low = (values - high.astype(jnp.float32)).astype(jnp.bfloat16)
    return high, low


def three_pass(lhs, rhs, dims):
    lhs_hi, lhs_lo = split_bf16(lhs)
    rhs_hi, rhs_lo = split_bf16(rhs)

    def one(a, b):
        return lax.dot_general(a, b, (dims, ((), ())), preferred_element_type=jnp.float32)

    return one(lhs_hi, rhs_hi) + (one(lhs_hi, rhs_lo) + one(lhs_lo, rhs_hi))


def exact_rows(picker, values):
    high = values.astype(jnp.bfloat16)
    rest = values - high.astype(jnp.float32)
    middle = rest.astype(jnp.bfloat16)
    low = (rest - middle.astype(jnp.float32)).astype(jnp.bfloat16)

    def one(piece):
        return lax.dot_general(
            picker, piece, (((1,), (1,)), ((), ())), preferred_element_type=jnp.float32
        )

    return one(high) + one(middle) + one(low)


def substep_kernel(with_flux, comp_total, x_ref, top_ref, bottom_ref, west_ref, east_ref, mix_ref, *rest):
    if with_flux:
        fluxes_ref, out_ref, flux_out_ref = rest
    else:
        out_ref, planes_ref = rest
    rows, cols, levels = x_ref.shape
    centre = x_ref[...]
    up = jnp.concatenate([top_ref[...], centre[:-1]], axis=0)
    down = jnp.concatenate([centre[1:], bottom_ref[...]], axis=0)
    column = lax.broadcasted_iota(jnp.int32, centre.shape, 1)
    west = jnp.where(column == 0, west_ref[...], pltpu.roll(centre, 1, 1))
    east = jnp.where(column == cols - 1, east_ref[...], pltpu.roll(centre, cols - 1, 1))
    smooth = centre + SMOOTHING * (up + down + west + east - 4.0 * centre)
    flat = smooth.reshape(rows * cols, levels)
    mixed = three_pass(flat, mix_ref[...], ((1,), (0,)))
    moved = flat + PHYSICS * jnp.tanh(mixed)
    out_ref[...] = moved.reshape(rows, cols, levels)
    if not with_flux:
        ocean = lax.axis_index("comp") == comp_total - 1

        @pl.when(ocean)
        def _():
            plane_row = lax.broadcasted_iota(jnp.int32, (8, levels), 0)
            plane_lane = lax.broadcasted_iota(jnp.int32, (8, levels), 1)
            pick_out = ((plane_row == 0) & (plane_lane == 0)).astype(jnp.bfloat16)
            pick_in = ((plane_row == 1) & (plane_lane == 0)).astype(jnp.bfloat16)
            planes_ref[...] = exact_rows(pick_out, moved) + exact_rows(
                pick_in, centre.reshape(rows * cols, levels)
            )

        @pl.when(jnp.logical_not(ocean))
        def _():
            planes_ref[...] = jnp.zeros_like(planes_ref)

    else:
        total = centre.reshape(rows * cols, levels) + moved
        flux_out_ref[...] = three_pass(fluxes_ref[...], total, ((1,), (1,)))


def substep(values, top, bottom, west, east, mixing, comp_total, fluxes_t=None):
    rows, cols, levels = values.shape
    blocks = rows // ROW_BLOCK
    top_rows = jnp.concatenate([top, values[ROW_BLOCK - 1 : rows - 1 : ROW_BLOCK]], axis=0)
    bottom_rows = jnp.concatenate([values[ROW_BLOCK:rows:ROW_BLOCK], bottom], axis=0)
    with_flux = fluxes_t is not None
    in_specs = [
        pl.BlockSpec((ROW_BLOCK, cols, levels), lambda i: (i, 0, 0)),
        pl.BlockSpec((1, cols, levels), lambda i: (i, 0, 0)),
        pl.BlockSpec((1, cols, levels), lambda i: (i, 0, 0)),
        pl.BlockSpec((ROW_BLOCK, 1, levels), lambda i: (i, 0, 0)),
        pl.BlockSpec((ROW_BLOCK, 1, levels), lambda i: (i, 0, 0)),
        pl.BlockSpec((levels, levels), lambda i: (0, 0)),
    ]
    operands = [values, top_rows, bottom_rows, west, east, mixing]
    out_shape = [jax.ShapeDtypeStruct(values.shape, jnp.float32)]
    out_specs = [pl.BlockSpec((ROW_BLOCK, cols, levels), lambda i: (i, 0, 0))]
    if not with_flux:
        out_shape.append(jax.ShapeDtypeStruct((8, rows * cols), jnp.float32))
        out_specs.append(pl.BlockSpec((8, ROW_BLOCK * cols), lambda i: (0, i)))
    if with_flux:
        flux_count = fluxes_t.shape[0]
        in_specs.append(pl.BlockSpec((flux_count, levels), lambda i: (0, 0)))
        operands.append(fluxes_t)
        out_shape.append(jax.ShapeDtypeStruct((flux_count, rows * cols), jnp.float32))
        out_specs.append(pl.BlockSpec((flux_count, ROW_BLOCK * cols), lambda i: (0, i)))
    cells = rows * cols
    flops = 6 * cells * levels * levels + (6 * cells * levels * 8 if with_flux else 0)
    result = pl.pallas_call(
        functools.partial(substep_kernel, with_flux, comp_total),
        grid=(blocks,),
        in_specs=in_specs,
        out_specs=out_specs,
        out_shape=out_shape,
        cost_estimate=pl.CostEstimate(
            flops=flops, transcendentals=cells * levels, bytes_accessed=8 * cells * levels
        ),
    )(*operands)
    return result


def column_physics(values, mixing):
    return jnp.tanh(jnp.einsum("rck,kj->rcj", values, mixing, precision=HIGHEST))


def earlier_same(owners, usable):
    positions = jnp.arange(owners.shape[0], dtype=jnp.int32)
    before = (
        (owners[None, :] == owners[:, None])
        & (positions[None, :] < positions[:, None])
        & usable[None, :]
    )
    return jnp.sum(before.astype(jnp.int32), axis=1)


def pack_rows(blocks, owners, labels, usable, slots_each, owner_total):
    ranks = earlier_same(owners, usable)
    target_slot = owners * slots_each + ranks
    slot_ids = jnp.arange(owner_total * slots_each, dtype=jnp.int32)
    placing = (slot_ids[:, None] == target_slot[None, :]) & usable[None, :]
    packed = jnp.dot(
        placing.astype(jnp.bfloat16), blocks, preferred_element_type=jnp.float32
    ).astype(jnp.bfloat16)
    placed_labels = jnp.sum(jnp.where(placing, labels[None, :] + 1, 0), axis=1) - 1
    return (
        packed.reshape(owner_total, slots_each, blocks.shape[1]),
        placed_labels.reshape(owner_total, slots_each),
        target_slot,
    )


MESH_IDS = pl.DeviceIdType.MESH


def tile_device(comp, tile, lon_total):
    return (comp, tile // lon_total, tile % lon_total)


def gather_kernel(offsets, shape, send_ref, out_ref, land, send_sems, recv_sems):
    comp_total, lat_total, lon_total = shape
    comp = lax.axis_index("comp")
    tiles = lat_total * lon_total
    tile = lax.axis_index("lat") * lon_total + lax.axis_index("lon")
    ocean = comp_total - 1
    count = len(offsets)
    barrier = pltpu.get_barrier_semaphore()

    @pl.when(comp != ocean)
    def _():
        for off in offsets:
            target = tile_device(ocean, (tile + off) % tiles, lon_total)
            pl.semaphore_signal(barrier, 1, device_id=target, device_id_type=MESH_IDS)
        pl.semaphore_wait(barrier, count)
        copies = []
        for k, off in enumerate(offsets):
            target = tile_device(ocean, (tile + off) % tiles, lon_total)
            copy = pltpu.make_async_remote_copy(
                src_ref=send_ref.at[k],
                dst_ref=land.at[comp * count + k],
                send_sem=send_sems.at[k],
                recv_sem=recv_sems.at[comp * count + k],
                device_id=target,
                device_id_type=MESH_IDS,
            )
            copy.start()
            copies.append(copy)
        for copy in copies:
            copy.wait_send()
        out_ref[...] = jnp.zeros_like(out_ref)

    @pl.when(comp == ocean)
    def _():
        for source_comp in range(ocean):
            for off in offsets:
                source = tile_device(source_comp, (tile + tiles - off) % tiles, lon_total)
                pl.semaphore_signal(barrier, 1, device_id=source, device_id_type=MESH_IDS)
        pl.semaphore_wait(barrier, count * ocean)
        for source_comp in range(ocean):
            for k, off in enumerate(offsets):
                source = tile_device(source_comp, (tile + tiles - off) % tiles, lon_total)
                slot = source_comp * count + k
                pltpu.make_async_remote_copy(
                    src_ref=send_ref.at[k],
                    dst_ref=land.at[slot],
                    send_sem=send_sems.at[k],
                    recv_sem=recv_sems.at[slot],
                    device_id=source,
                    device_id_type=MESH_IDS,
                ).wait_recv()
        out_ref[...] = land[...]


def gather_to_ocean(blocks, offsets, shape):
    count = len(offsets)
    senders = (shape[0] - 1) * count
    slot_shape = blocks.shape[1:]
    return pl.pallas_call(
        functools.partial(gather_kernel, tuple(offsets), tuple(shape)),
        out_shape=jax.ShapeDtypeStruct((senders,) + slot_shape, blocks.dtype),
        in_specs=[pl.BlockSpec(memory_space=pltpu.VMEM)],
        out_specs=pl.BlockSpec(memory_space=pltpu.VMEM),
        scratch_shapes=[
            pltpu.VMEM((senders,) + slot_shape, blocks.dtype),
            pltpu.SemaphoreType.DMA((count,)),
            pltpu.SemaphoreType.DMA((senders,)),
        ],
        compiler_params=pltpu.CompilerParams(collective_id=0, has_side_effects=True),
    )(blocks)


def spread_kernel(offsets, shape, surface_ref, out_ref, land, send_sems, recv_sems):
    comp_total, lat_total, lon_total = shape
    comp = lax.axis_index("comp")
    tiles = lat_total * lon_total
    tile = lax.axis_index("lat") * lon_total + lax.axis_index("lon")
    ocean = comp_total - 1
    count = len(offsets)
    barrier = pltpu.get_barrier_semaphore()

    @pl.when(comp == ocean)
    def _():
        for target_comp in range(ocean):
            for off in offsets:
                target = tile_device(target_comp, (tile + tiles - off) % tiles, lon_total)
                pl.semaphore_signal(barrier, 1, device_id=target, device_id_type=MESH_IDS)
        pl.semaphore_wait(barrier, count * ocean)
        copies = []
        for target_comp in range(ocean):
            for k, off in enumerate(offsets):
                target = tile_device(target_comp, (tile + tiles - off) % tiles, lon_total)
                copy = pltpu.make_async_remote_copy(
                    src_ref=surface_ref.at[target_comp * count + k],
                    dst_ref=land.at[k],
                    send_sem=send_sems.at[target_comp * count + k],
                    recv_sem=recv_sems.at[k],
                    device_id=target,
                    device_id_type=MESH_IDS,
                )
                copy.start()
                copies.append(copy)
        for copy in copies:
            copy.wait_send()
        out_ref[...] = jnp.zeros_like(out_ref)

    @pl.when(comp != ocean)
    def _():
        for off in offsets:
            source = tile_device(ocean, (tile + off) % tiles, lon_total)
            pl.semaphore_signal(barrier, 1, device_id=source, device_id_type=MESH_IDS)
        pl.semaphore_wait(barrier, count)
        for k, off in enumerate(offsets):
            source = tile_device(ocean, (tile + off) % tiles, lon_total)
            pltpu.make_async_remote_copy(
                src_ref=surface_ref.at[k],
                dst_ref=land.at[k],
                send_sem=send_sems.at[k],
                recv_sem=recv_sems.at[k],
                device_id=source,
                device_id_type=MESH_IDS,
            ).wait_recv()
        out_ref[...] = land[...]


def spread_from_ocean(replies, offsets, shape):
    count = len(offsets)
    senders = (shape[0] - 1) * count
    slot_shape = replies.shape[1:]
    return pl.pallas_call(
        functools.partial(spread_kernel, tuple(offsets), tuple(shape)),
        out_shape=jax.ShapeDtypeStruct((count,) + slot_shape, replies.dtype),
        in_specs=[pl.BlockSpec(memory_space=pltpu.VMEM)],
        out_specs=pl.BlockSpec(memory_space=pltpu.VMEM),
        scratch_shapes=[
            pltpu.VMEM((count,) + slot_shape, replies.dtype),
            pltpu.SemaphoreType.DMA((senders,)),
            pltpu.SemaphoreType.DMA((count,)),
        ],
        compiler_params=pltpu.CompilerParams(collective_id=1, has_side_effects=True),
    )(replies)


def ocean_update_kernel(flag_ref, base_ref, state_ref, sea_ref, forcing_ref, spread_ref, out_ref):
    rows, cols, levels = base_ref.shape
    flux_count = forcing_ref.shape[0]

    def block(base_block, state_block, sea_block, forcing_block, out_block):
        ocean_block(base_block, state_block, sea_block, forcing_block, spread_ref, out_block)

    @pl.when(flag_ref[0] == 1)
    def _():
        pltpu.emit_pipeline(
            block,
            grid=(rows // UPDATE_BLOCK,),
            in_specs=[
                pl.BlockSpec((UPDATE_BLOCK, cols, levels), lambda i: (i, 0, 0)),
                pl.BlockSpec((UPDATE_BLOCK, cols, levels), lambda i: (i, 0, 0)),
                pl.BlockSpec((8, UPDATE_BLOCK * cols), lambda i: (0, i)),
                pl.BlockSpec((flux_count, UPDATE_BLOCK * cols), lambda i: (0, i)),
            ],
            out_specs=[pl.BlockSpec((UPDATE_BLOCK, cols, levels), lambda i: (i, 0, 0))],
        )(base_ref, state_ref, sea_ref, forcing_ref, out_ref)


def ocean_block(first_ref, state_ref, sea_ref, forcing_ref, spread_ref, out_ref):
    rows, cols, levels = first_ref.shape
    forcing = forcing_ref[...]
    spread = spread_ref[...]
    forcing_hi = forcing.astype(jnp.bfloat16)
    forcing_lo = (forcing - forcing_hi.astype(jnp.float32)).astype(jnp.bfloat16)
    spread_hi = spread.astype(jnp.bfloat16)
    spread_lo = (spread - spread_hi.astype(jnp.float32)).astype(jnp.bfloat16)

    def one(a, b):
        return lax.dot_general(a, b, (((0,), (0,)), ((), ())), preferred_element_type=jnp.float32)

    stacked = jnp.concatenate(
        [forcing_hi.astype(jnp.float32), forcing_hi.astype(jnp.float32), forcing_lo.astype(jnp.float32)],
        axis=0,
    ).astype(jnp.bfloat16)
    spread_stack = jnp.concatenate(
        [spread_hi.astype(jnp.float32), spread_lo.astype(jnp.float32), spread_hi.astype(jnp.float32)],
        axis=0,
    ).astype(jnp.bfloat16)
    added = one(stacked, spread_stack)
    lane_row = lax.broadcasted_iota(jnp.int32, (8, levels), 0)
    ones = (lane_row == 0).astype(jnp.bfloat16)
    picks = jnp.where(lax.broadcasted_iota(jnp.int32, sea_ref.shape, 0) == 0, sea_ref[...], 0)
    mask = one(picks.astype(jnp.bfloat16), ones)
    moved = first_ref[...].reshape(rows * cols, levels) + added
    kept = jnp.where(mask > 0.5, moved, state_ref[...].reshape(rows * cols, levels))
    out_ref[...] = kept.reshape(rows, cols, levels)


def ocean_update(first, state, sea_rows, forcing, ocean_map, comp_total):
    rows, cols, levels = first.shape
    flux_count = forcing.shape[0]
    cells = rows * cols
    flag = (lax.axis_index("comp") == comp_total - 1).astype(jnp.int32).reshape(1)
    return pl.pallas_call(
        ocean_update_kernel,
        out_shape=jax.ShapeDtypeStruct(first.shape, jnp.float32),
        in_specs=[
            pl.BlockSpec(memory_space=pltpu.SMEM),
            pl.BlockSpec(memory_space=pl.ANY),
            pl.BlockSpec(memory_space=pl.ANY),
            pl.BlockSpec(memory_space=pl.ANY),
            pl.BlockSpec(memory_space=pl.ANY),
            pl.BlockSpec(memory_space=pltpu.VMEM),
        ],
        out_specs=pl.BlockSpec(memory_space=pl.ANY),
        input_output_aliases={1: 0},
        cost_estimate=pl.CostEstimate(
            flops=8 * cells * levels * flux_count, transcendentals=0, bytes_accessed=12 * cells * levels
        ),
    )(flag, first, state, sea_rows, forcing, ocean_map)


def scatter_regrid_kernel(labels_ref, fluxes_ref, weights_ref, out_ref, binned_ref):
    entries = fluxes_ref.shape[0]
    weight_count, tile_rows, block_len = weights_ref.shape
    flux_count = fluxes_ref.shape[1]
    binned_ref[...] = jnp.zeros_like(binned_ref)

    def add_one(e, carry):
        label = labels_ref[e]
        binned_ref[label] = binned_ref[label] + fluxes_ref[e]
        return carry

    lax.fori_loop(0, entries, add_one, 0, unroll=8)
    out_ref[...] = jnp.zeros_like(out_ref)

    def regrid_one(w, carry):
        start = pl.multiple_of(w * tile_rows, tile_rows)
        block = binned_ref[pl.ds(start, tile_rows)].reshape(tile_rows * flux_count, block_len)
        high = block.astype(jnp.bfloat16)
        low = (block - high.astype(jnp.float32)).astype(jnp.bfloat16)
        weight = weights_ref[w]
        out_ref[...] += jnp.dot(high, weight, preferred_element_type=jnp.float32) + jnp.dot(
            low, weight, preferred_element_type=jnp.float32
        )
        return carry

    lax.fori_loop(0, weight_count, regrid_one, 0)


def scatter_regrid(labels, fluxes, weights):
    entries, flux_count, block_len = fluxes.shape
    weight_count, tile_rows, _ = weights.shape
    return pl.pallas_call(
        scatter_regrid_kernel,
        out_shape=jax.ShapeDtypeStruct((tile_rows * flux_count, block_len), jnp.float32),
        in_specs=[
            pl.BlockSpec(memory_space=pltpu.SMEM),
            pl.BlockSpec(memory_space=pltpu.VMEM),
            pl.BlockSpec(memory_space=pltpu.VMEM),
        ],
        out_specs=pl.BlockSpec(memory_space=pltpu.VMEM),
        scratch_shapes=[pltpu.VMEM((weight_count * tile_rows, flux_count, block_len), jnp.float32)],
        compiler_params=pltpu.CompilerParams(vmem_limit_bytes=48 * 1024 * 1024),
        cost_estimate=pl.CostEstimate(
            flops=4 * weight_count * tile_rows * flux_count * block_len * block_len,
            transcendentals=0,
            bytes_accessed=entries * flux_count * block_len * 4 + weight_count * tile_rows * block_len * 2,
        ),
    )(labels, fluxes, weights)


def halo_kernel(shape, values_ref, rows_out, cols_out, rows_land, cols_land, send_sems, recv_sems):
    comp_total, lat_total, lon_total = shape
    bands = comp_total * lat_total
    band = lax.axis_index("comp") * lat_total + lax.axis_index("lat")
    lon = lax.axis_index("lon")
    rows, cols, _ = values_ref.shape
    up = (band + 1) % bands
    down = (band + bands - 1) % bands
    up_device = (up // lat_total, up % lat_total, lon)
    down_device = (down // lat_total, down % lat_total, lon)
    east_device = (band // lat_total, band % lat_total, (lon + 1) % lon_total)
    west_device = (band // lat_total, band % lat_total, (lon + lon_total - 1) % lon_total)
    barrier = pltpu.get_barrier_semaphore()
    for device in (up_device, down_device, east_device, west_device):
        pl.semaphore_signal(barrier, 1, device_id=device, device_id_type=MESH_IDS)
    pl.semaphore_wait(barrier, 4)
    plan = [
        (values_ref.at[pl.ds(rows - 1, 1)], rows_land.at[0], up_device),
        (values_ref.at[pl.ds(0, 1)], rows_land.at[1], down_device),
        (values_ref.at[:, pl.ds(cols - 1, 1)], cols_land.at[0], east_device),
        (values_ref.at[:, pl.ds(0, 1)], cols_land.at[1], west_device),
    ]
    copies = []
    for slot, (source, target, device) in enumerate(plan):
        copy = pltpu.make_async_remote_copy(
            src_ref=source,
            dst_ref=target,
            send_sem=send_sems.at[slot],
            recv_sem=recv_sems.at[slot],
            device_id=device,
            device_id_type=MESH_IDS,
        )
        copy.start()
        copies.append(copy)
    for copy in copies:
        copy.wait_send()
    for copy in copies:
        copy.wait_recv()
    rows_out[...] = rows_land[...]
    cols_out[...] = cols_land[...]


def halo_edges(values, shape, collective):
    rows, cols, levels = values.shape
    return pl.pallas_call(
        functools.partial(halo_kernel, tuple(shape)),
        out_shape=(
            jax.ShapeDtypeStruct((2, 1, cols, levels), values.dtype),
            jax.ShapeDtypeStruct((2, rows, 1, levels), values.dtype),
        ),
        in_specs=[pl.BlockSpec(memory_space=pl.ANY)],
        out_specs=(
            pl.BlockSpec(memory_space=pltpu.VMEM),
            pl.BlockSpec(memory_space=pltpu.VMEM),
        ),
        scratch_shapes=[
            pltpu.VMEM((2, 1, cols, levels), values.dtype),
            pltpu.VMEM((2, rows, 1, levels), values.dtype),
            pltpu.SemaphoreType.DMA((4,)),
            pltpu.SemaphoreType.DMA((4,)),
        ],
        compiler_params=pltpu.CompilerParams(collective_id=collective, has_side_effects=True),
    )(values)


def local(
    state, land_mask, intersection_list, mix_atm, mix_ocn, flux_map, ocean_map, regrid_weights
):
    tile_rows, block_len, levels = state.shape
    flux_count = flux_map.shape[1]
    weight_count = regrid_weights.shape[0]
    intersections = intersection_list.shape[2]
    comp_count = lax.axis_size("comp")
    lat_count = lax.axis_size("lat")
    lon_count = lax.axis_size("lon")
    tile_count = lat_count * lon_count
    reach = min(4, lon_count)
    neighbour_count = 2 * reach
    capacity = intersections * tile_rows // neighbour_count
    width = flux_count * block_len
    comp_index = lax.axis_index("comp")
    tile_index = lax.axis_index("lat") * lon_count + lax.axis_index("lon")
    band = comp_index * lat_count + lax.axis_index("lat")
    ocean_band = (comp_count - 1) * lat_count
    ocean_side = comp_index == comp_count - 1
    lower_valid = (band > 0) & ((band - 1 >= ocean_band) == (band >= ocean_band))
    upper_valid = (band < comp_count * lat_count - 1) & (
        (band + 1 >= ocean_band) == (band >= ocean_band)
    )
    sea_cells = land_mask == 1

    mesh_shape = (comp_count, lat_count, lon_count)

    def halos(values, collective):
        rows, cols = halo_edges(values, mesh_shape, collective)
        top = jnp.where(lower_valid, rows[0], 0.0)
        bottom = jnp.where(upper_valid, rows[1], 0.0)
        return top, bottom, cols[0], cols[1]

    top, bottom, west, east = halos(state, 2)
    mixing = jnp.where(ocean_side, mix_ocn, mix_atm)
    first, first_planes = substep(state, top, bottom, west, east, mixing, comp_count)
    first_top = first_planes[0].reshape(tile_rows, block_len)
    state_top = first_planes[1].reshape(tile_rows, block_len)
    top, bottom, west, east = halos(first, 3)

    def atmosphere_second(values, top, bottom, west, east):
        moved, total = substep(values, top, bottom, west, east, mix_atm, comp_count, flux_map.T)
        total = total.reshape(flux_count, tile_rows, block_len)
        sent = jnp.where(sea_cells[None], 0.5 * total, 0.0).astype(jnp.bfloat16)
        return moved, sent

    def ocean_second(values, top, bottom, west, east):
        return values, jnp.zeros((flux_count, tile_rows, block_len), jnp.bfloat16)

    second, flux_sent = lax.cond(
        ocean_side, ocean_second, atmosphere_second, first, top, bottom, west, east
    )
    entry_list = intersection_list.reshape(tile_rows * intersections, 3)
    owners = entry_list[:, 0]
    targets = entry_list[:, 1]
    weight_ids = entry_list[:, 2]
    labels = weight_ids * tile_rows + targets
    entry_blocks = jnp.repeat(flux_sent.transpose(1, 0, 2), intersections, axis=0).reshape(
        tile_rows * intersections, width
    )
    lane = jnp.arange(128, dtype=jnp.int32)[None, :]
    label_lanes = jnp.where(
        lane == 0, weight_ids[:, None], jnp.where(lane == 1, targets[:, None], 0)
    ).astype(jnp.bfloat16)
    entry_blocks = jnp.concatenate([entry_blocks, label_lanes], axis=1)
    sending = jnp.broadcast_to(jnp.logical_not(ocean_side), owners.shape)
    offsets = [
        (n // reach * lon_count + n % reach - (reach - 1) // 2) % tile_count
        for n in range(neighbour_count)
    ]
    offset_table = jnp.array(offsets, jnp.int32)
    distance = (owners - tile_index + tile_count) % tile_count
    neighbour_ids = jnp.sum(
        jnp.where(
            distance[:, None] == offset_table[None, :],
            jnp.arange(neighbour_count, dtype=jnp.int32)[None, :],
            0,
        ),
        axis=1,
    )
    packed, _, entry_slots = pack_rows(entry_blocks, neighbour_ids, labels, sending, capacity, neighbour_count)
    arrived = gather_to_ocean(packed, offsets, mesh_shape)
    weights_low = regrid_weights
    weights_wide = regrid_weights.astype(jnp.float32)
    senders = (comp_count - 1) * neighbour_count

    def ocean_reply(values_top, arrived):
        flat = arrived.reshape(-1, width + 128)
        arrived_labels = flat[:, width].astype(jnp.int32) * tile_rows + flat[:, width + 1].astype(
            jnp.int32
        )
        fluxes = flat[:, :width].astype(jnp.float32).reshape(-1, flux_count, block_len)
        forcing = scatter_regrid(arrived_labels, fluxes, weights_low)
        forcing = forcing.reshape(tile_rows, flux_count, block_len).transpose(1, 0, 2)
        lifted = jnp.sum(forcing * ocean_map[:, 0][:, None, None], axis=0)
        top_level = jnp.where(sea_cells, values_top + lifted, state_top)
        table = jnp.einsum("db,wab->wda", top_level, weights_wide, precision=HIGHEST)
        replies = jnp.take(table.reshape(weight_count * tile_rows, block_len), arrived_labels, axis=0)
        return forcing, replies.reshape(senders, capacity, block_len), top_level

    def atmosphere_reply(values_top, arrived):
        return (
            jnp.zeros((flux_count, tile_rows, block_len), jnp.float32),
            jnp.zeros((senders, capacity, block_len), jnp.float32),
            values_top,
        )

    forcing, replies, ocean_top = lax.cond(
        ocean_side, ocean_reply, atmosphere_reply, first_top, arrived
    )
    atmosphere_top = lax.cond(
        ocean_side,
        lambda values: jnp.zeros((tile_rows, block_len), jnp.float32),
        lambda values: values[:, :, 0],
        second,
    )
    replies, atmosphere_top = lax.optimization_barrier((replies, atmosphere_top))
    answers = spread_from_ocean(replies, offsets, mesh_shape)
    per_entry = jnp.take(
        answers.reshape(neighbour_count * capacity, block_len), entry_slots, axis=0
    )
    returned = per_entry.reshape(tile_rows, intersections, block_len).sum(axis=1)
    second, forcing, answers = lax.optimization_barrier((second, forcing, answers))
    sea_rows = jnp.broadcast_to(
        sea_cells.astype(jnp.int32).reshape(1, tile_rows * block_len), (8, tile_rows * block_len)
    )
    final_state = ocean_update(
        second,
        state,
        sea_rows,
        forcing.reshape(flux_count, tile_rows * block_len),
        ocean_map,
        comp_count,
    )
    surface_out = jnp.where(
        ocean_side, ocean_top, jnp.where(sea_cells, returned, atmosphere_top)
    )
    return (final_state, surface_out)


def solution(mesh):
    placed = (
        P(("comp", "lat"), "lon", None),
        P(("comp", "lat"), "lon"),
        P(("comp", "lat"), "lon", None, None),
        P(),
        P(),
        P(),
        P(),
        P(),
    )
    return jax.shard_map(
        local,
        mesh=mesh,
        in_specs=placed,
        out_specs=(P(("comp", "lat"), "lon", None), P(("comp", "lat"), "lon")),
        check_vma=False,
    )
```

```python
import jax
import jax.numpy as jnp
from jax import lax
from jax.experimental import pallas as pl
from jax.experimental.pallas import tpu as pltpu
from jax.sharding import PartitionSpec as P
import functools

SMOOTHING = 0.2
PHYSICS = 0.5
HIGHEST = lax.Precision.HIGHEST
ROW_BLOCK = 32
UPDATE_BLOCK = 32


def split_bf16(values):
    high = values.astype(jnp.bfloat16)
    low = (values - high.astype(jnp.float32)).astype(jnp.bfloat16)
    return high, low


def three_pass(lhs, rhs, dims):
    lhs_hi, lhs_lo = split_bf16(lhs)
    rhs_hi, rhs_lo = split_bf16(rhs)

    def one(a, b):
        return lax.dot_general(a, b, (dims, ((), ())), preferred_element_type=jnp.float32)

    return one(lhs_hi, rhs_hi) + (one(lhs_hi, rhs_lo) + one(lhs_lo, rhs_hi))


def exact_rows(picker, values):
    high = values.astype(jnp.bfloat16)
    rest = values - high.astype(jnp.float32)
    middle = rest.astype(jnp.bfloat16)
    low = (rest - middle.astype(jnp.float32)).astype(jnp.bfloat16)

    def one(piece):
        return lax.dot_general(
            picker, piece, (((1,), (1,)), ((), ())), preferred_element_type=jnp.float32
        )

    return one(high) + one(middle) + one(low)


def substep_kernel(with_flux, comp_total, x_ref, top_ref, bottom_ref, west_ref, east_ref, mix_ref, *rest):
    if with_flux:
        fluxes_ref, out_ref, flux_out_ref = rest
    else:
        out_ref, planes_ref = rest
    rows, cols, levels = x_ref.shape
    centre = x_ref[...]
    up = jnp.concatenate([top_ref[...], centre[:-1]], axis=0)
    down = jnp.concatenate([centre[1:], bottom_ref[...]], axis=0)
    column = lax.broadcasted_iota(jnp.int32, centre.shape, 1)
    west = jnp.where(column == 0, west_ref[...], pltpu.roll(centre, 1, 1))
    east = jnp.where(column == cols - 1, east_ref[...], pltpu.roll(centre, cols - 1, 1))
    smooth = centre + SMOOTHING * (up + down + west + east - 4.0 * centre)
    flat = smooth.reshape(rows * cols, levels)
    mixed = three_pass(flat, mix_ref[...], ((1,), (0,)))
    moved = flat + PHYSICS * jnp.tanh(mixed)
    out_ref[...] = moved.reshape(rows, cols, levels)
    if not with_flux:
        ocean = lax.axis_index("comp") == comp_total - 1

        @pl.when(ocean)
        def _():
            plane_row = lax.broadcasted_iota(jnp.int32, (8, levels), 0)
            plane_lane = lax.broadcasted_iota(jnp.int32, (8, levels), 1)
            pick_out = ((plane_row == 0) & (plane_lane == 0)).astype(jnp.bfloat16)
            pick_in = ((plane_row == 1) & (plane_lane == 0)).astype(jnp.bfloat16)
            planes_ref[...] = exact_rows(pick_out, moved) + exact_rows(
                pick_in, centre.reshape(rows * cols, levels)
            )

        @pl.when(jnp.logical_not(ocean))
        def _():
            planes_ref[...] = jnp.zeros_like(planes_ref)

    else:
        total = centre.reshape(rows * cols, levels) + moved
        flux_out_ref[...] = three_pass(fluxes_ref[...], total, ((1,), (1,)))


def substep(values, top, bottom, west, east, mixing, comp_total, fluxes_t=None):
    rows, cols, levels = values.shape
    blocks = rows // ROW_BLOCK
    top_rows = jnp.concatenate([top, values[ROW_BLOCK - 1 : rows - 1 : ROW_BLOCK]], axis=0)
    bottom_rows = jnp.concatenate([values[ROW_BLOCK:rows:ROW_BLOCK], bottom], axis=0)
    with_flux = fluxes_t is not None
    in_specs = [
        pl.BlockSpec((ROW_BLOCK, cols, levels), lambda i: (i, 0, 0)),
        pl.BlockSpec((1, cols, levels), lambda i: (i, 0, 0)),
        pl.BlockSpec((1, cols, levels), lambda i: (i, 0, 0)),
        pl.BlockSpec((ROW_BLOCK, 1, levels), lambda i: (i, 0, 0)),
        pl.BlockSpec((ROW_BLOCK, 1, levels), lambda i: (i, 0, 0)),
        pl.BlockSpec((levels, levels), lambda i: (0, 0)),
    ]
    operands = [values, top_rows, bottom_rows, west, east, mixing]
    out_shape = [jax.ShapeDtypeStruct(values.shape, jnp.float32)]
    out_specs = [pl.BlockSpec((ROW_BLOCK, cols, levels), lambda i: (i, 0, 0))]
    if not with_flux:
        out_shape.append(jax.ShapeDtypeStruct((8, rows * cols), jnp.float32))
        out_specs.append(pl.BlockSpec((8, ROW_BLOCK * cols), lambda i: (0, i)))
    if with_flux:
        flux_count = fluxes_t.shape[0]
        in_specs.append(pl.BlockSpec((flux_count, levels), lambda i: (0, 0)))
        operands.append(fluxes_t)
        out_shape.append(jax.ShapeDtypeStruct((flux_count, rows * cols), jnp.float32))
        out_specs.append(pl.BlockSpec((flux_count, ROW_BLOCK * cols), lambda i: (0, i)))
    cells = rows * cols
    flops = 6 * cells * levels * levels + (6 * cells * levels * 8 if with_flux else 0)
    result = pl.pallas_call(
        functools.partial(substep_kernel, with_flux, comp_total),
        grid=(blocks,),
        in_specs=in_specs,
        out_specs=out_specs,
        out_shape=out_shape,
        cost_estimate=pl.CostEstimate(
            flops=flops, transcendentals=cells * levels, bytes_accessed=8 * cells * levels
        ),
    )(*operands)
    return result


def column_physics(values, mixing):
    return jnp.tanh(jnp.einsum("rck,kj->rcj", values, mixing, precision=HIGHEST))


def earlier_same(owners, usable):
    positions = jnp.arange(owners.shape[0], dtype=jnp.int32)
    before = (
        (owners[None, :] == owners[:, None])
        & (positions[None, :] < positions[:, None])
        & usable[None, :]
    )
    return jnp.sum(before.astype(jnp.int32), axis=1)


def pack_rows(blocks, owners, labels, usable, slots_each, owner_total):
    ranks = earlier_same(owners, usable)
    target_slot = owners * slots_each + ranks
    slot_ids = jnp.arange(owner_total * slots_each, dtype=jnp.int32)
    placing = (slot_ids[:, None] == target_slot[None, :]) & usable[None, :]
    packed = jnp.dot(
        placing.astype(jnp.bfloat16), blocks, preferred_element_type=jnp.float32
    ).astype(jnp.bfloat16)
    placed_labels = jnp.sum(jnp.where(placing, labels[None, :] + 1, 0), axis=1) - 1
    return (
        packed.reshape(owner_total, slots_each, blocks.shape[1]),
        placed_labels.reshape(owner_total, slots_each),
        target_slot,
    )


MESH_IDS = pl.DeviceIdType.MESH


def tile_device(comp, tile, lon_total):
    return (comp, tile // lon_total, tile % lon_total)


def gather_kernel(offsets, shape, send_ref, out_ref, land, send_sems, recv_sems):
    comp_total, lat_total, lon_total = shape
    comp = lax.axis_index("comp")
    tiles = lat_total * lon_total
    tile = lax.axis_index("lat") * lon_total + lax.axis_index("lon")
    ocean = comp_total - 1
    count = len(offsets)
    barrier = pltpu.get_barrier_semaphore()

    @pl.when(comp != ocean)
    def _():
        for off in offsets:
            target = tile_device(ocean, (tile + off) % tiles, lon_total)
            pl.semaphore_signal(barrier, 1, device_id=target, device_id_type=MESH_IDS)
        pl.semaphore_wait(barrier, count)
        copies = []
        for k, off in enumerate(offsets):
            target = tile_device(ocean, (tile + off) % tiles, lon_total)
            copy = pltpu.make_async_remote_copy(
                src_ref=send_ref.at[k],
                dst_ref=land.at[comp * count + k],
                send_sem=send_sems.at[k],
                recv_sem=recv_sems.at[comp * count + k],
                device_id=target,
                device_id_type=MESH_IDS,
            )
            copy.start()
            copies.append(copy)
        for copy in copies:
            copy.wait_send()
        out_ref[...] = jnp.zeros_like(out_ref)

    @pl.when(comp == ocean)
    def _():
        for source_comp in range(ocean):
            for off in offsets:
                source = tile_device(source_comp, (tile + tiles - off) % tiles, lon_total)
                pl.semaphore_signal(barrier, 1, device_id=source, device_id_type=MESH_IDS)
        pl.semaphore_wait(barrier, count * ocean)
        for source_comp in range(ocean):
            for k, off in enumerate(offsets):
                source = tile_device(source_comp, (tile + tiles - off) % tiles, lon_total)
                slot = source_comp * count + k
                pltpu.make_async_remote_copy(
                    src_ref=send_ref.at[k],
                    dst_ref=land.at[slot],
                    send_sem=send_sems.at[k],
                    recv_sem=recv_sems.at[slot],
                    device_id=source,
                    device_id_type=MESH_IDS,
                ).wait_recv()
        out_ref[...] = land[...]


def gather_to_ocean(blocks, offsets, shape):
    count = len(offsets)
    senders = (shape[0] - 1) * count
    slot_shape = blocks.shape[1:]
    return pl.pallas_call(
        functools.partial(gather_kernel, tuple(offsets), tuple(shape)),
        out_shape=jax.ShapeDtypeStruct((senders,) + slot_shape, blocks.dtype),
        in_specs=[pl.BlockSpec(memory_space=pltpu.VMEM)],
        out_specs=pl.BlockSpec(memory_space=pltpu.VMEM),
        scratch_shapes=[
            pltpu.VMEM((senders,) + slot_shape, blocks.dtype),
            pltpu.SemaphoreType.DMA((count,)),
            pltpu.SemaphoreType.DMA((senders,)),
        ],
        compiler_params=pltpu.CompilerParams(collective_id=0, has_side_effects=True),
    )(blocks)


def spread_kernel(offsets, shape, surface_ref, out_ref, land, send_sems, recv_sems):
    comp_total, lat_total, lon_total = shape
    comp = lax.axis_index("comp")
    tiles = lat_total * lon_total
    tile = lax.axis_index("lat") * lon_total + lax.axis_index("lon")
    ocean = comp_total - 1
    count = len(offsets)
    barrier = pltpu.get_barrier_semaphore()

    @pl.when(comp == ocean)
    def _():
        for target_comp in range(ocean):
            for off in offsets:
                target = tile_device(target_comp, (tile + tiles - off) % tiles, lon_total)
                pl.semaphore_signal(barrier, 1, device_id=target, device_id_type=MESH_IDS)
        pl.semaphore_wait(barrier, count * ocean)
        copies = []
        for target_comp in range(ocean):
            for k, off in enumerate(offsets):
                target = tile_device(target_comp, (tile + tiles - off) % tiles, lon_total)
                copy = pltpu.make_async_remote_copy(
                    src_ref=surface_ref.at[target_comp * count + k],
                    dst_ref=land.at[k],
                    send_sem=send_sems.at[target_comp * count + k],
                    recv_sem=recv_sems.at[k],
                    device_id=target,
                    device_id_type=MESH_IDS,
                )
                copy.start()
                copies.append(copy)
        for copy in copies:
            copy.wait_send()
        out_ref[...] = jnp.zeros_like(out_ref)

    @pl.when(comp != ocean)
    def _():
        for off in offsets:
            source = tile_device(ocean, (tile + off) % tiles, lon_total)
            pl.semaphore_signal(barrier, 1, device_id=source, device_id_type=MESH_IDS)
        pl.semaphore_wait(barrier, count)
        for k, off in enumerate(offsets):
            source = tile_device(ocean, (tile + off) % tiles, lon_total)
            pltpu.make_async_remote_copy(
                src_ref=surface_ref.at[k],
                dst_ref=land.at[k],
                send_sem=send_sems.at[k],
                recv_sem=recv_sems.at[k],
                device_id=source,
                device_id_type=MESH_IDS,
            ).wait_recv()
        out_ref[...] = land[...]


def spread_from_ocean(replies, offsets, shape):
    count = len(offsets)
    senders = (shape[0] - 1) * count
    slot_shape = replies.shape[1:]
    return pl.pallas_call(
        functools.partial(spread_kernel, tuple(offsets), tuple(shape)),
        out_shape=jax.ShapeDtypeStruct((count,) + slot_shape, replies.dtype),
        in_specs=[pl.BlockSpec(memory_space=pltpu.VMEM)],
        out_specs=pl.BlockSpec(memory_space=pltpu.VMEM),
        scratch_shapes=[
            pltpu.VMEM((count,) + slot_shape, replies.dtype),
            pltpu.SemaphoreType.DMA((senders,)),
            pltpu.SemaphoreType.DMA((count,)),
        ],
        compiler_params=pltpu.CompilerParams(collective_id=1, has_side_effects=True),
    )(replies)


def ocean_update_kernel(flag_ref, base_ref, state_ref, sea_ref, forcing_ref, spread_ref, out_ref):
    rows, cols, levels = base_ref.shape
    flux_count = forcing_ref.shape[0]

    def block(base_block, state_block, sea_block, forcing_block, out_block):
        ocean_block(base_block, state_block, sea_block, forcing_block, spread_ref, out_block)

    @pl.when(flag_ref[0] == 1)
    def _():
        pltpu.emit_pipeline(
            block,
            grid=(rows // UPDATE_BLOCK,),
            in_specs=[
                pl.BlockSpec((UPDATE_BLOCK, cols, levels), lambda i: (i, 0, 0)),
                pl.BlockSpec((UPDATE_BLOCK, cols, levels), lambda i: (i, 0, 0)),
                pl.BlockSpec((8, UPDATE_BLOCK * cols), lambda i: (0, i)),
                pl.BlockSpec((flux_count, UPDATE_BLOCK * cols), lambda i: (0, i)),
            ],
            out_specs=[pl.BlockSpec((UPDATE_BLOCK, cols, levels), lambda i: (i, 0, 0))],
        )(base_ref, state_ref, sea_ref, forcing_ref, out_ref)


def ocean_block(first_ref, state_ref, sea_ref, forcing_ref, spread_ref, out_ref):
    rows, cols, levels = first_ref.shape
    forcing = forcing_ref[...]
    spread = spread_ref[...]
    forcing_hi = forcing.astype(jnp.bfloat16)
    forcing_lo = (forcing - forcing_hi.astype(jnp.float32)).astype(jnp.bfloat16)
    spread_hi = spread.astype(jnp.bfloat16)
    spread_lo = (spread - spread_hi.astype(jnp.float32)).astype(jnp.bfloat16)

    def one(a, b):
        return lax.dot_general(a, b, (((0,), (0,)), ((), ())), preferred_element_type=jnp.float32)

    stacked = jnp.concatenate(
        [forcing_hi.astype(jnp.float32), forcing_hi.astype(jnp.float32), forcing_lo.astype(jnp.float32)],
        axis=0,
    ).astype(jnp.bfloat16)
    spread_stack = jnp.concatenate(
        [spread_hi.astype(jnp.float32), spread_lo.astype(jnp.float32), spread_hi.astype(jnp.float32)],
        axis=0,
    ).astype(jnp.bfloat16)
    added = one(stacked, spread_stack)
    lane_row = lax.broadcasted_iota(jnp.int32, (8, levels), 0)
    ones = (lane_row == 0).astype(jnp.bfloat16)
    picks = jnp.where(lax.broadcasted_iota(jnp.int32, sea_ref.shape, 0) == 0, sea_ref[...], 0)
    mask = one(picks.astype(jnp.bfloat16), ones)
    moved = first_ref[...].reshape(rows * cols, levels) + added
    kept = jnp.where(mask > 0.5, moved, state_ref[...].reshape(rows * cols, levels))
    out_ref[...] = kept.reshape(rows, cols, levels)


def ocean_update(first, state, sea_rows, forcing, ocean_map, comp_total):
    rows, cols, levels = first.shape
    flux_count = forcing.shape[0]
    cells = rows * cols
    flag = (lax.axis_index("comp") == comp_total - 1).astype(jnp.int32).reshape(1)
    return pl.pallas_call(
        ocean_update_kernel,
        out_shape=jax.ShapeDtypeStruct(first.shape, jnp.float32),
        in_specs=[
            pl.BlockSpec(memory_space=pltpu.SMEM),
            pl.BlockSpec(memory_space=pl.ANY),
            pl.BlockSpec(memory_space=pl.ANY),
            pl.BlockSpec(memory_space=pl.ANY),
            pl.BlockSpec(memory_space=pl.ANY),
            pl.BlockSpec(memory_space=pltpu.VMEM),
        ],
        out_specs=pl.BlockSpec(memory_space=pl.ANY),
        input_output_aliases={1: 0},
        cost_estimate=pl.CostEstimate(
            flops=8 * cells * levels * flux_count, transcendentals=0, bytes_accessed=12 * cells * levels
        ),
    )(flag, first, state, sea_rows, forcing, ocean_map)


def scatter_regrid_kernel(labels_ref, fluxes_ref, weights_ref, out_ref, binned_ref):
    entries = fluxes_ref.shape[0]
    weight_count, tile_rows, block_len = weights_ref.shape
    flux_count = fluxes_ref.shape[1]
    binned_ref[...] = jnp.zeros_like(binned_ref)

    def add_one(e, carry):
        label = labels_ref[e]
        binned_ref[label] = binned_ref[label] + fluxes_ref[e]
        return carry

    lax.fori_loop(0, entries, add_one, 0, unroll=8)
    out_ref[...] = jnp.zeros_like(out_ref)

    def regrid_one(w, carry):
        start = pl.multiple_of(w * tile_rows, tile_rows)
        block = binned_ref[pl.ds(start, tile_rows)].reshape(tile_rows * flux_count, block_len)
        high = block.astype(jnp.bfloat16)
        low = (block - high.astype(jnp.float32)).astype(jnp.bfloat16)
        weight = weights_ref[w]
        out_ref[...] += jnp.dot(high, weight, preferred_element_type=jnp.float32) + jnp.dot(
            low, weight, preferred_element_type=jnp.float32
        )
        return carry

    lax.fori_loop(0, weight_count, regrid_one, 0)


def scatter_regrid(labels, fluxes, weights):
    entries, flux_count, block_len = fluxes.shape
    weight_count, tile_rows, _ = weights.shape
    return pl.pallas_call(
        scatter_regrid_kernel,
        out_shape=jax.ShapeDtypeStruct((tile_rows * flux_count, block_len), jnp.float32),
        in_specs=[
            pl.BlockSpec(memory_space=pltpu.SMEM),
            pl.BlockSpec(memory_space=pltpu.VMEM),
            pl.BlockSpec(memory_space=pltpu.VMEM),
        ],
        out_specs=pl.BlockSpec(memory_space=pltpu.VMEM),
        scratch_shapes=[pltpu.VMEM((weight_count * tile_rows, flux_count, block_len), jnp.float32)],
        compiler_params=pltpu.CompilerParams(vmem_limit_bytes=48 * 1024 * 1024),
        cost_estimate=pl.CostEstimate(
            flops=4 * weight_count * tile_rows * flux_count * block_len * block_len,
            transcendentals=0,
            bytes_accessed=entries * flux_count * block_len * 4 + weight_count * tile_rows * block_len * 2,
        ),
    )(labels, fluxes, weights)


def halo_kernel(shape, values_ref, rows_out, cols_out, rows_land, cols_land, send_sems, recv_sems):
    comp_total, lat_total, lon_total = shape
    bands = comp_total * lat_total
    band = lax.axis_index("comp") * lat_total + lax.axis_index("lat")
    lon = lax.axis_index("lon")
    rows, cols, _ = values_ref.shape
    up = (band + 1) % bands
    down = (band + bands - 1) % bands
    up_device = (up // lat_total, up % lat_total, lon)
    down_device = (down // lat_total, down % lat_total, lon)
    east_device = (band // lat_total, band % lat_total, (lon + 1) % lon_total)
    west_device = (band // lat_total, band % lat_total, (lon + lon_total - 1) % lon_total)
    barrier = pltpu.get_barrier_semaphore()
    for device in (up_device, down_device, east_device, west_device):
        pl.semaphore_signal(barrier, 1, device_id=device, device_id_type=MESH_IDS)
    pl.semaphore_wait(barrier, 4)
    plan = [
        (values_ref.at[pl.ds(rows - 1, 1)], rows_land.at[0], up_device),
        (values_ref.at[pl.ds(0, 1)], rows_land.at[1], down_device),
        (values_ref.at[:, pl.ds(cols - 1, 1)], cols_land.at[0], east_device),
        (values_ref.at[:, pl.ds(0, 1)], cols_land.at[1], west_device),
    ]
    copies = []
    for slot, (source, target, device) in enumerate(plan):
        copy = pltpu.make_async_remote_copy(
            src_ref=source,
            dst_ref=target,
            send_sem=send_sems.at[slot],
            recv_sem=recv_sems.at[slot],
            device_id=device,
            device_id_type=MESH_IDS,
        )
        copy.start()
        copies.append(copy)
    for copy in copies:
        copy.wait_send()
    for copy in copies:
        copy.wait_recv()
    rows_out[...] = rows_land[...]
    cols_out[...] = cols_land[...]


def halo_edges(values, shape, collective):
    rows, cols, levels = values.shape
    return pl.pallas_call(
        functools.partial(halo_kernel, tuple(shape)),
        out_shape=(
            jax.ShapeDtypeStruct((2, 1, cols, levels), values.dtype),
            jax.ShapeDtypeStruct((2, rows, 1, levels), values.dtype),
        ),
        in_specs=[pl.BlockSpec(memory_space=pl.ANY)],
        out_specs=(
            pl.BlockSpec(memory_space=pltpu.VMEM),
            pl.BlockSpec(memory_space=pltpu.VMEM),
        ),
        scratch_shapes=[
            pltpu.VMEM((2, 1, cols, levels), values.dtype),
            pltpu.VMEM((2, rows, 1, levels), values.dtype),
            pltpu.SemaphoreType.DMA((4,)),
            pltpu.SemaphoreType.DMA((4,)),
        ],
        compiler_params=pltpu.CompilerParams(collective_id=collective, has_side_effects=True),
    )(values)


def local(
    state, land_mask, intersection_list, mix_atm, mix_ocn, flux_map, ocean_map, regrid_weights
):
    tile_rows, block_len, levels = state.shape
    flux_count = flux_map.shape[1]
    weight_count = regrid_weights.shape[0]
    intersections = intersection_list.shape[2]
    comp_count = lax.axis_size("comp")
    lat_count = lax.axis_size("lat")
    lon_count = lax.axis_size("lon")
    tile_count = lat_count * lon_count
    reach = min(4, lon_count)
    neighbour_count = 2 * reach
    capacity = intersections * tile_rows // neighbour_count
    width = flux_count * block_len
    comp_index = lax.axis_index("comp")
    tile_index = lax.axis_index("lat") * lon_count + lax.axis_index("lon")
    band = comp_index * lat_count + lax.axis_index("lat")
    ocean_band = (comp_count - 1) * lat_count
    ocean_side = comp_index == comp_count - 1
    lower_valid = (band > 0) & ((band - 1 >= ocean_band) == (band >= ocean_band))
    upper_valid = (band < comp_count * lat_count - 1) & (
        (band + 1 >= ocean_band) == (band >= ocean_band)
    )
    sea_cells = land_mask == 1

    mesh_shape = (comp_count, lat_count, lon_count)

    def halos(values, collective):
        rows, cols = halo_edges(values, mesh_shape, collective)
        top = jnp.where(lower_valid, rows[0], 0.0)
        bottom = jnp.where(upper_valid, rows[1], 0.0)
        return top, bottom, cols[0], cols[1]

    top, bottom, west, east = halos(state, 2)
    mixing = jnp.where(ocean_side, mix_ocn, mix_atm)
    first, first_planes = substep(state, top, bottom, west, east, mixing, comp_count)
    first_top = first_planes[0].reshape(tile_rows, block_len)
    state_top = first_planes[1].reshape(tile_rows, block_len)
    top, bottom, west, east = halos(first, 3)

    def atmosphere_second(values, top, bottom, west, east):
        moved, total = substep(values, top, bottom, west, east, mix_atm, comp_count, flux_map.T)
        total = total.reshape(flux_count, tile_rows, block_len)
        sent = jnp.where(sea_cells[None], 0.5 * total, 0.0).astype(jnp.bfloat16)
        return moved, sent

    def ocean_second(values, top, bottom, west, east):
        return values, jnp.zeros((flux_count, tile_rows, block_len), jnp.bfloat16)

    second, flux_sent = lax.cond(
        ocean_side, ocean_second, atmosphere_second, first, top, bottom, west, east
    )
    entry_list = intersection_list.reshape(tile_rows * intersections, 3)
    owners = entry_list[:, 0]
    targets = entry_list[:, 1]
    weight_ids = entry_list[:, 2]
    labels = weight_ids * tile_rows + targets
    entry_blocks = jnp.repeat(flux_sent.transpose(1, 0, 2), intersections, axis=0).reshape(
        tile_rows * intersections, width
    )
    lane = jnp.arange(128, dtype=jnp.int32)[None, :]
    label_lanes = jnp.where(
        lane == 0, weight_ids[:, None], jnp.where(lane == 1, targets[:, None], 0)
    ).astype(jnp.bfloat16)
    entry_blocks = jnp.concatenate([entry_blocks, label_lanes], axis=1)
    sending = jnp.broadcast_to(jnp.logical_not(ocean_side), owners.shape)
    offsets = [
        (n // reach * lon_count + n % reach - (reach - 1) // 2) % tile_count
        for n in range(neighbour_count)
    ]
    offset_table = jnp.array(offsets, jnp.int32)
    distance = (owners - tile_index + tile_count) % tile_count
    neighbour_ids = jnp.sum(
        jnp.where(
            distance[:, None] == offset_table[None, :],
            jnp.arange(neighbour_count, dtype=jnp.int32)[None, :],
            0,
        ),
        axis=1,
    )
    packed, _, entry_slots = pack_rows(entry_blocks, neighbour_ids, labels, sending, capacity, neighbour_count)
    arrived = gather_to_ocean(packed, offsets, mesh_shape)
    weights_low = regrid_weights
    weights_wide = regrid_weights.astype(jnp.float32)
    senders = (comp_count - 1) * neighbour_count

    def ocean_reply(values_top, arrived):
        flat = arrived.reshape(-1, width + 128)
        arrived_labels = flat[:, width].astype(jnp.int32) * tile_rows + flat[:, width + 1].astype(
            jnp.int32
        )
        fluxes = flat[:, :width].astype(jnp.float32).reshape(-1, flux_count, block_len)
        forcing = scatter_regrid(arrived_labels, fluxes, weights_low)
        forcing = forcing.reshape(tile_rows, flux_count, block_len).transpose(1, 0, 2)
        lifted = jnp.sum(forcing * ocean_map[:, 0][:, None, None], axis=0)
        top_level = jnp.where(sea_cells, values_top + lifted, state_top)
        table = jnp.einsum("db,wab->wda", top_level, weights_wide, precision=HIGHEST)
        replies = jnp.take(table.reshape(weight_count * tile_rows, block_len), arrived_labels, axis=0)
        return forcing, replies.reshape(senders, capacity, block_len), top_level

    def atmosphere_reply(values_top, arrived):
        return (
            jnp.zeros((flux_count, tile_rows, block_len), jnp.float32),
            jnp.zeros((senders, capacity, block_len), jnp.float32),
            values_top,
        )

    forcing, replies, ocean_top = lax.cond(
        ocean_side, ocean_reply, atmosphere_reply, first_top, arrived
    )
    atmosphere_top = lax.cond(
        ocean_side,
        lambda values: jnp.zeros((tile_rows, block_len), jnp.float32),
        lambda values: values[:, :, 0],
        second,
    )
    replies, atmosphere_top = lax.optimization_barrier((replies, atmosphere_top))
    answers = spread_from_ocean(replies, offsets, mesh_shape)
    per_entry = jnp.take(
        answers.reshape(neighbour_count * capacity, block_len), entry_slots, axis=0
    )
    returned = per_entry.reshape(tile_rows, intersections, block_len).sum(axis=1)
    second, forcing, answers = lax.optimization_barrier((second, forcing, answers))
    sea_rows = jnp.broadcast_to(
        sea_cells.astype(jnp.int32).reshape(1, tile_rows * block_len), (8, tile_rows * block_len)
    )
    final_state = ocean_update(
        second,
        state,
        sea_rows,
        forcing.reshape(flux_count, tile_rows * block_len),
        ocean_map,
        comp_count,
    )
    surface_out = jnp.where(
        ocean_side, ocean_top, jnp.where(sea_cells, returned, atmosphere_top)
    )
    return (final_state, surface_out)


def solution(mesh):
    placed = (
        P(("comp", "lat"), "lon", None),
        P(("comp", "lat"), "lon"),
        P(("comp", "lat"), "lon", None, None),
        P(),
        P(),
        P(),
        P(),
        P(),
    )
    return jax.shard_map(
        local,
        mesh=mesh,
        in_specs=placed,
        out_specs=(P(("comp", "lat"), "lon", None), P(("comp", "lat"), "lon")),
        check_vma=False,
    )
```

```python
import jax
import jax.numpy as jnp
from jax import lax
from jax.experimental import pallas as pl
from jax.experimental.pallas import tpu as pltpu
from jax.sharding import PartitionSpec as P
import functools

SMOOTHING = 0.2
PHYSICS = 0.5
HIGHEST = lax.Precision.HIGHEST
ROW_BLOCK = 64
UPDATE_BLOCK = 32


def split_bf16(values):
    high = values.astype(jnp.bfloat16)
    low = (values - high.astype(jnp.float32)).astype(jnp.bfloat16)
    return high, low


def three_pass(lhs, rhs, dims):
    lhs_hi, lhs_lo = split_bf16(lhs)
    rhs_hi, rhs_lo = split_bf16(rhs)

    def one(a, b):
        return lax.dot_general(a, b, (dims, ((), ())), preferred_element_type=jnp.float32)

    return one(lhs_hi, rhs_hi) + (one(lhs_hi, rhs_lo) + one(lhs_lo, rhs_hi))


def exact_rows(picker, values):
    high = values.astype(jnp.bfloat16)
    rest = values - high.astype(jnp.float32)
    middle = rest.astype(jnp.bfloat16)
    low = (rest - middle.astype(jnp.float32)).astype(jnp.bfloat16)

    def one(piece):
        return lax.dot_general(
            picker, piece, (((1,), (1,)), ((), ())), preferred_element_type=jnp.float32
        )

    return one(high) + one(middle) + one(low)


def substep_kernel(with_flux, comp_total, x_ref, top_ref, bottom_ref, west_ref, east_ref, mix_ref, *rest):
    if with_flux:
        fluxes_ref, out_ref, flux_out_ref = rest
    else:
        out_ref, planes_ref = rest
    rows, cols, levels = x_ref.shape
    centre = x_ref[...]
    up = jnp.concatenate([top_ref[...], centre[:-1]], axis=0)
    down = jnp.concatenate([centre[1:], bottom_ref[...]], axis=0)
    column = lax.broadcasted_iota(jnp.int32, centre.shape, 1)
    west = jnp.where(column == 0, west_ref[...], pltpu.roll(centre, 1, 1))
    east = jnp.where(column == cols - 1, east_ref[...], pltpu.roll(centre, cols - 1, 1))
    smooth = centre + SMOOTHING * (up + down + west + east - 4.0 * centre)
    flat = smooth.reshape(rows * cols, levels)
    mixed = three_pass(flat, mix_ref[...], ((1,), (0,)))
    moved = flat + PHYSICS * jnp.tanh(mixed)
    out_ref[...] = moved.reshape(rows, cols, levels)
    if not with_flux:
        ocean = lax.axis_index("comp") == comp_total - 1

        @pl.when(ocean)
        def _():
            plane_row = lax.broadcasted_iota(jnp.int32, (8, levels), 0)
            plane_lane = lax.broadcasted_iota(jnp.int32, (8, levels), 1)
            pick_out = ((plane_row == 0) & (plane_lane == 0)).astype(jnp.bfloat16)
            pick_in = ((plane_row == 1) & (plane_lane == 0)).astype(jnp.bfloat16)
            planes_ref[...] = exact_rows(pick_out, moved) + exact_rows(
                pick_in, centre.reshape(rows * cols, levels)
            )

        @pl.when(jnp.logical_not(ocean))
        def _():
            planes_ref[...] = jnp.zeros_like(planes_ref)

    else:
        total = centre.reshape(rows * cols, levels) + moved
        flux_out_ref[...] = three_pass(fluxes_ref[...], total, ((1,), (1,)))


def substep(values, top, bottom, west, east, mixing, comp_total, fluxes_t=None):
    rows, cols, levels = values.shape
    blocks = rows // ROW_BLOCK
    top_rows = jnp.concatenate([top, values[ROW_BLOCK - 1 : rows - 1 : ROW_BLOCK]], axis=0)
    bottom_rows = jnp.concatenate([values[ROW_BLOCK:rows:ROW_BLOCK], bottom], axis=0)
    with_flux = fluxes_t is not None
    in_specs = [
        pl.BlockSpec((ROW_BLOCK, cols, levels), lambda i: (i, 0, 0)),
        pl.BlockSpec((1, cols, levels), lambda i: (i, 0, 0)),
        pl.BlockSpec((1, cols, levels), lambda i: (i, 0, 0)),
        pl.BlockSpec((ROW_BLOCK, 1, levels), lambda i: (i, 0, 0)),
        pl.BlockSpec((ROW_BLOCK, 1, levels), lambda i: (i, 0, 0)),
        pl.BlockSpec((levels, levels), lambda i: (0, 0)),
    ]
    operands = [values, top_rows, bottom_rows, west, east, mixing]
    out_shape = [jax.ShapeDtypeStruct(values.shape, jnp.float32)]
    out_specs = [pl.BlockSpec((ROW_BLOCK, cols, levels), lambda i: (i, 0, 0))]
    if not with_flux:
        out_shape.append(jax.ShapeDtypeStruct((8, rows * cols), jnp.float32))
        out_specs.append(pl.BlockSpec((8, ROW_BLOCK * cols), lambda i: (0, i)))
    if with_flux:
        flux_count = fluxes_t.shape[0]
        in_specs.append(pl.BlockSpec((flux_count, levels), lambda i: (0, 0)))
        operands.append(fluxes_t)
        out_shape.append(jax.ShapeDtypeStruct((flux_count, rows * cols), jnp.float32))
        out_specs.append(pl.BlockSpec((flux_count, ROW_BLOCK * cols), lambda i: (0, i)))
    cells = rows * cols
    flops = 6 * cells * levels * levels + (6 * cells * levels * 8 if with_flux else 0)
    result = pl.pallas_call(
        functools.partial(substep_kernel, with_flux, comp_total),
        grid=(blocks,),
        in_specs=in_specs,
        out_specs=out_specs,
        out_shape=out_shape,
        cost_estimate=pl.CostEstimate(
            flops=flops, transcendentals=cells * levels, bytes_accessed=8 * cells * levels
        ),
    )(*operands)
    return result


def column_physics(values, mixing):
    return jnp.tanh(jnp.einsum("rck,kj->rcj", values, mixing, precision=HIGHEST))


def earlier_same(owners, usable):
    positions = jnp.arange(owners.shape[0], dtype=jnp.int32)
    before = (
        (owners[None, :] == owners[:, None])
        & (positions[None, :] < positions[:, None])
        & usable[None, :]
    )
    return jnp.sum(before.astype(jnp.int32), axis=1)


def pack_rows(blocks, owners, labels, usable, slots_each, owner_total):
    ranks = earlier_same(owners, usable)
    target_slot = owners * slots_each + ranks
    slot_ids = jnp.arange(owner_total * slots_each, dtype=jnp.int32)
    placing = (slot_ids[:, None] == target_slot[None, :]) & usable[None, :]
    packed = jnp.dot(
        placing.astype(jnp.bfloat16), blocks, preferred_element_type=jnp.float32
    ).astype(jnp.bfloat16)
    placed_labels = jnp.sum(jnp.where(placing, labels[None, :] + 1, 0), axis=1) - 1
    return (
        packed.reshape(owner_total, slots_each, blocks.shape[1]),
        placed_labels.reshape(owner_total, slots_each),
        target_slot,
    )


MESH_IDS = pl.DeviceIdType.MESH


def tile_device(comp, tile, lon_total):
    return (comp, tile // lon_total, tile % lon_total)


def gather_kernel(offsets, shape, send_ref, out_ref, land, send_sems, recv_sems):
    comp_total, lat_total, lon_total = shape
    comp = lax.axis_index("comp")
    tiles = lat_total * lon_total
    tile = lax.axis_index("lat") * lon_total + lax.axis_index("lon")
    ocean = comp_total - 1
    count = len(offsets)
    barrier = pltpu.get_barrier_semaphore()

    @pl.when(comp != ocean)
    def _():
        for off in offsets:
            target = tile_device(ocean, (tile + off) % tiles, lon_total)
            pl.semaphore_signal(barrier, 1, device_id=target, device_id_type=MESH_IDS)
        pl.semaphore_wait(barrier, count)
        copies = []
        for k, off in enumerate(offsets):
            target = tile_device(ocean, (tile + off) % tiles, lon_total)
            copy = pltpu.make_async_remote_copy(
                src_ref=send_ref.at[k],
                dst_ref=land.at[comp * count + k],
                send_sem=send_sems.at[k],
                recv_sem=recv_sems.at[comp * count + k],
                device_id=target,
                device_id_type=MESH_IDS,
            )
            copy.start()
            copies.append(copy)
        for copy in copies:
            copy.wait_send()
        out_ref[...] = jnp.zeros_like(out_ref)

    @pl.when(comp == ocean)
    def _():
        for source_comp in range(ocean):
            for off in offsets:
                source = tile_device(source_comp, (tile + tiles - off) % tiles, lon_total)
                pl.semaphore_signal(barrier, 1, device_id=source, device_id_type=MESH_IDS)
        pl.semaphore_wait(barrier, count * ocean)
        for source_comp in range(ocean):
            for k, off in enumerate(offsets):
                source = tile_device(source_comp, (tile + tiles - off) % tiles, lon_total)
                slot = source_comp * count + k
                pltpu.make_async_remote_copy(
                    src_ref=send_ref.at[k],
                    dst_ref=land.at[slot],
                    send_sem=send_sems.at[k],
                    recv_sem=recv_sems.at[slot],
                    device_id=source,
                    device_id_type=MESH_IDS,
                ).wait_recv()
        out_ref[...] = land[...]


def gather_to_ocean(blocks, offsets, shape):
    count = len(offsets)
    senders = (shape[0] - 1) * count
    slot_shape = blocks.shape[1:]
    return pl.pallas_call(
        functools.partial(gather_kernel, tuple(offsets), tuple(shape)),
        out_shape=jax.ShapeDtypeStruct((senders,) + slot_shape, blocks.dtype),
        in_specs=[pl.BlockSpec(memory_space=pltpu.VMEM)],
        out_specs=pl.BlockSpec(memory_space=pltpu.VMEM),
        scratch_shapes=[
            pltpu.VMEM((senders,) + slot_shape, blocks.dtype),
            pltpu.SemaphoreType.DMA((count,)),
            pltpu.SemaphoreType.DMA((senders,)),
        ],
        compiler_params=pltpu.CompilerParams(collective_id=0, has_side_effects=True),
    )(blocks)


def spread_kernel(offsets, shape, surface_ref, out_ref, land, send_sems, recv_sems):
    comp_total, lat_total, lon_total = shape
    comp = lax.axis_index("comp")
    tiles = lat_total * lon_total
    tile = lax.axis_index("lat") * lon_total + lax.axis_index("lon")
    ocean = comp_total - 1
    count = len(offsets)
    barrier = pltpu.get_barrier_semaphore()

    @pl.when(comp == ocean)
    def _():
        for target_comp in range(ocean):
            for off in offsets:
                target = tile_device(target_comp, (tile + tiles - off) % tiles, lon_total)
                pl.semaphore_signal(barrier, 1, device_id=target, device_id_type=MESH_IDS)
        pl.semaphore_wait(barrier, count * ocean)
        copies = []
        for target_comp in range(ocean):
            for k, off in enumerate(offsets):
                target = tile_device(target_comp, (tile + tiles - off) % tiles, lon_total)
                copy = pltpu.make_async_remote_copy(
                    src_ref=surface_ref.at[target_comp * count + k],
                    dst_ref=land.at[k],
                    send_sem=send_sems.at[target_comp * count + k],
                    recv_sem=recv_sems.at[k],
                    device_id=target,
                    device_id_type=MESH_IDS,
                )
                copy.start()
                copies.append(copy)
        for copy in copies:
            copy.wait_send()
        out_ref[...] = jnp.zeros_like(out_ref)

    @pl.when(comp != ocean)
    def _():
        for off in offsets:
            source = tile_device(ocean, (tile + off) % tiles, lon_total)
            pl.semaphore_signal(barrier, 1, device_id=source, device_id_type=MESH_IDS)
        pl.semaphore_wait(barrier, count)
        for k, off in enumerate(offsets):
            source = tile_device(ocean, (tile + off) % tiles, lon_total)
            pltpu.make_async_remote_copy(
                src_ref=surface_ref.at[k],
                dst_ref=land.at[k],
                send_sem=send_sems.at[k],
                recv_sem=recv_sems.at[k],
                device_id=source,
                device_id_type=MESH_IDS,
            ).wait_recv()
        out_ref[...] = land[...]


def spread_from_ocean(replies, offsets, shape):
    count = len(offsets)
    senders = (shape[0] - 1) * count
    slot_shape = replies.shape[1:]
    return pl.pallas_call(
        functools.partial(spread_kernel, tuple(offsets), tuple(shape)),
        out_shape=jax.ShapeDtypeStruct((count,) + slot_shape, replies.dtype),
        in_specs=[pl.BlockSpec(memory_space=pltpu.VMEM)],
        out_specs=pl.BlockSpec(memory_space=pltpu.VMEM),
        scratch_shapes=[
            pltpu.VMEM((count,) + slot_shape, replies.dtype),
            pltpu.SemaphoreType.DMA((senders,)),
            pltpu.SemaphoreType.DMA((count,)),
        ],
        compiler_params=pltpu.CompilerParams(collective_id=1, has_side_effects=True),
    )(replies)


def ocean_update_kernel(flag_ref, base_ref, state_ref, sea_ref, forcing_ref, spread_ref, out_ref):
    rows, cols, levels = base_ref.shape
    flux_count = forcing_ref.shape[0]

    def block(base_block, state_block, sea_block, forcing_block, out_block):
        ocean_block(base_block, state_block, sea_block, forcing_block, spread_ref, out_block)

    @pl.when(flag_ref[0] == 1)
    def _():
        pltpu.emit_pipeline(
            block,
            grid=(rows // UPDATE_BLOCK,),
            in_specs=[
                pl.BlockSpec((UPDATE_BLOCK, cols, levels), lambda i: (i, 0, 0)),
                pl.BlockSpec((UPDATE_BLOCK, cols, levels), lambda i: (i, 0, 0)),
                pl.BlockSpec((8, UPDATE_BLOCK * cols), lambda i: (0, i)),
                pl.BlockSpec((flux_count, UPDATE_BLOCK * cols), lambda i: (0, i)),
            ],
            out_specs=[pl.BlockSpec((UPDATE_BLOCK, cols, levels), lambda i: (i, 0, 0))],
        )(base_ref, state_ref, sea_ref, forcing_ref, out_ref)


def ocean_block(first_ref, state_ref, sea_ref, forcing_ref, spread_ref, out_ref):
    rows, cols, levels = first_ref.shape
    forcing = forcing_ref[...]
    spread = spread_ref[...]
    forcing_hi = forcing.astype(jnp.bfloat16)
    forcing_lo = (forcing - forcing_hi.astype(jnp.float32)).astype(jnp.bfloat16)
    spread_hi = spread.astype(jnp.bfloat16)
    spread_lo = (spread - spread_hi.astype(jnp.float32)).astype(jnp.bfloat16)

    def one(a, b):
        return lax.dot_general(a, b, (((0,), (0,)), ((), ())), preferred_element_type=jnp.float32)

    stacked = jnp.concatenate(
        [forcing_hi.astype(jnp.float32), forcing_hi.astype(jnp.float32), forcing_lo.astype(jnp.float32)],
        axis=0,
    ).astype(jnp.bfloat16)
    spread_stack = jnp.concatenate(
        [spread_hi.astype(jnp.float32), spread_lo.astype(jnp.float32), spread_hi.astype(jnp.float32)],
        axis=0,
    ).astype(jnp.bfloat16)
    added = one(stacked, spread_stack)
    lane_row = lax.broadcasted_iota(jnp.int32, (8, levels), 0)
    ones = (lane_row == 0).astype(jnp.bfloat16)
    picks = jnp.where(lax.broadcasted_iota(jnp.int32, sea_ref.shape, 0) == 0, sea_ref[...], 0)
    mask = one(picks.astype(jnp.bfloat16), ones)
    moved = first_ref[...].reshape(rows * cols, levels) + added
    kept = jnp.where(mask > 0.5, moved, state_ref[...].reshape(rows * cols, levels))
    out_ref[...] = kept.reshape(rows, cols, levels)


def ocean_update(first, state, sea_rows, forcing, ocean_map, comp_total):
    rows, cols, levels = first.shape
    flux_count = forcing.shape[0]
    cells = rows * cols
    flag = (lax.axis_index("comp") == comp_total - 1).astype(jnp.int32).reshape(1)
    return pl.pallas_call(
        ocean_update_kernel,
        out_shape=jax.ShapeDtypeStruct(first.shape, jnp.float32),
        in_specs=[
            pl.BlockSpec(memory_space=pltpu.SMEM),
            pl.BlockSpec(memory_space=pl.ANY),
            pl.BlockSpec(memory_space=pl.ANY),
            pl.BlockSpec(memory_space=pl.ANY),
            pl.BlockSpec(memory_space=pl.ANY),
            pl.BlockSpec(memory_space=pltpu.VMEM),
        ],
        out_specs=pl.BlockSpec(memory_space=pl.ANY),
        input_output_aliases={1: 0},
        cost_estimate=pl.CostEstimate(
            flops=8 * cells * levels * flux_count, transcendentals=0, bytes_accessed=12 * cells * levels
        ),
    )(flag, first, state, sea_rows, forcing, ocean_map)


def scatter_regrid_kernel(labels_ref, fluxes_ref, weights_ref, out_ref, binned_ref):
    entries = fluxes_ref.shape[0]
    weight_count, tile_rows, block_len = weights_ref.shape
    flux_count = fluxes_ref.shape[1]
    binned_ref[...] = jnp.zeros_like(binned_ref)

    def add_one(e, carry):
        label = labels_ref[e]
        binned_ref[label] = binned_ref[label] + fluxes_ref[e]
        return carry

    lax.fori_loop(0, entries, add_one, 0, unroll=8)
    out_ref[...] = jnp.zeros_like(out_ref)

    def regrid_one(w, carry):
        start = pl.multiple_of(w * tile_rows, tile_rows)
        block = binned_ref[pl.ds(start, tile_rows)].reshape(tile_rows * flux_count, block_len)
        high = block.astype(jnp.bfloat16)
        low = (block - high.astype(jnp.float32)).astype(jnp.bfloat16)
        weight = weights_ref[w]
        out_ref[...] += jnp.dot(high, weight, preferred_element_type=jnp.float32) + jnp.dot(
            low, weight, preferred_element_type=jnp.float32
        )
        return carry

    lax.fori_loop(0, weight_count, regrid_one, 0)


def scatter_regrid(labels, fluxes, weights):
    entries, flux_count, block_len = fluxes.shape
    weight_count, tile_rows, _ = weights.shape
    return pl.pallas_call(
        scatter_regrid_kernel,
        out_shape=jax.ShapeDtypeStruct((tile_rows * flux_count, block_len), jnp.float32),
        in_specs=[
            pl.BlockSpec(memory_space=pltpu.SMEM),
            pl.BlockSpec(memory_space=pltpu.VMEM),
            pl.BlockSpec(memory_space=pltpu.VMEM),
        ],
        out_specs=pl.BlockSpec(memory_space=pltpu.VMEM),
        scratch_shapes=[pltpu.VMEM((weight_count * tile_rows, flux_count, block_len), jnp.float32)],
        compiler_params=pltpu.CompilerParams(vmem_limit_bytes=48 * 1024 * 1024),
        cost_estimate=pl.CostEstimate(
            flops=4 * weight_count * tile_rows * flux_count * block_len * block_len,
            transcendentals=0,
            bytes_accessed=entries * flux_count * block_len * 4 + weight_count * tile_rows * block_len * 2,
        ),
    )(labels, fluxes, weights)


def halo_kernel(shape, values_ref, rows_out, cols_out, rows_land, cols_land, send_sems, recv_sems):
    comp_total, lat_total, lon_total = shape
    bands = comp_total * lat_total
    band = lax.axis_index("comp") * lat_total + lax.axis_index("lat")
    lon = lax.axis_index("lon")
    rows, cols, _ = values_ref.shape
    up = (band + 1) % bands
    down = (band + bands - 1) % bands
    up_device = (up // lat_total, up % lat_total, lon)
    down_device = (down // lat_total, down % lat_total, lon)
    east_device = (band // lat_total, band % lat_total, (lon + 1) % lon_total)
    west_device = (band // lat_total, band % lat_total, (lon + lon_total - 1) % lon_total)
    barrier = pltpu.get_barrier_semaphore()
    for device in (up_device, down_device, east_device, west_device):
        pl.semaphore_signal(barrier, 1, device_id=device, device_id_type=MESH_IDS)
    pl.semaphore_wait(barrier, 4)
    plan = [
        (values_ref.at[pl.ds(rows - 1, 1)], rows_land.at[0], up_device),
        (values_ref.at[pl.ds(0, 1)], rows_land.at[1], down_device),
        (values_ref.at[:, pl.ds(cols - 1, 1)], cols_land.at[0], east_device),
        (values_ref.at[:, pl.ds(0, 1)], cols_land.at[1], west_device),
    ]
    copies = []
    for slot, (source, target, device) in enumerate(plan):
        copy = pltpu.make_async_remote_copy(
            src_ref=source,
            dst_ref=target,
            send_sem=send_sems.at[slot],
            recv_sem=recv_sems.at[slot],
            device_id=device,
            device_id_type=MESH_IDS,
        )
        copy.start()
        copies.append(copy)
    for copy in copies:
        copy.wait_send()
    for copy in copies:
        copy.wait_recv()
    rows_out[...] = rows_land[...]
    cols_out[...] = cols_land[...]


def halo_edges(values, shape, collective):
    rows, cols, levels = values.shape
    return pl.pallas_call(
        functools.partial(halo_kernel, tuple(shape)),
        out_shape=(
            jax.ShapeDtypeStruct((2, 1, cols, levels), values.dtype),
            jax.ShapeDtypeStruct((2, rows, 1, levels), values.dtype),
        ),
        in_specs=[pl.BlockSpec(memory_space=pl.ANY)],
        out_specs=(
            pl.BlockSpec(memory_space=pltpu.VMEM),
            pl.BlockSpec(memory_space=pltpu.VMEM),
        ),
        scratch_shapes=[
            pltpu.VMEM((2, 1, cols, levels), values.dtype),
            pltpu.VMEM((2, rows, 1, levels), values.dtype),
            pltpu.SemaphoreType.DMA((4,)),
            pltpu.SemaphoreType.DMA((4,)),
        ],
        compiler_params=pltpu.CompilerParams(collective_id=collective, has_side_effects=True),
    )(values)


def local(
    state, land_mask, intersection_list, mix_atm, mix_ocn, flux_map, ocean_map, regrid_weights
):
    tile_rows, block_len, levels = state.shape
    flux_count = flux_map.shape[1]
    weight_count = regrid_weights.shape[0]
    intersections = intersection_list.shape[2]
    comp_count = lax.axis_size("comp")
    lat_count = lax.axis_size("lat")
    lon_count = lax.axis_size("lon")
    tile_count = lat_count * lon_count
    reach = min(4, lon_count)
    neighbour_count = 2 * reach
    capacity = intersections * tile_rows // neighbour_count
    width = flux_count * block_len
    comp_index = lax.axis_index("comp")
    tile_index = lax.axis_index("lat") * lon_count + lax.axis_index("lon")
    band = comp_index * lat_count + lax.axis_index("lat")
    ocean_band = (comp_count - 1) * lat_count
    ocean_side = comp_index == comp_count - 1
    lower_valid = (band > 0) & ((band - 1 >= ocean_band) == (band >= ocean_band))
    upper_valid = (band < comp_count * lat_count - 1) & (
        (band + 1 >= ocean_band) == (band >= ocean_band)
    )
    sea_cells = land_mask == 1

    mesh_shape = (comp_count, lat_count, lon_count)

    def halos(values, collective):
        rows, cols = halo_edges(values, mesh_shape, collective)
        top = jnp.where(lower_valid, rows[0], 0.0)
        bottom = jnp.where(upper_valid, rows[1], 0.0)
        return top, bottom, cols[0], cols[1]

    top, bottom, west, east = halos(state, 2)
    mixing = jnp.where(ocean_side, mix_ocn, mix_atm)
    first, first_planes = substep(state, top, bottom, west, east, mixing, comp_count)
    first_top = first_planes[0].reshape(tile_rows, block_len)
    state_top = first_planes[1].reshape(tile_rows, block_len)
    top, bottom, west, east = halos(first, 3)

    def atmosphere_second(values, top, bottom, west, east):
        moved, total = substep(values, top, bottom, west, east, mix_atm, comp_count, flux_map.T)
        total = total.reshape(flux_count, tile_rows, block_len)
        sent = jnp.where(sea_cells[None], 0.5 * total, 0.0).astype(jnp.bfloat16)
        return moved, sent

    def ocean_second(values, top, bottom, west, east):
        return values, jnp.zeros((flux_count, tile_rows, block_len), jnp.bfloat16)

    second, flux_sent = lax.cond(
        ocean_side, ocean_second, atmosphere_second, first, top, bottom, west, east
    )
    entry_list = intersection_list.reshape(tile_rows * intersections, 3)
    owners = entry_list[:, 0]
    targets = entry_list[:, 1]
    weight_ids = entry_list[:, 2]
    labels = weight_ids * tile_rows + targets
    entry_blocks = jnp.repeat(flux_sent.transpose(1, 0, 2), intersections, axis=0).reshape(
        tile_rows * intersections, width
    )
    lane = jnp.arange(128, dtype=jnp.int32)[None, :]
    label_lanes = jnp.where(
        lane == 0, weight_ids[:, None], jnp.where(lane == 1, targets[:, None], 0)
    ).astype(jnp.bfloat16)
    entry_blocks = jnp.concatenate([entry_blocks, label_lanes], axis=1)
    sending = jnp.broadcast_to(jnp.logical_not(ocean_side), owners.shape)
    offsets = [
        (n // reach * lon_count + n % reach - (reach - 1) // 2) % tile_count
        for n in range(neighbour_count)
    ]
    offset_table = jnp.array(offsets, jnp.int32)
    distance = (owners - tile_index + tile_count) % tile_count
    neighbour_ids = jnp.sum(
        jnp.where(
            distance[:, None] == offset_table[None, :],
            jnp.arange(neighbour_count, dtype=jnp.int32)[None, :],
            0,
        ),
        axis=1,
    )
    packed, _, entry_slots = pack_rows(entry_blocks, neighbour_ids, labels, sending, capacity, neighbour_count)
    arrived = gather_to_ocean(packed, offsets, mesh_shape)
    weights_low = regrid_weights
    weights_wide = regrid_weights.astype(jnp.float32)
    senders = (comp_count - 1) * neighbour_count

    def ocean_reply(values_top, arrived):
        flat = arrived.reshape(-1, width + 128)
        arrived_labels = flat[:, width].astype(jnp.int32) * tile_rows + flat[:, width + 1].astype(
            jnp.int32
        )
        fluxes = flat[:, :width].astype(jnp.float32).reshape(-1, flux_count, block_len)
        forcing = scatter_regrid(arrived_labels, fluxes, weights_low)
        forcing = forcing.reshape(tile_rows, flux_count, block_len).transpose(1, 0, 2)
        lifted = jnp.sum(forcing * ocean_map[:, 0][:, None, None], axis=0)
        top_level = jnp.where(sea_cells, values_top + lifted, state_top)
        table = jnp.einsum("db,wab->wda", top_level, weights_wide, precision=HIGHEST)
        replies = jnp.take(table.reshape(weight_count * tile_rows, block_len), arrived_labels, axis=0)
        return forcing, replies.reshape(senders, capacity, block_len), top_level

    def atmosphere_reply(values_top, arrived):
        return (
            jnp.zeros((flux_count, tile_rows, block_len), jnp.float32),
            jnp.zeros((senders, capacity, block_len), jnp.float32),
            values_top,
        )

    forcing, replies, ocean_top = lax.cond(
        ocean_side, ocean_reply, atmosphere_reply, first_top, arrived
    )
    atmosphere_top = lax.cond(
        ocean_side,
        lambda values: jnp.zeros((tile_rows, block_len), jnp.float32),
        lambda values: values[:, :, 0],
        second,
    )
    replies, atmosphere_top = lax.optimization_barrier((replies, atmosphere_top))
    answers = spread_from_ocean(replies, offsets, mesh_shape)
    per_entry = jnp.take(
        answers.reshape(neighbour_count * capacity, block_len), entry_slots, axis=0
    )
    returned = per_entry.reshape(tile_rows, intersections, block_len).sum(axis=1)
    second, forcing, answers = lax.optimization_barrier((second, forcing, answers))
    sea_rows = jnp.broadcast_to(
        sea_cells.astype(jnp.int32).reshape(1, tile_rows * block_len), (8, tile_rows * block_len)
    )
    final_state = ocean_update(
        second,
        state,
        sea_rows,
        forcing.reshape(flux_count, tile_rows * block_len),
        ocean_map,
        comp_count,
    )
    surface_out = jnp.where(
        ocean_side, ocean_top, jnp.where(sea_cells, returned, atmosphere_top)
    )
    return (final_state, surface_out)


def solution(mesh):
    placed = (
        P(("comp", "lat"), "lon", None),
        P(("comp", "lat"), "lon"),
        P(("comp", "lat"), "lon", None, None),
        P(),
        P(),
        P(),
        P(),
        P(),
    )
    return jax.shard_map(
        local,
        mesh=mesh,
        in_specs=placed,
        out_specs=(P(("comp", "lat"), "lon", None), P(("comp", "lat"), "lon")),
        check_vma=False,
    )
```

```python
import jax
import jax.numpy as jnp
from jax import lax
from jax.experimental import pallas as pl
from jax.experimental.pallas import tpu as pltpu
from jax.sharding import PartitionSpec as P
import functools

SMOOTHING = 0.2
PHYSICS = 0.5
HIGHEST = lax.Precision.HIGHEST
ROW_BLOCK = 32
UPDATE_BLOCK = 64


def split_bf16(values):
    high = values.astype(jnp.bfloat16)
    low = (values - high.astype(jnp.float32)).astype(jnp.bfloat16)
    return high, low


def three_pass(lhs, rhs, dims):
    lhs_hi, lhs_lo = split_bf16(lhs)
    rhs_hi, rhs_lo = split_bf16(rhs)

    def one(a, b):
        return lax.dot_general(a, b, (dims, ((), ())), preferred_element_type=jnp.float32)

    return one(lhs_hi, rhs_hi) + (one(lhs_hi, rhs_lo) + one(lhs_lo, rhs_hi))


def exact_rows(picker, values):
    high = values.astype(jnp.bfloat16)
    rest = values - high.astype(jnp.float32)
    middle = rest.astype(jnp.bfloat16)
    low = (rest - middle.astype(jnp.float32)).astype(jnp.bfloat16)

    def one(piece):
        return lax.dot_general(
            picker, piece, (((1,), (1,)), ((), ())), preferred_element_type=jnp.float32
        )

    return one(high) + one(middle) + one(low)


def substep_kernel(with_flux, comp_total, x_ref, top_ref, bottom_ref, west_ref, east_ref, mix_ref, *rest):
    if with_flux:
        fluxes_ref, out_ref, flux_out_ref = rest
    else:
        out_ref, planes_ref = rest
    rows, cols, levels = x_ref.shape
    centre = x_ref[...]
    up = jnp.concatenate([top_ref[...], centre[:-1]], axis=0)
    down = jnp.concatenate([centre[1:], bottom_ref[...]], axis=0)
    column = lax.broadcasted_iota(jnp.int32, centre.shape, 1)
    west = jnp.where(column == 0, west_ref[...], pltpu.roll(centre, 1, 1))
    east = jnp.where(column == cols - 1, east_ref[...], pltpu.roll(centre, cols - 1, 1))
    smooth = centre + SMOOTHING * (up + down + west + east - 4.0 * centre)
    flat = smooth.reshape(rows * cols, levels)
    mixed = three_pass(flat, mix_ref[...], ((1,), (0,)))
    moved = flat + PHYSICS * jnp.tanh(mixed)
    out_ref[...] = moved.reshape(rows, cols, levels)
    if not with_flux:
        ocean = lax.axis_index("comp") == comp_total - 1

        @pl.when(ocean)
        def _():
            plane_row = lax.broadcasted_iota(jnp.int32, (8, levels), 0)
            plane_lane = lax.broadcasted_iota(jnp.int32, (8, levels), 1)
            pick_out = ((plane_row == 0) & (plane_lane == 0)).astype(jnp.bfloat16)
            pick_in = ((plane_row == 1) & (plane_lane == 0)).astype(jnp.bfloat16)
            planes_ref[...] = exact_rows(pick_out, moved) + exact_rows(
                pick_in, centre.reshape(rows * cols, levels)
            )

        @pl.when(jnp.logical_not(ocean))
        def _():
            planes_ref[...] = jnp.zeros_like(planes_ref)

    else:
        total = centre.reshape(rows * cols, levels) + moved
        flux_out_ref[...] = three_pass(fluxes_ref[...], total, ((1,), (1,)))


def substep(values, top, bottom, west, east, mixing, comp_total, fluxes_t=None):
    rows, cols, levels = values.shape
    blocks = rows // ROW_BLOCK
    top_rows = jnp.concatenate([top, values[ROW_BLOCK - 1 : rows - 1 : ROW_BLOCK]], axis=0)
    bottom_rows = jnp.concatenate([values[ROW_BLOCK:rows:ROW_BLOCK], bottom], axis=0)
    with_flux = fluxes_t is not None
    in_specs = [
        pl.BlockSpec((ROW_BLOCK, cols, levels), lambda i: (i, 0, 0)),
        pl.BlockSpec((1, cols, levels), lambda i: (i, 0, 0)),
        pl.BlockSpec((1, cols, levels), lambda i: (i, 0, 0)),
        pl.BlockSpec((ROW_BLOCK, 1, levels), lambda i: (i, 0, 0)),
        pl.BlockSpec((ROW_BLOCK, 1, levels), lambda i: (i, 0, 0)),
        pl.BlockSpec((levels, levels), lambda i: (0, 0)),
    ]
    operands = [values, top_rows, bottom_rows, west, east, mixing]
    out_shape = [jax.ShapeDtypeStruct(values.shape, jnp.float32)]
    out_specs = [pl.BlockSpec((ROW_BLOCK, cols, levels), lambda i: (i, 0, 0))]
    if not with_flux:
        out_shape.append(jax.ShapeDtypeStruct((8, rows * cols), jnp.float32))
        out_specs.append(pl.BlockSpec((8, ROW_BLOCK * cols), lambda i: (0, i)))
    if with_flux:
        flux_count = fluxes_t.shape[0]
        in_specs.append(pl.BlockSpec((flux_count, levels), lambda i: (0, 0)))
        operands.append(fluxes_t)
        out_shape.append(jax.ShapeDtypeStruct((flux_count, rows * cols), jnp.float32))
        out_specs.append(pl.BlockSpec((flux_count, ROW_BLOCK * cols), lambda i: (0, i)))
    cells = rows * cols
    flops = 6 * cells * levels * levels + (6 * cells * levels * 8 if with_flux else 0)
    result = pl.pallas_call(
        functools.partial(substep_kernel, with_flux, comp_total),
        grid=(blocks,),
        in_specs=in_specs,
        out_specs=out_specs,
        out_shape=out_shape,
        cost_estimate=pl.CostEstimate(
            flops=flops, transcendentals=cells * levels, bytes_accessed=8 * cells * levels
        ),
    )(*operands)
    return result


def column_physics(values, mixing):
    return jnp.tanh(jnp.einsum("rck,kj->rcj", values, mixing, precision=HIGHEST))


def earlier_same(owners, usable):
    positions = jnp.arange(owners.shape[0], dtype=jnp.int32)
    before = (
        (owners[None, :] == owners[:, None])
        & (positions[None, :] < positions[:, None])
        & usable[None, :]
    )
    return jnp.sum(before.astype(jnp.int32), axis=1)


def pack_rows(blocks, owners, labels, usable, slots_each, owner_total):
    ranks = earlier_same(owners, usable)
    target_slot = owners * slots_each + ranks
    slot_ids = jnp.arange(owner_total * slots_each, dtype=jnp.int32)
    placing = (slot_ids[:, None] == target_slot[None, :]) & usable[None, :]
    packed = jnp.dot(
        placing.astype(jnp.bfloat16), blocks, preferred_element_type=jnp.float32
    ).astype(jnp.bfloat16)
    placed_labels = jnp.sum(jnp.where(placing, labels[None, :] + 1, 0), axis=1) - 1
    return (
        packed.reshape(owner_total, slots_each, blocks.shape[1]),
        placed_labels.reshape(owner_total, slots_each),
        target_slot,
    )


MESH_IDS = pl.DeviceIdType.MESH


def tile_device(comp, tile, lon_total):
    return (comp, tile // lon_total, tile % lon_total)


def gather_kernel(offsets, shape, send_ref, out_ref, land, send_sems, recv_sems):
    comp_total, lat_total, lon_total = shape
    comp = lax.axis_index("comp")
    tiles = lat_total * lon_total
    tile = lax.axis_index("lat") * lon_total + lax.axis_index("lon")
    ocean = comp_total - 1
    count = len(offsets)
    barrier = pltpu.get_barrier_semaphore()

    @pl.when(comp != ocean)
    def _():
        for off in offsets:
            target = tile_device(ocean, (tile + off) % tiles, lon_total)
            pl.semaphore_signal(barrier, 1, device_id=target, device_id_type=MESH_IDS)
        pl.semaphore_wait(barrier, count)
        copies = []
        for k, off in enumerate(offsets):
            target = tile_device(ocean, (tile + off) % tiles, lon_total)
            copy = pltpu.make_async_remote_copy(
                src_ref=send_ref.at[k],
                dst_ref=land.at[comp * count + k],
                send_sem=send_sems.at[k],
                recv_sem=recv_sems.at[comp * count + k],
                device_id=target,
                device_id_type=MESH_IDS,
            )
            copy.start()
            copies.append(copy)
        for copy in copies:
            copy.wait_send()
        out_ref[...] = jnp.zeros_like(out_ref)

    @pl.when(comp == ocean)
    def _():
        for source_comp in range(ocean):
            for off in offsets:
                source = tile_device(source_comp, (tile + tiles - off) % tiles, lon_total)
                pl.semaphore_signal(barrier, 1, device_id=source, device_id_type=MESH_IDS)
        pl.semaphore_wait(barrier, count * ocean)
        for source_comp in range(ocean):
            for k, off in enumerate(offsets):
                source = tile_device(source_comp, (tile + tiles - off) % tiles, lon_total)
                slot = source_comp * count + k
                pltpu.make_async_remote_copy(
                    src_ref=send_ref.at[k],
                    dst_ref=land.at[slot],
                    send_sem=send_sems.at[k],
                    recv_sem=recv_sems.at[slot],
                    device_id=source,
                    device_id_type=MESH_IDS,
                ).wait_recv()
        out_ref[...] = land[...]


def gather_to_ocean(blocks, offsets, shape):
    count = len(offsets)
    senders = (shape[0] - 1) * count
    slot_shape = blocks.shape[1:]
    return pl.pallas_call(
        functools.partial(gather_kernel, tuple(offsets), tuple(shape)),
        out_shape=jax.ShapeDtypeStruct((senders,) + slot_shape, blocks.dtype),
        in_specs=[pl.BlockSpec(memory_space=pltpu.VMEM)],
        out_specs=pl.BlockSpec(memory_space=pltpu.VMEM),
        scratch_shapes=[
            pltpu.VMEM((senders,) + slot_shape, blocks.dtype),
            pltpu.SemaphoreType.DMA((count,)),
            pltpu.SemaphoreType.DMA((senders,)),
        ],
        compiler_params=pltpu.CompilerParams(collective_id=0, has_side_effects=True),
    )(blocks)


def spread_kernel(offsets, shape, surface_ref, out_ref, land, send_sems, recv_sems):
    comp_total, lat_total, lon_total = shape
    comp = lax.axis_index("comp")
    tiles = lat_total * lon_total
    tile = lax.axis_index("lat") * lon_total + lax.axis_index("lon")
    ocean = comp_total - 1
    count = len(offsets)
    barrier = pltpu.get_barrier_semaphore()

    @pl.when(comp == ocean)
    def _():
        for target_comp in range(ocean):
            for off in offsets:
                target = tile_device(target_comp, (tile + tiles - off) % tiles, lon_total)
                pl.semaphore_signal(barrier, 1, device_id=target, device_id_type=MESH_IDS)
        pl.semaphore_wait(barrier, count * ocean)
        copies = []
        for target_comp in range(ocean):
            for k, off in enumerate(offsets):
                target = tile_device(target_comp, (tile + tiles - off) % tiles, lon_total)
                copy = pltpu.make_async_remote_copy(
                    src_ref=surface_ref.at[target_comp * count + k],
                    dst_ref=land.at[k],
                    send_sem=send_sems.at[target_comp * count + k],
                    recv_sem=recv_sems.at[k],
                    device_id=target,
                    device_id_type=MESH_IDS,
                )
                copy.start()
                copies.append(copy)
        for copy in copies:
            copy.wait_send()
        out_ref[...] = jnp.zeros_like(out_ref)

    @pl.when(comp != ocean)
    def _():
        for off in offsets:
            source = tile_device(ocean, (tile + off) % tiles, lon_total)
            pl.semaphore_signal(barrier, 1, device_id=source, device_id_type=MESH_IDS)
        pl.semaphore_wait(barrier, count)
        for k, off in enumerate(offsets):
            source = tile_device(ocean, (tile + off) % tiles, lon_total)
            pltpu.make_async_remote_copy(
                src_ref=surface_ref.at[k],
                dst_ref=land.at[k],
                send_sem=send_sems.at[k],
                recv_sem=recv_sems.at[k],
                device_id=source,
                device_id_type=MESH_IDS,
            ).wait_recv()
        out_ref[...] = land[...]


def spread_from_ocean(replies, offsets, shape):
    count = len(offsets)
    senders = (shape[0] - 1) * count
    slot_shape = replies.shape[1:]
    return pl.pallas_call(
        functools.partial(spread_kernel, tuple(offsets), tuple(shape)),
        out_shape=jax.ShapeDtypeStruct((count,) + slot_shape, replies.dtype),
        in_specs=[pl.BlockSpec(memory_space=pltpu.VMEM)],
        out_specs=pl.BlockSpec(memory_space=pltpu.VMEM),
        scratch_shapes=[
            pltpu.VMEM((count,) + slot_shape, replies.dtype),
            pltpu.SemaphoreType.DMA((senders,)),
            pltpu.SemaphoreType.DMA((count,)),
        ],
        compiler_params=pltpu.CompilerParams(collective_id=1, has_side_effects=True),
    )(replies)


def ocean_update_kernel(flag_ref, base_ref, state_ref, sea_ref, forcing_ref, spread_ref, out_ref):
    rows, cols, levels = base_ref.shape
    flux_count = forcing_ref.shape[0]

    def block(base_block, state_block, sea_block, forcing_block, out_block):
        ocean_block(base_block, state_block, sea_block, forcing_block, spread_ref, out_block)

    @pl.when(flag_ref[0] == 1)
    def _():
        pltpu.emit_pipeline(
            block,
            grid=(rows // UPDATE_BLOCK,),
            in_specs=[
                pl.BlockSpec((UPDATE_BLOCK, cols, levels), lambda i: (i, 0, 0)),
                pl.BlockSpec((UPDATE_BLOCK, cols, levels), lambda i: (i, 0, 0)),
                pl.BlockSpec((8, UPDATE_BLOCK * cols), lambda i: (0, i)),
                pl.BlockSpec((flux_count, UPDATE_BLOCK * cols), lambda i: (0, i)),
            ],
            out_specs=[pl.BlockSpec((UPDATE_BLOCK, cols, levels), lambda i: (i, 0, 0))],
        )(base_ref, state_ref, sea_ref, forcing_ref, out_ref)


def ocean_block(first_ref, state_ref, sea_ref, forcing_ref, spread_ref, out_ref):
    rows, cols, levels = first_ref.shape
    forcing = forcing_ref[...]
    spread = spread_ref[...]
    forcing_hi = forcing.astype(jnp.bfloat16)
    forcing_lo = (forcing - forcing_hi.astype(jnp.float32)).astype(jnp.bfloat16)
    spread_hi = spread.astype(jnp.bfloat16)
    spread_lo = (spread - spread_hi.astype(jnp.float32)).astype(jnp.bfloat16)

    def one(a, b):
        return lax.dot_general(a, b, (((0,), (0,)), ((), ())), preferred_element_type=jnp.float32)

    stacked = jnp.concatenate(
        [forcing_hi.astype(jnp.float32), forcing_hi.astype(jnp.float32), forcing_lo.astype(jnp.float32)],
        axis=0,
    ).astype(jnp.bfloat16)
    spread_stack = jnp.concatenate(
        [spread_hi.astype(jnp.float32), spread_lo.astype(jnp.float32), spread_hi.astype(jnp.float32)],
        axis=0,
    ).astype(jnp.bfloat16)
    added = one(stacked, spread_stack)
    lane_row = lax.broadcasted_iota(jnp.int32, (8, levels), 0)
    ones = (lane_row == 0).astype(jnp.bfloat16)
    picks = jnp.where(lax.broadcasted_iota(jnp.int32, sea_ref.shape, 0) == 0, sea_ref[...], 0)
    mask = one(picks.astype(jnp.bfloat16), ones)
    moved = first_ref[...].reshape(rows * cols, levels) + added
    kept = jnp.where(mask > 0.5, moved, state_ref[...].reshape(rows * cols, levels))
    out_ref[...] = kept.reshape(rows, cols, levels)


def ocean_update(first, state, sea_rows, forcing, ocean_map, comp_total):
    rows, cols, levels = first.shape
    flux_count = forcing.shape[0]
    cells = rows * cols
    flag = (lax.axis_index("comp") == comp_total - 1).astype(jnp.int32).reshape(1)
    return pl.pallas_call(
        ocean_update_kernel,
        out_shape=jax.ShapeDtypeStruct(first.shape, jnp.float32),
        in_specs=[
            pl.BlockSpec(memory_space=pltpu.SMEM),
            pl.BlockSpec(memory_space=pl.ANY),
            pl.BlockSpec(memory_space=pl.ANY),
            pl.BlockSpec(memory_space=pl.ANY),
            pl.BlockSpec(memory_space=pl.ANY),
            pl.BlockSpec(memory_space=pltpu.VMEM),
        ],
        out_specs=pl.BlockSpec(memory_space=pl.ANY),
        input_output_aliases={1: 0},
        cost_estimate=pl.CostEstimate(
            flops=8 * cells * levels * flux_count, transcendentals=0, bytes_accessed=12 * cells * levels
        ),
    )(flag, first, state, sea_rows, forcing, ocean_map)


def scatter_regrid_kernel(labels_ref, fluxes_ref, weights_ref, out_ref, binned_ref):
    entries = fluxes_ref.shape[0]
    weight_count, tile_rows, block_len = weights_ref.shape
    flux_count = fluxes_ref.shape[1]
    binned_ref[...] = jnp.zeros_like(binned_ref)

    def add_one(e, carry):
        label = labels_ref[e]
        binned_ref[label] = binned_ref[label] + fluxes_ref[e]
        return carry

    lax.fori_loop(0, entries, add_one, 0, unroll=8)
    out_ref[...] = jnp.zeros_like(out_ref)

    def regrid_one(w, carry):
        start = pl.multiple_of(w * tile_rows, tile_rows)
        block = binned_ref[pl.ds(start, tile_rows)].reshape(tile_rows * flux_count, block_len)
        high = block.astype(jnp.bfloat16)
        low = (block - high.astype(jnp.float32)).astype(jnp.bfloat16)
        weight = weights_ref[w]
        out_ref[...] += jnp.dot(high, weight, preferred_element_type=jnp.float32) + jnp.dot(
            low, weight, preferred_element_type=jnp.float32
        )
        return carry

    lax.fori_loop(0, weight_count, regrid_one, 0)


def scatter_regrid(labels, fluxes, weights):
    entries, flux_count, block_len = fluxes.shape
    weight_count, tile_rows, _ = weights.shape
    return pl.pallas_call(
        scatter_regrid_kernel,
        out_shape=jax.ShapeDtypeStruct((tile_rows * flux_count, block_len), jnp.float32),
        in_specs=[
            pl.BlockSpec(memory_space=pltpu.SMEM),
            pl.BlockSpec(memory_space=pltpu.VMEM),
            pl.BlockSpec(memory_space=pltpu.VMEM),
        ],
        out_specs=pl.BlockSpec(memory_space=pltpu.VMEM),
        scratch_shapes=[pltpu.VMEM((weight_count * tile_rows, flux_count, block_len), jnp.float32)],
        compiler_params=pltpu.CompilerParams(vmem_limit_bytes=48 * 1024 * 1024),
        cost_estimate=pl.CostEstimate(
            flops=4 * weight_count * tile_rows * flux_count * block_len * block_len,
            transcendentals=0,
            bytes_accessed=entries * flux_count * block_len * 4 + weight_count * tile_rows * block_len * 2,
        ),
    )(labels, fluxes, weights)


def halo_kernel(shape, values_ref, rows_out, cols_out, rows_land, cols_land, send_sems, recv_sems):
    comp_total, lat_total, lon_total = shape
    bands = comp_total * lat_total
    band = lax.axis_index("comp") * lat_total + lax.axis_index("lat")
    lon = lax.axis_index("lon")
    rows, cols, _ = values_ref.shape
    up = (band + 1) % bands
    down = (band + bands - 1) % bands
    up_device = (up // lat_total, up % lat_total, lon)
    down_device = (down // lat_total, down % lat_total, lon)
    east_device = (band // lat_total, band % lat_total, (lon + 1) % lon_total)
    west_device = (band // lat_total, band % lat_total, (lon + lon_total - 1) % lon_total)
    barrier = pltpu.get_barrier_semaphore()
    for device in (up_device, down_device, east_device, west_device):
        pl.semaphore_signal(barrier, 1, device_id=device, device_id_type=MESH_IDS)
    pl.semaphore_wait(barrier, 4)
    plan = [
        (values_ref.at[pl.ds(rows - 1, 1)], rows_land.at[0], up_device),
        (values_ref.at[pl.ds(0, 1)], rows_land.at[1], down_device),
        (values_ref.at[:, pl.ds(cols - 1, 1)], cols_land.at[0], east_device),
        (values_ref.at[:, pl.ds(0, 1)], cols_land.at[1], west_device),
    ]
    copies = []
    for slot, (source, target, device) in enumerate(plan):
        copy = pltpu.make_async_remote_copy(
            src_ref=source,
            dst_ref=target,
            send_sem=send_sems.at[slot],
            recv_sem=recv_sems.at[slot],
            device_id=device,
            device_id_type=MESH_IDS,
        )
        copy.start()
        copies.append(copy)
    for copy in copies:
        copy.wait_send()
    for copy in copies:
        copy.wait_recv()
    rows_out[...] = rows_land[...]
    cols_out[...] = cols_land[...]


def halo_edges(values, shape, collective):
    rows, cols, levels = values.shape
    return pl.pallas_call(
        functools.partial(halo_kernel, tuple(shape)),
        out_shape=(
            jax.ShapeDtypeStruct((2, 1, cols, levels), values.dtype),
            jax.ShapeDtypeStruct((2, rows, 1, levels), values.dtype),
        ),
        in_specs=[pl.BlockSpec(memory_space=pl.ANY)],
        out_specs=(
            pl.BlockSpec(memory_space=pltpu.VMEM),
            pl.BlockSpec(memory_space=pltpu.VMEM),
        ),
        scratch_shapes=[
            pltpu.VMEM((2, 1, cols, levels), values.dtype),
            pltpu.VMEM((2, rows, 1, levels), values.dtype),
            pltpu.SemaphoreType.DMA((4,)),
            pltpu.SemaphoreType.DMA((4,)),
        ],
        compiler_params=pltpu.CompilerParams(collective_id=collective, has_side_effects=True),
    )(values)


def local(
    state, land_mask, intersection_list, mix_atm, mix_ocn, flux_map, ocean_map, regrid_weights
):
    tile_rows, block_len, levels = state.shape
    flux_count = flux_map.shape[1]
    weight_count = regrid_weights.shape[0]
    intersections = intersection_list.shape[2]
    comp_count = lax.axis_size("comp")
    lat_count = lax.axis_size("lat")
    lon_count = lax.axis_size("lon")
    tile_count = lat_count * lon_count
    reach = min(4, lon_count)
    neighbour_count = 2 * reach
    capacity = intersections * tile_rows // neighbour_count
    width = flux_count * block_len
    comp_index = lax.axis_index("comp")
    tile_index = lax.axis_index("lat") * lon_count + lax.axis_index("lon")
    band = comp_index * lat_count + lax.axis_index("lat")
    ocean_band = (comp_count - 1) * lat_count
    ocean_side = comp_index == comp_count - 1
    lower_valid = (band > 0) & ((band - 1 >= ocean_band) == (band >= ocean_band))
    upper_valid = (band < comp_count * lat_count - 1) & (
        (band + 1 >= ocean_band) == (band >= ocean_band)
    )
    sea_cells = land_mask == 1

    mesh_shape = (comp_count, lat_count, lon_count)

    def halos(values, collective):
        rows, cols = halo_edges(values, mesh_shape, collective)
        top = jnp.where(lower_valid, rows[0], 0.0)
        bottom = jnp.where(upper_valid, rows[1], 0.0)
        return top, bottom, cols[0], cols[1]

    top, bottom, west, east = halos(state, 2)
    mixing = jnp.where(ocean_side, mix_ocn, mix_atm)
    first, first_planes = substep(state, top, bottom, west, east, mixing, comp_count)
    first_top = first_planes[0].reshape(tile_rows, block_len)
    state_top = first_planes[1].reshape(tile_rows, block_len)
    top, bottom, west, east = halos(first, 3)

    def atmosphere_second(values, top, bottom, west, east):
        moved, total = substep(values, top, bottom, west, east, mix_atm, comp_count, flux_map.T)
        total = total.reshape(flux_count, tile_rows, block_len)
        sent = jnp.where(sea_cells[None], 0.5 * total, 0.0).astype(jnp.bfloat16)
        return moved, sent

    def ocean_second(values, top, bottom, west, east):
        return values, jnp.zeros((flux_count, tile_rows, block_len), jnp.bfloat16)

    second, flux_sent = lax.cond(
        ocean_side, ocean_second, atmosphere_second, first, top, bottom, west, east
    )
    entry_list = intersection_list.reshape(tile_rows * intersections, 3)
    owners = entry_list[:, 0]
    targets = entry_list[:, 1]
    weight_ids = entry_list[:, 2]
    labels = weight_ids * tile_rows + targets
    entry_blocks = jnp.repeat(flux_sent.transpose(1, 0, 2), intersections, axis=0).reshape(
        tile_rows * intersections, width
    )
    lane = jnp.arange(128, dtype=jnp.int32)[None, :]
    label_lanes = jnp.where(
        lane == 0, weight_ids[:, None], jnp.where(lane == 1, targets[:, None], 0)
    ).astype(jnp.bfloat16)
    entry_blocks = jnp.concatenate([entry_blocks, label_lanes], axis=1)
    sending = jnp.broadcast_to(jnp.logical_not(ocean_side), owners.shape)
    offsets = [
        (n // reach * lon_count + n % reach - (reach - 1) // 2) % tile_count
        for n in range(neighbour_count)
    ]
    offset_table = jnp.array(offsets, jnp.int32)
    distance = (owners - tile_index + tile_count) % tile_count
    neighbour_ids = jnp.sum(
        jnp.where(
            distance[:, None] == offset_table[None, :],
            jnp.arange(neighbour_count, dtype=jnp.int32)[None, :],
            0,
        ),
        axis=1,
    )
    packed, _, entry_slots = pack_rows(entry_blocks, neighbour_ids, labels, sending, capacity, neighbour_count)
    arrived = gather_to_ocean(packed, offsets, mesh_shape)
    weights_low = regrid_weights
    weights_wide = regrid_weights.astype(jnp.float32)
    senders = (comp_count - 1) * neighbour_count

    def ocean_reply(values_top, arrived):
        flat = arrived.reshape(-1, width + 128)
        arrived_labels = flat[:, width].astype(jnp.int32) * tile_rows + flat[:, width + 1].astype(
            jnp.int32
        )
        fluxes = flat[:, :width].astype(jnp.float32).reshape(-1, flux_count, block_len)
        forcing = scatter_regrid(arrived_labels, fluxes, weights_low)
        forcing = forcing.reshape(tile_rows, flux_count, block_len).transpose(1, 0, 2)
        lifted = jnp.sum(forcing * ocean_map[:, 0][:, None, None], axis=0)
        top_level = jnp.where(sea_cells, values_top + lifted, state_top)
        table = jnp.einsum("db,wab->wda", top_level, weights_wide, precision=HIGHEST)
        replies = jnp.take(table.reshape(weight_count * tile_rows, block_len), arrived_labels, axis=0)
        return forcing, replies.reshape(senders, capacity, block_len), top_level

    def atmosphere_reply(values_top, arrived):
        return (
            jnp.zeros((flux_count, tile_rows, block_len), jnp.float32),
            jnp.zeros((senders, capacity, block_len), jnp.float32),
            values_top,
        )

    forcing, replies, ocean_top = lax.cond(
        ocean_side, ocean_reply, atmosphere_reply, first_top, arrived
    )
    atmosphere_top = lax.cond(
        ocean_side,
        lambda values: jnp.zeros((tile_rows, block_len), jnp.float32),
        lambda values: values[:, :, 0],
        second,
    )
    replies, atmosphere_top = lax.optimization_barrier((replies, atmosphere_top))
    answers = spread_from_ocean(replies, offsets, mesh_shape)
    per_entry = jnp.take(
        answers.reshape(neighbour_count * capacity, block_len), entry_slots, axis=0
    )
    returned = per_entry.reshape(tile_rows, intersections, block_len).sum(axis=1)
    second, forcing, answers = lax.optimization_barrier((second, forcing, answers))
    sea_rows = jnp.broadcast_to(
        sea_cells.astype(jnp.int32).reshape(1, tile_rows * block_len), (8, tile_rows * block_len)
    )
    final_state = ocean_update(
        second,
        state,
        sea_rows,
        forcing.reshape(flux_count, tile_rows * block_len),
        ocean_map,
        comp_count,
    )
    surface_out = jnp.where(
        ocean_side, ocean_top, jnp.where(sea_cells, returned, atmosphere_top)
    )
    return (final_state, surface_out)


def solution(mesh):
    placed = (
        P(("comp", "lat"), "lon", None),
        P(("comp", "lat"), "lon"),
        P(("comp", "lat"), "lon", None, None),
        P(),
        P(),
        P(),
        P(),
        P(),
    )
    return jax.shard_map(
        local,
        mesh=mesh,
        in_specs=placed,
        out_specs=(P(("comp", "lat"), "lon", None), P(("comp", "lat"), "lon")),
        check_vma=False,
    )
```

```python
import jax
import jax.numpy as jnp
from jax import lax
from jax.experimental import pallas as pl
from jax.experimental.pallas import tpu as pltpu
from jax.sharding import PartitionSpec as P
import functools

SMOOTHING = 0.2
PHYSICS = 0.5
HIGHEST = lax.Precision.HIGHEST
ROW_BLOCK = 32
UPDATE_BLOCK = 64


def split_bf16(values):
    high = values.astype(jnp.bfloat16)
    low = (values - high.astype(jnp.float32)).astype(jnp.bfloat16)
    return high, low


def three_pass(lhs, rhs, dims):
    lhs_hi, lhs_lo = split_bf16(lhs)
    rhs_hi, rhs_lo = split_bf16(rhs)

    def one(a, b):
        return lax.dot_general(a, b, (dims, ((), ())), preferred_element_type=jnp.float32)

    return one(lhs_hi, rhs_hi) + (one(lhs_hi, rhs_lo) + one(lhs_lo, rhs_hi))


def exact_rows(picker, values):
    high = values.astype(jnp.bfloat16)
    rest = values - high.astype(jnp.float32)
    middle = rest.astype(jnp.bfloat16)
    low = (rest - middle.astype(jnp.float32)).astype(jnp.bfloat16)

    def one(piece):
        return lax.dot_general(
            picker, piece, (((1,), (1,)), ((), ())), preferred_element_type=jnp.float32
        )

    return one(high) + one(middle) + one(low)


def substep_kernel(with_flux, comp_total, x_ref, top_ref, bottom_ref, west_ref, east_ref, mix_ref, *rest):
    if with_flux:
        fluxes_ref, out_ref, flux_out_ref = rest
    else:
        out_ref, planes_ref = rest
    rows, cols, levels = x_ref.shape
    centre = x_ref[...]
    up = jnp.concatenate([top_ref[...], centre[:-1]], axis=0)
    down = jnp.concatenate([centre[1:], bottom_ref[...]], axis=0)
    column = lax.broadcasted_iota(jnp.int32, centre.shape, 1)
    west = jnp.where(column == 0, west_ref[...], pltpu.roll(centre, 1, 1))
    east = jnp.where(column == cols - 1, east_ref[...], pltpu.roll(centre, cols - 1, 1))
    smooth = centre + SMOOTHING * (up + down + west + east - 4.0 * centre)
    flat = smooth.reshape(rows * cols, levels)
    mixed = three_pass(flat, mix_ref[...], ((1,), (0,)))
    moved = flat + PHYSICS * jnp.tanh(mixed)
    out_ref[...] = moved.reshape(rows, cols, levels)
    if not with_flux:
        ocean = lax.axis_index("comp") == comp_total - 1

        @pl.when(ocean)
        def _():
            plane_row = lax.broadcasted_iota(jnp.int32, (8, levels), 0)
            plane_lane = lax.broadcasted_iota(jnp.int32, (8, levels), 1)
            pick_out = ((plane_row == 0) & (plane_lane == 0)).astype(jnp.bfloat16)
            pick_in = ((plane_row == 1) & (plane_lane == 0)).astype(jnp.bfloat16)
            planes_ref[...] = exact_rows(pick_out, moved) + exact_rows(
                pick_in, centre.reshape(rows * cols, levels)
            )

        @pl.when(jnp.logical_not(ocean))
        def _():
            planes_ref[...] = jnp.zeros_like(planes_ref)

    else:
        total = centre.reshape(rows * cols, levels) + moved
        flux_out_ref[...] = three_pass(fluxes_ref[...], total, ((1,), (1,)))


def substep(values, top, bottom, west, east, mixing, comp_total, fluxes_t=None):
    rows, cols, levels = values.shape
    blocks = rows // ROW_BLOCK
    top_rows = jnp.concatenate([top, values[ROW_BLOCK - 1 : rows - 1 : ROW_BLOCK]], axis=0)
    bottom_rows = jnp.concatenate([values[ROW_BLOCK:rows:ROW_BLOCK], bottom], axis=0)
    with_flux = fluxes_t is not None
    in_specs = [
        pl.BlockSpec((ROW_BLOCK, cols, levels), lambda i: (i, 0, 0)),
        pl.BlockSpec((1, cols, levels), lambda i: (i, 0, 0)),
        pl.BlockSpec((1, cols, levels), lambda i: (i, 0, 0)),
        pl.BlockSpec((ROW_BLOCK, 1, levels), lambda i: (i, 0, 0)),
        pl.BlockSpec((ROW_BLOCK, 1, levels), lambda i: (i, 0, 0)),
        pl.BlockSpec((levels, levels), lambda i: (0, 0)),
    ]
    operands = [values, top_rows, bottom_rows, west, east, mixing]
    out_shape = [jax.ShapeDtypeStruct(values.shape, jnp.float32)]
    out_specs = [pl.BlockSpec((ROW_BLOCK, cols, levels), lambda i: (i, 0, 0))]
    if not with_flux:
        out_shape.append(jax.ShapeDtypeStruct((8, rows * cols), jnp.float32))
        out_specs.append(pl.BlockSpec((8, ROW_BLOCK * cols), lambda i: (0, i)))
    if with_flux:
        flux_count = fluxes_t.shape[0]
        in_specs.append(pl.BlockSpec((flux_count, levels), lambda i: (0, 0)))
        operands.append(fluxes_t)
        out_shape.append(jax.ShapeDtypeStruct((flux_count, rows * cols), jnp.float32))
        out_specs.append(pl.BlockSpec((flux_count, ROW_BLOCK * cols), lambda i: (0, i)))
    cells = rows * cols
    flops = 6 * cells * levels * levels + (6 * cells * levels * 8 if with_flux else 0)
    result = pl.pallas_call(
        functools.partial(substep_kernel, with_flux, comp_total),
        grid=(blocks,),
        in_specs=in_specs,
        out_specs=out_specs,
        out_shape=out_shape,
        cost_estimate=pl.CostEstimate(
            flops=flops, transcendentals=cells * levels, bytes_accessed=8 * cells * levels
        ),
    )(*operands)
    return result


def column_physics(values, mixing):
    return jnp.tanh(jnp.einsum("rck,kj->rcj", values, mixing, precision=HIGHEST))


def earlier_same(owners, usable):
    positions = jnp.arange(owners.shape[0], dtype=jnp.int32)
    before = (
        (owners[None, :] == owners[:, None])
        & (positions[None, :] < positions[:, None])
        & usable[None, :]
    )
    return jnp.sum(before.astype(jnp.int32), axis=1)


def pack_rows(blocks, owners, labels, usable, slots_each, owner_total):
    ranks = earlier_same(owners, usable)
    target_slot = owners * slots_each + ranks
    slot_ids = jnp.arange(owner_total * slots_each, dtype=jnp.int32)
    placing = (slot_ids[:, None] == target_slot[None, :]) & usable[None, :]
    packed = jnp.dot(
        placing.astype(jnp.bfloat16), blocks, preferred_element_type=jnp.float32
    ).astype(jnp.bfloat16)
    placed_labels = jnp.sum(jnp.where(placing, labels[None, :] + 1, 0), axis=1) - 1
    return (
        packed.reshape(owner_total, slots_each, blocks.shape[1]),
        placed_labels.reshape(owner_total, slots_each),
        target_slot,
    )


MESH_IDS = pl.DeviceIdType.MESH


def tile_device(comp, tile, lon_total):
    return (comp, tile // lon_total, tile % lon_total)


def gather_kernel(offsets, shape, send_ref, out_ref, land, send_sems, recv_sems):
    comp_total, lat_total, lon_total = shape
    comp = lax.axis_index("comp")
    tiles = lat_total * lon_total
    tile = lax.axis_index("lat") * lon_total + lax.axis_index("lon")
    ocean = comp_total - 1
    count = len(offsets)
    barrier = pltpu.get_barrier_semaphore()

    @pl.when(comp != ocean)
    def _():
        for off in offsets:
            target = tile_device(ocean, (tile + off) % tiles, lon_total)
            pl.semaphore_signal(barrier, 1, device_id=target, device_id_type=MESH_IDS)
        pl.semaphore_wait(barrier, count)
        copies = []
        for k, off in enumerate(offsets):
            target = tile_device(ocean, (tile + off) % tiles, lon_total)
            copy = pltpu.make_async_remote_copy(
                src_ref=send_ref.at[k],
                dst_ref=land.at[comp * count + k],
                send_sem=send_sems.at[k],
                recv_sem=recv_sems.at[comp * count + k],
                device_id=target,
                device_id_type=MESH_IDS,
            )
            copy.start()
            copies.append(copy)
        for copy in copies:
            copy.wait_send()
        out_ref[...] = jnp.zeros_like(out_ref)

    @pl.when(comp == ocean)
    def _():
        for source_comp in range(ocean):
            for off in offsets:
                source = tile_device(source_comp, (tile + tiles - off) % tiles, lon_total)
                pl.semaphore_signal(barrier, 1, device_id=source, device_id_type=MESH_IDS)
        pl.semaphore_wait(barrier, count * ocean)
        for source_comp in range(ocean):
            for k, off in enumerate(offsets):
                source = tile_device(source_comp, (tile + tiles - off) % tiles, lon_total)
                slot = source_comp * count + k
                pltpu.make_async_remote_copy(
                    src_ref=send_ref.at[k],
                    dst_ref=land.at[slot],
                    send_sem=send_sems.at[k],
                    recv_sem=recv_sems.at[slot],
                    device_id=source,
                    device_id_type=MESH_IDS,
                ).wait_recv()
        out_ref[...] = land[...]


def gather_to_ocean(blocks, offsets, shape):
    count = len(offsets)
    senders = (shape[0] - 1) * count
    slot_shape = blocks.shape[1:]
    return pl.pallas_call(
        functools.partial(gather_kernel, tuple(offsets), tuple(shape)),
        out_shape=jax.ShapeDtypeStruct((senders,) + slot_shape, blocks.dtype),
        in_specs=[pl.BlockSpec(memory_space=pltpu.VMEM)],
        out_specs=pl.BlockSpec(memory_space=pltpu.VMEM),
        scratch_shapes=[
            pltpu.VMEM((senders,) + slot_shape, blocks.dtype),
            pltpu.SemaphoreType.DMA((count,)),
            pltpu.SemaphoreType.DMA((senders,)),
        ],
        compiler_params=pltpu.CompilerParams(collective_id=0, has_side_effects=True),
    )(blocks)


def spread_kernel(offsets, shape, surface_ref, out_ref, land, send_sems, recv_sems):
    comp_total, lat_total, lon_total = shape
    comp = lax.axis_index("comp")
    tiles = lat_total * lon_total
    tile = lax.axis_index("lat") * lon_total + lax.axis_index("lon")
    ocean = comp_total - 1
    count = len(offsets)
    barrier = pltpu.get_barrier_semaphore()

    @pl.when(comp == ocean)
    def _():
        for target_comp in range(ocean):
            for off in offsets:
                target = tile_device(target_comp, (tile + tiles - off) % tiles, lon_total)
                pl.semaphore_signal(barrier, 1, device_id=target, device_id_type=MESH_IDS)
        pl.semaphore_wait(barrier, count * ocean)
        copies = []
        for target_comp in range(ocean):
            for k, off in enumerate(offsets):
                target = tile_device(target_comp, (tile + tiles - off) % tiles, lon_total)
                copy = pltpu.make_async_remote_copy(
                    src_ref=surface_ref.at[target_comp * count + k],
                    dst_ref=land.at[k],
                    send_sem=send_sems.at[target_comp * count + k],
                    recv_sem=recv_sems.at[k],
                    device_id=target,
                    device_id_type=MESH_IDS,
                )
                copy.start()
                copies.append(copy)
        for copy in copies:
            copy.wait_send()
        out_ref[...] = jnp.zeros_like(out_ref)

    @pl.when(comp != ocean)
    def _():
        for off in offsets:
            source = tile_device(ocean, (tile + off) % tiles, lon_total)
            pl.semaphore_signal(barrier, 1, device_id=source, device_id_type=MESH_IDS)
        pl.semaphore_wait(barrier, count)
        for k, off in enumerate(offsets):
            source = tile_device(ocean, (tile + off) % tiles, lon_total)
            pltpu.make_async_remote_copy(
                src_ref=surface_ref.at[k],
                dst_ref=land.at[k],
                send_sem=send_sems.at[k],
                recv_sem=recv_sems.at[k],
                device_id=source,
                device_id_type=MESH_IDS,
            ).wait_recv()
        out_ref[...] = land[...]


def spread_from_ocean(replies, offsets, shape):
    count = len(offsets)
    senders = (shape[0] - 1) * count
    slot_shape = replies.shape[1:]
    return pl.pallas_call(
        functools.partial(spread_kernel, tuple(offsets), tuple(shape)),
        out_shape=jax.ShapeDtypeStruct((count,) + slot_shape, replies.dtype),
        in_specs=[pl.BlockSpec(memory_space=pltpu.VMEM)],
        out_specs=pl.BlockSpec(memory_space=pltpu.VMEM),
        scratch_shapes=[
            pltpu.VMEM((count,) + slot_shape, replies.dtype),
            pltpu.SemaphoreType.DMA((senders,)),
            pltpu.SemaphoreType.DMA((count,)),
        ],
        compiler_params=pltpu.CompilerParams(collective_id=1, has_side_effects=True),
    )(replies)


def ocean_update_kernel(flag_ref, base_ref, state_ref, sea_ref, forcing_ref, spread_ref, out_ref):
    rows, cols, levels = base_ref.shape
    flux_count = forcing_ref.shape[0]

    def block(base_block, state_block, sea_block, forcing_block, out_block):
        ocean_block(base_block, state_block, sea_block, forcing_block, spread_ref, out_block)

    @pl.when(flag_ref[0] == 1)
    def _():
        pltpu.emit_pipeline(
            block,
            grid=(rows // UPDATE_BLOCK,),
            in_specs=[
                pl.BlockSpec((UPDATE_BLOCK, cols, levels), lambda i: (i, 0, 0)),
                pl.BlockSpec((UPDATE_BLOCK, cols, levels), lambda i: (i, 0, 0)),
                pl.BlockSpec((8, UPDATE_BLOCK * cols), lambda i: (0, i)),
                pl.BlockSpec((flux_count, UPDATE_BLOCK * cols), lambda i: (0, i)),
            ],
            out_specs=[pl.BlockSpec((UPDATE_BLOCK, cols, levels), lambda i: (i, 0, 0))],
        )(base_ref, state_ref, sea_ref, forcing_ref, out_ref)


def ocean_block(first_ref, state_ref, sea_ref, forcing_ref, spread_ref, out_ref):
    rows, cols, levels = first_ref.shape
    forcing = forcing_ref[...]
    spread = spread_ref[...]
    forcing_hi = forcing.astype(jnp.bfloat16)
    forcing_lo = (forcing - forcing_hi.astype(jnp.float32)).astype(jnp.bfloat16)
    spread_hi = spread.astype(jnp.bfloat16)
    spread_lo = (spread - spread_hi.astype(jnp.float32)).astype(jnp.bfloat16)

    def one(a, b):
        return lax.dot_general(a, b, (((0,), (0,)), ((), ())), preferred_element_type=jnp.float32)

    stacked = jnp.concatenate(
        [forcing_hi.astype(jnp.float32), forcing_hi.astype(jnp.float32), forcing_lo.astype(jnp.float32)],
        axis=0,
    ).astype(jnp.bfloat16)
    spread_stack = jnp.concatenate(
        [spread_hi.astype(jnp.float32), spread_lo.astype(jnp.float32), spread_hi.astype(jnp.float32)],
        axis=0,
    ).astype(jnp.bfloat16)
    added = one(stacked, spread_stack)
    lane_row = lax.broadcasted_iota(jnp.int32, (8, levels), 0)
    ones = (lane_row == 0).astype(jnp.bfloat16)
    picks = jnp.where(lax.broadcasted_iota(jnp.int32, sea_ref.shape, 0) == 0, sea_ref[...], 0)
    mask = one(picks.astype(jnp.bfloat16), ones)
    moved = first_ref[...].reshape(rows * cols, levels) + added
    kept = jnp.where(mask > 0.5, moved, state_ref[...].reshape(rows * cols, levels))
    out_ref[...] = kept.reshape(rows, cols, levels)


def ocean_update(first, state, sea_rows, forcing, ocean_map, comp_total):
    rows, cols, levels = first.shape
    flux_count = forcing.shape[0]
    cells = rows * cols
    flag = (lax.axis_index("comp") == comp_total - 1).astype(jnp.int32).reshape(1)
    return pl.pallas_call(
        ocean_update_kernel,
        out_shape=jax.ShapeDtypeStruct(first.shape, jnp.float32),
        in_specs=[
            pl.BlockSpec(memory_space=pltpu.SMEM),
            pl.BlockSpec(memory_space=pl.ANY),
            pl.BlockSpec(memory_space=pl.ANY),
            pl.BlockSpec(memory_space=pl.ANY),
            pl.BlockSpec(memory_space=pl.ANY),
            pl.BlockSpec(memory_space=pltpu.VMEM),
        ],
        out_specs=pl.BlockSpec(memory_space=pl.ANY),
        input_output_aliases={1: 0},
        cost_estimate=pl.CostEstimate(
            flops=8 * cells * levels * flux_count, transcendentals=0, bytes_accessed=12 * cells * levels
        ),
    )(flag, first, state, sea_rows, forcing, ocean_map)


def scatter_regrid_kernel(labels_ref, fluxes_ref, weights_ref, out_ref, binned_ref):
    entries = fluxes_ref.shape[0]
    weight_count, tile_rows, block_len = weights_ref.shape
    flux_count = fluxes_ref.shape[1]
    binned_ref[...] = jnp.zeros_like(binned_ref)

    def add_one(e, carry):
        label = labels_ref[e]
        binned_ref[label] = binned_ref[label] + fluxes_ref[e]
        return carry

    lax.fori_loop(0, entries, add_one, 0, unroll=8)
    out_ref[...] = jnp.zeros_like(out_ref)

    def regrid_one(w, carry):
        start = pl.multiple_of(w * tile_rows, tile_rows)
        block = binned_ref[pl.ds(start, tile_rows)].reshape(tile_rows * flux_count, block_len)
        high = block.astype(jnp.bfloat16)
        low = (block - high.astype(jnp.float32)).astype(jnp.bfloat16)
        weight = weights_ref[w]
        out_ref[...] += jnp.dot(high, weight, preferred_element_type=jnp.float32) + jnp.dot(
            low, weight, preferred_element_type=jnp.float32
        )
        return carry

    lax.fori_loop(0, weight_count, regrid_one, 0, unroll=4)


def scatter_regrid(labels, fluxes, weights):
    entries, flux_count, block_len = fluxes.shape
    weight_count, tile_rows, _ = weights.shape
    return pl.pallas_call(
        scatter_regrid_kernel,
        out_shape=jax.ShapeDtypeStruct((tile_rows * flux_count, block_len), jnp.float32),
        in_specs=[
            pl.BlockSpec(memory_space=pltpu.SMEM),
            pl.BlockSpec(memory_space=pltpu.VMEM),
            pl.BlockSpec(memory_space=pltpu.VMEM),
        ],
        out_specs=pl.BlockSpec(memory_space=pltpu.VMEM),
        scratch_shapes=[pltpu.VMEM((weight_count * tile_rows, flux_count, block_len), jnp.float32)],
        compiler_params=pltpu.CompilerParams(vmem_limit_bytes=48 * 1024 * 1024),
        cost_estimate=pl.CostEstimate(
            flops=4 * weight_count * tile_rows * flux_count * block_len * block_len,
            transcendentals=0,
            bytes_accessed=entries * flux_count * block_len * 4 + weight_count * tile_rows * block_len * 2,
        ),
    )(labels, fluxes, weights)


def halo_kernel(shape, values_ref, rows_out, cols_out, rows_land, cols_land, send_sems, recv_sems):
    comp_total, lat_total, lon_total = shape
    bands = comp_total * lat_total
    band = lax.axis_index("comp") * lat_total + lax.axis_index("lat")
    lon = lax.axis_index("lon")
    rows, cols, _ = values_ref.shape
    up = (band + 1) % bands
    down = (band + bands - 1) % bands
    up_device = (up // lat_total, up % lat_total, lon)
    down_device = (down // lat_total, down % lat_total, lon)
    east_device = (band // lat_total, band % lat_total, (lon + 1) % lon_total)
    west_device = (band // lat_total, band % lat_total, (lon + lon_total - 1) % lon_total)
    barrier = pltpu.get_barrier_semaphore()
    for device in (up_device, down_device, east_device, west_device):
        pl.semaphore_signal(barrier, 1, device_id=device, device_id_type=MESH_IDS)
    pl.semaphore_wait(barrier, 4)
    plan = [
        (values_ref.at[pl.ds(rows - 1, 1)], rows_land.at[0], up_device),
        (values_ref.at[pl.ds(0, 1)], rows_land.at[1], down_device),
        (values_ref.at[:, pl.ds(cols - 1, 1)], cols_land.at[0], east_device),
        (values_ref.at[:, pl.ds(0, 1)], cols_land.at[1], west_device),
    ]
    copies = []
    for slot, (source, target, device) in enumerate(plan):
        copy = pltpu.make_async_remote_copy(
            src_ref=source,
            dst_ref=target,
            send_sem=send_sems.at[slot],
            recv_sem=recv_sems.at[slot],
            device_id=device,
            device_id_type=MESH_IDS,
        )
        copy.start()
        copies.append(copy)
    for copy in copies:
        copy.wait_send()
    for copy in copies:
        copy.wait_recv()
    rows_out[...] = rows_land[...]
    cols_out[...] = cols_land[...]


def halo_edges(values, shape, collective):
    rows, cols, levels = values.shape
    return pl.pallas_call(
        functools.partial(halo_kernel, tuple(shape)),
        out_shape=(
            jax.ShapeDtypeStruct((2, 1, cols, levels), values.dtype),
            jax.ShapeDtypeStruct((2, rows, 1, levels), values.dtype),
        ),
        in_specs=[pl.BlockSpec(memory_space=pl.ANY)],
        out_specs=(
            pl.BlockSpec(memory_space=pltpu.VMEM),
            pl.BlockSpec(memory_space=pltpu.VMEM),
        ),
        scratch_shapes=[
            pltpu.VMEM((2, 1, cols, levels), values.dtype),
            pltpu.VMEM((2, rows, 1, levels), values.dtype),
            pltpu.SemaphoreType.DMA((4,)),
            pltpu.SemaphoreType.DMA((4,)),
        ],
        compiler_params=pltpu.CompilerParams(collective_id=collective, has_side_effects=True),
    )(values)


def local(
    state, land_mask, intersection_list, mix_atm, mix_ocn, flux_map, ocean_map, regrid_weights
):
    tile_rows, block_len, levels = state.shape
    flux_count = flux_map.shape[1]
    weight_count = regrid_weights.shape[0]
    intersections = intersection_list.shape[2]
    comp_count = lax.axis_size("comp")
    lat_count = lax.axis_size("lat")
    lon_count = lax.axis_size("lon")
    tile_count = lat_count * lon_count
    reach = min(4, lon_count)
    neighbour_count = 2 * reach
    capacity = intersections * tile_rows // neighbour_count
    width = flux_count * block_len
    comp_index = lax.axis_index("comp")
    tile_index = lax.axis_index("lat") * lon_count + lax.axis_index("lon")
    band = comp_index * lat_count + lax.axis_index("lat")
    ocean_band = (comp_count - 1) * lat_count
    ocean_side = comp_index == comp_count - 1
    lower_valid = (band > 0) & ((band - 1 >= ocean_band) == (band >= ocean_band))
    upper_valid = (band < comp_count * lat_count - 1) & (
        (band + 1 >= ocean_band) == (band >= ocean_band)
    )
    sea_cells = land_mask == 1

    mesh_shape = (comp_count, lat_count, lon_count)

    def halos(values, collective):
        rows, cols = halo_edges(values, mesh_shape, collective)
        top = jnp.where(lower_valid, rows[0], 0.0)
        bottom = jnp.where(upper_valid, rows[1], 0.0)
        return top, bottom, cols[0], cols[1]

    top, bottom, west, east = halos(state, 2)
    mixing = jnp.where(ocean_side, mix_ocn, mix_atm)
    first, first_planes = substep(state, top, bottom, west, east, mixing, comp_count)
    first_top = first_planes[0].reshape(tile_rows, block_len)
    state_top = first_planes[1].reshape(tile_rows, block_len)
    top, bottom, west, east = halos(first, 3)

    def atmosphere_second(values, top, bottom, west, east):
        moved, total = substep(values, top, bottom, west, east, mix_atm, comp_count, flux_map.T)
        total = total.reshape(flux_count, tile_rows, block_len)
        sent = jnp.where(sea_cells[None], 0.5 * total, 0.0).astype(jnp.bfloat16)
        return moved, sent

    def ocean_second(values, top, bottom, west, east):
        return values, jnp.zeros((flux_count, tile_rows, block_len), jnp.bfloat16)

    second, flux_sent = lax.cond(
        ocean_side, ocean_second, atmosphere_second, first, top, bottom, west, east
    )
    entry_list = intersection_list.reshape(tile_rows * intersections, 3)
    owners = entry_list[:, 0]
    targets = entry_list[:, 1]
    weight_ids = entry_list[:, 2]
    labels = weight_ids * tile_rows + targets
    entry_blocks = jnp.repeat(flux_sent.transpose(1, 0, 2), intersections, axis=0).reshape(
        tile_rows * intersections, width
    )
    lane = jnp.arange(128, dtype=jnp.int32)[None, :]
    label_lanes = jnp.where(
        lane == 0, weight_ids[:, None], jnp.where(lane == 1, targets[:, None], 0)
    ).astype(jnp.bfloat16)
    entry_blocks = jnp.concatenate([entry_blocks, label_lanes], axis=1)
    sending = jnp.broadcast_to(jnp.logical_not(ocean_side), owners.shape)
    offsets = [
        (n // reach * lon_count + n % reach - (reach - 1) // 2) % tile_count
        for n in range(neighbour_count)
    ]
    offset_table = jnp.array(offsets, jnp.int32)
    distance = (owners - tile_index + tile_count) % tile_count
    neighbour_ids = jnp.sum(
        jnp.where(
            distance[:, None] == offset_table[None, :],
            jnp.arange(neighbour_count, dtype=jnp.int32)[None, :],
            0,
        ),
        axis=1,
    )
    packed, _, entry_slots = pack_rows(entry_blocks, neighbour_ids, labels, sending, capacity, neighbour_count)
    arrived = gather_to_ocean(packed, offsets, mesh_shape)
    weights_low = regrid_weights
    weights_wide = regrid_weights.astype(jnp.float32)
    senders = (comp_count - 1) * neighbour_count

    def ocean_reply(values_top, arrived):
        flat = arrived.reshape(-1, width + 128)
        arrived_labels = flat[:, width].astype(jnp.int32) * tile_rows + flat[:, width + 1].astype(
            jnp.int32
        )
        fluxes = flat[:, :width].astype(jnp.float32).reshape(-1, flux_count, block_len)
        forcing = scatter_regrid(arrived_labels, fluxes, weights_low)
        forcing = forcing.reshape(tile_rows, flux_count, block_len).transpose(1, 0, 2)
        lifted = jnp.sum(forcing * ocean_map[:, 0][:, None, None], axis=0)
        top_level = jnp.where(sea_cells, values_top + lifted, state_top)
        table = jnp.einsum("db,wab->wda", top_level, weights_wide, precision=HIGHEST)
        replies = jnp.take(table.reshape(weight_count * tile_rows, block_len), arrived_labels, axis=0)
        return forcing, replies.reshape(senders, capacity, block_len), top_level

    def atmosphere_reply(values_top, arrived):
        return (
            jnp.zeros((flux_count, tile_rows, block_len), jnp.float32),
            jnp.zeros((senders, capacity, block_len), jnp.float32),
            values_top,
        )

    forcing, replies, ocean_top = lax.cond(
        ocean_side, ocean_reply, atmosphere_reply, first_top, arrived
    )
    atmosphere_top = lax.cond(
        ocean_side,
        lambda values: jnp.zeros((tile_rows, block_len), jnp.float32),
        lambda values: values[:, :, 0],
        second,
    )
    replies, atmosphere_top = lax.optimization_barrier((replies, atmosphere_top))
    answers = spread_from_ocean(replies, offsets, mesh_shape)
    per_entry = jnp.take(
        answers.reshape(neighbour_count * capacity, block_len), entry_slots, axis=0
    )
    returned = per_entry.reshape(tile_rows, intersections, block_len).sum(axis=1)
    second, forcing, answers = lax.optimization_barrier((second, forcing, answers))
    sea_rows = jnp.broadcast_to(
        sea_cells.astype(jnp.int32).reshape(1, tile_rows * block_len), (8, tile_rows * block_len)
    )
    final_state = ocean_update(
        second,
        state,
        sea_rows,
        forcing.reshape(flux_count, tile_rows * block_len),
        ocean_map,
        comp_count,
    )
    surface_out = jnp.where(
        ocean_side, ocean_top, jnp.where(sea_cells, returned, atmosphere_top)
    )
    return (final_state, surface_out)


def solution(mesh):
    placed = (
        P(("comp", "lat"), "lon", None),
        P(("comp", "lat"), "lon"),
        P(("comp", "lat"), "lon", None, None),
        P(),
        P(),
        P(),
        P(),
        P(),
    )
    return jax.shard_map(
        local,
        mesh=mesh,
        in_specs=placed,
        out_specs=(P(("comp", "lat"), "lon", None), P(("comp", "lat"), "lon")),
        check_vma=False,
    )
```
